32 devices in a mesh: rep: 4 (over y, core), shard: 8 (over z, x).
Axes of the slice: x: 2, y: 2, z: 4, core: 2. Of those that a mesh axis runs over, the one named last changes fastest.
Arguments:
- inputs: bfloat16 [32, 1024, 768], P(('rep', 'shard')), may hold values from -6 to 6
- piece_starts: int32 [32, 2], P(('rep', 'shard')), may hold values from 0 to 768
- routes: int32 [32, 1024, 2], P(('rep', 'shard')), may hold values from 0 to 3, all different within a row; in each aligned block of 1024 rows (0 to 1023, 1024 to 2047, ..., all dimensions but the last counted through in order) at most 576 rows name the same one
- attn_gain: bfloat16 [768], P('shard'), may hold values from 0.099609375 to 1.8984375
- query_weight: bfloat16 [768, 768], P('shard'), may hold values from -0.21875 to 0.21875
- key_weight: bfloat16 [768, 768], P('shard'), may hold values from -0.21875 to 0.21875
- value_weight: bfloat16 [768, 768], P('shard'), may hold values from -0.21875 to 0.21875
- out_weight: bfloat16 [768, 768], P('shard'), may hold values from -1.75 to 1.75
- ffn_gain: bfloat16 [768], P('shard'), may hold values from 0.099609375 to 1.8984375
- router_weight: bfloat16 [768, 4], P('shard'), may hold values from -0.21875 to 0.21875
- expert_gate: bfloat16 [4, 768, 2048], P(None, None, 'shard'), may hold values from -0.21875 to 0.21875
- expert_up: bfloat16 [4, 768, 2048], P(None, None, 'shard'), may hold values from -0.21875 to 0.21875
- expert_down: bfloat16 [4, 2048, 768], P(None, 'shard'), may hold values from -0.375 to 0.375
- shared_gate: bfloat16 [768, 2048], P(None, 'shard'), may hold values from -0.21875 to 0.21875
- shared_up: bfloat16 [768, 2048], P(None, 'shard'), may hold values from -0.21875 to 0.21875
- shared_down: bfloat16 [2048, 768], P('shard'), may hold values from -0.25 to 0.25
- cotangent: bfloat16 [32, 1024, 768], P(('rep', 'shard')), may hold values from -6 to 6
Outputs:
- outputs: bfloat16 [32, 1024, 768], P(('rep', 'shard'))
- grad_inputs: float32 [32, 1024, 768], P(('rep', 'shard'))
- grad_attn_gain: float32 [768], P('shard')
- grad_query: float32 [768, 768], P('shard')
- grad_key: float32 [768, 768], P('shard')
- grad_value: float32 [768, 768], P('shard')
- grad_out: float32 [768, 768], P('shard')
- grad_ffn_gain: float32 [768], P('shard')
- grad_router: float32 [768, 4], P('shard')
- grad_expert_gate: float32 [4, 768, 2048], P(None, None, 'shard')
- grad_expert_up: float32 [4, 768, 2048], P(None, None, 'shard')
- grad_expert_down: float32 [4, 2048, 768], P(None, 'shard')
- grad_shared_gate: float32 [768, 2048], P(None, 'shard')
- grad_shared_up: float32 [768, 2048], P(None, 'shard')
- grad_shared_down: float32 [2048, 768], P('shard')
The draws below stay inside these ranges and needn't reach their ends.
Inputs may be any that keep to these rules, and one draw needn't show every extreme that they name: `routes`: each token names 2 different experts. Among the 1024 tokens of one device (aligned blocks), every expert is named by at most 576 tokens, a bound that some block reaches.
All inputs are finite; a program needn't handle non-finite values.
Results may differ from the reference program's by a relative error of at most 0.019.
Values may be sent and summed in bfloat16 or wider, within the bound.
A program may use at most 384 MiB of HBM per device.

```python
import math
import jax
import jax.numpy as jnp
import numpy as np
from jax import lax

D = 768
HEADS = 12
HEAD_DIM = 64
FF = 2048
FS = 2048
EXPERTS = 4
TOP = 2
LEN = 1024
PIECE = 256
PIECES = 2
TOK_DEV = 1024
SEQS = 32
CAP = 576


def place_ends(drawn, stream_key, smallest, high):
    longest = drawn.shape.index(max(drawn.shape))
    spots = []
    for shift in (0, 1):
        where = [jax.random.randint(jax.random.fold_in(stream_key, axis), (), 0, length) for axis, length in enumerate(drawn.shape)]
        where[longest] = (where[longest] + shift) % drawn.shape[longest]
        spots.append(tuple(where))
    return drawn.at[spots[0]].set(smallest).at[spots[1]].set(high)


def levels(stream_key, shape, split, smallest, high):
    loudness, own = 1.0, jax.random.fold_in(stream_key, 6)
    for dim, parts in split:
        heights = jnp.exp(jax.random.uniform(jax.random.fold_in(own, dim), (parts,), jnp.float32, smallest / len(split), high / len(split)))
        loudness = loudness * jnp.repeat(heights, shape[dim] // parts).reshape([-1 if axis == dim else 1 for axis in range(len(shape))])
    return loudness


def routed_block(key, own, number, rows, number_of, top, reach, lean):
    ranking = jax.random.permutation(key, number_of)
    heavy_load, common = load_shares(number_of, rows * top, reach, lean, True), load_shares(number_of, rows * top, reach, lean, False)
    places = jnp.arange(number_of)

    def named(sizes, turn):
        used = int((sizes > 0).sum())
        fixed = max(1, used // 4)
        shifted = fixed + (places - fixed + turn * (used - fixed)) % max(1, number_of - fixed)
        return jnp.zeros((number_of,), jnp.int32).at[ranking[jnp.where(places < fixed, places, shifted)]].set(jnp.asarray(sizes, jnp.int32))

    sizes = jnp.where(number % 4 == 0, named(heavy_load, number // 4), named(common, number - number // 4 - 1))
    mixed = jax.random.permutation(jax.random.fold_in(own, 3), number_of)
    giver, taker = mixed[0:number_of // 2 * 2:2], mixed[1:number_of // 2 * 2:2]
    room = jnp.minimum(sizes[giver] - 1, reach - sizes[taker]) // 2
    room = jnp.where((giver == ranking[0]) | (taker == ranking[0]) | (sizes[taker] == 0), 0, jnp.maximum(room, 0))
    shifted = jax.random.randint(jax.random.fold_in(own, 4), (number_of // 2,), 0, 1 << 20) % (room + 1)
    sizes = sizes.at[giver].add(-shifted).at[taker].add(shifted)
    labels = jnp.searchsorted(jnp.cumsum(sizes), jnp.arange(rows * top), side="right").astype(jnp.int32)
    listing = labels.reshape(top, rows).T
    listing = listing[jax.random.permutation(jax.random.fold_in(own, 1), rows)]
    turn = jax.random.randint(jax.random.fold_in(own, 2), (rows, 1), 0, top)
    return jnp.take_along_axis(listing, (jnp.arange(top)[None, :] + turn) % top, axis=1)


def load_shares(amount, total, reach, skew, full):
    loads = [(1 << 20) // math.isqrt(standing ** skew) + 1 for standing in range(1, amount + 1)]
    largest = reach if full else min(reach, max(-(-total // amount), total * loads[0] // sum(loads)))
    least = 1 if total - largest >= amount - 1 else 0
    given, spare = [largest] + [least] * (amount - 1), total - largest - least * (amount - 1)
    while spare > 0:
        candidates = [i for i in range(1, amount) if given[i] < largest] or [i for i in range(1, amount) if given[i] < reach]
        pool, remaining = sum([loads[i] for i in candidates]), spare
        for i in candidates:
            addition = min(reach - given[i], max(1, remaining * loads[i] // pool), spare)
            given[i] = given[i] + addition
            spare = spare - addition
    return np.array(given)


def centred(own_key, extent, spread, most, pieces=(), kind=jnp.bfloat16):
    level = levels(own_key, extent, pieces, -0.22, 0.18) if pieces else 1.0
    values = jax.random.normal(own_key, extent, jnp.float32) * spread * level
    return jnp.minimum(jnp.maximum(values, -most), most).astype(kind)


def setup_inputs(seed: int = 0) -> dict:
    streams_of = jax.random.split(jax.random.key(seed), 18)
    inputs = centred(streams_of[0], (SEQS, LEN, D), 1.0, 6.0, ((0, 32),))
    piece_starts = place_ends(jax.random.randint(streams_of[1], (SEQS, PIECES), 0, LEN - PIECE + 1), jax.random.fold_in(streams_of[1], 1), 0, LEN - PIECE).astype(jnp.int32)
    routes_keys = jax.random.split(jax.random.fold_in(streams_of[2], 1), SEQS * LEN // TOK_DEV)
    routes_turns = jax.random.permutation(jax.random.fold_in(streams_of[2], 3), SEQS * LEN // TOK_DEV)
    routes = jax.vmap(lambda own, number: routed_block(jax.random.fold_in(streams_of[2], 2), own, number, TOK_DEV, EXPERTS, TOP, CAP, 1))(routes_keys, routes_turns).reshape((SEQS, LEN, TOP))
    attn_gain = jnp.clip(1.0 + 0.18 * jax.random.normal(streams_of[3], (D,), jnp.float32), 0.099609375, 1.8984375).astype(jnp.bfloat16)
    query_weight = centred(streams_of[4], (D, D), D ** -0.5, 0.21875, ((0, 8),))
    key_weight = centred(streams_of[5], (D, D), D ** -0.5, 0.21875, ((0, 8),))
    value_weight = centred(streams_of[6], (D, D), D ** -0.5, 0.21875, ((0, 8),))
    out_weight = centred(streams_of[7], (D, D), (max(D // 64, 1)) ** -0.5, 1.75, ((0, 8),))
    ffn_gain = jnp.clip(1.0 + 0.18 * jax.random.normal(streams_of[8], (D,), jnp.float32), 0.099609375, 1.8984375).astype(jnp.bfloat16)
    router_weight = centred(streams_of[9], (D, EXPERTS), D ** -0.5, 0.21875, ((0, 8),))
    expert_gate = centred(streams_of[10], (EXPERTS, D, FF), D ** -0.5, 0.21875, ((2, 8),))
    expert_up = centred(streams_of[11], (EXPERTS, D, FF), D ** -0.5, 0.21875, ((2, 8),))
    expert_down = centred(streams_of[12], (EXPERTS, FF, D), (FF // 8) ** -0.5, 0.375, ((1, 8),))
    shared_gate = centred(streams_of[13], (D, FS), D ** -0.5, 0.21875, ((1, 8),))
    shared_up = centred(streams_of[14], (D, FS), D ** -0.5, 0.21875, ((1, 8),))
    shared_down = centred(streams_of[15], (FS, D), (FS // 4) ** -0.5, 0.25, ((0, 8),))
    cotangent = centred(streams_of[16], (SEQS, LEN, D), 1.0, 6.0, ((0, 32),))
    return {"inputs": inputs, "piece_starts": piece_starts, "routes": routes, "attn_gain": attn_gain, "query_weight": query_weight, "key_weight": key_weight, "value_weight": value_weight, "out_weight": out_weight, "ffn_gain": ffn_gain, "router_weight": router_weight, "expert_gate": expert_gate, "expert_up": expert_up, "expert_down": expert_down, "shared_gate": shared_gate, "shared_up": shared_up, "shared_down": shared_down, "cotangent": cotangent}


@jax.custom_vjp
def low(v):
    return lax.optimization_barrier(v.astype(jnp.bfloat16)).astype(jnp.float32)

@jax.custom_vjp
def low_back(v):
    return v

def low_keep(v):
    return (low(v), None)

def low_pass(kept, grad):
    return (grad,)

def back_keep(v):
    return (v, None)

def back_low(kept, grad):
    return (low(grad),)
low.defvjp(low_keep, low_pass)
low_back.defvjp(back_keep, back_low)
epsilon = 1e-06
masked_score = -1e+30
precise = lax.Precision.HIGHEST

def rms_normed(tensor, gain_row):
    return tensor * lax.rsqrt(lax.optimization_barrier(jnp.mean(tensor * tensor, axis=-1, keepdims=True)) + epsilon) * gain_row

def rope_tables():
    positions = jnp.arange(LEN, dtype=jnp.float32)
    inverse_freq = 10000.0 ** (-2.0 * jnp.arange(HEAD_DIM // 2, dtype=jnp.float32) / HEAD_DIM)
    angle_table = positions[:, None] * inverse_freq[None, :]
    return (jnp.cos(angle_table)[:, None, :], jnp.sin(angle_table)[:, None, :])

def rotate(tensor, cosine_table, sine_table):
    half_dim = tensor.shape[-1] // 2
    first_half = tensor[..., :half_dim]
    second_half = tensor[..., half_dim:]
    return jnp.concatenate([first_half * cosine_table - second_half * sine_table, second_half * cosine_table + first_half * sine_table], axis=-1)

def allowed_mask(query_pos, key_pos, starts):
    causal = key_pos[None, :] <= query_pos[:, None]
    query_in = (query_pos[None, :] >= starts[:, None]) & (query_pos[None, :] < starts[:, None] + PIECE)
    key_in = (key_pos[None, :] >= starts[:, None]) & (key_pos[None, :] < starts[:, None] + PIECE)
    return causal | jnp.any(query_in[:, :, None] & key_in[:, None, :], axis=0)

def attend_one(entry):
    query_rot, key_rot, value_heads, starts = entry
    positions = jnp.arange(LEN)
    scores = low_back(jnp.einsum('qhd,khd->hqk', query_rot, key_rot, precision=precise) * HEAD_DIM ** (-0.5))
    scores = jnp.where(allowed_mask(positions, positions, starts)[None], scores, masked_score)
    attn_probs = low(jax.nn.softmax(scores, axis=-1))
    mixed = jnp.einsum('hqk,khd->qhd', attn_probs, value_heads, precision=precise)
    return mixed.reshape(LEN, HEADS * HEAD_DIM)

def swiglu(normed, gate_mat, up_mat, down_mat):
    gate_h = low_back(jnp.einsum('gld,df->glf', normed, gate_mat, precision=precise))
    up_h = low_back(jnp.einsum('gld,df->glf', normed, up_mat, precision=precise))
    hidden = low(jax.nn.silu(gate_h) * up_h)
    return low_back(jnp.einsum('glf,fd->gld', hidden, down_mat, precision=precise))

def forward_group(inputs, starts, routes, attn_gain, query_weight, key_weight, value_weight, out_weight, ffn_gain, router_weight, expert_gate, expert_up, expert_down, shared_gate, shared_up, shared_down):
    per_group = inputs.shape[0]
    head_shape = (per_group, LEN, HEADS, HEAD_DIM)
    cosine_table, sine_table = rope_tables()
    normed_one = low(rms_normed(inputs, attn_gain))

    def project(weight):
        return jnp.einsum('gld,de->gle', normed_one, weight, precision=precise)
    query_rot = low(rotate(low_back(project(query_weight)).reshape(head_shape), cosine_table, sine_table))
    key_rot = low(rotate(low_back(project(key_weight)).reshape(head_shape), cosine_table, sine_table))
    value_heads = low(low_back(project(value_weight))).reshape(head_shape)
    attended = lax.map(jax.checkpoint(attend_one), (query_rot, key_rot, value_heads, starts))
    attended = low(low_back(attended))
    middle = inputs + low_back(jnp.einsum('gld,de->gle', attended, out_weight, precision=precise))
    normed_two = low(rms_normed(middle, ffn_gain))
    logits = low_back(jnp.einsum('gld,de->gle', normed_two, router_weight, precision=precise))
    router_probs = jax.nn.softmax(logits, axis=-1)
    chosen = lax.optimization_barrier(jnp.sum((routes[..., None] == jnp.arange(EXPERTS)).astype(jnp.float32), axis=-2))
    gate_probs = router_probs * chosen
    mixture = swiglu(normed_two, shared_gate, shared_up, shared_down)
    for expert in range(EXPERTS):
        expert_out = swiglu(normed_two, expert_gate[expert], expert_up[expert], expert_down[expert])
        mixture = mixture + gate_probs[..., expert:expert + 1] * expert_out
    return middle + mixture

def reference(inputs, piece_starts, routes, attn_gain, query_weight, key_weight, value_weight, out_weight, ffn_gain, router_weight, expert_gate, expert_up, expert_down, shared_gate, shared_up, shared_down, cotangent):
    weights = tuple((weight.astype(jnp.float32) for weight in (attn_gain, query_weight, key_weight, value_weight, out_weight, ffn_gain, router_weight, expert_gate, expert_up, expert_down, shared_gate, shared_up, shared_down)))
    per_group = math.gcd(SEQS, 4)
    group_count = SEQS // per_group
    stacked = (inputs.astype(jnp.float32).reshape(group_count, per_group, LEN, D), piece_starts.reshape(group_count, per_group, PIECES), routes.reshape(group_count, per_group, LEN, TOP), cotangent.astype(jnp.float32).reshape(group_count, per_group, LEN, D))

    def advance(running, element):
        group_inputs, group_starts, group_routes, group_cot = element

        def run_layer(layer_inputs, *params):
            return forward_group(layer_inputs, group_starts, group_routes, *params)
        result, pullback = jax.vjp(run_layer, group_inputs, *weights)
        grad_list = pullback(group_cot)
        running = tuple((before + after for before, after in zip(running, grad_list[1:])))
        return (running, (result.astype(jnp.bfloat16), grad_list[0]))
    initial = tuple((jnp.zeros_like(weight) for weight in weights))
    totals, (results, grad_groups) = lax.scan(advance, initial, stacked)
    return (results.reshape(SEQS, LEN, D), grad_groups.reshape(SEQS, LEN, D), totals[0], totals[1], totals[2], totals[3], totals[4], totals[5], totals[6], totals[7], totals[8], totals[9], totals[10], totals[11], totals[12])
```

```python
import functools

import jax
import jax.numpy as jnp
from jax import lax
from jax.experimental import pallas as pl
from jax.experimental.pallas import tpu as pltpu
from jax.sharding import PartitionSpec as P

HEADS = 12
PIECE = 256
CAP = 576
EPSILON = 1e-06
MASKED = -1e30
F32, BF = jnp.float32, jnp.bfloat16
AXES = ("rep", "shard")
TILE = 256
SLOTS = 8
VMEM_LIMIT = 62 * 2**20
ANY = pl.BlockSpec(memory_space=pl.ANY)
SMEM = pl.BlockSpec(memory_space=pltpu.SMEM)
VMEM = pl.BlockSpec(memory_space=pltpu.VMEM)


def dot(a, b, i, j):
    return lax.dot_general(a, b, (((i,), (j,)), ((), ())), preferred_element_type=F32)


def nn(a, b):
    return dot(a, b, 1, 0)


def nt(a, b):
    return dot(a, b, 1, 1)


def tn(a, b):
    return dot(a, b, 0, 0)


def iota(shape, dim):
    return lax.broadcasted_iota(jnp.int32, shape, dim)


def ones_where(cond):
    return jnp.where(cond, 1.0, 0.0).astype(BF)


def call(kernel, out_shape, in_specs, out_specs, scratch=(), flops=0, moved=0, grid=None):
    extra = {} if grid is None else {"grid": grid}
    return pl.pallas_call(
        kernel,
        out_shape=out_shape,
        in_specs=in_specs,
        out_specs=out_specs,
        scratch_shapes=list(scratch),
        compiler_params=pltpu.CompilerParams(vmem_limit_bytes=VMEM_LIMIT),
        cost_estimate=pl.CostEstimate(flops=flops, bytes_accessed=moved, transcendentals=0),
        **extra,
    )


def shape(dims, dtype=BF):
    return jax.ShapeDtypeStruct(dims, dtype)


def permute(x, move):
    reps, shards = lax.axis_size("rep"), lax.axis_size("shard")
    pairs = []
    for r in range(reps):
        for s in range(shards):
            to_r, to_s = move(r, s)
            pairs.append((r * shards + s, to_r * shards + to_s))
    return lax.ppermute(x, AXES, pairs)


def to_rep(x, offset):
    return permute(x, lambda r, s: (r ^ offset, s))


def to_x(x):
    return permute(x, lambda r, s: (r, s ^ 1))


def to_z(x, d):
    shards = lax.axis_size("shard")
    return permute(x, lambda r, s: (r, (s + 2 * d) % shards))


def after(x, dep):
    return lax.optimization_barrier((x, dep))[0]


def gather_slots(piece):
    near = [piece] + [to_z(piece, -d) for d in (1, 2, 3)]
    return near + [to_x(part) for part in near]


def scatter_slots(parts):
    far = [to_x(parts[4 + d]) for d in range(4)]
    near = [(parts[d].astype(F32) + far[d].astype(F32)) for d in range(4)]
    got = [to_z(near[d].astype(BF), d).astype(F32) for d in (1, 2, 3)]
    return near[0] + got[0] + got[1] + got[2]


def prep_kernel(info, routes, routes_t, cot, rank_out, slot_out, *packed):
    tokens = cot.shape[0]
    rep = info[0]
    first, second = routes_t[0:1, :], routes_t[1:2, :]
    expert = iota((8, tokens), 0)
    chosen = (expert == first) | (expert == second)
    upper = ones_where(iota((tokens, tokens), 0) <= iota((tokens, tokens), 1))
    rank = nn(ones_where(chosen), upper) - 1.0
    rank_out[...] = jnp.where(chosen, rank, -1.0)
    lane = iota((tokens, 128), 1)
    one, two = routes[:, 0:1], routes[:, 1:2]
    lower = ones_where(iota((tokens, tokens), 0) >= iota((tokens, tokens), 1))
    place = nn(lower, ones_where((lane == one) | (lane == two))) - 1.0
    place = place + ((lane ^ rep) * CAP).astype(F32)
    slot_one = jnp.sum(jnp.where(lane == one, place, 0.0), axis=1, keepdims=True)
    slot_two = jnp.sum(jnp.where(lane == two, place, 0.0), axis=1, keepdims=True)
    slot_out[...] = jnp.where(lane < 64, slot_one, slot_two)
    for o, out in enumerate(packed):
        row = rank_out[pl.ds(rep ^ o, 1), :]
        pick = ones_where(iota((CAP, tokens), 0).astype(F32) == row)
        out[...] = nn(pick, cot[...]).astype(BF)


def spin(block, cosine, sine):
    lane = iota(block.shape, 1)
    partner = jnp.where(lane % 64 < 32, pltpu.roll(block, 96, 1), pltpu.roll(block, 32, 1))
    return block * cosine + partner * sine


def qkv_kernel(
    info, x, own, other, cosine, sine, q, k, v, wq, wk, wv, wo, ext, ext_all, sems
):
    tokens, width = x.shape
    rows = own.shape[1] - 16
    half = rows // 2

    def copies(low, high):
        made = []
        for j in range(SLOTS):
            at = pl.ds(pl.multiple_of(info[2 + j] * half, 32), half)
            made.append((low.at[j, pl.ds(0, half)], wq.at[at]))
            made.append((low.at[j, pl.ds(half, half)], wk.at[at]))
            made.append((low.at[j, pl.ds(rows, 16)], ext_all.at[j]))
            made.append((high.at[j, pl.ds(0, half)], wv.at[at]))
            made.append((high.at[j, pl.ds(half, half)], wo.at[at]))
        return [pltpu.make_async_copy(a, b, sems.at[i]) for i, (a, b) in enumerate(made)]

    @pl.when(info[1] == 0)
    def _():
        for copy in copies(own, other):
            copy.start()

    @pl.when(info[1] != 0)
    def _():
        for copy in copies(other, own):
            copy.start()

    for copy in copies(own, other):
        copy.wait()
    gathered = ext_all[0].astype(F32)
    for j in range(1, SLOTS):
        gathered = gathered + ext_all[j].astype(F32)
    ext[...] = gathered
    gain = gathered[4:5, :]

    def tile(t, carry):
        at = pl.ds(pl.multiple_of(t * TILE, TILE), TILE)
        rows_in = x[at, :].astype(F32)
        scale = lax.rsqrt(jnp.mean(rows_in * rows_in, axis=1, keepdims=True) + EPSILON)
        normed = (rows_in * scale * gain).astype(BF)
        cos_t, sin_t = cosine[at, :], sine[at, :]
        for weight, out, factor in ((wq, q, 0.125), (wk, k, 1.0)):
            full = nn(normed, weight[...])
            for b in range(width // 128):
                turned = spin(full[:, b * 128 : (b + 1) * 128], cos_t, sin_t)
                out[at, b * 128 : (b + 1) * 128] = turned.astype(BF) * jnp.asarray(factor, BF)
        v[at, :] = nn(normed, wv[...]).astype(BF)
        return carry

    lax.fori_loop(0, tokens // TILE, tile, 0)


def fill_bias(starts, bias):
    tokens = bias.shape[0]

    def tile(t, carry):
        at = pl.ds(pl.multiple_of(t * TILE, TILE), TILE)
        query = iota((TILE, tokens), 0) + t * TILE
        key = iota((TILE, tokens), 1)
        allowed = key <= query
        for n in range(2):
            begin = starts[0, n]
            inside = (query >= begin) & (query < begin + PIECE)
            allowed = allowed | (inside & (key >= begin) & (key < begin + PIECE))
        bias[at, :] = jnp.where(allowed, 0.0, MASKED)
        return carry

    lax.fori_loop(0, tokens // TILE, tile, 0)


def keep_half(block, h):
    low = iota(block.shape, 1) < 64
    return jnp.where(low if h == 0 else ~low, block.astype(F32), 0.0).astype(BF)


def biased(scores, bias, begin, free, end):
    tail = scores[:, free:] + bias[begin : begin + TILE, free:end]
    return tail if free == 0 else jnp.concatenate([scores[:, :free], tail], axis=1)


def attend_kernel(starts, q, k, v, out, lse, bias):
    tokens = q.shape[0]

    @pl.when(pl.program_id(0) == 0)
    def _():
        fill_bias(starts, bias)

    keys = k[...]
    low = iota((tokens, 128), 1) < 64
    values = v[...].astype(F32)
    value_one = [
        jnp.where(low, values, 1.0).astype(BF),
        jnp.where(low, 1.0, values).astype(BF),
    ]
    low = iota((TILE, 128), 1) < 64
    for t in range(tokens // TILE):
        begin = t * TILE
        end = min(tokens, begin + TILE + PIECE)
        block = q[begin : begin + TILE, :]
        results, totals = [], []
        for h in range(2):
            scores = nt(keep_half(block, h), keys[:end])
            scores = biased(scores, bias, begin, begin, end)
            row_max = jnp.max(scores, axis=1, keepdims=True)
            probs = jnp.exp(scores - row_max).astype(BF)
            mixed = nn(probs, value_one[h][:end])
            total = pltpu.roll(mixed, 64, 1)
            results.append(mixed / total)
            totals.append(row_max + jnp.log(total))
        out[begin : begin + TILE, :] = jnp.where(low, results[0], results[1]).astype(BF)
        lse[begin : begin + TILE, :] = jnp.where(low, totals[0], totals[1])


def router_rows(ext):
    rows = jnp.where(iota(ext.shape, 0) < 4, ext[...], 0.0)
    return jnp.concatenate([rows, jnp.zeros((112, ext.shape[1]), F32)], axis=0).astype(BF)


def route_probs(normed, router):
    logits = nt(normed, router)
    logits = jnp.where(iota(logits.shape, 1) < 4, logits, MASKED)
    raised = jnp.exp(logits - jnp.max(logits, axis=1, keepdims=True))
    return raised / jnp.sum(raised, axis=1, keepdims=True)


def middle_kernel(info, x, attended, wo, ext, rank, middle, normed, probs, *packed):
    tokens = x.shape[0]
    rep = info[0]
    gain = ext[5:6, :]
    router = router_rows(ext)

    def tile(t, carry):
        at = pl.ds(pl.multiple_of(t * TILE, TILE), TILE)
        rows = x[at, :].astype(F32) + nn(attended[at, :], wo[...])
        scale = lax.rsqrt(jnp.mean(rows * rows, axis=1, keepdims=True) + EPSILON)
        middle[at, :] = rows
        unit = (rows * scale * gain).astype(BF)
        normed[at, :] = unit
        probs[at, :] = route_probs(unit, router)
        return carry

    lax.fori_loop(0, tokens // TILE, tile, 0)
    for o, out in enumerate(packed):
        row = rank[pl.ds(rep ^ o, 1), :]
        pick = ones_where(iota((CAP, tokens), 0).astype(F32) == row)
        out[...] = nn(pick, normed[...]).astype(BF)


CHUNK = 512


def ffn_kernel(blocks, weights, unit, routed, chained, *refs):
    refs = list(refs)

    def take(n):
        taken = refs[:n]
        del refs[:n]
        return taken

    info, ext = take(2)
    xs, cs = take(blocks), take(blocks)
    slots = take(weights)
    before = take(weights) if chained else None
    outs, dxs = take(blocks), take(blocks)
    grads = take(weights)
    out_acc, dx_acc, gate, wbuf, dw_acc, dw_out = take(6)
    prior = take(1)[0] if chained else None
    in_sems, out_sems = take(2)
    prior_sems = take(1)[0] if chained else None
    rows = xs[0].shape[0]
    per = CHUNK // unit
    chunks = 4

    def pieces(k, banks):
        return [(banks[i // SLOTS], i % SLOTS) for i in range(k * per, (k + 1) * per)]

    def view(bank, j):
        return bank

    def ref_of(banks, k, i):
        n = k * per + i
        if weights == SLOTS:
            return banks[n]
        return banks[n % 2].at[n // 2]

    def loads(banks, buffer, sems, k, b):
        return [
            pltpu.make_async_copy(
                ref_of(banks, k, i), buffer.at[b, :, :, pl.ds(i * unit, unit)], sems.at[b, i]
            )
            for i in range(per)
        ]

    def stores(k, b):
        return [
            pltpu.make_async_copy(
                dw_out.at[b, :, :, pl.ds(i * unit, unit)], ref_of(grads, k, i), out_sems.at[b, i]
            )
            for i in range(per)
        ]

    def start_loads(k, b):
        for copy in loads(slots, wbuf, in_sems, k, b):
            copy.start()
        if chained:
            for copy in loads(before, prior, prior_sems, k, b):
                copy.start()

    start_loads(0, 0)
    if routed:
        router = router_rows(ext)
        for n in range(blocks):
            probs = route_probs(xs[n][...], router)
            lane = iota(probs.shape, 1)
            gate[n] = jnp.sum(jnp.where(lane == info[0], probs, 0.0), axis=1, keepdims=True)

    def chunk(k, carry):
        b = lax.rem(k, 2)
        for nxt in range(1, chunks):

            @pl.when(k + 1 == nxt)
            def _():
                start_loads(nxt, nxt % 2)

        for copy in loads(slots, wbuf, in_sems, 0, b):
            copy.wait()
        for n in range(blocks):
            x, c = xs[n][...], cs[n][...]
            wg, wu, wd = wbuf[b, 0], wbuf[b, 1], wbuf[b, 2]
            gate_h, up_h, back_h = nn(x, wg), nn(x, wu), nn(c, wd)
            sigma = 1.0 / (1.0 + jnp.exp(-gate_h))
            silu = gate_h * sigma
            hidden = silu * up_h
            if routed:
                share = gate[n]
                scaled = back_h * share
                weighted = (hidden * share).astype(BF)
            else:
                scaled, weighted = back_h, hidden.astype(BF)
            d_up = (scaled * silu).astype(BF)
            d_gate = (scaled * up_h * (sigma + silu * (1.0 - sigma))).astype(BF)
            product = nt(hidden.astype(BF), wd)
            d_rows = nt(d_gate, wg) + nt(d_up, wu)
            parts = (tn(x, d_gate), tn(x, d_up), tn(c, weighted))
            if routed:
                pairs = (hidden * back_h).astype(BF)
                d_share = nt(jnp.ones((16, CHUNK), BF), pairs)

            @pl.when(k == 0)
            def _():
                out_acc[n] = product
                dx_acc[n, 0:rows, :] = d_rows
                if routed:
                    dx_acc[n, rows : rows + 16, :] = jnp.zeros((16, d_rows.shape[1]), F32)
                    dx_acc[n, rows : rows + 16, 0:rows] = d_share

            @pl.when(k != 0)
            def _():
                out_acc[n] += product
                dx_acc[n, 0:rows, :] += d_rows
                if routed:
                    dx_acc[n, rows : rows + 16, 0:rows] += d_share

            for i in range(3):
                if n == 0:
                    dw_acc[i] = parts[i]
                else:
                    dw_acc[i] += parts[i]

        @pl.when(k >= 2)
        def _():
            for copy in stores(0, b):
                copy.wait()

        if chained:
            for copy in loads(before, prior, prior_sems, 0, b):
                copy.wait()
            for i in range(3):
                dw_out[b, i] = (dw_acc[i] + prior[b, i].astype(F32)).astype(BF)
        else:
            for i in range(3):
                dw_out[b, i] = dw_acc[i].astype(BF)
        for now in range(chunks):

            @pl.when(k == now)
            def _():
                for copy in stores(now, now % 2):
                    copy.start()

        return carry

    lax.fori_loop(0, chunks, chunk, 0)
    for n in range(blocks):
        outs[n][...] = out_acc[n].astype(BF)
        dxs[n][...] = dx_acc[n].astype(BF)
    for b in range(2):
        for copy in stores(0, b):
            copy.wait()


def ffn(info, ext, xs, cs, slots, before, unit, routed):
    blocks, rows, width = len(xs), xs[0].shape[0], xs[0].shape[1]
    chained = before is not None
    extra = 16 if routed else 0
    weights = len(slots)
    per = CHUNK // unit
    operands = [info, ext, *xs, *cs, *slots] + (list(before) if chained else [])
    in_specs = [SMEM, VMEM] + [VMEM] * (2 * blocks) + [ANY] * (weights * (2 if chained else 1))
    outs = [shape((rows, width))] * blocks + [shape((rows + extra, width))] * blocks
    outs += [shape(w.shape) for w in slots]
    out_specs = [VMEM] * (2 * blocks) + [ANY] * weights
    scratch = [
        pltpu.VMEM((blocks, rows, width), F32),
        pltpu.VMEM((blocks, rows + extra, width), F32),
        pltpu.VMEM((blocks, rows, 1), F32),
        pltpu.VMEM((2, 3, width, CHUNK), BF),
        pltpu.VMEM((3, width, CHUNK), F32),
        pltpu.VMEM((2, 3, width, CHUNK), BF),
    ]
    if chained:
        scratch.append(pltpu.VMEM((2, 3, width, CHUNK), BF))
    scratch += [pltpu.SemaphoreType.DMA((2, per)), pltpu.SemaphoreType.DMA((2, per))]
    if chained:
        scratch.append(pltpu.SemaphoreType.DMA((2, per)))
    results = call(
        functools.partial(ffn_kernel, blocks, weights, unit, routed, chained),
        outs,
        in_specs,
        out_specs,
        scratch,
        flops=18 * blocks * rows * width * 4 * CHUNK,
        moved=30 * 2**20,
    )(*operands)
    return results[:blocks], results[blocks : 2 * blocks], results[2 * blocks :]


def combine_kernel(
    info, slot, d0, d1, d2, d3, d_shared, probs, middle, normed, cot, ext, attended, wo,
    d_middle, d_attended, grad_wo, grad_ext, branch, router_acc, gain_acc,
):
    tokens, width = middle.shape
    rep = info[0]
    gain = ext[5:6, :]
    router = router_rows(ext)
    router_acc[...] = jnp.zeros_like(router_acc)
    gain_acc[...] = jnp.zeros_like(gain_acc)

    def tile(t, carry):
        at = pl.ds(pl.multiple_of(t * TILE, TILE), TILE)
        slot_one, slot_two = slot[at, 0:1], slot[at, 64:65]
        d_normed = d_shared[at, :].astype(F32)
        lane = iota((TILE, 128), 1)
        d_gates = jnp.zeros((TILE, 128), F32)
        for o, d in enumerate((d0, d1, d2, d3)):
            place = (iota((TILE, CAP), 1) + o * CAP).astype(F32)
            hit = (place == slot_one) | (place == slot_two)
            d_normed = d_normed + nn(ones_where(hit), d[0:CAP, :])
            share = d[CAP : CAP + 16, 0:CAP].astype(F32)[0:1, :]
            d_share = jnp.sum(jnp.where(hit, share, 0.0), axis=1, keepdims=True)
            d_gates = d_gates + jnp.where(lane == (rep ^ o), d_share, 0.0)
        p = probs[at, :]
        inner = jnp.sum(d_gates * p, axis=1, keepdims=True)
        d_logits = (p * (d_gates - inner)).astype(BF)
        d_normed = d_normed + nn(d_logits, router)
        router_acc[...] += tn(d_logits, normed[at, :])
        rows = middle[at, :]
        scale = lax.rsqrt(jnp.mean(rows * rows, axis=1, keepdims=True) + EPSILON)
        unit = rows * scale
        gain_acc[...] += jnp.sum((d_normed * unit).reshape(TILE // 8, 8, width), axis=0)
        w = d_normed * gain
        inner = jnp.mean(w * unit, axis=1, keepdims=True)
        total = cot[at, :].astype(F32) + scale * (w - unit * inner)
        d_middle[at, :] = total
        rounded = total.astype(BF)
        branch[at, :] = rounded
        d_attended[at, :] = nt(rounded, wo[...]).astype(BF)
        return carry

    lax.fori_loop(0, tokens // TILE, tile, 0)
    grad_wo[...] = tn(attended[...], branch[...]).astype(BF)
    row = iota((16, width), 0)
    total = jnp.sum(gain_acc[...], axis=0, keepdims=True)
    grad_ext[...] = jnp.where(row < 4, router_acc[0:16, :], jnp.where(row == 5, total, 0.0))


def output_kernel(info, slot, o0, o1, o2, o3, shared, probs, middle, out):
    tokens = middle.shape[0]
    rep = info[0]

    def tile(t, carry):
        at = pl.ds(pl.multiple_of(t * TILE, TILE), TILE)
        slot_one, slot_two = slot[at, 0:1], slot[at, 64:65]
        total = middle[at, :] + shared[at, :].astype(F32)
        p = probs[at, :]
        lane = iota((TILE, 128), 1)
        for o, rows in enumerate((o0, o1, o2, o3)):
            place = (iota((TILE, CAP), 1) + o * CAP).astype(F32)
            hit = (place == slot_one) | (place == slot_two)
            share = jnp.sum(jnp.where(lane == (rep ^ o), p, 0.0), axis=1, keepdims=True)
            total = total + nn(jnp.where(hit, share, 0.0).astype(BF), rows[...])
        out[at, :] = total.astype(BF)
        return carry

    lax.fori_loop(0, tokens // TILE, tile, 0)


def attend_back_kernel(
    starts, q, k, v, d_out, out, lse, cosine, sine, dq, dk, dv, bias, dk_acc, dv_acc
):
    tokens = q.shape[0]

    @pl.when(pl.program_id(0) == 0)
    def _():
        fill_bias(starts, bias)

    keys, values = k[...], v[...]
    half_keys = [keep_half(keys, 0), keep_half(keys, 1)]
    dk_acc[...] = jnp.zeros_like(dk_acc)
    dv_acc[...] = jnp.zeros_like(dv_acc)
    low = iota((TILE, 128), 1) < 64
    for t in range(tokens // TILE):
        begin = t * TILE
        end = min(tokens, begin + TILE + PIECE)
        at = slice(begin, begin + TILE)
        block, grad = q[at, :], d_out[at, :]
        product = grad.astype(F32) * out[at, :].astype(F32)
        block_lse = lse[at, :]
        d_block = None
        for h in range(2):
            block_h, grad_h = keep_half(block, h), keep_half(grad, h)
            scores = nt(block_h, keys[:end])
            scores = biased(scores, bias, begin, begin, end)
            probs = jnp.exp(scores - block_lse[:, 64 * h : 64 * h + 1])
            d_probs = nt(grad_h, values[:end])
            inner = jnp.sum(
                jnp.where(low if h == 0 else ~low, product, 0.0), axis=1, keepdims=True
            )
            d_scores = (probs * (d_probs - inner)).astype(BF)
            part = nn(d_scores, half_keys[h][:end])
            d_block = part if d_block is None else d_block + part
            dk_acc[0:end, :] += tn(d_scores, block_h)
            dv_acc[0:end, :] += tn(probs.astype(BF), grad_h)
        dq[at, :] = spin(d_block * 0.125, cosine[at, :], -sine[at, :]).astype(BF)
    dk[...] = spin(dk_acc[...], cosine[...], -sine[...]).astype(BF)
    dv[...] = dv_acc[...].astype(BF)


def tail_kernel(
    info, x, ext, dq, dk, dv, wq, wk, wv, d_middle, grad_wo, grad_ext,
    grad_in, mine, theirs, normed_all, gw, gain_acc,
):
    tokens, width = x.shape
    gain = ext[4:5, :]
    gain_acc[...] = jnp.zeros_like(gain_acc)

    def tile(t, carry):
        at = pl.ds(pl.multiple_of(t * TILE, TILE), TILE)
        rows = x[at, :].astype(F32)
        scale = lax.rsqrt(jnp.mean(rows * rows, axis=1, keepdims=True) + EPSILON)
        unit = rows * scale
        normed_all[at, :] = (unit * gain).astype(BF)
        d_normed = nt(dq[at, :], wq[...]) + nt(dk[at, :], wk[...]) + nt(dv[at, :], wv[...])
        gain_acc[...] += jnp.sum((d_normed * unit).reshape(TILE // 8, 8, width), axis=0)
        w = d_normed * gain
        inner = jnp.mean(w * unit, axis=1, keepdims=True)
        grad_in[at, :] = d_middle[at, :] + scale * (w - unit * inner)
        return carry

    lax.fori_loop(0, tokens // TILE, tile, 0)
    for i, d in enumerate((dq, dk, dv)):
        gw[i] = tn(normed_all[...], d[...]).astype(BF)
    row = iota((16, width), 0)
    total = jnp.sum(gain_acc[...], axis=0, keepdims=True)
    small = (grad_ext[...] + jnp.where(row == 4, total, 0.0)).astype(BF)
    half = width // SLOTS

    def fill(low, high):
        for j in range(SLOTS):
            at = pl.ds(pl.multiple_of(info[2 + j] * half, 32), half)
            low[j, 0:half, :] = gw[0, at, :]
            low[j, half : 2 * half, :] = gw[1, at, :]
            low[j, 2 * half : 2 * half + 16, :] = small
            high[j, 0:half, :] = gw[2, at, :]
            high[j, half : 2 * half, :] = grad_wo[at, :]
            high[j, 2 * half : 2 * half + 16, :] = jnp.zeros((16, width), BF)

    @pl.when(info[1] == 0)
    def _():
        fill(mine, theirs)

    @pl.when(info[1] != 0)
    def _():
        fill(theirs, mine)


def rope_tables(length, head_dim):
    positions = jnp.arange(length, dtype=F32)
    inverse_freq = 10000.0 ** (-2.0 * jnp.arange(head_dim // 2, dtype=F32) / head_dim)
    angle = positions[:, None] * inverse_freq[None, :]
    cosine, sine = jnp.cos(angle), jnp.sin(angle)
    return (
        jnp.concatenate([cosine] * 4, axis=1),
        jnp.concatenate([-sine, sine, -sine, sine], axis=1),
    )


def body(
    inputs,
    piece_starts,
    routes,
    attn_gain,
    query_weight,
    key_weight,
    value_weight,
    out_weight,
    ffn_gain,
    router_weight,
    expert_gate,
    expert_up,
    expert_down,
    shared_gate,
    shared_up,
    shared_down,
    cotangent,
):
    _, tokens, width = inputs.shape
    shards = lax.axis_size("shard")
    rep, shard = lax.axis_index("rep"), lax.axis_index("shard")
    core = rep % 2
    ringed = shards == SLOTS
    rows = width // shards
    units = shared_gate.shape[1]
    x, cot, chosen = inputs[0], cotangent[0], routes[0]
    if ringed:
        z, x_side = shard // 2, shard % 2
        order = [((z + d) % 4) * 2 + (x_side ^ b) for b in range(2) for d in range(4)]
    else:
        order = list(range(SLOTS))
    info = jnp.stack([jnp.asarray(n, jnp.int32) for n in [rep, core] + order])

    small = jnp.concatenate([router_weight.T, attn_gain[None], ffn_gain[None]], axis=0)
    small = jnp.pad(small, ((0, 10), (0, 0)))
    small = lax.dynamic_update_slice(jnp.zeros((16, width), BF), small, (0, shard * rows))
    blank = jnp.zeros((16, width), BF)
    if ringed:
        half_one = jnp.concatenate([query_weight, key_weight, small], axis=0)
        half_two = jnp.concatenate([value_weight, out_weight, blank], axis=0)
        piece = jnp.where(core == 0, half_one, half_two)
        attn_parts = gather_slots(piece)
        attn_own = jnp.stack(attn_parts)
        attn_other = to_rep(attn_own, 1)
    else:
        full = [
            lax.all_gather(w, "shard", axis=0, tiled=True).reshape(SLOTS, -1, width)
            for w in (query_weight, key_weight, value_weight, out_weight)
        ]
        small = lax.psum(small.astype(F32), "shard").astype(BF)
        small = jnp.concatenate([small[None], jnp.zeros((7, 16, width), BF)], axis=0)
        half_one = jnp.concatenate([full[0], full[1], small], axis=1)
        half_two = jnp.concatenate([full[2], full[3], jnp.zeros_like(small)], axis=1)
        attn_own = jnp.where(core == 0, half_one, half_two)
        attn_other = jnp.where(core == 0, half_two, half_one)

    shared_pack = jnp.stack([shared_gate, shared_up, shared_down.T])
    my_half = lax.dynamic_slice_in_dim(shared_pack, core * (units // 2), units // 2, 2)
    expert_pack = jnp.stack([expert_gate[rep], expert_up[rep], expert_down[rep].T])
    if ringed:
        my_half = after(my_half, attn_own)
        shared_own = jnp.stack(gather_slots(my_half))
        shared_other = to_rep(shared_own, 1)
        expert_pack = after(expert_pack, shared_own)
        expert_slots = gather_slots(expert_pack)
    else:

        def slotted(part):
            every = lax.all_gather(part, "shard")
            every = every.reshape(SLOTS, shards // SLOTS, 3, width, part.shape[2])
            return every.transpose(0, 2, 3, 1, 4).reshape(SLOTS, 3, width, -1)

        shared_own = slotted(my_half)
        shared_other = to_rep(shared_own, 1)
        expert_every = slotted(expert_pack)
        expert_slots = [expert_every[j] for j in range(SLOTS)]

    packed = [shape((CAP, width))] * 4
    rank, slot, *cot_out = call(
        prep_kernel,
        [shape((8, tokens), F32), shape((tokens, 128), F32)] + packed,
        [SMEM, VMEM, VMEM, VMEM],
        [VMEM] * 6,
        flops=2 * tokens * width * CAP * 4,
        moved=8 * 2**20,
    )(info, chosen, chosen.T, cot)
    cot_in = [cot_out[0]] + [to_rep(cot_out[o], o) for o in (1, 2, 3)]

    cosine, sine = rope_tables(tokens, width // HEADS)
    token_f = shape((tokens, width))
    square = shape((width, width))
    q, k, v, wq, wk, wv, wo, ext = call(
        qkv_kernel,
        [token_f] * 3 + [square] * 4 + [shape((16, width), F32)],
        [SMEM, VMEM, ANY, ANY, VMEM, VMEM],
        [VMEM] * 8,
        [pltpu.VMEM((SLOTS, 16, width), BF), pltpu.SemaphoreType.DMA((5 * SLOTS,))],
        flops=6 * tokens * width * width,
        moved=16 * 2**20,
    )(info, x, attn_own, attn_other, cosine, sine)

    pair = pl.BlockSpec((tokens, 128), lambda i: (0, i))
    table = pl.BlockSpec((tokens, 128), lambda i: (0, 0))
    attended, lse = call(
        attend_kernel,
        [token_f, shape((tokens, width), F32)],
        [SMEM, pair, pair, pair],
        [pair, pair],
        [pltpu.VMEM((tokens, tokens), F32)],
        flops=16 * tokens * tokens * width,
        moved=10 * 2**20,
        grid=(width // 128,),
    )(piece_starts, q, k, v)

    middle, normed, probs, *x_out = call(
        middle_kernel,
        [shape((tokens, width), F32), token_f, shape((tokens, 128), F32)] + packed,
        [SMEM] + [VMEM] * 5,
        [VMEM] * 7,
        flops=2 * tokens * width * (width + CAP * 4),
        moved=14 * 2**20,
    )(info, x, attended, wo, ext, rank)

    x_in = [x_out[0]] + [to_rep(x_out[o], o) for o in (1, 2, 3)]
    shared_out, shared_dx, shared_grads = ffn(
        info,
        ext,
        [normed],
        [cot],
        [shared_own, shared_other],
        None,
        units // 2 if ringed else 128,
        False,
    )
    unit = units if ringed else 256
    far_out, far_dx, far_grads = ffn(
        info, ext, x_in[2:], cot_in[2:], expert_slots, None, unit, True
    )
    far_dx = [to_rep(far_dx[0], 2), to_rep(far_dx[1], 3)]
    near_out, near_dx, grads = ffn(
        info, ext, x_in[:2], cot_in[:2], expert_slots, far_grads, unit, True
    )
    d_rows = [near_dx[0], to_rep(near_dx[1], 1)] + far_dx
    out_rows = [near_out[0], to_rep(near_out[1], 1), to_rep(far_out[0], 2), to_rep(far_out[1], 3)]

    d_middle, d_attended, grad_wo, grad_ext = call(
        combine_kernel,
        [shape((tokens, width), F32), token_f, square, shape((16, width), F32)],
        [SMEM] + [VMEM] * 13,
        [VMEM] * 4,
        [
            pltpu.VMEM((tokens, width), BF),
            pltpu.VMEM((128, width), F32),
            pltpu.VMEM((8, width), F32),
        ],
        flops=2 * tokens * width * (2 * width + 4 * CAP),
        moved=24 * 2**20,
    )(info, slot, *d_rows, shared_dx[0], probs, middle, normed, cot, ext, attended, wo)
    outputs = call(
        output_kernel,
        token_f,
        [SMEM] + [VMEM] * 8,
        VMEM,
        flops=2 * tokens * width * 4 * CAP,
        moved=12 * 2**20,
    )(info, slot, *out_rows, shared_out[0], probs, middle)

    dq, dk, dv = call(
        attend_back_kernel,
        [token_f] * 3,
        [SMEM] + [pair] * 6 + [table] * 2,
        [pair] * 3,
        [
            pltpu.VMEM((tokens, tokens), F32),
            pltpu.VMEM((tokens, 128), F32),
            pltpu.VMEM((tokens, 128), F32),
        ],
        flops=40 * tokens * tokens * width,
        moved=14 * 2**20,
        grid=(width // 128,),
    )(piece_starts, q, k, v, d_attended, attended, lse, cosine, sine)

    grad_rows = shape((SLOTS, 2 * (width // SLOTS) + 16, width))
    grad_in, mine, theirs = call(
        tail_kernel,
        [shape((tokens, width), F32), grad_rows, grad_rows],
        [SMEM] + [VMEM] * 11,
        [VMEM] * 3,
        [
            pltpu.VMEM((tokens, width), BF),
            pltpu.VMEM((3, width, width), BF),
            pltpu.VMEM((8, width), F32),
        ],
        flops=12 * tokens * width * width,
        moved=24 * 2**20,
    )(info, x, ext, dq, dk, dv, wq, wk, wv, d_middle, grad_wo, grad_ext)

    def over_rep(total):
        total = total.astype(BF)
        return [total] + [to_rep(total, o) for o in (1, 2, 3)]

    def absolute(parts, dtype):
        stacked = jnp.stack(parts)
        return jnp.take(stacked, jnp.arange(4) ^ rep, axis=0).astype(dtype)

    def unslot(every, part_units):
        every = every.reshape(SLOTS, 3, width, shards // SLOTS, part_units)
        every = every.transpose(0, 3, 1, 2, 4).reshape(shards, 3, width, part_units)
        return lax.psum_scatter(every, "shard", scatter_dimension=0)

    shared_sum = shared_grads[0].astype(F32) + to_rep(shared_grads[1], 1).astype(F32)
    if ringed:
        shared_sum = shared_sum.astype(BF)
        shared_total = scatter_slots([shared_sum[j] for j in range(SLOTS)])
        expert_total = scatter_slots(grads)
    else:
        shared_total = unslot(shared_sum.astype(BF), units // 2).astype(F32)
        expert_total = unslot(jnp.stack(grads), units).astype(F32)
    shared_total = shared_total + to_rep(shared_total.astype(BF), 2).astype(F32)
    shared_pair = to_rep(shared_total.astype(BF), 1).astype(F32)
    shared_low = jnp.where(core == 0, shared_total, shared_pair)
    shared_high = jnp.where(core == 0, shared_pair, shared_total)
    shared_full = jnp.concatenate([shared_low, shared_high], axis=2)
    expert_full = absolute(over_rep(expert_total), F32)

    summed = mine.astype(F32) + to_rep(theirs, 1).astype(F32)
    if ringed:
        summed = summed.astype(BF)
        far = to_x(summed[4:])
        near = summed[:4].astype(F32) + far.astype(F32)
        near_low = near.astype(BF)
        attn_total = near[0]
        for d in (1, 2, 3):
            attn_total = attn_total + to_z(near_low[d], d).astype(F32)
    else:
        half = width // SLOTS
        summed = summed.astype(BF)
        one = lax.psum_scatter(summed[:, :half].reshape(width, width), "shard", tiled=True)
        two = lax.psum_scatter(
            summed[:, half : 2 * half].reshape(width, width), "shard", tiled=True
        )
        three = lax.psum(summed[0, 2 * half :].astype(F32), "shard")
        attn_total = jnp.concatenate([one.astype(F32), two.astype(F32), three], axis=0)
    attn_total = attn_total + to_rep(attn_total.astype(BF), 2).astype(F32)
    attn_pair = to_rep(attn_total.astype(BF), 1).astype(F32)
    first = jnp.where(core == 0, attn_total, attn_pair)
    second = jnp.where(core == 0, attn_pair, attn_total)
    tiny = lax.dynamic_slice(first[2 * rows :], (0, shard * rows), (16, rows))
    return (
        outputs[None],
        grad_in[None],
        tiny[4],
        first[:rows],
        first[rows : 2 * rows],
        second[:rows],
        second[rows : 2 * rows],
        tiny[5],
        tiny[:4].T,
        expert_full[:, 0],
        expert_full[:, 1],
        expert_full[:, 2].transpose(0, 2, 1),
        shared_full[0],
        shared_full[1],
        shared_full[2].T,
    )


def solution(mesh):
    in_specs = (
        P(("rep", "shard"), None, None),
        P(("rep", "shard"), None),
        P(("rep", "shard"), None, None),
        P("shard"),
        P("shard", None),
        P("shard", None),
        P("shard", None),
        P("shard", None),
        P("shard"),
        P("shard", None),
        P(None, None, "shard"),
        P(None, None, "shard"),
        P(None, "shard", None),
        P(None, "shard"),
        P(None, "shard"),
        P("shard", None),
        P(("rep", "shard"), None, None),
    )
    out_specs = (
        P(("rep", "shard"), None, None),
        P(("rep", "shard"), None, None),
        P("shard"),
        P("shard", None),
        P("shard", None),
        P("shard", None),
        P("shard", None),
        P("shard"),
        P("shard", None),
        P(None, None, "shard"),
        P(None, None, "shard"),
        P(None, "shard", None),
        P(None, "shard"),
        P(None, "shard"),
        P("shard", None),
    )
    return jax.shard_map(body, mesh=mesh, in_specs=in_specs, out_specs=out_specs, check_vma=False)
```

```python
import functools

import jax
import jax.numpy as jnp
from jax import lax
from jax.experimental import pallas as pl
from jax.experimental.pallas import tpu as pltpu
from jax.sharding import PartitionSpec as P

HEADS = 12
PIECE = 256
CAP = 576
EPSILON = 1e-06
MASKED = -1e30
F32, BF = jnp.float32, jnp.bfloat16
AXES = ("rep", "shard")
TILE = 256
SLOTS = 8
VMEM_LIMIT = 62 * 2**20
ANY = pl.BlockSpec(memory_space=pl.ANY)
SMEM = pl.BlockSpec(memory_space=pltpu.SMEM)
VMEM = pl.BlockSpec(memory_space=pltpu.VMEM)


def dot(a, b, i, j):
    return lax.dot_general(a, b, (((i,), (j,)), ((), ())), preferred_element_type=F32)


def nn(a, b):
    return dot(a, b, 1, 0)


def nt(a, b):
    return dot(a, b, 1, 1)


def tn(a, b):
    return dot(a, b, 0, 0)


def iota(shape, dim):
    return lax.broadcasted_iota(jnp.int32, shape, dim)


def ones_where(cond):
    return jnp.where(cond, 1.0, 0.0).astype(BF)


def call(
    kernel, out_shape, in_specs, out_specs, scratch=(), flops=0, moved=0, grid=None, group=None
):
    extra = {} if grid is None else {"grid": grid}
    params = {} if group is None else {"collective_id": group, "has_side_effects": True}
    return pl.pallas_call(
        kernel,
        out_shape=out_shape,
        in_specs=in_specs,
        out_specs=out_specs,
        scratch_shapes=list(scratch),
        compiler_params=pltpu.CompilerParams(vmem_limit_bytes=VMEM_LIMIT, **params),
        cost_estimate=pl.CostEstimate(flops=flops, bytes_accessed=moved, transcendentals=0),
        **extra,
    )


def shape(dims, dtype=BF):
    return jax.ShapeDtypeStruct(dims, dtype)


def permute(x, move):
    reps, shards = lax.axis_size("rep"), lax.axis_size("shard")
    pairs = []
    for r in range(reps):
        for s in range(shards):
            to_r, to_s = move(r, s)
            pairs.append((r * shards + s, to_r * shards + to_s))
    return lax.ppermute(x, AXES, pairs)


def to_rep(x, offset):
    return permute(x, lambda r, s: (r ^ offset, s))


def to_x(x):
    return permute(x, lambda r, s: (r, s ^ 1))


def to_z(x, d):
    shards = lax.axis_size("shard")
    return permute(x, lambda r, s: (r, (s + 2 * d) % shards))


def after(x, dep):
    return lax.optimization_barrier((x, dep))[0]


def gather_slots(piece):
    near = [piece] + [to_z(piece, -d) for d in (1, 2, 3)]
    return near + [to_x(part) for part in near]


def scatter_slots(parts):
    far = [to_x(parts[4 + d]) for d in range(4)]
    near = [(parts[d].astype(F32) + far[d].astype(F32)) for d in range(4)]
    got = [to_z(near[d].astype(BF), d).astype(F32) for d in (1, 2, 3)]
    return near[0] + got[0] + got[1] + got[2]


def spin(block, cosine, sine):
    lane = iota(block.shape, 1)
    partner = jnp.where(lane % 64 < 32, pltpu.roll(block, 96, 1), pltpu.roll(block, 32, 1))
    return block * cosine + partner * sine


def sibling(rep, o):
    return 2 * lax.rem(lax.div(rep, 2) + o // 2, 2) + lax.rem(lax.rem(rep, 2) + o % 2, 2)


def route_slots(rep, routes, routes_t, rank_out, slot_out):
    tokens = routes.shape[0]
    first, second = routes_t[0:1, :], routes_t[1:2, :]
    expert = iota((8, tokens), 0)
    chosen = (expert == first) | (expert == second)
    upper = ones_where(iota((tokens, tokens), 0) <= iota((tokens, tokens), 1))
    rank = nn(ones_where(chosen), upper) - 1.0
    rank_out[...] = jnp.where(chosen, rank, -1.0)
    lane = iota((tokens, 128), 1)
    one, two = routes[:, 0:1], routes[:, 1:2]
    lower = ones_where(iota((tokens, tokens), 0) >= iota((tokens, tokens), 1))
    place = nn(lower, ones_where((lane == one) | (lane == two))) - 1.0
    for o in range(1, 4):
        place = place + jnp.where(lane == sibling(rep, o), float(o * CAP), 0.0)
    slot_one = jnp.sum(jnp.where(lane == one, place, 0.0), axis=1, keepdims=True)
    slot_two = jnp.sum(jnp.where(lane == two, place, 0.0), axis=1, keepdims=True)
    slot_out[...] = jnp.where(lane < 64, slot_one, slot_two)


def pack_rows(rep, rank, source, packed):
    tokens = source.shape[0]
    for o, out in enumerate(packed):
        row = rank[pl.ds(sibling(rep, o), 1), :]
        pick = ones_where(iota((CAP, tokens), 0).astype(F32) == row)
        out[...] = nn(pick, source[...]).astype(BF)


def qkv_rows(x, ext, cosine, sine, wq, wk, wv, q, k, v):
    tokens, width = x.shape
    gain = ext[4:5, :]

    def tile(t, carry):
        at = pl.ds(pl.multiple_of(t * TILE, TILE), TILE)
        rows_in = x[at, :].astype(F32)
        scale = lax.rsqrt(jnp.mean(rows_in * rows_in, axis=1, keepdims=True) + EPSILON)
        normed = (rows_in * scale * gain).astype(BF)
        cos_t, sin_t = cosine[at, :], sine[at, :]
        for weight, out, factor in ((wq, q, 0.125), (wk, k, 1.0)):
            full = nn(normed, weight[...])
            for b in range(width // 128):
                turned = spin(full[:, b * 128 : (b + 1) * 128], cos_t, sin_t)
                out[at, b * 128 : (b + 1) * 128] = turned.astype(BF) * jnp.asarray(factor, BF)
        v[at, :] = nn(normed, wv[...]).astype(BF)
        return carry

    lax.fori_loop(0, tokens // TILE, tile, 0)


def when(cond, body):
    if cond is True:
        body()
    elif cond is not False:
        pl.when(cond)(body)


def both(one, two):
    if one is True or two is False:
        return two
    if two is True or one is False:
        return one
    return one & two


class Line:
    def __init__(self, rep, shard, bank, send, recv):
        self.rep, self.shard, self.bank = rep, shard, bank
        self.core, self.z = lax.rem(rep, 2), lax.div(shard, 2)
        self.x = lax.rem(shard, 2)
        self.send, self.recv = send, recv
        self.mate = rep + 1 - 2 * self.core
        self.across = shard + 1 - 2 * self.x
        self.started = []

    def near(self, k):
        if k == 0:
            return self.shard, True
        if k > 0:
            return lax.min(self.shard + 2 * k, 6 + self.x), self.z < 4 - k
        return lax.max(self.shard + 2 * k, self.x), self.z >= -k

    def copy(self, way, k, source, half, place, rep, shard):
        event = way * 7 + k + 3
        return pltpu.make_async_remote_copy(
            src_ref=source,
            dst_ref=self.bank.at[half, place],
            send_sem=self.send.at[event],
            recv_sem=self.recv.at[event],
            device_id=(rep, shard),
            device_id_type=pl.DeviceIdType.MESH,
        )

    def start(self, cond, way, k, source, half, place, rep, shard):
        copy = self.copy(way, k, source, half, place, rep, shard)
        when(cond, copy.start)
        self.started.append((cond, copy))

    def spread(self, k, source):
        place, here = self.near(k)
        if k <= 0 and k > -3:
            up, more = self.near(1)
            self.start(both(here, more), 0, k - 1, source, self.core, place, self.rep, up)
        if k >= 0 and k < 3:
            down, more = self.near(-1)
            self.start(both(here, more), 0, k + 1, source, self.core, place, self.rep, down)
        self.start(here, 1, k, source, self.core, place, self.rep, self.across)
        self.start(here, 2, k, source, self.core, place, self.mate, self.shard)

    def arrive(self, cond, way, k, half, place):
        copy = self.copy(way, k, self.bank.at[half, place], half, place, self.mate, self.shard)
        when(cond, copy.wait_recv)

    def along(self, k):
        place, here = self.near(k)
        self.arrive(here, 0, k, self.core, place)
        self.spread(k, self.bank.at[self.core, place])

    def over(self, k):
        place, here = self.near(k)
        place = place + 1 - 2 * self.x
        self.arrive(here, 1, k, self.core, place)
        piece = self.bank.at[self.core, place]
        self.start(here, 3, k, piece, self.core, place, self.mate, self.shard)

    def finish(self):
        for k in (0, 1, -1, 2, -2, 3, -3):
            place, here = self.near(k)
            self.arrive(here, 2, k, 1 - self.core, place)
            self.arrive(here, 3, k, 1 - self.core, place + 1 - 2 * self.x)
        for cond, copy in self.started:
            when(cond, copy.wait_send)


def meet(rep, shard, z_ways, others):
    barrier = pltpu.get_barrier_semaphore()
    z, x = lax.div(shard, 2), lax.rem(shard, 2)
    count = len(others)
    for to_rep_, to_shard in others:
        pl.semaphore_signal(
            barrier, inc=1, device_id=(to_rep_, to_shard), device_id_type=pl.DeviceIdType.MESH
        )
    if z_ways:
        for cond, to_shard in (
            (z < 3, lax.min(shard + 2, 6 + x)),
            (z > 0, lax.max(shard - 2, x)),
        ):

            @pl.when(cond)
            def _():
                pl.semaphore_signal(
                    barrier, inc=1, device_id=(rep, to_shard), device_id_type=pl.DeviceIdType.MESH
                )

        count = count + lax.min(z, 1) + lax.min(3 - z, 1)
    pl.semaphore_wait(barrier, count)


def head_kernel(
    routes, routes_t, cot, x, piece, cosine, sine,
    rank, slot, c0, c1, c2, c3, q, k, v, wq, wk, wv, wo, ext,
    bank, send, recv, own_sem,
):
    width = x.shape[1]
    half = width // SLOTS
    rep, shard = lax.axis_index("rep"), lax.axis_index("shard")
    line = Line(rep, shard, bank, send, recv)
    meet(rep, shard, True, [(line.mate, shard), (rep, line.across)])
    line.spread(0, piece)
    own = pltpu.make_async_copy(piece, bank.at[line.core, shard], own_sem)
    own.start()
    route_slots(rep, routes, routes_t, rank, slot)
    pack_rows(rep, rank, cot, (c0, c1, c2, c3))
    line.along(1)
    line.along(-1)
    line.over(0)
    line.along(2)
    line.along(-2)
    line.over(1)
    line.over(-1)
    line.along(3)
    line.along(-3)
    for step in (2, -2, 3, -3):
        line.over(step)
    own.wait()
    line.finish()
    gathered = bank[0, 0, 2 * half : 2 * half + 16, :].astype(F32)
    for j in range(1, SLOTS):
        gathered = gathered + bank[0, j, 2 * half : 2 * half + 16, :].astype(F32)
    ext[...] = gathered
    for j in range(SLOTS):
        at = slice(j * half, (j + 1) * half)
        wq[at, :] = bank[0, j, 0:half, :]
        wk[at, :] = bank[0, j, half : 2 * half, :]
        wv[at, :] = bank[1, j, 0:half, :]
        wo[at, :] = bank[1, j, half : 2 * half, :]
    qkv_rows(x, ext, cosine, sine, wq, wk, wv, q, k, v)


def plain_head_kernel(
    routes, routes_t, cot, x, cosine, sine, wq, wk, wv, ext,
    rank, slot, c0, c1, c2, c3, q, k, v,
):
    rep = lax.axis_index("rep")
    route_slots(rep, routes, routes_t, rank, slot)
    pack_rows(rep, rank, cot, (c0, c1, c2, c3))
    qkv_rows(x, ext, cosine, sine, wq, wk, wv, q, k, v)


def fill_bias(starts, bias):
    tokens = bias.shape[0]

    def tile(t, carry):
        at = pl.ds(pl.multiple_of(t * TILE, TILE), TILE)
        query = iota((TILE, tokens), 0) + t * TILE
        key = iota((TILE, tokens), 1)
        allowed = key <= query
        for n in range(2):
            begin = starts[0, n]
            inside = (query >= begin) & (query < begin + PIECE)
            allowed = allowed | (inside & (key >= begin) & (key < begin + PIECE))
        bias[at, :] = jnp.where(allowed, 0.0, MASKED)
        return carry

    lax.fori_loop(0, tokens // TILE, tile, 0)


def keep_half(block, h):
    low = iota(block.shape, 1) < 64
    return jnp.where(low if h == 0 else ~low, block.astype(F32), 0.0).astype(BF)


def biased(scores, bias, begin, free, end):
    tail = scores[:, free:] + bias[begin : begin + TILE, free:end]
    return tail if free == 0 else jnp.concatenate([scores[:, :free], tail], axis=1)


def attend_kernel(starts, q, k, v, out, lse, bias):
    tokens = q.shape[0]

    @pl.when(pl.program_id(0) == 0)
    def _():
        fill_bias(starts, bias)

    keys = k[...]
    low = iota((tokens, 128), 1) < 64
    values = v[...].astype(F32)
    value_one = [
        jnp.where(low, values, 1.0).astype(BF),
        jnp.where(low, 1.0, values).astype(BF),
    ]
    low = iota((TILE, 128), 1) < 64
    for t in range(tokens // TILE):
        begin = t * TILE
        end = min(tokens, begin + TILE + PIECE)
        block = q[begin : begin + TILE, :]
        results, totals = [], []
        for h in range(2):
            scores = nt(keep_half(block, h), keys[:end])
            scores = biased(scores, bias, begin, begin, end)
            row_max = jnp.max(scores, axis=1, keepdims=True)
            probs = jnp.exp(scores - row_max).astype(BF)
            mixed = nn(probs, value_one[h][:end])
            total = pltpu.roll(mixed, 64, 1)
            results.append(mixed / total)
            totals.append(row_max + jnp.log(total))
        out[begin : begin + TILE, :] = jnp.where(low, results[0], results[1]).astype(BF)
        lse[begin : begin + TILE, :] = jnp.where(low, totals[0], totals[1])


def router_rows(ext):
    rows = jnp.where(iota(ext.shape, 0) < 4, ext[...], 0.0)
    return jnp.concatenate([rows, jnp.zeros((112, ext.shape[1]), F32)], axis=0).astype(BF)


def route_probs(normed, router):
    logits = nt(normed, router)
    logits = jnp.where(iota(logits.shape, 1) < 4, logits, MASKED)
    raised = jnp.exp(logits - jnp.max(logits, axis=1, keepdims=True))
    return raised / jnp.sum(raised, axis=1, keepdims=True)


def middle_kernel(info, x, attended, wo, ext, rank, middle, normed, probs, *packed):
    tokens = x.shape[0]
    rep = info[0]
    gain = ext[5:6, :]
    router = router_rows(ext)

    def tile(t, carry):
        at = pl.ds(pl.multiple_of(t * TILE, TILE), TILE)
        rows = x[at, :].astype(F32) + nn(attended[at, :], wo[...])
        scale = lax.rsqrt(jnp.mean(rows * rows, axis=1, keepdims=True) + EPSILON)
        middle[at, :] = rows
        unit = (rows * scale * gain).astype(BF)
        normed[at, :] = unit
        probs[at, :] = route_probs(unit, router)
        return carry

    lax.fori_loop(0, tokens // TILE, tile, 0)
    for o, out in enumerate(packed):
        row = rank[pl.ds(rep ^ o, 1), :]
        pick = ones_where(iota((CAP, tokens), 0).astype(F32) == row)
        out[...] = nn(pick, normed[...]).astype(BF)


CHUNK = 512


def ffn_kernel(blocks, weights, unit, routed, chained, *refs):
    refs = list(refs)

    def take(n):
        taken = refs[:n]
        del refs[:n]
        return taken

    info, ext = take(2)
    xs, cs = take(blocks), take(blocks)
    slots = take(weights)
    before = take(weights) if chained else None
    outs, dxs = take(blocks), take(blocks)
    grads = take(weights)
    out_acc, dx_acc, gate, wbuf, dw_acc, dw_out = take(6)
    prior = take(1)[0] if chained else None
    in_sems, out_sems = take(2)
    prior_sems = take(1)[0] if chained else None
    rows = xs[0].shape[0]
    per = CHUNK // unit
    chunks = 4

    def pieces(k, banks):
        return [(banks[i // SLOTS], i % SLOTS) for i in range(k * per, (k + 1) * per)]

    def view(bank, j):
        return bank

    def ref_of(banks, k, i):
        n = k * per + i
        if weights == SLOTS:
            return banks[n]
        return banks[n % 2].at[n // 2]

    def loads(banks, buffer, sems, k, b):
        return [
            pltpu.make_async_copy(
                ref_of(banks, k, i), buffer.at[b, :, :, pl.ds(i * unit, unit)], sems.at[b, i]
            )
            for i in range(per)
        ]

    def stores(k, b):
        return [
            pltpu.make_async_copy(
                dw_out.at[b, :, :, pl.ds(i * unit, unit)], ref_of(grads, k, i), out_sems.at[b, i]
            )
            for i in range(per)
        ]

    def start_loads(k, b):
        for copy in loads(slots, wbuf, in_sems, k, b):
            copy.start()
        if chained:
            for copy in loads(before, prior, prior_sems, k, b):
                copy.start()

    start_loads(0, 0)
    if routed:
        router = router_rows(ext)
        for n in range(blocks):
            probs = route_probs(xs[n][...], router)
            lane = iota(probs.shape, 1)
            gate[n] = jnp.sum(jnp.where(lane == info[0], probs, 0.0), axis=1, keepdims=True)

    def chunk(k, carry):
        b = lax.rem(k, 2)
        for nxt in range(1, chunks):

            @pl.when(k + 1 == nxt)
            def _():
                start_loads(nxt, nxt % 2)

        for copy in loads(slots, wbuf, in_sems, 0, b):
            copy.wait()
        for n in range(blocks):
            x, c = xs[n][...], cs[n][...]
            wg, wu, wd = wbuf[b, 0], wbuf[b, 1], wbuf[b, 2]
            gate_h, up_h, back_h = nn(x, wg), nn(x, wu), nn(c, wd)
            sigma = 1.0 / (1.0 + jnp.exp(-gate_h))
            silu = gate_h * sigma
            hidden = silu * up_h
            if routed:
                share = gate[n]
                scaled = back_h * share
                weighted = (hidden * share).astype(BF)
            else:
                scaled, weighted = back_h, hidden.astype(BF)
            d_up = (scaled * silu).astype(BF)
            d_gate = (scaled * up_h * (sigma + silu * (1.0 - sigma))).astype(BF)
            product = nt(hidden.astype(BF), wd)
            d_rows = nt(d_gate, wg) + nt(d_up, wu)
            parts = (tn(x, d_gate), tn(x, d_up), tn(c, weighted))
            if routed:
                pairs = (hidden * back_h).astype(BF)
                d_share = nt(jnp.ones((16, CHUNK), BF), pairs)

            @pl.when(k == 0)
            def _():
                out_acc[n] = product
                dx_acc[n, 0:rows, :] = d_rows
                if routed:
                    dx_acc[n, rows : rows + 16, :] = jnp.zeros((16, d_rows.shape[1]), F32)
                    dx_acc[n, rows : rows + 16, 0:rows] = d_share

            @pl.when(k != 0)
            def _():
                out_acc[n] += product
                dx_acc[n, 0:rows, :] += d_rows
                if routed:
                    dx_acc[n, rows : rows + 16, 0:rows] += d_share

            for i in range(3):
                if n == 0:
                    dw_acc[i] = parts[i]
                else:
                    dw_acc[i] += parts[i]

        @pl.when(k >= 2)
        def _():
            for copy in stores(0, b):
                copy.wait()

        if chained:
            for copy in loads(before, prior, prior_sems, 0, b):
                copy.wait()
            for i in range(3):
                dw_out[b, i] = (dw_acc[i] + prior[b, i].astype(F32)).astype(BF)
        else:
            for i in range(3):
                dw_out[b, i] = dw_acc[i].astype(BF)
        for now in range(chunks):

            @pl.when(k == now)
            def _():
                for copy in stores(now, now % 2):
                    copy.start()

        return carry

    lax.fori_loop(0, chunks, chunk, 0)
    for n in range(blocks):
        outs[n][...] = out_acc[n].astype(BF)
        dxs[n][...] = dx_acc[n].astype(BF)
    for b in range(2):
        for copy in stores(0, b):
            copy.wait()


def ffn(info, ext, xs, cs, slots, before, unit, routed):
    blocks, rows, width = len(xs), xs[0].shape[0], xs[0].shape[1]
    chained = before is not None
    extra = 16 if routed else 0
    weights = len(slots)
    per = CHUNK // unit
    operands = [info, ext, *xs, *cs, *slots] + (list(before) if chained else [])
    in_specs = [SMEM, VMEM] + [VMEM] * (2 * blocks) + [ANY] * (weights * (2 if chained else 1))
    outs = [shape((rows, width))] * blocks + [shape((rows + extra, width))] * blocks
    outs += [shape(w.shape) for w in slots]
    out_specs = [VMEM] * (2 * blocks) + [ANY] * weights
    scratch = [
        pltpu.VMEM((blocks, rows, width), F32),
        pltpu.VMEM((blocks, rows + extra, width), F32),
        pltpu.VMEM((blocks, rows, 1), F32),
        pltpu.VMEM((2, 3, width, CHUNK), BF),
        pltpu.VMEM((3, width, CHUNK), F32),
        pltpu.VMEM((2, 3, width, CHUNK), BF),
    ]
    if chained:
        scratch.append(pltpu.VMEM((2, 3, width, CHUNK), BF))
    scratch += [pltpu.SemaphoreType.DMA((2, per)), pltpu.SemaphoreType.DMA((2, per))]
    if chained:
        scratch.append(pltpu.SemaphoreType.DMA((2, per)))
    results = call(
        functools.partial(ffn_kernel, blocks, weights, unit, routed, chained),
        outs,
        in_specs,
        out_specs,
        scratch,
        flops=18 * blocks * rows * width * 4 * CHUNK,
        moved=30 * 2**20,
    )(*operands)
    return results[:blocks], results[blocks : 2 * blocks], results[2 * blocks :]


def combine_kernel(
    info, slot, d0, d1, d2, d3, d_shared, probs, middle, normed, cot, ext, attended, wo,
    d_middle, d_attended, grad_wo, grad_ext, branch, router_acc, gain_acc,
):
    tokens, width = middle.shape
    rep = info[0]
    gain = ext[5:6, :]
    router = router_rows(ext)
    router_acc[...] = jnp.zeros_like(router_acc)
    gain_acc[...] = jnp.zeros_like(gain_acc)

    def tile(t, carry):
        at = pl.ds(pl.multiple_of(t * TILE, TILE), TILE)
        slot_one, slot_two = slot[at, 0:1], slot[at, 64:65]
        d_normed = d_shared[at, :].astype(F32)
        lane = iota((TILE, 128), 1)
        d_gates = jnp.zeros((TILE, 128), F32)
        for o, d in enumerate((d0, d1, d2, d3)):
            place = (iota((TILE, CAP), 1) + o * CAP).astype(F32)
            hit = (place == slot_one) | (place == slot_two)
            d_normed = d_normed + nn(ones_where(hit), d[0:CAP, :])
            share = d[CAP : CAP + 16, 0:CAP].astype(F32)[0:1, :]
            d_share = jnp.sum(jnp.where(hit, share, 0.0), axis=1, keepdims=True)
            d_gates = d_gates + jnp.where(lane == (rep ^ o), d_share, 0.0)
        p = probs[at, :]
        inner = jnp.sum(d_gates * p, axis=1, keepdims=True)
        d_logits = (p * (d_gates - inner)).astype(BF)
        d_normed = d_normed + nn(d_logits, router)
        router_acc[...] += tn(d_logits, normed[at, :])
        rows = middle[at, :]
        scale = lax.rsqrt(jnp.mean(rows * rows, axis=1, keepdims=True) + EPSILON)
        unit = rows * scale
        gain_acc[...] += jnp.sum((d_normed * unit).reshape(TILE // 8, 8, width), axis=0)
        w = d_normed * gain
        inner = jnp.mean(w * unit, axis=1, keepdims=True)
        total = cot[at, :].astype(F32) + scale * (w - unit * inner)
        d_middle[at, :] = total
        rounded = total.astype(BF)
        branch[at, :] = rounded
        d_attended[at, :] = nt(rounded, wo[...]).astype(BF)
        return carry

    lax.fori_loop(0, tokens // TILE, tile, 0)
    grad_wo[...] = tn(attended[...], branch[...]).astype(BF)
    row = iota((16, width), 0)
    total = jnp.sum(gain_acc[...], axis=0, keepdims=True)
    grad_ext[...] = jnp.where(row < 4, router_acc[0:16, :], jnp.where(row == 5, total, 0.0))


def output_kernel(info, slot, o0, o1, o2, o3, shared, probs, middle, out):
    tokens = middle.shape[0]
    rep = info[0]

    def tile(t, carry):
        at = pl.ds(pl.multiple_of(t * TILE, TILE), TILE)
        slot_one, slot_two = slot[at, 0:1], slot[at, 64:65]
        total = middle[at, :] + shared[at, :].astype(F32)
        p = probs[at, :]
        lane = iota((TILE, 128), 1)
        for o, rows in enumerate((o0, o1, o2, o3)):
            place = (iota((TILE, CAP), 1) + o * CAP).astype(F32)
            hit = (place == slot_one) | (place == slot_two)
            share = jnp.sum(jnp.where(lane == (rep ^ o), p, 0.0), axis=1, keepdims=True)
            total = total + nn(jnp.where(hit, share, 0.0).astype(BF), rows[...])
        out[at, :] = total.astype(BF)
        return carry

    lax.fori_loop(0, tokens // TILE, tile, 0)


def attend_back_kernel(
    starts, q, k, v, d_out, out, lse, cosine, sine, dq, dk, dv, bias, dk_acc, dv_acc
):
    tokens = q.shape[0]

    @pl.when(pl.program_id(0) == 0)
    def _():
        fill_bias(starts, bias)

    keys, values = k[...], v[...]
    half_keys = [keep_half(keys, 0), keep_half(keys, 1)]
    dk_acc[...] = jnp.zeros_like(dk_acc)
    dv_acc[...] = jnp.zeros_like(dv_acc)
    low = iota((TILE, 128), 1) < 64
    for t in range(tokens // TILE):
        begin = t * TILE
        end = min(tokens, begin + TILE + PIECE)
        at = slice(begin, begin + TILE)
        block, grad = q[at, :], d_out[at, :]
        product = grad.astype(F32) * out[at, :].astype(F32)
        block_lse = lse[at, :]
        d_block = None
        for h in range(2):
            block_h, grad_h = keep_half(block, h), keep_half(grad, h)
            scores = nt(block_h, keys[:end])
            scores = biased(scores, bias, begin, begin, end)
            probs = jnp.exp(scores - block_lse[:, 64 * h : 64 * h + 1])
            d_probs = nt(grad_h, values[:end])
            inner = jnp.sum(
                jnp.where(low if h == 0 else ~low, product, 0.0), axis=1, keepdims=True
            )
            d_scores = (probs * (d_probs - inner)).astype(BF)
            part = nn(d_scores, half_keys[h][:end])
            d_block = part if d_block is None else d_block + part
            dk_acc[0:end, :] += tn(d_scores, block_h)
            dv_acc[0:end, :] += tn(probs.astype(BF), grad_h)
        dq[at, :] = spin(d_block * 0.125, cosine[at, :], -sine[at, :]).astype(BF)
    dk[...] = spin(dk_acc[...], cosine[...], -sine[...]).astype(BF)
    dv[...] = dv_acc[...].astype(BF)


def tail_kernel(
    info, x, ext, dq, dk, dv, wq, wk, wv, d_middle, grad_wo, grad_ext,
    grad_in, mine, theirs, normed_all, gw, gain_acc,
):
    tokens, width = x.shape
    gain = ext[4:5, :]
    gain_acc[...] = jnp.zeros_like(gain_acc)

    def tile(t, carry):
        at = pl.ds(pl.multiple_of(t * TILE, TILE), TILE)
        rows = x[at, :].astype(F32)
        scale = lax.rsqrt(jnp.mean(rows * rows, axis=1, keepdims=True) + EPSILON)
        unit = rows * scale
        normed_all[at, :] = (unit * gain).astype(BF)
        d_normed = nt(dq[at, :], wq[...]) + nt(dk[at, :], wk[...]) + nt(dv[at, :], wv[...])
        gain_acc[...] += jnp.sum((d_normed * unit).reshape(TILE // 8, 8, width), axis=0)
        w = d_normed * gain
        inner = jnp.mean(w * unit, axis=1, keepdims=True)
        grad_in[at, :] = d_middle[at, :] + scale * (w - unit * inner)
        return carry

    lax.fori_loop(0, tokens // TILE, tile, 0)
    for i, d in enumerate((dq, dk, dv)):
        gw[i] = tn(normed_all[...], d[...]).astype(BF)
    row = iota((16, width), 0)
    total = jnp.sum(gain_acc[...], axis=0, keepdims=True)
    small = (grad_ext[...] + jnp.where(row == 4, total, 0.0)).astype(BF)
    half = width // SLOTS

    def fill(low, high):
        for j in range(SLOTS):
            at = pl.ds(pl.multiple_of(info[2 + j] * half, 32), half)
            low[j, 0:half, :] = gw[0, at, :]
            low[j, half : 2 * half, :] = gw[1, at, :]
            low[j, 2 * half : 2 * half + 16, :] = small
            high[j, 0:half, :] = gw[2, at, :]
            high[j, half : 2 * half, :] = grad_wo[at, :]
            high[j, 2 * half : 2 * half + 16, :] = jnp.zeros((16, width), BF)

    @pl.when(info[1] == 0)
    def _():
        fill(mine, theirs)

    @pl.when(info[1] != 0)
    def _():
        fill(theirs, mine)


def rope_tables(length, head_dim):
    positions = jnp.arange(length, dtype=F32)
    inverse_freq = 10000.0 ** (-2.0 * jnp.arange(head_dim // 2, dtype=F32) / head_dim)
    angle = positions[:, None] * inverse_freq[None, :]
    cosine, sine = jnp.cos(angle), jnp.sin(angle)
    return (
        jnp.concatenate([cosine] * 4, axis=1),
        jnp.concatenate([-sine, sine, -sine, sine], axis=1),
    )


def body(
    inputs,
    piece_starts,
    routes,
    attn_gain,
    query_weight,
    key_weight,
    value_weight,
    out_weight,
    ffn_gain,
    router_weight,
    expert_gate,
    expert_up,
    expert_down,
    shared_gate,
    shared_up,
    shared_down,
    cotangent,
):
    _, tokens, width = inputs.shape
    shards = lax.axis_size("shard")
    rep, shard = lax.axis_index("rep"), lax.axis_index("shard")
    core = rep % 2
    ringed = shards == SLOTS
    rows = width // shards
    units = shared_gate.shape[1]
    x, cot, chosen = inputs[0], cotangent[0], routes[0]
    if ringed:
        z, x_side = shard // 2, shard % 2
        order = [((z + d) % 4) * 2 + (x_side ^ b) for b in range(2) for d in range(4)]
    else:
        order = list(range(SLOTS))
    info = jnp.stack([jnp.asarray(n, jnp.int32) for n in [rep, core] + order])

    small = jnp.concatenate([router_weight.T, attn_gain[None], ffn_gain[None]], axis=0)
    small = jnp.pad(small, ((0, 10), (0, 0)))
    small = lax.dynamic_update_slice(jnp.zeros((16, width), BF), small, (0, shard * rows))
    blank = jnp.zeros((16, width), BF)
    if ringed:
        half_one = jnp.concatenate([query_weight, key_weight, small], axis=0)
        half_two = jnp.concatenate([value_weight, out_weight, blank], axis=0)
        piece = jnp.where(core == 0, half_one, half_two)
    else:
        wq, wk, wv, wo = [
            lax.all_gather(w, "shard", axis=0, tiled=True)
            for w in (query_weight, key_weight, value_weight, out_weight)
        ]
        ext = lax.psum(small.astype(F32), "shard")

    cosine, sine = rope_tables(tokens, width // HEADS)
    token_f = shape((tokens, width))
    square = shape((width, width))
    packed = [shape((CAP, width))] * 4
    outs = [shape((8, tokens), F32), shape((tokens, 128), F32)] + packed + [token_f] * 3
    work = 2 * tokens * width * (CAP * 4 + 3 * width)
    if ringed:
        rank, slot, *heads = call(
            head_kernel,
            outs + [square] * 4 + [shape((16, width), F32)],
            [VMEM] * 7,
            [VMEM] * 14,
            [
                pltpu.VMEM((2, SLOTS, 2 * rows + 16, width), BF),
                pltpu.SemaphoreType.DMA((28,)),
                pltpu.SemaphoreType.DMA((28,)),
                pltpu.SemaphoreType.DMA,
            ],
            flops=work,
            moved=24 * 2**20,
            group=0,
        )(chosen, chosen.T, cot, x, piece, cosine, sine)
        wq, wk, wv, wo, ext = heads[7:]
    else:
        rank, slot, *heads = call(
            plain_head_kernel, outs, [VMEM] * 10, [VMEM] * 9, flops=work, moved=24 * 2**20
        )(chosen, chosen.T, cot, x, cosine, sine, wq, wk, wv, ext)
    cot_out = heads[:4]
    q, k, v = heads[4:7]

    shared_pack = jnp.stack([shared_gate, shared_up, shared_down.T])
    my_half = lax.dynamic_slice_in_dim(shared_pack, core * (units // 2), units // 2, 2)
    expert_pack = jnp.stack([expert_gate[rep], expert_up[rep], expert_down[rep].T])
    if ringed:
        my_half = after(my_half, q)
        shared_own = jnp.stack(gather_slots(my_half))
        shared_other = to_rep(shared_own, 1)
        expert_pack = after(expert_pack, shared_own)
        expert_slots = gather_slots(expert_pack)
    else:

        def slotted(part):
            every = lax.all_gather(part, "shard")
            every = every.reshape(SLOTS, shards // SLOTS, 3, width, part.shape[2])
            return every.transpose(0, 2, 3, 1, 4).reshape(SLOTS, 3, width, -1)

        shared_own = slotted(my_half)
        shared_other = to_rep(shared_own, 1)
        expert_every = slotted(expert_pack)
        expert_slots = [expert_every[j] for j in range(SLOTS)]

    cot_in = [cot_out[0]] + [to_rep(cot_out[o], o) for o in (1, 2, 3)]

    pair = pl.BlockSpec((tokens, 128), lambda i: (0, i))
    table = pl.BlockSpec((tokens, 128), lambda i: (0, 0))
    attended, lse = call(
        attend_kernel,
        [token_f, shape((tokens, width), F32)],
        [SMEM, pair, pair, pair],
        [pair, pair],
        [pltpu.VMEM((tokens, tokens), F32)],
        flops=16 * tokens * tokens * width,
        moved=10 * 2**20,
        grid=(width // 128,),
    )(piece_starts, q, k, v)

    middle, normed, probs, *x_out = call(
        middle_kernel,
        [shape((tokens, width), F32), token_f, shape((tokens, 128), F32)] + packed,
        [SMEM] + [VMEM] * 5,
        [VMEM] * 7,
        flops=2 * tokens * width * (width + CAP * 4),
        moved=14 * 2**20,
    )(info, x, attended, wo, ext, rank)

    x_in = [x_out[0]] + [to_rep(x_out[o], o) for o in (1, 2, 3)]
    shared_out, shared_dx, shared_grads = ffn(
        info,
        ext,
        [normed],
        [cot],
        [shared_own, shared_other],
        None,
        units // 2 if ringed else 128,
        False,
    )
    unit = units if ringed else 256
    far_out, far_dx, far_grads = ffn(
        info, ext, x_in[2:], cot_in[2:], expert_slots, None, unit, True
    )
    far_dx = [to_rep(far_dx[0], 2), to_rep(far_dx[1], 3)]
    near_out, near_dx, grads = ffn(
        info, ext, x_in[:2], cot_in[:2], expert_slots, far_grads, unit, True
    )
    d_rows = [near_dx[0], to_rep(near_dx[1], 1)] + far_dx
    out_rows = [near_out[0], to_rep(near_out[1], 1), to_rep(far_out[0], 2), to_rep(far_out[1], 3)]

    d_middle, d_attended, grad_wo, grad_ext = call(
        combine_kernel,
        [shape((tokens, width), F32), token_f, square, shape((16, width), F32)],
        [SMEM] + [VMEM] * 13,
        [VMEM] * 4,
        [
            pltpu.VMEM((tokens, width), BF),
            pltpu.VMEM((128, width), F32),
            pltpu.VMEM((8, width), F32),
        ],
        flops=2 * tokens * width * (2 * width + 4 * CAP),
        moved=24 * 2**20,
    )(info, slot, *d_rows, shared_dx[0], probs, middle, normed, cot, ext, attended, wo)
    outputs = call(
        output_kernel,
        token_f,
        [SMEM] + [VMEM] * 8,
        VMEM,
        flops=2 * tokens * width * 4 * CAP,
        moved=12 * 2**20,
    )(info, slot, *out_rows, shared_out[0], probs, middle)

    dq, dk, dv = call(
        attend_back_kernel,
        [token_f] * 3,
        [SMEM] + [pair] * 6 + [table] * 2,
        [pair] * 3,
        [
            pltpu.VMEM((tokens, tokens), F32),
            pltpu.VMEM((tokens, 128), F32),
            pltpu.VMEM((tokens, 128), F32),
        ],
        flops=40 * tokens * tokens * width,
        moved=14 * 2**20,
        grid=(width // 128,),
    )(piece_starts, q, k, v, d_attended, attended, lse, cosine, sine)

    grad_rows = shape((SLOTS, 2 * (width // SLOTS) + 16, width))
    grad_in, mine, theirs = call(
        tail_kernel,
        [shape((tokens, width), F32), grad_rows, grad_rows],
        [SMEM] + [VMEM] * 11,
        [VMEM] * 3,
        [
            pltpu.VMEM((tokens, width), BF),
            pltpu.VMEM((3, width, width), BF),
            pltpu.VMEM((8, width), F32),
        ],
        flops=12 * tokens * width * width,
        moved=24 * 2**20,
    )(info, x, ext, dq, dk, dv, wq, wk, wv, d_middle, grad_wo, grad_ext)

    def over_rep(total):
        total = total.astype(BF)
        return [total] + [to_rep(total, o) for o in (1, 2, 3)]

    def absolute(parts, dtype):
        stacked = jnp.stack(parts)
        return jnp.take(stacked, jnp.arange(4) ^ rep, axis=0).astype(dtype)

    def unslot(every, part_units):
        every = every.reshape(SLOTS, 3, width, shards // SLOTS, part_units)
        every = every.transpose(0, 3, 1, 2, 4).reshape(shards, 3, width, part_units)
        return lax.psum_scatter(every, "shard", scatter_dimension=0)

    shared_sum = shared_grads[0].astype(F32) + to_rep(shared_grads[1], 1).astype(F32)
    if ringed:
        shared_sum = shared_sum.astype(BF)
        shared_total = scatter_slots([shared_sum[j] for j in range(SLOTS)])
        expert_total = scatter_slots(grads)
    else:
        shared_total = unslot(shared_sum.astype(BF), units // 2).astype(F32)
        expert_total = unslot(jnp.stack(grads), units).astype(F32)
    shared_total = shared_total + to_rep(shared_total.astype(BF), 2).astype(F32)
    shared_pair = to_rep(shared_total.astype(BF), 1).astype(F32)
    shared_low = jnp.where(core == 0, shared_total, shared_pair)
    shared_high = jnp.where(core == 0, shared_pair, shared_total)
    shared_full = jnp.concatenate([shared_low, shared_high], axis=2)
    expert_full = absolute(over_rep(expert_total), F32)

    summed = mine.astype(F32) + to_rep(theirs, 1).astype(F32)
    if ringed:
        summed = summed.astype(BF)
        far = to_x(summed[4:])
        near = summed[:4].astype(F32) + far.astype(F32)
        near_low = near.astype(BF)
        attn_total = near[0]
        for d in (1, 2, 3):
            attn_total = attn_total + to_z(near_low[d], d).astype(F32)
    else:
        half = width // SLOTS
        summed = summed.astype(BF)
        one = lax.psum_scatter(summed[:, :half].reshape(width, width), "shard", tiled=True)
        two = lax.psum_scatter(
            summed[:, half : 2 * half].reshape(width, width), "shard", tiled=True
        )
        three = lax.psum(summed[0, 2 * half :].astype(F32), "shard")
        attn_total = jnp.concatenate([one.astype(F32), two.astype(F32), three], axis=0)
    attn_total = attn_total + to_rep(attn_total.astype(BF), 2).astype(F32)
    attn_pair = to_rep(attn_total.astype(BF), 1).astype(F32)
    first = jnp.where(core == 0, attn_total, attn_pair)
    second = jnp.where(core == 0, attn_pair, attn_total)
    tiny = lax.dynamic_slice(first[2 * rows :], (0, shard * rows), (16, rows))
    return (
        outputs[None],
        grad_in[None],
        tiny[4],
        first[:rows],
        first[rows : 2 * rows],
        second[:rows],
        second[rows : 2 * rows],
        tiny[5],
        tiny[:4].T,
        expert_full[:, 0],
        expert_full[:, 1],
        expert_full[:, 2].transpose(0, 2, 1),
        shared_full[0],
        shared_full[1],
        shared_full[2].T,
    )


def solution(mesh):
    in_specs = (
        P(("rep", "shard"), None, None),
        P(("rep", "shard"), None),
        P(("rep", "shard"), None, None),
        P("shard"),
        P("shard", None),
        P("shard", None),
        P("shard", None),
        P("shard", None),
        P("shard"),
        P("shard", None),
        P(None, None, "shard"),
        P(None, None, "shard"),
        P(None, "shard", None),
        P(None, "shard"),
        P(None, "shard"),
        P("shard", None),
        P(("rep", "shard"), None, None),
    )
    out_specs = (
        P(("rep", "shard"), None, None),
        P(("rep", "shard"), None, None),
        P("shard"),
        P("shard", None),
        P("shard", None),
        P("shard", None),
        P("shard", None),
        P("shard"),
        P("shard", None),
        P(None, None, "shard"),
        P(None, None, "shard"),
        P(None, "shard", None),
        P(None, "shard"),
        P(None, "shard"),
        P("shard", None),
    )
    return jax.shard_map(body, mesh=mesh, in_specs=in_specs, out_specs=out_specs, check_vma=False)
```

```python
import functools

import jax
import jax.numpy as jnp
from jax import lax
from jax.experimental import pallas as pl
from jax.experimental.pallas import tpu as pltpu
from jax.sharding import PartitionSpec as P

HEADS = 12
PIECE = 256
CAP = 576
EPSILON = 1e-06
MASKED = -1e30
F32, BF = jnp.float32, jnp.bfloat16
AXES = ("rep", "shard")
TILE = 256
SLOTS = 8
VMEM_LIMIT = 62 * 2**20
ANY = pl.BlockSpec(memory_space=pl.ANY)
SMEM = pl.BlockSpec(memory_space=pltpu.SMEM)
VMEM = pl.BlockSpec(memory_space=pltpu.VMEM)


def dot(a, b, i, j):
    return lax.dot_general(a, b, (((i,), (j,)), ((), ())), preferred_element_type=F32)


def nn(a, b):
    return dot(a, b, 1, 0)


def nt(a, b):
    return dot(a, b, 1, 1)


def tn(a, b):
    return dot(a, b, 0, 0)


def iota(shape, dim):
    return lax.broadcasted_iota(jnp.int32, shape, dim)


def ones_where(cond):
    return jnp.where(cond, 1.0, 0.0).astype(BF)


def call(
    kernel, out_shape, in_specs, out_specs, scratch=(), flops=0, moved=0, grid=None, group=None,
    alias=None,
):
    extra = {} if grid is None else {"grid": grid}
    params = {} if group is None else {"collective_id": group, "has_side_effects": True}
    return pl.pallas_call(
        kernel,
        out_shape=out_shape,
        in_specs=in_specs,
        out_specs=out_specs,
        scratch_shapes=list(scratch),
        input_output_aliases=alias or {},
        compiler_params=pltpu.CompilerParams(vmem_limit_bytes=VMEM_LIMIT, **params),
        cost_estimate=pl.CostEstimate(flops=flops, bytes_accessed=moved, transcendentals=0),
        **extra,
    )


def shape(dims, dtype=BF):
    return jax.ShapeDtypeStruct(dims, dtype)


def permute(x, move):
    reps, shards = lax.axis_size("rep"), lax.axis_size("shard")
    pairs = []
    for r in range(reps):
        for s in range(shards):
            to_r, to_s = move(r, s)
            pairs.append((r * shards + s, to_r * shards + to_s))
    return lax.ppermute(x, AXES, pairs)


def to_rep(x, offset):
    return permute(x, lambda r, s: (r ^ offset, s))


def spin(block, cosine, sine):
    lane = iota(block.shape, 1)
    partner = jnp.where(lane % 64 < 32, pltpu.roll(block, 96, 1), pltpu.roll(block, 32, 1))
    return block * cosine + partner * sine


def sibling(rep, o):
    return 2 * lax.rem(lax.div(rep, 2) + o // 2, 2) + lax.rem(lax.rem(rep, 2) + o % 2, 2)


def route_slots(rep, routes, routes_t, rank_out, slot_out):
    tokens = routes.shape[0]
    first, second = routes_t[0:1, :], routes_t[1:2, :]
    expert = iota((8, tokens), 0)
    chosen = (expert == first) | (expert == second)
    upper = ones_where(iota((tokens, tokens), 0) <= iota((tokens, tokens), 1))
    rank = nn(ones_where(chosen), upper) - 1.0
    rank_out[...] = jnp.where(chosen, rank, -1.0)
    lane = iota((tokens, 128), 1)
    one, two = routes[:, 0:1], routes[:, 1:2]
    lower = ones_where(iota((tokens, tokens), 0) >= iota((tokens, tokens), 1))
    place = nn(lower, ones_where((lane == one) | (lane == two))) - 1.0
    for o in range(1, 4):
        place = place + jnp.where(lane == sibling(rep, o), float(o * CAP), 0.0)
    slot_one = jnp.sum(jnp.where(lane == one, place, 0.0), axis=1, keepdims=True)
    slot_two = jnp.sum(jnp.where(lane == two, place, 0.0), axis=1, keepdims=True)
    slot_out[...] = jnp.where(lane < 64, slot_one, slot_two)


def pack_rows(rep, rank, source, packed):
    tokens = source.shape[0]
    for o, out in enumerate(packed):
        row = rank[pl.ds(sibling(rep, o), 1), :]
        pick = ones_where(iota((CAP, tokens), 0).astype(F32) == row)
        out[...] = nn(pick, source[...]).astype(BF)


def qkv_rows(x, ext, cosine, sine, wq, wk, wv, q, k, v):
    tokens, width = x.shape
    gain = ext[4:5, :]

    def tile(t, carry):
        at = pl.ds(pl.multiple_of(t * TILE, TILE), TILE)
        rows_in = x[at, :].astype(F32)
        scale = lax.rsqrt(jnp.mean(rows_in * rows_in, axis=1, keepdims=True) + EPSILON)
        normed = (rows_in * scale * gain).astype(BF)
        cos_t, sin_t = cosine[at, :], sine[at, :]
        for weight, out, factor in ((wq, q, 0.125), (wk, k, 1.0)):
            full = nn(normed, weight[...])
            for b in range(width // 128):
                turned = spin(full[:, b * 128 : (b + 1) * 128], cos_t, sin_t)
                out[at, b * 128 : (b + 1) * 128] = turned.astype(BF) * jnp.asarray(factor, BF)
        v[at, :] = nn(normed, wv[...]).astype(BF)
        return carry

    lax.fori_loop(0, tokens // TILE, tile, 0)


def when(cond, body):
    if cond is True:
        body()
    elif cond is not False:
        pl.when(cond)(body)


def both(one, two):
    if one is True or two is False:
        return two
    if two is True or one is False:
        return one
    return one & two


class Net:
    def __init__(self, send, recv):
        self.rep, self.shard = lax.axis_index("rep"), lax.axis_index("shard")
        self.core, self.z = lax.rem(self.rep, 2), lax.div(self.shard, 2)
        self.x = lax.rem(self.shard, 2)
        self.mate = self.rep + 1 - 2 * self.core
        self.across = self.shard + 1 - 2 * self.x
        first = lax.max(self.z - 1, 1 - self.z)
        third = 3 * (1 - lax.div(self.z, 2))
        self.levels = [self.z, first, 6 - self.z - first - third, third]
        self.up = lax.min(self.shard + 2, 6 + self.x)
        self.down = lax.max(self.shard - 2, self.x)
        self.cousins = [self.rep] + [sibling(self.rep, o) for o in (1, 2, 3)]
        self.send, self.recv = send, recv
        self.count, self.open = 0, {}

    def event(self):
        self.count += 1
        return self.count - 1

    def place(self, n, side):
        return self.levels[n] * 2 + (self.x if side == 0 else 1 - self.x)

    def cycle(self, d):
        return lax.rem(self.z + d, 4) * 2 + self.x

    def copy(self, event, source, target, rep, shard):
        return pltpu.make_async_remote_copy(
            src_ref=source,
            dst_ref=target,
            send_sem=self.send.at[event],
            recv_sem=self.recv.at[event],
            device_id=(rep, shard),
            device_id_type=pl.DeviceIdType.MESH,
        )

    def put(self, event, source, target, rep, shard, cond=True):
        when(cond, self.copy(event, source, target, rep, shard).start)
        self.open[event] = (cond, source)

    def got(self, event, like, cond=True):
        when(cond, self.copy(event, like, like, self.mate, self.shard).wait_recv)

    def close(self):
        for event, (cond, source) in self.open.items():
            when(cond, self.copy(event, source, source, self.mate, self.shard).wait_send)

    def meet(self, z_ways, others):
        barrier = pltpu.get_barrier_semaphore()

        def greet(rep, shard):
            pl.semaphore_signal(
                barrier, inc=1, device_id=(rep, shard), device_id_type=pl.DeviceIdType.MESH
            )

        count = len(others)
        for rep, shard in others:
            greet(rep, shard)
        if z_ways == "line":
            when(self.z < 3, lambda: greet(self.rep, self.up))
            when(self.z > 0, lambda: greet(self.rep, self.down))
            count = count + lax.min(self.z, 1) + lax.min(3 - self.z, 1)
        if z_ways == "all":
            for d in (1, 2, 3):
                greet(self.rep, self.cycle(d))
            count = count + 3
        pl.semaphore_wait(barrier, count)


class Line:
    def __init__(self, net, bank):
        self.net, self.bank = net, bank
        self.events = {(way, k): net.event() for way in range(4) for k in range(-3, 4)}
        self.spots = {0: (net.shard, True)}
        for k in (1, 2, 3):
            self.spots[k] = (lax.min(net.shard + 2 * k, 6 + net.x), net.z < 4 - k)
            self.spots[-k] = (lax.max(net.shard - 2 * k, net.x), net.z >= k)
        self.flips = {k: spot + 1 - 2 * net.x for k, (spot, _) in self.spots.items()}
        self.onward = {k: both(self.spots[k][1], net.z < 3) for k in self.spots}
        self.back = {k: both(self.spots[k][1], net.z > 0) for k in self.spots}

    def spread(self, k, source):
        net, (spot, here) = self.net, self.spots[k]
        target = self.bank.at[net.core, spot]
        if -3 < k <= 0:
            event = self.events[0, k - 1]
            net.put(event, source, target, net.rep, net.up, self.onward[k])
        if 0 <= k < 3:
            event = self.events[0, k + 1]
            net.put(event, source, target, net.rep, net.down, self.back[k])
        net.put(self.events[1, k], source, target, net.rep, net.across, here)
        net.put(self.events[2, k], source, target, net.mate, net.shard, here)

    def along(self, k):
        spot, here = self.spots[k]
        piece = self.bank.at[self.net.core, spot]
        self.net.got(self.events[0, k], piece, here)
        self.spread(k, piece)

    def over(self, k):
        net, here = self.net, self.spots[k][1]
        piece = self.bank.at[net.core, self.flips[k]]
        net.got(self.events[1, k], piece, here)
        net.put(self.events[3, k], piece, piece, net.mate, net.shard, here)

    def finish(self):
        other = 1 - self.net.core
        for k in (0, 1, -1, 2, -2, 3, -3):
            spot, here = self.spots[k]
            self.net.got(self.events[2, k], self.bank.at[other, spot], here)
            self.net.got(self.events[3, k], self.bank.at[other, self.flips[k]], here)


def exchange(net, sources, targets):
    events = [net.event() for _ in range(3)]
    for o in (2, 3, 1):
        net.put(events[o - 1], sources[o - 1], targets[o - 1], net.cousins[o], net.shard)
    return [(events[o], targets[o]) for o in range(3)]


def head_kernel(
    routes, routes_t, cot, x, piece, cosine, sine,
    rank, slot, q, k, v, wq, wk, wv, wo, ext, c0, c1, c2, c3,
    bank, packed, send, recv, own_sem,
):
    width = x.shape[1]
    half = width // SLOTS
    net = Net(send, recv)
    line = Line(net, bank)
    peers = [(net.cousins[o], net.shard) for o in (1, 2, 3)]
    net.meet("line", peers + [(net.rep, net.across)])
    line.spread(0, piece)
    own = pltpu.make_async_copy(piece, bank.at[net.core, net.shard], own_sem)
    own.start()
    route_slots(net.rep, routes, routes_t, rank, slot)
    pack_rows(net.rep, rank, cot, [c0] + [packed.at[o] for o in range(3)])
    arrivals = exchange(net, [packed.at[o] for o in range(3)], (c1, c2, c3))
    line.along(1)
    line.along(-1)
    line.over(0)
    line.along(2)
    line.along(-2)
    line.over(1)
    line.over(-1)
    line.along(3)
    line.along(-3)
    for step in (2, -2, 3, -3):
        line.over(step)
    own.wait()
    line.finish()
    gathered = bank[0, 0, 2 * half : 2 * half + 16, :].astype(F32)
    for j in range(1, SLOTS):
        gathered = gathered + bank[0, j, 2 * half : 2 * half + 16, :].astype(F32)
    ext[...] = gathered
    for j in range(SLOTS):
        at = slice(j * half, (j + 1) * half)
        wq[at, :] = bank[0, j, 0:half, :]
        wk[at, :] = bank[0, j, half : 2 * half, :]
        wv[at, :] = bank[1, j, 0:half, :]
        wo[at, :] = bank[1, j, half : 2 * half, :]
    qkv_rows(x, ext, cosine, sine, wq, wk, wv, q, k, v)
    for event, like in arrivals:
        net.got(event, like)
    net.close()


def plain_head_kernel(
    routes, routes_t, cot, x, cosine, sine, wq, wk, wv, ext,
    rank, slot, q, k, v, c0, c1, c2, c3,
):
    rep = lax.axis_index("rep")
    route_slots(rep, routes, routes_t, rank, slot)
    pack_rows(rep, rank, cot, (c0, c1, c2, c3))
    qkv_rows(x, ext, cosine, sine, wq, wk, wv, q, k, v)


def fill_bias(starts, bias):
    tokens = bias.shape[0]

    def tile(t, carry):
        at = pl.ds(pl.multiple_of(t * TILE, TILE), TILE)
        query = iota((TILE, tokens), 0) + t * TILE
        key = iota((TILE, tokens), 1)
        allowed = key <= query
        for n in range(2):
            begin = starts[0, n]
            inside = (query >= begin) & (query < begin + PIECE)
            allowed = allowed | (inside & (key >= begin) & (key < begin + PIECE))
        bias[at, :] = jnp.where(allowed, 0.0, MASKED)
        return carry

    lax.fori_loop(0, tokens // TILE, tile, 0)


def keep_half(block, h):
    low = iota(block.shape, 1) < 64
    return jnp.where(low if h == 0 else ~low, block.astype(F32), 0.0).astype(BF)


def biased(scores, bias, begin, free, end):
    tail = scores[:, free:] + bias[begin : begin + TILE, free:end]
    return tail if free == 0 else jnp.concatenate([scores[:, :free], tail], axis=1)


def attend_pairs(q, k, v, out, lse, bias, step):
    tokens, width = q.shape

    def pair(i, carry):
        step(i)
        cols = pl.ds(pl.multiple_of(i * 128, 128), 128)
        keys = k[:, cols]
        low = iota((tokens, 128), 1) < 64
        values = v[:, cols].astype(F32)
        value_one = [
            jnp.where(low, values, 1.0).astype(BF),
            jnp.where(low, 1.0, values).astype(BF),
        ]
        low = iota((TILE, 128), 1) < 64
        for t in range(tokens // TILE):
            begin = t * TILE
            end = min(tokens, begin + TILE + PIECE)
            block = q[begin : begin + TILE, cols]
            results, totals = [], []
            for h in range(2):
                scores = nt(keep_half(block, h), keys[:end])
                scores = biased(scores, bias, begin, begin, end)
                row_max = jnp.max(scores, axis=1, keepdims=True)
                probs = jnp.exp(scores - row_max).astype(BF)
                mixed = nn(probs, value_one[h][:end])
                total = pltpu.roll(mixed, 64, 1)
                results.append(mixed / total)
                totals.append(row_max + jnp.log(total))
            out[begin : begin + TILE, cols] = jnp.where(low, results[0], results[1]).astype(BF)
            lse[begin : begin + TILE, cols] = jnp.where(low, totals[0], totals[1])
        return carry

    lax.fori_loop(0, width // 128, pair, 0)


def router_rows(ext):
    rows = jnp.where(iota(ext.shape, 0) < 4, ext[...], 0.0)
    return jnp.concatenate([rows, jnp.zeros((112, ext.shape[1]), F32)], axis=0).astype(BF)


def route_probs(normed, router):
    logits = nt(normed, router)
    logits = jnp.where(iota(logits.shape, 1) < 4, logits, MASKED)
    raised = jnp.exp(logits - jnp.max(logits, axis=1, keepdims=True))
    return raised / jnp.sum(raised, axis=1, keepdims=True)


def middle_rows(rep, x, attended, wo, ext, rank, middle, normed, probs, packed):
    tokens = x.shape[0]
    gain = ext[5:6, :]
    router = router_rows(ext)

    def tile(t, carry):
        at = pl.ds(pl.multiple_of(t * TILE, TILE), TILE)
        rows = x[at, :].astype(F32) + nn(attended[at, :], wo[...])
        scale = lax.rsqrt(jnp.mean(rows * rows, axis=1, keepdims=True) + EPSILON)
        middle[at, :] = rows
        unit = (rows * scale * gain).astype(BF)
        normed[at, :] = unit
        probs[at, :] = route_probs(unit, router)
        return carry

    lax.fori_loop(0, tokens // TILE, tile, 0)
    pack_rows(rep, rank, normed, packed)


def forward_kernel(
    starts, q, k, v, x, wo, ext, rank, shared_piece, expert_piece,
    attended, lse, middle, normed, probs, x0, x1, x2, x3, shared_bank, expert_bank,
    bias, send, recv,
):
    net = Net(send, recv)
    line = Line(net, shared_bank)
    z_events = [net.event(), net.event()]
    net.meet("line", [(net.mate, net.shard), (net.rep, net.across)])
    line.spread(0, shared_piece)
    fill_bias(starts, bias)

    def step(i):
        @pl.when(i == 3)
        def _():
            line.along(1)
            line.along(-1)
            line.over(0)

    attend_pairs(q, k, v, attended, lse, bias, step)
    line.along(2)
    line.along(-2)
    line.over(1)
    line.over(-1)
    mine = expert_bank.at[net.shard]
    net.put(z_events[0], expert_piece, mine, net.rep, net.up, net.z < 3)
    net.put(z_events[1], expert_piece, mine, net.rep, net.down, net.z > 0)
    middle_rows(net.rep, x, attended, wo, ext, rank, middle, normed, probs, (x0, x1, x2, x3))
    line.along(3)
    line.along(-3)
    for step_k in (2, -2, 3, -3):
        line.over(step_k)
    line.finish()
    net.got(z_events[0], mine, net.z > 0)
    net.got(z_events[1], mine, net.z < 3)
    net.close()


def plain_forward_kernel(
    starts, q, k, v, x, wo, ext, rank,
    attended, lse, middle, normed, probs, x0, x1, x2, x3, bias,
):
    fill_bias(starts, bias)
    attend_pairs(q, k, v, attended, lse, bias, lambda i: None)
    rep = lax.axis_index("rep")
    middle_rows(rep, x, attended, wo, ext, rank, middle, normed, probs, (x0, x1, x2, x3))


CHUNK, CHUNKS = 512, 4


def unit_bank(expert, ext, xs, cs, source, target, before, unit, outs, dxs, scratch, ready=None):
    out_acc, dx_acc, gate, wbuf, dw_acc, dw_out, in_sems, out_sems = scratch[:8]
    routed = expert is not None
    blocks, rows = len(xs), xs[0].shape[0]
    per = CHUNK // unit

    def loads(of, buffer, sems, k, b):
        return [
            pltpu.make_async_copy(
                of(k * per + i), buffer.at[b, :, :, pl.ds(i * unit, unit)], sems.at[b, i]
            )
            for i in range(per)
        ]

    def stores(k, b):
        return [
            pltpu.make_async_copy(
                dw_out.at[b, :, :, pl.ds(i * unit, unit)],
                target(k * per + i),
                out_sems.at[b, i],
            )
            for i in range(per)
        ]

    def start_loads(k, b):
        if ready is not None:
            ready(k)
        for copy in loads(source, wbuf, in_sems, k, b):
            copy.start()
        if before is not None:
            for copy in loads(before, scratch[8], scratch[9], k, b):
                copy.start()

    start_loads(0, 0)
    if routed:
        router = router_rows(ext)
        for n in range(blocks):
            probs = route_probs(xs[n][...], router)
            lane = iota(probs.shape, 1)
            gate[n] = jnp.sum(jnp.where(lane == expert, probs, 0.0), axis=1, keepdims=True)

    def chunk(k, carry):
        b = lax.rem(k, 2)
        for copy in loads(source, wbuf, in_sems, 0, b):
            copy.wait()
        for n in range(blocks):
            x, c = xs[n][...], cs[n][...]
            wg, wu, wd = wbuf[b, 0], wbuf[b, 1], wbuf[b, 2]
            gate_h, up_h, back_h = nn(x, wg), nn(x, wu), nn(c, wd)
            sigma = 1.0 / (1.0 + jnp.exp(-gate_h))
            silu = gate_h * sigma
            hidden = silu * up_h
            if routed:
                share = gate[n]
                scaled = back_h * share
                weighted = (hidden * share).astype(BF)
            else:
                scaled, weighted = back_h, hidden.astype(BF)
            d_up = (scaled * silu).astype(BF)
            d_gate = (scaled * up_h * (sigma + silu * (1.0 - sigma))).astype(BF)
            product = nt(hidden.astype(BF), wd)
            d_rows = nt(d_gate, wg) + nt(d_up, wu)
            parts = (tn(x, d_gate), tn(x, d_up), tn(c, weighted))
            if routed:
                pairs = (hidden * back_h).astype(BF)
                d_share = nt(jnp.ones((16, CHUNK), BF), pairs)

            @pl.when(k == 0)
            def _():
                out_acc[n] = product
                dx_acc[n, 0:rows, :] = d_rows
                if routed:
                    dx_acc[n, rows : rows + 16, :] = jnp.zeros((16, d_rows.shape[1]), F32)
                    dx_acc[n, rows : rows + 16, 0:rows] = d_share

            @pl.when(k != 0)
            def _():
                out_acc[n] += product
                dx_acc[n, 0:rows, :] += d_rows
                if routed:
                    dx_acc[n, rows : rows + 16, 0:rows] += d_share

            for i in range(3):
                if n == 0:
                    dw_acc[i] = parts[i]
                else:
                    dw_acc[i] += parts[i]

        for nxt in range(1, CHUNKS):

            @pl.when(k + 1 == nxt)
            def _():
                start_loads(nxt, nxt % 2)

        @pl.when(k >= 2)
        def _():
            for copy in stores(0, b):
                copy.wait()

        if before is not None:
            for copy in loads(before, scratch[8], scratch[9], 0, b):
                copy.wait()
            for i in range(3):
                dw_out[b, i] = (dw_acc[i] + scratch[8][b, i].astype(F32)).astype(BF)
        else:
            for i in range(3):
                dw_out[b, i] = dw_acc[i].astype(BF)
        for now in range(CHUNKS):

            @pl.when(k == now)
            def _():
                for copy in stores(now, now % 2):
                    copy.start()

        return carry

    lax.fori_loop(0, CHUNKS, chunk, 0)
    for n in range(blocks):
        outs[n][...] = out_acc[n].astype(BF)
        dxs[n][...] = dx_acc[n].astype(BF)
    for b in range(2):
        for copy in stores(0, b):
            copy.wait()


def unit_scratch(blocks, rows, extra, width, per, chained):
    scratch = [
        pltpu.VMEM((blocks, rows, width), F32),
        pltpu.VMEM((blocks, rows + extra, width), F32),
        pltpu.VMEM((blocks, rows, 1), F32),
        pltpu.VMEM((2, 3, width, CHUNK), BF),
        pltpu.VMEM((3, width, CHUNK), F32),
        pltpu.VMEM((2, 3, width, CHUNK), BF),
        pltpu.SemaphoreType.DMA((2, per)),
        pltpu.SemaphoreType.DMA((2, per)),
    ]
    if chained:
        scratch += [
            pltpu.VMEM((2, 3, width, CHUNK), BF),
            pltpu.SemaphoreType.DMA((2, per)),
        ]
    return scratch


def shared_kernel(
    x, c, piece, bank, x1, x2, x3, expert_piece, expert_in,
    out, dx, grads_own, grads_other, y1, y2, y3, experts,
    send, recv, *scratch,
):
    net = Net(send, recv)
    events = [net.event() for _ in range(6)]
    peers = [(net.cousins[o], net.shard) for o in (1, 2, 3)]
    net.meet("line", peers + [(net.rep, net.across)])
    arrivals = exchange(net, (x1, x2, x3), (y1, y2, y3))
    low, high = experts.at[net.down], experts.at[net.up]
    net.put(events[0], low, low, net.rep, net.up, (net.z > 0) & (net.z < 3))
    net.put(events[1], high, high, net.rep, net.down, (net.z > 0) & (net.z < 3))
    mine = experts.at[net.shard]
    net.put(events[2], expert_piece, mine, net.rep, net.across)
    near = experts.at[net.place(1, 0)]
    net.put(events[3], near, near, net.rep, net.across)
    below = experts.at[lax.max(net.shard - 4, net.x)]
    above = experts.at[lax.min(net.shard + 4, 6 + net.x)]

    def spot(n):
        return net.place(n % 4, n // 4 % 2)

    spots = [spot(n) for n in range(8)]
    halves = [net.core, 1 - net.core]

    def source(n):
        return piece if n == 0 else bank.at[halves[n // 8], spots[n % 8]]

    def target(n):
        return (grads_own, grads_other)[n // 8].at[spots[n % 8]]

    from_below, from_above = net.z > 1, net.z < 2
    last_up, last_down = net.z == 2, net.z == 1

    def ready(k):
        if k == 3:
            net.got(events[0], below, from_below)
            net.got(events[1], above, from_above)
            net.put(events[4], below, below, net.rep, net.up, last_up)
            net.put(events[5], above, above, net.rep, net.down, last_down)

    unit_bank(None, None, [x], [c], source, target, None, 128, [out], [dx], scratch, ready)
    for event, like in arrivals:
        net.got(event, like)
    net.got(events[2], mine)
    net.got(events[3], mine)
    net.got(events[4], mine, net.z == 3)
    net.got(events[5], mine, net.z == 0)
    net.close()


def far_kernel(
    ext, xa, xb, ca, cb, expert_piece, shared_other, expert_in,
    oa, ob, da, db, grads, shared_mate, experts,
    send, recv, *scratch,
):
    net = Net(send, recv)
    events = [net.event() for _ in range(3)]
    net.meet("none", [(net.rep, net.across), (net.mate, net.shard)])
    net.put(events[2], shared_other, shared_mate, net.mate, net.shard)
    for n in (2, 3):
        piece = experts.at[net.place(n, 0)]
        net.put(events[n - 2], piece, piece, net.rep, net.across)
    spots = [net.place(n // 2, n % 2) for n in range(8)]

    def source(n):
        return expert_piece if n == 0 else experts.at[spots[n]]

    def target(n):
        return grads.at[spots[n]]

    def ready(k):
        if k >= 2:
            net.got(events[k - 2], experts.at[spots[2 * k + 1]])

    unit_bank(
        net.rep, ext, [xa, xb], [ca, cb], source, target, None, 256, [oa, ob], [da, db],
        scratch, ready,
    )
    net.got(events[2], shared_mate)
    net.close()


def near_kernel(
    ext, xa, xb, ca, cb, expert_piece, experts, before, far_a, far_b, shared_own, shared_mate,
    oa, ob, da, grads, back_a, back_b, back_c, shared_x,
    db, part_a, part_b, part_sems, send, recv, *scratch,
):
    net = Net(send, recv)
    events = [net.event() for _ in range(7)]
    peers = [(net.cousins[o], net.shard) for o in (1, 2, 3)]
    net.meet("none", peers + [(net.rep, net.across)])
    sides = [net.cycle(d) + 1 - 2 * net.x for d in range(4)]
    rows = [lax.div(side, 2) for side in sides]
    parts = []
    for d in range(4):
        parts.append((shared_own.at[sides[d]], part_a.at[d]))
        parts.append((shared_mate.at[sides[d]], part_b.at[d]))
    parts = [pltpu.make_async_copy(a, b, part_sems.at[i]) for i, (a, b) in enumerate(parts)]
    for copy in parts:
        copy.start()
    net.put(events[0], far_a, back_a, net.cousins[2], net.shard)
    net.put(events[1], far_b, back_b, net.cousins[3], net.shard)
    for copy in parts:
        copy.wait()
    for d in (2, 1, 3, 0):
        part_a[d] = (part_a[d].astype(F32) + part_b[d].astype(F32)).astype(BF)
        net.put(events[3 + d], part_a.at[d], shared_x.at[rows[d]], net.rep, net.across)
    spots = [net.place(n // 2, n % 2) for n in range(8)]

    def source(n):
        return expert_piece if n == 0 else experts.at[spots[n]]

    unit_bank(
        net.rep, ext, [xa, xb], [ca, cb], source,
        lambda n: grads.at[spots[n]], lambda n: before.at[spots[n]],
        256, [oa, ob], [da, db], scratch,
    )
    net.put(events[2], db, back_c, net.mate, net.shard)
    net.got(events[0], back_a)
    net.got(events[1], back_b)
    net.got(events[2], back_c)
    for d in range(4):
        net.got(events[3 + d], shared_x.at[rows[d]])
    net.close()


def plain_bank_kernel(blocks, unit, routed, chained, ext, *refs):
    refs = list(refs)

    def take(n):
        taken = refs[:n]
        del refs[:n]
        return taken

    xs, cs = take(blocks), take(blocks)
    bank = take(1)[0]
    before = take(1)[0] if chained else None
    outs, dxs = take(blocks), take(blocks)
    grads = take(1)[0]
    unit_bank(
        lax.axis_index("rep") if routed else None,
        ext, xs, cs,
        lambda n: bank.at[n],
        lambda n: grads.at[n],
        (lambda n: before.at[n]) if chained else None,
        unit, outs, dxs, refs,
    )


def plain_bank(ext, xs, cs, bank, before, routed):
    blocks, (rows, width) = len(xs), xs[0].shape
    chained = before is not None
    extra, unit = (16 if routed else 0), bank.shape[3]
    operands = [ext, *xs, *cs, bank] + ([before] if chained else [])
    outs = [shape((rows, width))] * blocks + [shape((rows + extra, width))] * blocks
    results = call(
        functools.partial(plain_bank_kernel, blocks, unit, routed, chained),
        outs + [shape(bank.shape)],
        [VMEM] * (1 + 2 * blocks) + [ANY] * (2 if chained else 1),
        [VMEM] * (2 * blocks) + [ANY],
        unit_scratch(blocks, rows, extra, width, CHUNK // unit, chained),
        flops=18 * blocks * rows * width * 4 * CHUNK,
        moved=30 * 2**20,
    )(*operands)
    return results[:blocks], results[blocks : 2 * blocks], results[2 * blocks]


def combine_rows(
    slot, d0, d1, d2, d3, d_shared, probs, middle, normed, cot, ext, attended, wo,
    d_middle, d_attended, grad_wo, grad_ext, branch, router_acc, gain_acc,
):
    tokens, width = middle.shape
    rep = lax.axis_index("rep")
    gain = ext[5:6, :]
    router = router_rows(ext)
    router_acc[...] = jnp.zeros_like(router_acc)
    gain_acc[...] = jnp.zeros_like(gain_acc)

    def tile(t, carry):
        at = pl.ds(pl.multiple_of(t * TILE, TILE), TILE)
        slot_one, slot_two = slot[at, 0:1], slot[at, 64:65]
        d_normed = d_shared[at, :].astype(F32)
        lane = iota((TILE, 128), 1)
        d_gates = jnp.zeros((TILE, 128), F32)
        for o, d in enumerate((d0, d1, d2, d3)):
            place = (iota((TILE, CAP), 1) + o * CAP).astype(F32)
            hit = (place == slot_one) | (place == slot_two)
            d_normed = d_normed + nn(ones_where(hit), d[0:CAP, :])
            share = d[CAP : CAP + 16, 0:CAP].astype(F32)[0:1, :]
            d_share = jnp.sum(jnp.where(hit, share, 0.0), axis=1, keepdims=True)
            d_gates = d_gates + jnp.where(lane == sibling(rep, o), d_share, 0.0)
        p = probs[at, :]
        inner = jnp.sum(d_gates * p, axis=1, keepdims=True)
        d_logits = (p * (d_gates - inner)).astype(BF)
        d_normed = d_normed + nn(d_logits, router)
        router_acc[...] += tn(d_logits, normed[at, :])
        rows = middle[at, :]
        scale = lax.rsqrt(jnp.mean(rows * rows, axis=1, keepdims=True) + EPSILON)
        unit = rows * scale
        gain_acc[...] += jnp.sum((d_normed * unit).reshape(TILE // 8, 8, width), axis=0)
        w = d_normed * gain
        inner = jnp.mean(w * unit, axis=1, keepdims=True)
        total = cot[at, :].astype(F32) + scale * (w - unit * inner)
        d_middle[at, :] = total
        rounded = total.astype(BF)
        branch[at, :] = rounded
        d_attended[at, :] = nt(rounded, wo[...]).astype(BF)
        return carry

    lax.fori_loop(0, tokens // TILE, tile, 0)
    grad_wo[...] = tn(attended[...], branch[...]).astype(BF)
    row = iota((16, width), 0)
    total = jnp.sum(gain_acc[...], axis=0, keepdims=True)
    grad_ext[...] = jnp.where(row < 4, router_acc[0:16, :], jnp.where(row == 5, total, 0.0))


def output_rows(slot, o0, o1, o2, o3, shared, probs, middle, out, first, last):
    rep = lax.axis_index("rep")

    def tile(t, carry):
        at = pl.ds(pl.multiple_of(t * TILE, TILE), TILE)
        slot_one, slot_two = slot[at, 0:1], slot[at, 64:65]
        total = middle[at, :] + shared[at, :].astype(F32)
        p = probs[at, :]
        lane = iota((TILE, 128), 1)
        for o, rows in enumerate((o0, o1, o2, o3)):
            place = (iota((TILE, CAP), 1) + o * CAP).astype(F32)
            hit = (place == slot_one) | (place == slot_two)
            share = jnp.sum(jnp.where(lane == sibling(rep, o), p, 0.0), axis=1, keepdims=True)
            total = total + nn(jnp.where(hit, share, 0.0).astype(BF), rows[...])
        out[at, :] = total.astype(BF)
        return carry

    lax.fori_loop(first, last, tile, 0)


def back_pairs(
    q, k, v, d_out, out, lse, cosine, sine, dq, dk, dv, bias, dk_acc, dv_acc, step
):
    tokens, width = q.shape

    def pair(i, carry):
        step(i)
        cols = pl.ds(pl.multiple_of(i * 128, 128), 128)
        keys, values = k[:, cols], v[:, cols]
        half_keys = [keep_half(keys, 0), keep_half(keys, 1)]
        dk_acc[...] = jnp.zeros_like(dk_acc)
        dv_acc[...] = jnp.zeros_like(dv_acc)
        low = iota((TILE, 128), 1) < 64
        for t in range(tokens // TILE):
            begin = t * TILE
            end = min(tokens, begin + TILE + PIECE)
            at = slice(begin, begin + TILE)
            block, grad = q[at, cols], d_out[at, cols]
            product = grad.astype(F32) * out[at, cols].astype(F32)
            block_lse = lse[at, cols]
            d_block = None
            for h in range(2):
                block_h, grad_h = keep_half(block, h), keep_half(grad, h)
                scores = nt(block_h, keys[:end])
                scores = biased(scores, bias, begin, begin, end)
                probs = jnp.exp(scores - block_lse[:, 64 * h : 64 * h + 1])
                d_probs = nt(grad_h, values[:end])
                inner = jnp.sum(
                    jnp.where(low if h == 0 else ~low, product, 0.0), axis=1, keepdims=True
                )
                d_scores = (probs * (d_probs - inner)).astype(BF)
                part = nn(d_scores, half_keys[h][:end])
                d_block = part if d_block is None else d_block + part
                dk_acc[0:end, :] += tn(d_scores, block_h)
                dv_acc[0:end, :] += tn(probs.astype(BF), grad_h)
            dq[at, cols] = spin(d_block * 0.125, cosine[at, :], -sine[at, :]).astype(BF)
        dk[:, cols] = spin(dk_acc[...], cosine[...], -sine[...]).astype(BF)
        dv[:, cols] = dv_acc[...].astype(BF)
        return carry

    lax.fori_loop(0, width // 128, pair, 0)


def fetch(sources, targets, sems):
    copies = [pltpu.make_async_copy(a, b, sems.at[i]) for i, (a, b) in enumerate(zip(sources, targets))]
    for copy in copies:
        copy.start()
    for copy in copies:
        copy.wait()


class Reduce:
    def __init__(self, net, own, from_x, from_z, held, spare, sems):
        self.net, self.own, self.from_x, self.from_z = net, own, from_x, from_z
        self.held, self.spare, self.sems = held, spare, sems
        self.x_events = [net.event() for _ in range(4)]
        self.z_events = [net.event() for _ in range(3)]
        self.spots = [net.cycle(d) for d in range(4)]
        self.levels = [lax.div(spot, 2) for spot in self.spots]
        self.pieces = [held.at[d] for d in range(4)]

    def send_across(self):
        net = self.net
        for d in (2, 1, 3, 0):
            source = self.own[0].at[self.spots[d] + 1 - 2 * net.x]
            target = self.from_x.at[self.levels[d]]
            net.put(self.x_events[d], source, target, net.rep, net.across)

    def add_across(self, d, wait=True):
        net = self.net
        far = self.from_x.at[self.levels[d]]
        if wait:
            net.got(self.x_events[d], far)
        sources = [own.at[self.spots[d]] for own in self.own] + [far]
        targets = [self.held.at[d]] + [self.spare.at[i] for i in range(len(self.own))]
        fetch(sources, targets, self.sems)
        total = self.held[d].astype(F32)
        for i in range(len(self.own)):
            total = total + self.spare[i].astype(F32)
        self.held[d] = total.astype(BF)
        if d:
            target = self.from_z.at[d - 1]
            net.put(self.z_events[d - 1], self.pieces[d], target, net.rep, self.spots[d])

    def total(self, out):
        for d in (1, 2, 3):
            self.net.got(self.z_events[d - 1], self.from_z.at[d - 1])
        targets = [self.held.at[d] for d in (1, 2, 3)]
        self.settle()
        fetch([self.from_z.at[d] for d in range(3)], targets, self.sems)
        total = self.held[0].astype(F32)
        for d in (1, 2, 3):
            total = total + self.held[d].astype(F32)
        out[...] = total.astype(BF)

    def settle(self):
        for event in self.z_events:
            cond, source = self.net.open.pop(event)
            self.net.copy(event, source, source, self.net.rep, self.net.shard).wait_send()


def back_kernel(
    starts, slot, d0, d1, d2, d3, d_shared, probs, middle, normed, cot, ext, attended, wo,
    q, k, v, lse, cosine, sine,
    o1, o2, o3, grads, shared_own, shared_mate, shared_x,
    d_middle, grad_wo, grad_ext, dq, dk, dv, expert_total, shared_total,
    r1, r2, r3, expert_x, expert_z, shared_z,
    d_attended, branch, router_acc, gain_acc, bias, dk_acc, dv_acc,
    held, spare, held_s, spare_s, sems, send, recv,
):
    net = Net(send, recv)
    expert = Reduce(net, [grads], expert_x, expert_z, held, spare, sems)
    shared = Reduce(net, [shared_own, shared_mate], shared_x, shared_z, held_s, spare_s, sems)
    peers = [(net.cousins[o], net.shard) for o in (1, 2, 3)]
    net.meet("all", peers + [(net.rep, net.across)])
    expert.send_across()
    arrivals = exchange(net, (o1, o2, o3), (r1, r2, r3))
    for d in (2, 1, 3, 0):
        shared.add_across(d, False)
    combine_rows(
        slot, d0, d1, d2, d3, d_shared, probs, middle, normed, cot, ext, attended, wo,
        d_middle, d_attended, grad_wo, grad_ext, branch, router_acc, gain_acc,
    )
    fill_bias(starts, bias)
    expert.add_across(2)

    def step(i):
        @pl.when(i == 3)
        def _():
            expert.add_across(1)

    back_pairs(
        q, k, v, d_attended, attended, lse, cosine, sine, dq, dk, dv, bias, dk_acc, dv_acc, step
    )
    shared.total(shared_total)
    expert.add_across(3)
    expert.add_across(0)
    for event, like in arrivals:
        net.got(event, like)
    expert.total(expert_total)
    net.close()


def plain_back_kernel(
    starts, slot, d0, d1, d2, d3, d_shared, probs, middle, normed, cot, ext, attended, wo,
    q, k, v, lse, cosine, sine,
    d_middle, grad_wo, grad_ext, dq, dk, dv,
    d_attended, branch, router_acc, gain_acc, bias, dk_acc, dv_acc,
):
    combine_rows(
        slot, d0, d1, d2, d3, d_shared, probs, middle, normed, cot, ext, attended, wo,
        d_middle, d_attended, grad_wo, grad_ext, branch, router_acc, gain_acc,
    )
    fill_bias(starts, bias)
    back_pairs(
        q, k, v, d_attended, attended, lse, cosine, sine, dq, dk, dv, bias, dk_acc, dv_acc,
        lambda i: None,
    )


def norm_rows(x, ext, normed_all):
    gain = ext[4:5, :]

    def tile(t, carry):
        at = pl.ds(pl.multiple_of(t * TILE, TILE), TILE)
        rows = x[at, :].astype(F32)
        scale = lax.rsqrt(jnp.mean(rows * rows, axis=1, keepdims=True) + EPSILON)
        normed_all[at, :] = (rows * scale * gain).astype(BF)
        return carry

    lax.fori_loop(0, x.shape[0] // TILE, tile, 0)


def input_grad(x, ext, dq, dk, dv, wq, wk, wv, d_middle, grad_in, gain_acc):
    tokens, width = x.shape
    gain = ext[4:5, :]
    gain_acc[...] = jnp.zeros_like(gain_acc)

    def tile(t, carry):
        at = pl.ds(pl.multiple_of(t * TILE, TILE), TILE)
        rows = x[at, :].astype(F32)
        scale = lax.rsqrt(jnp.mean(rows * rows, axis=1, keepdims=True) + EPSILON)
        unit = rows * scale
        d_normed = nt(dq[at, :], wq[...]) + nt(dk[at, :], wk[...]) + nt(dv[at, :], wv[...])
        gain_acc[...] += jnp.sum((d_normed * unit).reshape(TILE // 8, 8, width), axis=0)
        w = d_normed * gain
        inner = jnp.mean(w * unit, axis=1, keepdims=True)
        grad_in[at, :] = d_middle[at, :] + scale * (w - unit * inner)
        return carry

    lax.fori_loop(0, tokens // TILE, tile, 0)


def tail_kernel(
    x, ext, dq, dk, dv, wq, wk, wv, d_middle, grad_wo, grad_ext,
    slot, o0, o1, o2, o3, shared_out, probs, middle, expert_total, shared_total,
    grad_in, outputs, weights, small, shared_pair, e1, e2, e3,
    normed_all, gain_acc, gw, from_mate, from_x, from_z, from_y, result, from_core,
    tiny, tiny_in, shared_in, shared_sum, send, recv,
):
    width = x.shape[1]
    half = width // SLOTS
    net = Net(send, recv)
    e_events = [net.event() for _ in range(3)]
    s_events = [net.event() for _ in range(2)]
    m_events = [net.event() for _ in range(2)]
    x_events = [[net.event() for _ in range(2)] for _ in range(4)]
    z_events = [[net.event() for _ in range(2)] for _ in range(3)]
    y_event, c_event = net.event(), net.event()
    t_events = [net.event() for _ in range(6)]
    net.meet(
        "all", [(net.mate, net.shard), (net.cousins[2], net.shard), (net.rep, net.across)]
    )
    far = net.cousins[2]
    net.put(s_events[0], shared_total, shared_in, far, net.shard)
    net.put(e_events[1], expert_total, e2, far, net.shard)
    net.put(e_events[0], expert_total, e1, net.mate, net.shard)
    norm_rows(x, ext, normed_all)
    spots = [lax.rem(i + 2 * net.core, 4) for i in range(4)]
    gw[spots[0]] = tn(normed_all[...], dq[...]).astype(BF)
    gw[spots[1]] = tn(normed_all[...], dk[...]).astype(BF)
    gw[spots[2]] = tn(normed_all[...], dv[...]).astype(BF)
    gw[spots[3]] = grad_wo[...]
    for i in range(2):
        net.put(m_events[i], gw.at[2 + i], from_mate.at[i], net.mate, net.shard)

    def rows_of(spot):
        return pl.ds(pl.multiple_of(spot * half, 32), half)

    mine = [rows_of(net.cycle(d)) for d in range(4)]
    theirs = [rows_of(net.cycle(d) + 1 - 2 * net.x) for d in range(4)]
    for i in range(2):
        net.got(m_events[i], from_mate.at[i])
        gw[i] = (gw[i].astype(F32) + from_mate[i].astype(F32)).astype(BF)
    for d in (2, 1, 3, 0):
        for i in range(2):
            net.put(
                x_events[d][i], gw.at[i, theirs[d]], from_x.at[d, i], net.rep, net.across
            )
    input_grad(x, ext, dq, dk, dv, wq, wk, wv, d_middle, grad_in, gain_acc)
    row = iota((16, width), 0)
    total = jnp.sum(gain_acc[...], axis=0, keepdims=True)
    tiny[0] = (grad_ext[...] + jnp.where(row == 4, total, 0.0)).astype(BF)
    net.put(t_events[0], tiny.at[0], tiny_in.at[0], net.mate, net.shard)

    def add_across(d):
        for i in range(2):
            net.got(x_events[d][i], from_x.at[d, i])
            summed = gw[i, mine[d], :].astype(F32) + from_x[d, i].astype(F32)
            gw[i, mine[d], :] = summed.astype(BF)
            if d:
                net.put(
                    z_events[d - 1][i], gw.at[i, mine[d]], from_z.at[d - 1, i],
                    net.rep, net.cycle(d),
                )

    def tiny_add(n, target_rep, target_shard):
        net.got(t_events[n], tiny_in.at[n])
        tiny[n + 1] = (tiny[n].astype(F32) + tiny_in[n].astype(F32)).astype(BF)
        if target_rep is not None:
            source, target = tiny.at[n + 1], tiny_in.at[n + 1]
            net.put(t_events[n + 1], source, target, target_rep, target_shard)

    add_across(2)
    tiny_add(0, net.rep, net.across)
    output_rows(slot, o0, o1, o2, o3, shared_out, probs, middle, outputs, 0, 2)
    add_across(1)
    tiny_add(1, far, net.shard)
    net.got(s_events[0], shared_in)
    shared_sum[...] = (shared_total[...].astype(F32) + shared_in[...].astype(F32)).astype(BF)
    shared_pair[0] = shared_sum[...]
    net.put(s_events[1], shared_sum, shared_pair.at[1], net.mate, net.shard)
    output_rows(slot, o0, o1, o2, o3, shared_out, probs, middle, outputs, 2, 4)
    tiny_add(2, None, None)
    for d in (1, 2, 3):
        net.put(t_events[2 + d], tiny.at[3], tiny_in.at[2 + d], net.rep, net.cycle(d))
    add_across(3)
    add_across(0)
    for i in range(2):
        total = gw[i, mine[0], :].astype(F32)
        for d in (1, 2, 3):
            net.got(z_events[d - 1][i], from_z.at[d - 1, i])
            total = total + from_z[d - 1, i].astype(F32)
        result[0, i] = total.astype(BF)
    net.put(y_event, result.at[0], from_y, far, net.shard)
    total = tiny[3].astype(F32)
    for d in (1, 2, 3):
        net.got(t_events[2 + d], tiny_in.at[2 + d])
        total = total + tiny_in[2 + d].astype(F32)
    small[...] = total.astype(BF).astype(F32)
    net.got(e_events[1], e2)
    net.put(e_events[2], e2, e3, net.mate, net.shard)
    net.got(y_event, from_y)
    result[1] = (result[0].astype(F32) + from_y[...].astype(F32)).astype(BF)
    net.put(c_event, result.at[1], from_core, net.mate, net.shard)
    for i in range(2):
        weights[spots[i]] = result[1, i].astype(F32)
    net.got(c_event, from_core)
    for i in range(2):
        weights[spots[2 + i]] = from_core[i].astype(F32)
    net.got(e_events[0], e1)
    net.got(s_events[1], shared_pair.at[1])
    net.got(e_events[2], e3)
    net.close()


def plain_tail_kernel(
    x, ext, dq, dk, dv, wq, wk, wv, d_middle,
    slot, o0, o1, o2, o3, shared_out, probs, middle,
    grad_in, outputs, gw, gain, normed_all, gain_acc,
):
    norm_rows(x, ext, normed_all)
    for i, d in enumerate((dq, dk, dv)):
        gw[i] = tn(normed_all[...], d[...]).astype(BF)
    input_grad(x, ext, dq, dk, dv, wq, wk, wv, d_middle, grad_in, gain_acc)
    gain[...] = gain_acc[...]
    output_rows(
        slot, o0, o1, o2, o3, shared_out, probs, middle, outputs, 0, x.shape[0] // TILE
    )


def finish_kernel(e0, e1, e2, e3, pair, gate, up, down, s_gate, s_up, s_down):
    rep = lax.axis_index("rep")
    core = lax.rem(rep, 2)
    for o, part in enumerate((e0, e1, e2, e3)):
        at = sibling(rep, o)
        gate[at] = part[0].astype(F32)
        up[at] = part[1].astype(F32)
        down[at] = part[2].astype(F32).T
    span = pair.shape[3]
    for side in range(2):

        @pl.when(core == side)
        def _():
            for n in range(2):
                at = (side + n) % 2 * span
                s_gate[:, at : at + span] = pair[n, 0].astype(F32)
                s_up[:, at : at + span] = pair[n, 1].astype(F32)
                s_down[at : at + span, :] = pair[n, 2].astype(F32).T


def rope_tables(length, head_dim):
    positions = jnp.arange(length, dtype=F32)
    inverse_freq = 10000.0 ** (-2.0 * jnp.arange(head_dim // 2, dtype=F32) / head_dim)
    angle = positions[:, None] * inverse_freq[None, :]
    cosine, sine = jnp.cos(angle), jnp.sin(angle)
    return (
        jnp.concatenate([cosine] * 4, axis=1),
        jnp.concatenate([-sine, sine, -sine, sine], axis=1),
    )


def body(
    inputs,
    piece_starts,
    routes,
    attn_gain,
    query_weight,
    key_weight,
    value_weight,
    out_weight,
    ffn_gain,
    router_weight,
    expert_gate,
    expert_up,
    expert_down,
    shared_gate,
    shared_up,
    shared_down,
    cotangent,
):
    _, tokens, width = inputs.shape
    shards = lax.axis_size("shard")
    rep, shard = lax.axis_index("rep"), lax.axis_index("shard")
    core = rep % 2
    ringed = shards == SLOTS
    rows = width // shards
    units = shared_gate.shape[1]
    x, cot, chosen = inputs[0], cotangent[0], routes[0]
    small = jnp.concatenate([router_weight.T, attn_gain[None], ffn_gain[None]], axis=0)
    small = jnp.pad(small, ((0, 10), (0, 0)))
    small = lax.dynamic_update_slice(jnp.zeros((16, width), BF), small, (0, shard * rows))
    blank = jnp.zeros((16, width), BF)
    if ringed:
        half_one = jnp.concatenate([query_weight, key_weight, small], axis=0)
        half_two = jnp.concatenate([value_weight, out_weight, blank], axis=0)
        piece = jnp.where(core == 0, half_one, half_two)
    else:
        wq, wk, wv, wo = [
            lax.all_gather(w, "shard", axis=0, tiled=True)
            for w in (query_weight, key_weight, value_weight, out_weight)
        ]
        ext = lax.psum(small.astype(F32), "shard")

    shared_pack = jnp.stack([shared_gate, shared_up, shared_down.T])
    my_half = lax.dynamic_slice_in_dim(shared_pack, core * (units // 2), units // 2, 2)
    expert_pack = jnp.stack([expert_gate[rep], expert_up[rep], expert_down[rep].T])

    cosine, sine = rope_tables(tokens, width // HEADS)
    token_f = shape((tokens, width))
    square = shape((width, width))
    packed = [shape((CAP, width))] * 4
    outs = [shape((8, tokens), F32), shape((tokens, 128), F32)] + [token_f] * 3
    work = 2 * tokens * width * (CAP * 4 + 3 * width)
    if ringed:
        rank, slot, q, k, v, *heads = call(
            head_kernel,
            outs + [square] * 4 + [shape((16, width), F32)] + packed,
            [VMEM] * 7,
            [VMEM] * 10 + [VMEM] + [ANY] * 3,
            [
                pltpu.VMEM((2, SLOTS, 2 * rows + 16, width), BF),
                pltpu.VMEM((3, CAP, width), BF),
                pltpu.SemaphoreType.DMA((31,)),
                pltpu.SemaphoreType.DMA((31,)),
                pltpu.SemaphoreType.DMA,
            ],
            flops=work,
            moved=24 * 2**20,
            group=0,
        )(chosen, chosen.T, cot, x, piece, cosine, sine)
        wq, wk, wv, wo, ext, *cot_in = heads
    else:
        rank, slot, q, k, v, *cot_out = call(
            plain_head_kernel, outs + packed, [VMEM] * 10, [VMEM] * 9, flops=work,
            moved=24 * 2**20,
        )(chosen, chosen.T, cot, x, cosine, sine, wq, wk, wv, ext)
        cot_in = [cot_out[0]] + [to_rep(cot_out[o], o) for o in (1, 2, 3)]

    outs = [token_f, shape((tokens, width), F32), shape((tokens, width), F32), token_f]
    outs += [shape((tokens, 128), F32)] + packed
    work = 2 * tokens * width * (8 * tokens + width + 4 * CAP)
    bias = pltpu.VMEM((tokens, tokens), F32)
    if ringed:
        attended, lse, middle, normed, probs, *x_out, shared_bank, expert_bank = call(
            forward_kernel,
            outs + [shape((2, SLOTS) + my_half.shape), shape((SLOTS,) + expert_pack.shape)],
            [SMEM] + [VMEM] * 7 + [ANY] * 2,
            [VMEM] * 9 + [ANY] * 2,
            [bias, pltpu.SemaphoreType.DMA((30,)), pltpu.SemaphoreType.DMA((30,))],
            flops=work,
            moved=30 * 2**20,
            group=1,
        )(piece_starts, q, k, v, x, wo, ext, rank, my_half, expert_pack)
    else:
        attended, lse, middle, normed, probs, *x_out = call(
            plain_forward_kernel, outs, [SMEM] + [VMEM] * 7, [VMEM] * 9, [bias], flops=work,
            moved=30 * 2**20,
        )(piece_starts, q, k, v, x, wo, ext, rank)

    rows_out = shape((CAP, width))
    rows_back = shape((CAP + 16, width))
    if ringed:
        half_grads = shape((SLOTS,) + my_half.shape)
        shared_out, shared_dx, grads_own, grads_other, y1, y2, y3, expert_bank = call(
            shared_kernel,
            [token_f] * 2 + [half_grads] * 2 + packed[:3] + [shape(expert_bank.shape)],
            [VMEM] * 2 + [ANY] * 7,
            [VMEM] * 2 + [ANY] * 6,
            [pltpu.SemaphoreType.DMA((9,)), pltpu.SemaphoreType.DMA((9,))]
            + unit_scratch(1, tokens, 0, width, 4, False),
            flops=18 * tokens * width * CHUNK * CHUNKS,
            moved=30 * 2**20,
            group=2,
            alias={8: 7},
        )(normed, cot, my_half, shared_bank, *x_out[1:], expert_pack, expert_bank)
        x_in = [x_out[0], y1, y2, y3]
        bank = shape(expert_bank.shape)
        far_a, far_b, da, db, before, shared_mate, expert_bank = call(
            far_kernel,
            [rows_out] * 2 + [rows_back] * 2 + [bank, half_grads, bank],
            [VMEM] * 5 + [ANY] * 3,
            [VMEM] * 4 + [ANY] * 3,
            [pltpu.SemaphoreType.DMA((3,)), pltpu.SemaphoreType.DMA((3,))]
            + unit_scratch(2, CAP, 16, width, 2, False),
            flops=36 * CAP * width * CHUNK * CHUNKS,
            moved=30 * 2**20,
            group=3,
            alias={7: 6},
        )(ext, *x_in[2:], *cot_in[2:], expert_pack, grads_other, expert_bank)
        half_x = (4,) + my_half.shape
        near_a, near_b, d0, grads, d2, d3, d1, shared_x = call(
            near_kernel,
            [rows_out] * 2 + [rows_back, bank] + [rows_back] * 3 + [shape(half_x)],
            [VMEM] * 5 + [ANY] * 7,
            [VMEM] * 3 + [ANY] * 5,
            [
                pltpu.VMEM((CAP + 16, width), BF),
                pltpu.VMEM(half_x, BF),
                pltpu.VMEM(half_x, BF),
                pltpu.SemaphoreType.DMA((8,)),
                pltpu.SemaphoreType.DMA((7,)),
                pltpu.SemaphoreType.DMA((7,)),
            ]
            + unit_scratch(2, CAP, 16, width, 2, True),
            flops=36 * CAP * width * CHUNK * CHUNKS,
            moved=30 * 2**20,
            group=4,
        )(
            ext, *x_in[:2], *cot_in[:2], expert_pack, expert_bank, before, da, db,
            grads_own, shared_mate,
        )
        d_rows = [d0, d1, d2, d3]
    else:

        def slotted(part):
            every = lax.all_gather(part, "shard")
            every = every.reshape(SLOTS, shards // SLOTS, 3, width, part.shape[2])
            return every.transpose(0, 2, 3, 1, 4).reshape(SLOTS, 3, width, -1)

        shared_bank = slotted(my_half)
        shared_bank = jnp.concatenate([shared_bank, to_rep(shared_bank, 1)], axis=0)
        expert_bank = slotted(expert_pack)
        x_in = [x_out[0]] + [to_rep(x_out[o], o) for o in (1, 2, 3)]
        (shared_out,), (shared_dx,), shared_grads = plain_bank(
            ext, [normed], [cot], shared_bank, None, False
        )
        grads_own, grads_other = shared_grads[:SLOTS], shared_grads[SLOTS:]
        (far_a, far_b), (da, db), before = plain_bank(
            ext, x_in[2:], cot_in[2:], expert_bank, None, True
        )
        (near_a, near_b), (d0, d1), grads = plain_bank(
            ext, x_in[:2], cot_in[:2], expert_bank, before, True
        )
        d_rows = [d0, to_rep(d1, 1), to_rep(da, 2), to_rep(db, 3)]
    wide = shape((tokens, width), F32)
    outs = [wide, square, shape((16, width), F32)] + [token_f] * 3
    operands = (piece_starts, slot, *d_rows, shared_dx, probs, middle, normed, cot, ext, attended)
    operands += (wo, q, k, v, lse, cosine, sine)
    specs = [SMEM] + [VMEM] * 19
    scratch = [
        pltpu.VMEM((tokens, width), BF),
        pltpu.VMEM((tokens, width), BF),
        pltpu.VMEM((128, width), F32),
        pltpu.VMEM((8, width), F32),
        bias,
        pltpu.VMEM((tokens, 128), F32),
        pltpu.VMEM((tokens, 128), F32),
    ]
    work = 2 * tokens * width * (2 * width + 4 * CAP) + 40 * tokens * tokens * width
    if ringed:
        bank_x, bank_z = (4,) + expert_pack.shape, (3,) + expert_pack.shape
        half_z = (3,) + my_half.shape
        d_middle, grad_wo, grad_ext, dq, dk, dv, expert_total, shared_total, *back = call(
            back_kernel,
            outs
            + [shape(expert_pack.shape), shape(my_half.shape)]
            + [rows_out] * 3
            + [shape(bank_x), shape(bank_z), shape(half_z)],
            specs + [ANY] * 7,
            [VMEM] * 8 + [ANY] * 6,
            scratch
            + [
                pltpu.VMEM(bank_x, BF),
                pltpu.VMEM((1,) + expert_pack.shape, BF),
                pltpu.VMEM(half_x, BF),
                pltpu.VMEM((2,) + my_half.shape, BF),
                pltpu.SemaphoreType.DMA((3,)),
                pltpu.SemaphoreType.DMA((17,)),
                pltpu.SemaphoreType.DMA((17,)),
            ],
            flops=work,
            moved=40 * 2**20,
            group=5,
        )(*operands, near_b, far_a, far_b, grads, grads_own, shared_mate, shared_x)
        operands = (x, ext, dq, dk, dv, wq, wk, wv, d_middle, grad_wo, grad_ext)
        operands += (slot, near_a, *back[:3], shared_out, probs, middle)
        strip = (2, width // SLOTS, width)
        grad_in, outputs, weights, small, shared_pair, e1, e2, e3 = call(
            tail_kernel,
            [wide, token_f, shape((4, rows, width), F32), shape((16, width), F32)]
            + [shape((2,) + my_half.shape)]
            + [shape(expert_pack.shape)] * 3,
            [VMEM] * 19 + [ANY, VMEM],
            [VMEM] * 5 + [ANY] * 3,
            [
                pltpu.VMEM((tokens, width), BF),
                pltpu.VMEM((8, width), F32),
                pltpu.VMEM((4, width, width), BF),
                pltpu.VMEM((2, width, width), BF),
                pltpu.VMEM((4,) + strip, BF),
                pltpu.VMEM((3,) + strip, BF),
                pltpu.VMEM(strip, BF),
                pltpu.VMEM((2,) + strip, BF),
                pltpu.VMEM(strip, BF),
                pltpu.VMEM((4, 16, width), BF),
                pltpu.VMEM((6, 16, width), BF),
                pltpu.VMEM(my_half.shape, BF),
                pltpu.VMEM(my_half.shape, BF),
                pltpu.SemaphoreType.DMA((29,)),
                pltpu.SemaphoreType.DMA((29,)),
            ],
            flops=2 * tokens * width * (6 * width + 4 * CAP),
            moved=40 * 2**20,
            group=6,
        )(*operands, expert_total, shared_total)
        banks = [shape((4, width, units), F32)] * 2 + [shape((4, units, width), F32)]
        banks += [shape((width, units), F32)] * 2 + [shape((units, width), F32)]
        finals = call(finish_kernel, banks, [VMEM] * 5, [VMEM] * 6, moved=18 * 2**20)(
            expert_total, e1, e2, e3, shared_pair
        )
        grad_q, grad_k, grad_v, grad_o = (weights[i] for i in range(4))
    else:
        d_middle, grad_wo, grad_ext, dq, dk, dv = call(
            plain_back_kernel, outs, specs, [VMEM] * 6, scratch, flops=work, moved=40 * 2**20
        )(*operands)
        out_rows = [near_a, to_rep(near_b, 1), to_rep(far_a, 2), to_rep(far_b, 3)]
        grad_in, outputs, gw, gain = call(
            plain_tail_kernel,
            [wide, token_f, shape((3, width, width)), shape((8, width), F32)],
            [VMEM] * 17,
            [VMEM] * 4,
            [pltpu.VMEM((tokens, width), BF), pltpu.VMEM((8, width), F32)],
            flops=2 * tokens * width * (6 * width + 4 * CAP),
            moved=40 * 2**20,
        )(
            x, ext, dq, dk, dv, wq, wk, wv, d_middle, slot, *out_rows, shared_out, probs, middle
        )

        def over_rep(total):
            return lax.psum(total.astype(BF), "rep").astype(F32)

        def unslot(every, part_units):
            every = every.reshape(SLOTS, 3, width, shards // SLOTS, part_units)
            every = every.transpose(0, 3, 1, 2, 4).reshape(shards, 3, width, part_units)
            return lax.psum_scatter(every, "shard", scatter_dimension=0)

        grad_q, grad_k, grad_v, grad_o = (
            over_rep(lax.psum_scatter(w, "shard", tiled=True))
            for w in (gw[0], gw[1], gw[2], grad_wo)
        )
        small = grad_ext.at[4].add(jnp.sum(gain, axis=0))
        small = lax.psum(small, ("rep", "shard"))
        shared_sum = grads_own.astype(F32) + to_rep(grads_other, 1).astype(F32)
        total = unslot(shared_sum.astype(BF), units // 2).astype(F32)
        total = (total + to_rep(total.astype(BF), 2).astype(F32)).astype(BF)
        mate = to_rep(total, 1)
        shared_full = jnp.concatenate(
            [jnp.where(core == 0, total, mate), jnp.where(core == 0, mate, total)], axis=2
        ).astype(F32)
        expert_total = unslot(grads, units).astype(BF)
        parts = jnp.stack([expert_total] + [to_rep(expert_total, o) for o in (1, 2, 3)])
        full = jnp.take(parts, jnp.arange(4) ^ rep, axis=0).astype(F32)
        finals = (full[:, 0], full[:, 1], full[:, 2].transpose(0, 2, 1))
        finals += (shared_full[0], shared_full[1], shared_full[2].T)
    tiny = lax.dynamic_slice(small, (0, shard * rows), (16, rows))
    return (
        outputs[None],
        grad_in[None],
        tiny[4],
        grad_q,
        grad_k,
        grad_v,
        grad_o,
        tiny[5],
        tiny[:4].T,
        *finals,
    )


def solution(mesh):
    in_specs = (
        P(("rep", "shard"), None, None),
        P(("rep", "shard"), None),
        P(("rep", "shard"), None, None),
        P("shard"),
        P("shard", None),
        P("shard", None),
        P("shard", None),
        P("shard", None),
        P("shard"),
        P("shard", None),
        P(None, None, "shard"),
        P(None, None, "shard"),
        P(None, "shard", None),
        P(None, "shard"),
        P(None, "shard"),
        P("shard", None),
        P(("rep", "shard"), None, None),
    )
    out_specs = (
        P(("rep", "shard"), None, None),
        P(("rep", "shard"), None, None),
        P("shard"),
        P("shard", None),
        P("shard", None),
        P("shard", None),
        P("shard", None),
        P("shard"),
        P("shard", None),
        P(None, None, "shard"),
        P(None, None, "shard"),
        P(None, "shard", None),
        P(None, "shard"),
        P(None, "shard"),
        P("shard", None),
    )
    return jax.shard_map(body, mesh=mesh, in_specs=in_specs, out_specs=out_specs, check_vma=False)
```

```python
import functools

import jax
import jax.numpy as jnp
from jax import lax
from jax.experimental import pallas as pl
from jax.experimental.pallas import tpu as pltpu
from jax.sharding import PartitionSpec as P

HEADS = 12
PIECE = 256
CAP = 576
EPSILON = 1e-06
MASKED = -1e30
F32, BF = jnp.float32, jnp.bfloat16
AXES = ("rep", "shard")
TILE = 256
SLOTS = 8
VMEM_LIMIT = 62 * 2**20
ANY = pl.BlockSpec(memory_space=pl.ANY)
SMEM = pl.BlockSpec(memory_space=pltpu.SMEM)
VMEM = pl.BlockSpec(memory_space=pltpu.VMEM)


def dot(a, b, i, j):
    return lax.dot_general(a, b, (((i,), (j,)), ((), ())), preferred_element_type=F32)


def nn(a, b):
    return dot(a, b, 1, 0)


def nt(a, b):
    return dot(a, b, 1, 1)


def tn(a, b):
    return dot(a, b, 0, 0)


def iota(shape, dim):
    return lax.broadcasted_iota(jnp.int32, shape, dim)


def ones_where(cond):
    return jnp.where(cond, 1.0, 0.0).astype(BF)


def call(
    kernel, out_shape, in_specs, out_specs, scratch=(), flops=0, moved=0, grid=None, group=None,
    alias=None,
):
    extra = {} if grid is None else {"grid": grid}
    params = {} if group is None else {"collective_id": group, "has_side_effects": True}
    return pl.pallas_call(
        kernel,
        out_shape=out_shape,
        in_specs=in_specs,
        out_specs=out_specs,
        scratch_shapes=list(scratch),
        input_output_aliases=alias or {},
        compiler_params=pltpu.CompilerParams(vmem_limit_bytes=VMEM_LIMIT, **params),
        cost_estimate=pl.CostEstimate(flops=flops, bytes_accessed=moved, transcendentals=0),
        **extra,
    )


def shape(dims, dtype=BF):
    return jax.ShapeDtypeStruct(dims, dtype)


def permute(x, move):
    reps, shards = lax.axis_size("rep"), lax.axis_size("shard")
    pairs = []
    for r in range(reps):
        for s in range(shards):
            to_r, to_s = move(r, s)
            pairs.append((r * shards + s, to_r * shards + to_s))
    return lax.ppermute(x, AXES, pairs)


def to_rep(x, offset):
    return permute(x, lambda r, s: (r ^ offset, s))


def spin(block, cosine, sine):
    lane = iota(block.shape, 1)
    partner = jnp.where(lane % 64 < 32, pltpu.roll(block, 96, 1), pltpu.roll(block, 32, 1))
    return block * cosine + partner * sine


def sibling(rep, o):
    return 2 * lax.rem(lax.div(rep, 2) + o // 2, 2) + lax.rem(lax.rem(rep, 2) + o % 2, 2)


def route_slots(rep, routes, routes_t, rank_out, slot_out):
    tokens = routes.shape[0]
    first, second = routes_t[0:1, :], routes_t[1:2, :]
    expert = iota((8, tokens), 0)
    chosen = (expert == first) | (expert == second)
    upper = ones_where(iota((tokens, tokens), 0) <= iota((tokens, tokens), 1))
    rank = nn(ones_where(chosen), upper) - 1.0
    rank_out[...] = jnp.where(chosen, rank, -1.0)
    lane = iota((tokens, 128), 1)
    one, two = routes[:, 0:1], routes[:, 1:2]
    lower = ones_where(iota((tokens, tokens), 0) >= iota((tokens, tokens), 1))
    place = nn(lower, ones_where((lane == one) | (lane == two))) - 1.0
    for o in range(1, 4):
        place = place + jnp.where(lane == sibling(rep, o), float(o * CAP), 0.0)
    slot_one = jnp.sum(jnp.where(lane == one, place, 0.0), axis=1, keepdims=True)
    slot_two = jnp.sum(jnp.where(lane == two, place, 0.0), axis=1, keepdims=True)
    slot_out[...] = jnp.where(lane < 64, slot_one, slot_two)


def pack_rows(rep, rank, source, packed):
    tokens = source.shape[0]
    for o, out in enumerate(packed):
        row = rank[pl.ds(sibling(rep, o), 1), :]
        pick = ones_where(iota((CAP, tokens), 0).astype(F32) == row)
        out[...] = nn(pick, source[...]).astype(BF)


def qkv_rows(x, ext, cosine, sine, wq, wk, wv, q, k, v):
    tokens, width = x.shape
    gain = ext[4:5, :]

    def tile(t, carry):
        at = pl.ds(pl.multiple_of(t * TILE, TILE), TILE)
        rows_in = x[at, :].astype(F32)
        scale = lax.rsqrt(jnp.mean(rows_in * rows_in, axis=1, keepdims=True) + EPSILON)
        normed = (rows_in * scale * gain).astype(BF)
        cos_t, sin_t = cosine[at, :], sine[at, :]
        for weight, out, factor in ((wq, q, 0.125), (wk, k, 1.0)):
            full = nn(normed, weight[...])
            for b in range(width // 128):
                turned = spin(full[:, b * 128 : (b + 1) * 128], cos_t, sin_t)
                out[at, b * 128 : (b + 1) * 128] = turned.astype(BF) * jnp.asarray(factor, BF)
        v[at, :] = nn(normed, wv[...]).astype(BF)
        return carry

    lax.fori_loop(0, tokens // TILE, tile, 0)


def when(cond, body):
    if cond is True:
        body()
    elif cond is not False:
        pl.when(cond)(body)


def both(one, two):
    if one is True or two is False:
        return two
    if two is True or one is False:
        return one
    return one & two


class Net:
    def __init__(self, send, recv):
        self.rep, self.shard = lax.axis_index("rep"), lax.axis_index("shard")
        self.core, self.z = lax.rem(self.rep, 2), lax.div(self.shard, 2)
        self.x = lax.rem(self.shard, 2)
        self.mate = self.rep + 1 - 2 * self.core
        self.across = self.shard + 1 - 2 * self.x
        first = lax.max(self.z - 1, 1 - self.z)
        third = 3 * (1 - lax.div(self.z, 2))
        self.levels = [self.z, first, 6 - self.z - first - third, third]
        self.up = lax.min(self.shard + 2, 6 + self.x)
        self.down = lax.max(self.shard - 2, self.x)
        self.cousins = [self.rep] + [sibling(self.rep, o) for o in (1, 2, 3)]
        self.send, self.recv = send, recv
        self.count, self.open = 0, {}

    def event(self):
        self.count += 1
        return self.count - 1

    def place(self, n, side):
        return self.levels[n] * 2 + (self.x if side == 0 else 1 - self.x)

    def cycle(self, d):
        return lax.rem(self.z + d, 4) * 2 + self.x

    def copy(self, event, source, target, rep, shard):
        return pltpu.make_async_remote_copy(
            src_ref=source,
            dst_ref=target,
            send_sem=self.send.at[event],
            recv_sem=self.recv.at[event],
            device_id=(rep, shard),
            device_id_type=pl.DeviceIdType.MESH,
        )

    def put(self, event, source, target, rep, shard, cond=True):
        when(cond, self.copy(event, source, target, rep, shard).start)
        self.open[event] = (cond, source)

    def got(self, event, like, cond=True):
        when(cond, self.copy(event, like, like, self.mate, self.shard).wait_recv)

    def settle(self, event):
        cond, source = self.open.pop(event)
        when(cond, self.copy(event, source, source, self.mate, self.shard).wait_send)

    def close(self):
        for event, (cond, source) in self.open.items():
            when(cond, self.copy(event, source, source, self.mate, self.shard).wait_send)

    def meet(self, z_ways, others):
        barrier = pltpu.get_barrier_semaphore()

        def greet(rep, shard):
            pl.semaphore_signal(
                barrier, inc=1, device_id=(rep, shard), device_id_type=pl.DeviceIdType.MESH
            )

        count = len(others)
        for rep, shard in others:
            greet(rep, shard)
        if z_ways == "line":
            when(self.z < 3, lambda: greet(self.rep, self.up))
            when(self.z > 0, lambda: greet(self.rep, self.down))
            count = count + lax.min(self.z, 1) + lax.min(3 - self.z, 1)
        if z_ways == "all":
            for d in (1, 2, 3):
                greet(self.rep, self.cycle(d))
            count = count + 3
        pl.semaphore_wait(barrier, count)


class Line:
    def __init__(self, net, bank, ways=4):
        self.net, self.bank = net, bank
        self.events = {(way, k): net.event() for way in range(ways) for k in range(-3, 4)}
        self.spots = {0: (net.shard, True)}
        for k in (1, 2, 3):
            self.spots[k] = (lax.min(net.shard + 2 * k, 6 + net.x), net.z < 4 - k)
            self.spots[-k] = (lax.max(net.shard - 2 * k, net.x), net.z >= k)
        self.flips = {k: spot + 1 - 2 * net.x for k, (spot, _) in self.spots.items()}
        self.onward = {k: both(self.spots[k][1], net.z < 3) for k in self.spots}
        self.back = {k: both(self.spots[k][1], net.z > 0) for k in self.spots}

    def spread(self, k, source):
        net, (spot, here) = self.net, self.spots[k]
        target = self.bank.at[net.core, spot]
        if -3 < k <= 0:
            event = self.events[0, k - 1]
            net.put(event, source, target, net.rep, net.up, self.onward[k])
        if 0 <= k < 3:
            event = self.events[0, k + 1]
            net.put(event, source, target, net.rep, net.down, self.back[k])
        net.put(self.events[1, k], source, target, net.rep, net.across, here)
        net.put(self.events[2, k], source, target, net.mate, net.shard, here)

    def along(self, k):
        spot, here = self.spots[k]
        piece = self.bank.at[self.net.core, spot]
        self.net.got(self.events[0, k], piece, here)
        self.spread(k, piece)

    def over(self, k):
        net, here = self.net, self.spots[k][1]
        piece = self.bank.at[net.core, self.flips[k]]
        net.got(self.events[1, k], piece, here)
        net.put(self.events[3, k], piece, piece, net.mate, net.shard, here)

    def finish(self):
        other = 1 - self.net.core
        for k in (0, 1, -1, 2, -2, 3, -3):
            spot, here = self.spots[k]
            self.net.got(self.events[2, k], self.bank.at[other, spot], here)
            self.net.got(self.events[3, k], self.bank.at[other, self.flips[k]], here)


class Spread:
    def __init__(self, net, piece, bank):
        self.net, self.piece, self.bank = net, piece, bank
        self.line = Line(net, bank, 8)
        self.events, self.spots, self.flips = self.line.events, self.line.spots, self.line.flips
        self.half = piece.shape[1] // 2
        y = lax.div(net.rep, 2)
        self.rows = [pl.ds(pl.multiple_of(n * self.half, 128), self.half) for n in (y, 1 - y)]
        self.far = net.cousins[2]

    def view(self, core, spot, rows):
        return self.bank.at[core, spot, :, self.rows[rows], :]

    def begin(self):
        net = self.net
        source = self.piece.at[:, self.rows[0], :]
        target = self.view(net.core, net.shard, 0)
        net.put(self.events[0, -1], source, target, net.rep, net.up, self.line.onward[0])
        net.put(self.events[0, 1], source, target, net.rep, net.down, self.line.back[0])
        net.put(self.events[1, 0], source, target, net.rep, net.across)
        whole = self.bank.at[net.core, net.shard]
        net.put(self.events[2, 0], self.piece, whole, net.mate, net.shard)

    def hand(self, way, k, here, piece):
        net = self.net
        net.put(self.events[way + 4, k], piece, piece, self.far, net.shard, here)
        net.put(self.events[way + 2, k], piece, piece, net.mate, net.shard, here)

    def along(self, k):
        net, (spot, here) = self.net, self.spots[k]
        piece = self.view(net.core, spot, 0)
        net.got(self.events[0, k], piece, here)
        if -3 < k < 0:
            net.put(self.events[0, k - 1], piece, piece, net.rep, net.up, self.line.onward[k])
        if 0 < k < 3:
            net.put(self.events[0, k + 1], piece, piece, net.rep, net.down, self.line.back[k])
        net.put(self.events[1, k], piece, piece, net.rep, net.across, here)
        self.hand(0, k, here, piece)

    def over(self, k):
        net, here = self.net, self.spots[k][1]
        piece = self.view(net.core, self.flips[k], 0)
        net.got(self.events[1, k], piece, here)
        self.hand(1, k, here, piece)

    def relay(self, way, k):
        net, here = self.net, self.spots[k][1]
        spot = self.spots[k][0] if way == 0 else self.flips[k]
        piece = self.view(net.core, spot, 1)
        net.got(self.events[way + 4, k], piece, here)
        net.put(self.events[way + 6, k], piece, piece, net.mate, net.shard, here)

    def finish(self):
        net, other = self.net, 1 - self.net.core
        net.got(self.events[2, 0], self.bank.at[other, net.shard])
        for k in (0, 1, -1, 2, -2, 3, -3):
            spot, here = self.spots[k]
            if k:
                net.got(self.events[2, k], self.view(other, spot, 0), here)
                net.got(self.events[6, k], self.view(other, spot, 1), here)
            net.got(self.events[3, k], self.view(other, self.flips[k], 0), here)
            net.got(self.events[7, k], self.view(other, self.flips[k], 1), here)


def exchange(net, sources, targets):
    events = [net.event() for _ in range(3)]
    for o in (2, 3, 1):
        net.put(events[o - 1], sources[o - 1], targets[o - 1], net.cousins[o], net.shard)
    return [(events[o], targets[o]) for o in range(3)]


def head_kernel(
    routes, routes_t, cot, x, piece, cosine, sine,
    rank, slot, q, k, v, wq, wk, wv, wo, ext, c0, c1, c2, c3,
    bank, packed, send, recv, own_sem,
):
    width = x.shape[1]
    half = width // SLOTS
    net = Net(send, recv)
    line = Line(net, bank)
    peers = [(net.cousins[o], net.shard) for o in (1, 2, 3)]
    net.meet("line", peers + [(net.rep, net.across)])
    line.spread(0, piece)
    own = pltpu.make_async_copy(piece, bank.at[net.core, net.shard], own_sem)
    own.start()
    route_slots(net.rep, routes, routes_t, rank, slot)
    pack_rows(net.rep, rank, cot, [c0] + [packed.at[o] for o in range(3)])
    arrivals = exchange(net, [packed.at[o] for o in range(3)], (c1, c2, c3))
    line.along(1)
    line.along(-1)
    line.over(0)
    line.along(2)
    line.along(-2)
    line.over(1)
    line.over(-1)
    line.along(3)
    line.along(-3)
    for step in (2, -2, 3, -3):
        line.over(step)
    own.wait()
    line.finish()
    gathered = bank[0, 0, 2 * half : 2 * half + 16, :].astype(F32)
    for j in range(1, SLOTS):
        gathered = gathered + bank[0, j, 2 * half : 2 * half + 16, :].astype(F32)
    ext[...] = gathered
    for j in range(SLOTS):
        at = slice(j * half, (j + 1) * half)
        wq[at, :] = bank[0, j, 0:half, :]
        wk[at, :] = bank[0, j, half : 2 * half, :]
        wv[at, :] = bank[1, j, 0:half, :]
        wo[at, :] = bank[1, j, half : 2 * half, :]
    qkv_rows(x, ext, cosine, sine, wq, wk, wv, q, k, v)
    for event, like in arrivals:
        net.got(event, like)
    net.close()


def plain_head_kernel(
    routes, routes_t, cot, x, cosine, sine, wq, wk, wv, ext,
    rank, slot, q, k, v, c0, c1, c2, c3,
):
    rep = lax.axis_index("rep")
    route_slots(rep, routes, routes_t, rank, slot)
    pack_rows(rep, rank, cot, (c0, c1, c2, c3))
    qkv_rows(x, ext, cosine, sine, wq, wk, wv, q, k, v)


def fill_bias(starts, bias):
    tokens = bias.shape[0]

    def tile(t, carry):
        at = pl.ds(pl.multiple_of(t * TILE, TILE), TILE)
        query = iota((TILE, tokens), 0) + t * TILE
        key = iota((TILE, tokens), 1)
        allowed = key <= query
        for n in range(2):
            begin = starts[0, n]
            inside = (query >= begin) & (query < begin + PIECE)
            allowed = allowed | (inside & (key >= begin) & (key < begin + PIECE))
        bias[at, :] = jnp.where(allowed, 0.0, MASKED)
        return carry

    lax.fori_loop(0, tokens // TILE, tile, 0)


def keep_half(block, h):
    low = iota(block.shape, 1) < 64
    return jnp.where(low if h == 0 else ~low, block.astype(F32), 0.0).astype(BF)


def biased(scores, bias, begin, free, end):
    tail = scores[:, free:] + bias[begin : begin + TILE, free:end]
    return tail if free == 0 else jnp.concatenate([scores[:, :free], tail], axis=1)


def attend_pairs(q, k, v, out, lse, bias, step):
    tokens, width = q.shape

    def pair(i, carry):
        step(i)
        cols = pl.ds(pl.multiple_of(i * 128, 128), 128)
        keys = k[:, cols]
        low = iota((tokens, 128), 1) < 64
        values = v[:, cols].astype(F32)
        value_one = [
            jnp.where(low, values, 1.0).astype(BF),
            jnp.where(low, 1.0, values).astype(BF),
        ]
        low = iota((TILE, 128), 1) < 64
        for t in range(tokens // TILE):
            begin = t * TILE
            end = min(tokens, begin + TILE + PIECE)
            block = q[begin : begin + TILE, cols]
            results, totals = [], []
            for h in range(2):
                scores = nt(keep_half(block, h), keys[:end])
                scores = biased(scores, bias, begin, begin, end)
                row_max = jnp.max(scores, axis=1, keepdims=True)
                probs = jnp.exp(scores - row_max).astype(BF)
                mixed = nn(probs, value_one[h][:end])
                total = pltpu.roll(mixed, 64, 1)
                results.append(mixed / total)
                totals.append(row_max + jnp.log(total))
            out[begin : begin + TILE, cols] = jnp.where(low, results[0], results[1]).astype(BF)
            lse[begin : begin + TILE, cols] = jnp.where(low, totals[0], totals[1])
        return carry

    lax.fori_loop(0, width // 128, pair, 0)


def router_rows(ext):
    rows = jnp.where(iota(ext.shape, 0) < 4, ext[...], 0.0)
    return jnp.concatenate([rows, jnp.zeros((112, ext.shape[1]), F32)], axis=0).astype(BF)


def route_probs(normed, router):
    logits = nt(normed, router)
    logits = jnp.where(iota(logits.shape, 1) < 4, logits, MASKED)
    raised = jnp.exp(logits - jnp.max(logits, axis=1, keepdims=True))
    return raised / jnp.sum(raised, axis=1, keepdims=True)


def middle_rows(rep, x, attended, wo, ext, rank, middle, normed, probs, packed):
    tokens = x.shape[0]
    gain = ext[5:6, :]
    router = router_rows(ext)

    def tile(t, carry):
        at = pl.ds(pl.multiple_of(t * TILE, TILE), TILE)
        rows = x[at, :].astype(F32) + nn(attended[at, :], wo[...])
        scale = lax.rsqrt(jnp.mean(rows * rows, axis=1, keepdims=True) + EPSILON)
        middle[at, :] = rows
        unit = (rows * scale * gain).astype(BF)
        normed[at, :] = unit
        probs[at, :] = route_probs(unit, router)
        return carry

    lax.fori_loop(0, tokens // TILE, tile, 0)
    pack_rows(rep, rank, normed, packed)


def forward_kernel(
    starts, q, k, v, x, wo, ext, rank, shared_piece, expert_piece,
    attended, lse, middle, normed, probs, x0, x1, x2, x3, shared_bank, expert_bank,
    bias, send, recv,
):
    net = Net(send, recv)
    spread = Spread(net, shared_piece, shared_bank)
    events = [net.event() for _ in range(3)]
    mine = expert_bank.at[net.shard]
    net.meet("line", [(net.mate, net.shard), (net.rep, net.across), (spread.far, net.shard)])
    spread.begin()
    fill_bias(starts, bias)

    def step(i):
        @pl.when(i == 2)
        def _():
            spread.along(1)
            spread.along(-1)
            spread.over(0)

        @pl.when(i == 4)
        def _():
            spread.along(2)
            spread.along(-2)
            spread.over(1)
            spread.over(-1)
            spread.relay(1, 0)
            spread.relay(0, 1)
            spread.relay(0, -1)

    attend_pairs(q, k, v, attended, lse, bias, step)
    spread.along(3)
    spread.along(-3)
    net.put(events[0], expert_piece, mine, net.rep, net.up, net.z < 3)
    net.put(events[1], expert_piece, mine, net.rep, net.down, net.z > 0)
    spread.over(2)
    spread.over(-2)
    middle_rows(net.rep, x, attended, wo, ext, rank, middle, normed, probs, (x0, x1, x2, x3))
    spread.over(3)
    spread.over(-3)
    net.put(events[2], expert_piece, mine, net.rep, net.across)
    for way, k_step in ((1, 1), (1, -1), (0, 2), (0, -2), (1, 2), (1, -2)):
        spread.relay(way, k_step)
    for way, k_step in ((0, 3), (0, -3), (1, 3), (1, -3)):
        spread.relay(way, k_step)
    spread.finish()
    net.got(events[0], mine, net.z > 0)
    net.got(events[1], mine, net.z < 3)
    net.got(events[2], mine)
    net.close()


def plain_forward_kernel(
    starts, q, k, v, x, wo, ext, rank,
    attended, lse, middle, normed, probs, x0, x1, x2, x3, bias,
):
    fill_bias(starts, bias)
    attend_pairs(q, k, v, attended, lse, bias, lambda i: None)
    rep = lax.axis_index("rep")
    middle_rows(rep, x, attended, wo, ext, rank, middle, normed, probs, (x0, x1, x2, x3))


CHUNK, CHUNKS = 512, 4


def unit_bank(
    expert, ext, xs, cs, source, target, before, unit, outs, dxs, scratch, ready=None,
    emit=None, reclaim=None,
):
    out_acc, dx_acc, gate, wbuf, dw_acc, dw_out, in_sems, out_sems = scratch[:8]
    routed = expert is not None
    blocks, rows = len(xs), xs[0].shape[0]
    per = CHUNK // unit

    def loads(of, buffer, sems, k, b):
        return [
            pltpu.make_async_copy(
                of(k * per + i), buffer.at[b, :, :, pl.ds(i * unit, unit)], sems.at[b, i]
            )
            for i in range(per)
        ]

    def stores(k, b):
        return [
            pltpu.make_async_copy(
                dw_out.at[b, :, :, pl.ds(i * unit, unit)],
                target(k * per + i),
                out_sems.at[b, i],
            )
            for i in range(per)
        ]

    def start_loads(k, b):
        if ready is not None:
            ready(k)
        for copy in loads(source, wbuf, in_sems, k, b):
            copy.start()
        if before is not None:
            for copy in loads(before, scratch[8], scratch[9], k, b):
                copy.start()

    start_loads(0, 0)
    if routed:
        router = router_rows(ext)
        for n in range(blocks):
            probs = route_probs(xs[n][...], router)
            lane = iota(probs.shape, 1)
            gate[n] = jnp.sum(jnp.where(lane == expert, probs, 0.0), axis=1, keepdims=True)

    def chunk(k, carry):
        b = lax.rem(k, 2)
        for copy in loads(source, wbuf, in_sems, 0, b):
            copy.wait()
        for n in range(blocks):
            x, c = xs[n][...], cs[n][...]
            wg, wu, wd = wbuf[b, 0], wbuf[b, 1], wbuf[b, 2]
            gate_h, up_h, back_h = nn(x, wg), nn(x, wu), nn(c, wd)
            sigma = 1.0 / (1.0 + jnp.exp(-gate_h))
            silu = gate_h * sigma
            hidden = silu * up_h
            if routed:
                share = gate[n]
                scaled = back_h * share
                weighted = (hidden * share).astype(BF)
            else:
                scaled, weighted = back_h, hidden.astype(BF)
            d_up = (scaled * silu).astype(BF)
            d_gate = (scaled * up_h * (sigma + silu * (1.0 - sigma))).astype(BF)
            product = nt(hidden.astype(BF), wd)
            d_rows = nt(d_gate, wg) + nt(d_up, wu)
            parts = (tn(x, d_gate), tn(x, d_up), tn(c, weighted))
            if routed:
                pairs = (hidden * back_h).astype(BF)
                d_share = nt(jnp.ones((16, CHUNK), BF), pairs)

            @pl.when(k == 0)
            def _():
                out_acc[n] = product
                dx_acc[n, 0:rows, :] = d_rows
                if routed:
                    dx_acc[n, rows : rows + 16, :] = jnp.zeros((16, d_rows.shape[1]), F32)
                    dx_acc[n, rows : rows + 16, 0:rows] = d_share

            @pl.when(k != 0)
            def _():
                out_acc[n] += product
                dx_acc[n, 0:rows, :] += d_rows
                if routed:
                    dx_acc[n, rows : rows + 16, 0:rows] += d_share

            for i in range(3):
                if n == 0:
                    dw_acc[i] = parts[i]
                else:
                    dw_acc[i] += parts[i]

        for nxt in range(1, CHUNKS):

            @pl.when(k + 1 == nxt)
            def _():
                start_loads(nxt, nxt % 2)

        @pl.when(k >= 2)
        def _():
            for copy in stores(0, b):
                copy.wait()

        if reclaim is not None:
            for now in (2, 3):
                when(k == now, functools.partial(reclaim, now))
        if before is not None:
            for copy in loads(before, scratch[8], scratch[9], 0, b):
                copy.wait()
            for i in range(3):
                dw_out[b, i] = (dw_acc[i] + scratch[8][b, i].astype(F32)).astype(BF)
        else:
            for i in range(3):
                dw_out[b, i] = dw_acc[i].astype(BF)
        for now in range(CHUNKS):

            @pl.when(k == now)
            def _():
                for copy in stores(now, now % 2):
                    copy.start()
                if emit is not None:
                    emit(now)

        return carry

    lax.fori_loop(0, CHUNKS, chunk, 0)
    for n in range(blocks):
        outs[n][...] = out_acc[n].astype(BF)
        dxs[n][...] = dx_acc[n].astype(BF)
    for b in range(2):
        for copy in stores(0, b):
            copy.wait()


def unit_scratch(blocks, rows, extra, width, per, chained):
    scratch = [
        pltpu.VMEM((blocks, rows, width), F32),
        pltpu.VMEM((blocks, rows + extra, width), F32),
        pltpu.VMEM((blocks, rows, 1), F32),
        pltpu.VMEM((2, 3, width, CHUNK), BF),
        pltpu.VMEM((3, width, CHUNK), F32),
        pltpu.VMEM((2, 3, width, CHUNK), BF),
        pltpu.SemaphoreType.DMA((2, per)),
        pltpu.SemaphoreType.DMA((2, per)),
    ]
    if chained:
        scratch += [
            pltpu.VMEM((2, 3, width, CHUNK), BF),
            pltpu.SemaphoreType.DMA((2, per)),
        ]
    return scratch


def shared_kernel(
    x, c, piece, bank, x1, x2, x3, expert_piece, expert_in,
    out, dx, grads_own, grads_other, y1, y2, y3, experts,
    send, recv, *scratch,
):
    net = Net(send, recv)
    events = [net.event() for _ in range(6)]
    peers = [(net.cousins[o], net.shard) for o in (1, 2, 3)]
    net.meet("line", peers + [(net.rep, net.across)])
    arrivals = exchange(net, (x1, x2, x3), (y1, y2, y3))
    low, high = experts.at[net.down], experts.at[net.up]
    net.put(events[0], low, low, net.rep, net.up, (net.z > 0) & (net.z < 3))
    net.put(events[1], high, high, net.rep, net.down, (net.z > 0) & (net.z < 3))
    near, next_near = experts.at[net.place(1, 0)], experts.at[net.place(2, 0)]
    net.put(events[2], near, near, net.rep, net.across)
    below = experts.at[lax.max(net.shard - 4, net.x)]
    above = experts.at[lax.min(net.shard + 4, 6 + net.x)]

    def spot(n):
        return net.place(n % 4, n // 4 % 2)

    spots = [spot(n) for n in range(8)]
    halves = [net.core, 1 - net.core]

    def source(n):
        return piece if n == 0 else bank.at[halves[n // 8], spots[n % 8]]

    def target(n):
        return (grads_own, grads_other)[n // 8].at[spots[n % 8]]

    from_below, from_above = net.z > 1, net.z < 2
    last_up, last_down = net.z == 2, net.z == 1

    def ready(k):
        if k == 2:
            net.got(events[0], below, from_below)
            net.got(events[1], above, from_above)
            net.put(events[3], next_near, next_near, net.rep, net.across)
            net.put(events[4], below, below, net.rep, net.up, last_up)
            net.put(events[5], above, above, net.rep, net.down, last_down)

    unit_bank(None, None, [x], [c], source, target, None, 128, [out], [dx], scratch, ready)
    for event, like in arrivals:
        net.got(event, like)
    net.got(events[2], near)
    net.got(events[3], near)
    net.got(events[4], near, net.z == 3)
    net.got(events[5], near, net.z == 0)
    net.close()


def far_kernel(
    ext, xa, xb, ca, cb, expert_piece, shared_own, shared_other, expert_in,
    oa, ob, da, db, grads, shared_mate, shared_x, experts,
    part_a, part_b, part_sems, send, recv, *scratch,
):
    net = Net(send, recv)
    events = [net.event() for _ in range(6)]
    net.meet("none", [(net.rep, net.across), (net.mate, net.shard)])
    last = experts.at[net.place(3, 0)]
    net.put(events[0], last, last, net.rep, net.across)
    net.put(events[1], shared_other, shared_mate, net.mate, net.shard)
    spots = [net.place(n // 2, n % 2) for n in range(8)]
    sides = [net.cycle(d) + 1 - 2 * net.x for d in range(4)]
    rows = [shared_x.at[lax.div(side, 2)] for side in sides]
    pieces = [part_a.at[d] for d in range(4)]

    def source(n):
        return expert_piece if n == 0 else experts.at[spots[n]]

    def target(n):
        return grads.at[spots[n]]

    def ready(k):
        if k == 1:
            net.got(events[1], shared_mate)
            fetch(
                [shared_own.at[side] for side in sides] + [shared_mate.at[side] for side in sides],
                [part_a.at[d] for d in range(4)] + [part_b.at[d] for d in range(4)],
                part_sems,
            )
            for d in (2, 1, 3, 0):
                part_a[d] = (part_a[d].astype(F32) + part_b[d].astype(F32)).astype(BF)
                net.put(events[2 + d], pieces[d], rows[d], net.rep, net.across)
        if k == 3:
            net.got(events[0], last)

    unit_bank(
        net.rep, ext, [xa, xb], [ca, cb], source, target, None, 256, [oa, ob], [da, db],
        scratch, ready,
    )
    for d in range(4):
        net.got(events[2 + d], rows[d])
    net.close()


def near_kernel(
    ext, xa, xb, ca, cb, expert_piece, experts, before, far_a, far_b,
    shared_own, shared_mate, shared_x,
    oa, ob, da, shared_total, grads, back_a, back_b, back_c, expert_x, shared_z,
    db, held, spare, sems, send, recv, *scratch,
):
    net = Net(send, recv)
    events = [net.event() for _ in range(5)]
    shared = Reduce(net, [shared_own, shared_mate], shared_x, shared_z, held, spare, sems)
    peers = [(net.cousins[o], net.shard) for o in (1, 2, 3)]
    net.meet("all", peers + [(net.rep, net.across)])
    net.put(events[0], far_a, back_a, net.cousins[2], net.shard)
    net.put(events[1], far_b, back_b, net.cousins[3], net.shard)
    for d in (2, 1, 3, 0):
        shared.add_across(d, False)
    spots = [net.place(3 - n // 2, n % 2) for n in range(8)]
    own_slot = 6
    dw_out, halves = scratch[5], []
    for b in range(2):
        halves.append(dw_out.at[b, :, :, pl.ds(256, 256)])
    targets = [expert_x.at[net.levels[3]], expert_x.at[net.levels[2]]]

    def source(n):
        return expert_piece if n == own_slot else experts.at[spots[n]]

    def emit(now):
        if now < 2:
            net.put(events[3 + now], halves[now], targets[now], net.rep, net.across)

    def reclaim(now):
        half = halves[now - 2]
        net.copy(events[1 + now], half, half, net.mate, net.shard).wait_send()

    unit_bank(
        net.rep, ext, [xa, xb], [ca, cb], source,
        lambda n: grads.at[spots[n]], lambda n: before.at[spots[n]],
        256, [oa, ob], [da, db], scratch, None, emit, reclaim,
    )
    for n in range(2):
        net.open.pop(events[3 + n])
    net.put(events[2], db, back_c, net.mate, net.shard)
    shared.total(shared_total)
    net.got(events[0], back_a)
    net.got(events[1], back_b)
    net.got(events[2], back_c)
    for n in range(2):
        net.got(events[3 + n], targets[n])
    net.close()


def plain_bank_kernel(blocks, unit, routed, chained, ext, *refs):
    refs = list(refs)

    def take(n):
        taken = refs[:n]
        del refs[:n]
        return taken

    xs, cs = take(blocks), take(blocks)
    bank = take(1)[0]
    before = take(1)[0] if chained else None
    outs, dxs = take(blocks), take(blocks)
    grads = take(1)[0]
    unit_bank(
        lax.axis_index("rep") if routed else None,
        ext, xs, cs,
        lambda n: bank.at[n],
        lambda n: grads.at[n],
        (lambda n: before.at[n]) if chained else None,
        unit, outs, dxs, refs,
    )


def plain_bank(ext, xs, cs, bank, before, routed):
    blocks, (rows, width) = len(xs), xs[0].shape
    chained = before is not None
    extra, unit = (16 if routed else 0), bank.shape[3]
    operands = [ext, *xs, *cs, bank] + ([before] if chained else [])
    outs = [shape((rows, width))] * blocks + [shape((rows + extra, width))] * blocks
    results = call(
        functools.partial(plain_bank_kernel, blocks, unit, routed, chained),
        outs + [shape(bank.shape)],
        [VMEM] * (1 + 2 * blocks) + [ANY] * (2 if chained else 1),
        [VMEM] * (2 * blocks) + [ANY],
        unit_scratch(blocks, rows, extra, width, CHUNK // unit, chained),
        flops=18 * blocks * rows * width * 4 * CHUNK,
        moved=30 * 2**20,
    )(*operands)
    return results[:blocks], results[blocks : 2 * blocks], results[2 * blocks]


def combine_rows(
    slot, d0, d1, d2, d3, d_shared, probs, middle, normed, cot, ext, attended, wo,
    d_middle, d_attended, grad_wo, grad_ext, branch, router_acc, gain_acc,
):
    tokens, width = middle.shape
    rep = lax.axis_index("rep")
    gain = ext[5:6, :]
    router = router_rows(ext)
    router_acc[...] = jnp.zeros_like(router_acc)
    gain_acc[...] = jnp.zeros_like(gain_acc)

    def tile(t, carry):
        at = pl.ds(pl.multiple_of(t * TILE, TILE), TILE)
        slot_one, slot_two = slot[at, 0:1], slot[at, 64:65]
        d_normed = d_shared[at, :].astype(F32)
        lane = iota((TILE, 128), 1)
        d_gates = jnp.zeros((TILE, 128), F32)
        for o, d in enumerate((d0, d1, d2, d3)):
            place = (iota((TILE, CAP), 1) + o * CAP).astype(F32)
            hit = (place == slot_one) | (place == slot_two)
            d_normed = d_normed + nn(ones_where(hit), d[0:CAP, :])
            share = d[CAP : CAP + 16, 0:CAP].astype(F32)[0:1, :]
            d_share = jnp.sum(jnp.where(hit, share, 0.0), axis=1, keepdims=True)
            d_gates = d_gates + jnp.where(lane == sibling(rep, o), d_share, 0.0)
        p = probs[at, :]
        inner = jnp.sum(d_gates * p, axis=1, keepdims=True)
        d_logits = (p * (d_gates - inner)).astype(BF)
        d_normed = d_normed + nn(d_logits, router)
        router_acc[...] += tn(d_logits, normed[at, :])
        rows = middle[at, :]
        scale = lax.rsqrt(jnp.mean(rows * rows, axis=1, keepdims=True) + EPSILON)
        unit = rows * scale
        gain_acc[...] += jnp.sum((d_normed * unit).reshape(TILE // 8, 8, width), axis=0)
        w = d_normed * gain
        inner = jnp.mean(w * unit, axis=1, keepdims=True)
        total = cot[at, :].astype(F32) + scale * (w - unit * inner)
        d_middle[at, :] = total
        rounded = total.astype(BF)
        branch[at, :] = rounded
        d_attended[at, :] = nt(rounded, wo[...]).astype(BF)
        return carry

    lax.fori_loop(0, tokens // TILE, tile, 0)
    grad_wo[...] = tn(attended[...], branch[...]).astype(BF)
    row = iota((16, width), 0)
    total = jnp.sum(gain_acc[...], axis=0, keepdims=True)
    grad_ext[...] = jnp.where(row < 4, router_acc[0:16, :], jnp.where(row == 5, total, 0.0))


def output_rows(slot, o0, o1, o2, o3, shared, probs, middle, out, first, last):
    rep = lax.axis_index("rep")

    def tile(t, carry):
        at = pl.ds(pl.multiple_of(t * TILE, TILE), TILE)
        slot_one, slot_two = slot[at, 0:1], slot[at, 64:65]
        total = middle[at, :] + shared[at, :].astype(F32)
        p = probs[at, :]
        lane = iota((TILE, 128), 1)
        for o, rows in enumerate((o0, o1, o2, o3)):
            place = (iota((TILE, CAP), 1) + o * CAP).astype(F32)
            hit = (place == slot_one) | (place == slot_two)
            share = jnp.sum(jnp.where(lane == sibling(rep, o), p, 0.0), axis=1, keepdims=True)
            total = total + nn(jnp.where(hit, share, 0.0).astype(BF), rows[...])
        out[at, :] = total.astype(BF)
        return carry

    lax.fori_loop(first, last, tile, 0)


def back_pairs(
    q, k, v, d_out, out, lse, cosine, sine, dq, dk, dv, bias, dk_acc, dv_acc, step
):
    tokens, width = q.shape

    def pair(i, carry):
        step(i)
        cols = pl.ds(pl.multiple_of(i * 128, 128), 128)
        keys, values = k[:, cols], v[:, cols]
        half_keys = [keep_half(keys, 0), keep_half(keys, 1)]
        dk_acc[...] = jnp.zeros_like(dk_acc)
        dv_acc[...] = jnp.zeros_like(dv_acc)
        low = iota((TILE, 128), 1) < 64
        for t in range(tokens // TILE):
            begin = t * TILE
            end = min(tokens, begin + TILE + PIECE)
            at = slice(begin, begin + TILE)
            block, grad = q[at, cols], d_out[at, cols]
            product = grad.astype(F32) * out[at, cols].astype(F32)
            block_lse = lse[at, cols]
            d_block = None
            for h in range(2):
                block_h, grad_h = keep_half(block, h), keep_half(grad, h)
                scores = nt(block_h, keys[:end])
                scores = biased(scores, bias, begin, begin, end)
                probs = jnp.exp(scores - block_lse[:, 64 * h : 64 * h + 1])
                d_probs = nt(grad_h, values[:end])
                inner = jnp.sum(
                    jnp.where(low if h == 0 else ~low, product, 0.0), axis=1, keepdims=True
                )
                d_scores = (probs * (d_probs - inner)).astype(BF)
                part = nn(d_scores, half_keys[h][:end])
                d_block = part if d_block is None else d_block + part
                dk_acc[0:end, :] += tn(d_scores, block_h)
                dv_acc[0:end, :] += tn(probs.astype(BF), grad_h)
            dq[at, cols] = spin(d_block * 0.125, cosine[at, :], -sine[at, :]).astype(BF)
        dk[:, cols] = spin(dk_acc[...], cosine[...], -sine[...]).astype(BF)
        dv[:, cols] = dv_acc[...].astype(BF)
        return carry

    lax.fori_loop(0, width // 128, pair, 0)


def fetch(sources, targets, sems):
    copies = [pltpu.make_async_copy(a, b, sems.at[i]) for i, (a, b) in enumerate(zip(sources, targets))]
    for copy in copies:
        copy.start()
    for copy in copies:
        copy.wait()


class Reduce:
    def __init__(self, net, own, from_x, from_z, held, spare, sems):
        self.net, self.own, self.from_x, self.from_z = net, own, from_x, from_z
        self.held, self.spare, self.sems = held, spare, sems
        self.x_events = [net.event() for _ in range(4)]
        self.z_events = [net.event() for _ in range(3)]
        self.spots = [net.cycle(d) for d in range(4)]
        self.levels = [lax.div(spot, 2) for spot in self.spots]
        self.pieces = [held.at[d] for d in range(4)]

    def send_across(self):
        net = self.net
        for d in (2, 1, 3, 0):
            source = self.own[0].at[self.spots[d] + 1 - 2 * net.x]
            target = self.from_x.at[self.levels[d]]
            net.put(self.x_events[d], source, target, net.rep, net.across)

    def add_across(self, d, wait=True):
        net = self.net
        far = self.from_x.at[self.levels[d]]
        if wait:
            net.got(self.x_events[d], far)
        sources = [own.at[self.spots[d]] for own in self.own] + [far]
        targets = [self.held.at[d]] + [self.spare.at[i] for i in range(len(self.own))]
        fetch(sources, targets, self.sems)
        total = self.held[d].astype(F32)
        for i in range(len(self.own)):
            total = total + self.spare[i].astype(F32)
        self.held[d] = total.astype(BF)
        if d:
            target = self.from_z.at[d - 1]
            net.put(self.z_events[d - 1], self.pieces[d], target, net.rep, self.spots[d])

    def total(self, out):
        for d in (1, 2, 3):
            self.net.got(self.z_events[d - 1], self.from_z.at[d - 1])
        targets = [self.held.at[d] for d in (1, 2, 3)]
        self.settle()
        fetch([self.from_z.at[d] for d in range(3)], targets, self.sems)
        total = self.held[0].astype(F32)
        for d in (1, 2, 3):
            total = total + self.held[d].astype(F32)
        out[...] = total.astype(BF)

    def settle(self):
        for event in self.z_events:
            self.net.settle(event)


class Chain:
    def __init__(self, net, own, from_x, up_in, down_in, held, spare, sems):
        self.net, self.own, self.from_x = net, own, from_x
        self.up_in, self.down_in = up_in, down_in
        self.held, self.spare, self.sems = held, spare, sems
        self.events = {(way, d): net.event() for way in range(2) for d in (1, 2, 3)}
        self.spots = [net.place(n, 0) for n in range(4)]
        self.sends, self.gets = {}, {}
        z = net.z
        for d in (1, 2, 3):
            self.sends[0, d] = (held.at[lax.min(z + d, 3)], z < 4 - d)
            self.sends[1, d] = (held.at[lax.max(z - d, 0)], z > d - 1)
            self.gets[0, d] = (lax.min(z + d - 1, 3), (z > 0) & (z < 5 - d))
            self.gets[1, d] = (lax.max(z - d + 1, 0), (z < 3) & (z > d - 2))

    def level(self, n):
        to = self.net.levels[n]
        far = self.from_x.at[to]
        fetch([self.own.at[self.spots[n]], far], [self.held.at[to], self.spare.at[0]], self.sems)
        self.held[to] = (self.held[to].astype(F32) + self.spare[0].astype(F32)).astype(BF)

    def send(self, d):
        net = self.net
        for way, to, into in ((0, net.up, self.up_in), (1, net.down, self.down_in)):
            source, here = self.sends[way, d]
            net.put(self.events[way, d], source, into.at[d - 1], net.rep, to, here)

    def take(self, d):
        for way, into in ((0, self.up_in), (1, self.down_in)):
            to, here = self.gets[way, d]

            def add():
                self.net.copy(
                    self.events[way, d], into.at[d - 1], into.at[d - 1],
                    self.net.mate, self.net.shard,
                ).wait_recv()
                fetch([into.at[d - 1]], [self.spare.at[0]], self.sems)
                total = self.held[to].astype(F32) + self.spare[0].astype(F32)
                self.held[to] = total.astype(BF)

            when(here, add)


def back_kernel(
    starts, slot, d0, d1, d2, d3, d_shared, probs, middle, normed, cot, ext, attended, wo,
    q, k, v, lse, cosine, sine,
    o1, o2, o3, grads, expert_x_in,
    d_middle, grad_wo, grad_ext, dq, dk, dv, expert_total,
    r1, r2, r3, up_in, down_in, expert_x,
    d_attended, branch, router_acc, gain_acc, bias, dk_acc, dv_acc,
    held, spare, sems, send, recv,
):
    net = Net(send, recv)
    x_events = [net.event() for _ in range(2)]
    chain = Chain(net, grads, expert_x, up_in, down_in, held, spare, sems)
    peers = [(net.cousins[o], net.shard) for o in (1, 2, 3)]
    net.meet("line", peers + [(net.rep, net.across)])
    targets = [expert_x.at[net.levels[n]] for n in range(2)]
    for n in (1, 0):
        source = grads.at[net.place(n, 1)]
        net.put(x_events[n], source, targets[n], net.rep, net.across)
    arrivals = exchange(net, (o1, o2, o3), (r1, r2, r3))
    chain.level(3)
    chain.send(3)
    chain.level(2)
    combine_rows(
        slot, d0, d1, d2, d3, d_shared, probs, middle, normed, cot, ext, attended, wo,
        d_middle, d_attended, grad_wo, grad_ext, branch, router_acc, gain_acc,
    )
    fill_bias(starts, bias)
    chain.take(3)
    chain.send(2)

    def step(i):
        @pl.when(i == 1)
        def _():
            net.got(x_events[1], targets[1])
            chain.level(1)

        @pl.when(i == 4)
        def _():
            chain.take(2)
            chain.send(1)

    back_pairs(
        q, k, v, d_attended, attended, lse, cosine, sine, dq, dk, dv, bias, dk_acc, dv_acc, step
    )
    net.got(x_events[0], targets[0])
    chain.level(0)
    for event, like in arrivals:
        net.got(event, like)
    chain.take(1)
    expert_total[...] = held[net.z]
    net.close()


def plain_back_kernel(
    starts, slot, d0, d1, d2, d3, d_shared, probs, middle, normed, cot, ext, attended, wo,
    q, k, v, lse, cosine, sine,
    d_middle, grad_wo, grad_ext, dq, dk, dv,
    d_attended, branch, router_acc, gain_acc, bias, dk_acc, dv_acc,
):
    combine_rows(
        slot, d0, d1, d2, d3, d_shared, probs, middle, normed, cot, ext, attended, wo,
        d_middle, d_attended, grad_wo, grad_ext, branch, router_acc, gain_acc,
    )
    fill_bias(starts, bias)
    back_pairs(
        q, k, v, d_attended, attended, lse, cosine, sine, dq, dk, dv, bias, dk_acc, dv_acc,
        lambda i: None,
    )


def norm_rows(x, ext, normed_all):
    gain = ext[4:5, :]

    def tile(t, carry):
        at = pl.ds(pl.multiple_of(t * TILE, TILE), TILE)
        rows = x[at, :].astype(F32)
        scale = lax.rsqrt(jnp.mean(rows * rows, axis=1, keepdims=True) + EPSILON)
        normed_all[at, :] = (rows * scale * gain).astype(BF)
        return carry

    lax.fori_loop(0, x.shape[0] // TILE, tile, 0)


def input_grad(x, ext, dq, dk, dv, wq, wk, wv, d_middle, grad_in, gain_acc):
    tokens, width = x.shape
    gain = ext[4:5, :]
    gain_acc[...] = jnp.zeros_like(gain_acc)

    def tile(t, carry):
        at = pl.ds(pl.multiple_of(t * TILE, TILE), TILE)
        rows = x[at, :].astype(F32)
        scale = lax.rsqrt(jnp.mean(rows * rows, axis=1, keepdims=True) + EPSILON)
        unit = rows * scale
        d_normed = nt(dq[at, :], wq[...]) + nt(dk[at, :], wk[...]) + nt(dv[at, :], wv[...])
        gain_acc[...] += jnp.sum((d_normed * unit).reshape(TILE // 8, 8, width), axis=0)
        w = d_normed * gain
        inner = jnp.mean(w * unit, axis=1, keepdims=True)
        grad_in[at, :] = d_middle[at, :] + scale * (w - unit * inner)
        return carry

    lax.fori_loop(0, tokens // TILE, tile, 0)


def tail_kernel(
    x, ext, dq, dk, dv, wq, wk, wv, d_middle, grad_wo, grad_ext,
    slot, o0, o1, o2, o3, shared_out, probs, middle, expert_total, shared_total,
    grad_in, outputs, weights, small, shared_pair, e1, e2, e3,
    normed_all, gain_acc, gw, from_mate, from_x, from_z, from_y, result, from_core,
    tiny, tiny_in, shared_in, shared_sum, send, recv,
):
    width = x.shape[1]
    half = width // SLOTS
    net = Net(send, recv)
    e_events = [net.event() for _ in range(3)]
    s_events = [net.event() for _ in range(2)]
    m_events = [net.event() for _ in range(2)]
    x_events = [[net.event() for _ in range(2)] for _ in range(4)]
    z_events = [[net.event() for _ in range(2)] for _ in range(3)]
    y_event, c_event = net.event(), net.event()
    t_events = [net.event() for _ in range(6)]
    net.meet(
        "all", [(net.mate, net.shard), (net.cousins[2], net.shard), (net.rep, net.across)]
    )
    far = net.cousins[2]
    net.put(s_events[0], shared_total, shared_in, far, net.shard)
    net.put(e_events[1], expert_total, e2, far, net.shard)
    net.put(e_events[0], expert_total, e1, net.mate, net.shard)
    norm_rows(x, ext, normed_all)
    spots = [lax.rem(i + 2 * net.core, 4) for i in range(4)]
    gw[spots[0]] = tn(normed_all[...], dq[...]).astype(BF)
    gw[spots[1]] = tn(normed_all[...], dk[...]).astype(BF)
    gw[spots[2]] = tn(normed_all[...], dv[...]).astype(BF)
    gw[spots[3]] = grad_wo[...]
    for i in range(2):
        net.put(m_events[i], gw.at[2 + i], from_mate.at[i], net.mate, net.shard)

    def rows_of(spot):
        return pl.ds(pl.multiple_of(spot * half, 32), half)

    mine = [rows_of(net.cycle(d)) for d in range(4)]
    theirs = [rows_of(net.cycle(d) + 1 - 2 * net.x) for d in range(4)]
    for i in range(2):
        net.got(m_events[i], from_mate.at[i])
        gw[i] = (gw[i].astype(F32) + from_mate[i].astype(F32)).astype(BF)
    for d in (2, 1, 3, 0):
        for i in range(2):
            net.put(
                x_events[d][i], gw.at[i, theirs[d]], from_x.at[d, i], net.rep, net.across
            )
    input_grad(x, ext, dq, dk, dv, wq, wk, wv, d_middle, grad_in, gain_acc)
    row = iota((16, width), 0)
    total = jnp.sum(gain_acc[...], axis=0, keepdims=True)
    tiny[0] = (grad_ext[...] + jnp.where(row == 4, total, 0.0)).astype(BF)
    net.put(t_events[0], tiny.at[0], tiny_in.at[0], net.mate, net.shard)

    def add_across(d):
        for i in range(2):
            net.got(x_events[d][i], from_x.at[d, i])
            summed = gw[i, mine[d], :].astype(F32) + from_x[d, i].astype(F32)
            gw[i, mine[d], :] = summed.astype(BF)
            if d:
                net.put(
                    z_events[d - 1][i], gw.at[i, mine[d]], from_z.at[d - 1, i],
                    net.rep, net.cycle(d),
                )

    def tiny_add(n, target_rep, target_shard):
        net.got(t_events[n], tiny_in.at[n])
        tiny[n + 1] = (tiny[n].astype(F32) + tiny_in[n].astype(F32)).astype(BF)
        if target_rep is not None:
            source, target = tiny.at[n + 1], tiny_in.at[n + 1]
            net.put(t_events[n + 1], source, target, target_rep, target_shard)

    add_across(2)
    tiny_add(0, net.rep, net.across)
    output_rows(slot, o0, o1, o2, o3, shared_out, probs, middle, outputs, 0, 2)
    add_across(1)
    tiny_add(1, far, net.shard)
    net.got(s_events[0], shared_in)
    shared_sum[...] = (shared_total[...].astype(F32) + shared_in[...].astype(F32)).astype(BF)
    shared_pair[0] = shared_sum[...]
    net.put(s_events[1], shared_sum, shared_pair.at[1], net.mate, net.shard)
    output_rows(slot, o0, o1, o2, o3, shared_out, probs, middle, outputs, 2, 4)
    tiny_add(2, None, None)
    for d in (1, 2, 3):
        net.put(t_events[2 + d], tiny.at[3], tiny_in.at[2 + d], net.rep, net.cycle(d))
    add_across(3)
    add_across(0)
    for i in range(2):
        total = gw[i, mine[0], :].astype(F32)
        for d in (1, 2, 3):
            net.got(z_events[d - 1][i], from_z.at[d - 1, i])
            total = total + from_z[d - 1, i].astype(F32)
        result[0, i] = total.astype(BF)
    net.put(y_event, result.at[0], from_y, far, net.shard)
    total = tiny[3].astype(F32)
    for d in (1, 2, 3):
        net.got(t_events[2 + d], tiny_in.at[2 + d])
        total = total + tiny_in[2 + d].astype(F32)
    small[...] = total.astype(BF).astype(F32)
    net.got(e_events[1], e2)
    net.put(e_events[2], e2, e3, net.mate, net.shard)
    net.got(y_event, from_y)
    result[1] = (result[0].astype(F32) + from_y[...].astype(F32)).astype(BF)
    net.put(c_event, result.at[1], from_core, net.mate, net.shard)
    for i in range(2):
        weights[spots[i]] = result[1, i].astype(F32)
    net.got(c_event, from_core)
    for i in range(2):
        weights[spots[2 + i]] = from_core[i].astype(F32)
    net.got(e_events[0], e1)
    net.got(s_events[1], shared_pair.at[1])
    net.got(e_events[2], e3)
    net.close()


def plain_tail_kernel(
    x, ext, dq, dk, dv, wq, wk, wv, d_middle,
    slot, o0, o1, o2, o3, shared_out, probs, middle,
    grad_in, outputs, gw, gain, normed_all, gain_acc,
):
    norm_rows(x, ext, normed_all)
    for i, d in enumerate((dq, dk, dv)):
        gw[i] = tn(normed_all[...], d[...]).astype(BF)
    input_grad(x, ext, dq, dk, dv, wq, wk, wv, d_middle, grad_in, gain_acc)
    gain[...] = gain_acc[...]
    output_rows(
        slot, o0, o1, o2, o3, shared_out, probs, middle, outputs, 0, x.shape[0] // TILE
    )


def finish_kernel(e0, e1, e2, e3, pair, gate, up, down, s_gate, s_up, s_down):
    rep = lax.axis_index("rep")
    core = lax.rem(rep, 2)
    for o, part in enumerate((e0, e1, e2, e3)):
        at = sibling(rep, o)
        gate[at] = part[0].astype(F32)
        up[at] = part[1].astype(F32)
        down[at] = part[2].astype(F32).T
    span = pair.shape[3]
    for side in range(2):

        @pl.when(core == side)
        def _():
            for n in range(2):
                at = (side + n) % 2 * span
                s_gate[:, at : at + span] = pair[n, 0].astype(F32)
                s_up[:, at : at + span] = pair[n, 1].astype(F32)
                s_down[at : at + span, :] = pair[n, 2].astype(F32).T


def rope_tables(length, head_dim):
    positions = jnp.arange(length, dtype=F32)
    inverse_freq = 10000.0 ** (-2.0 * jnp.arange(head_dim // 2, dtype=F32) / head_dim)
    angle = positions[:, None] * inverse_freq[None, :]
    cosine, sine = jnp.cos(angle), jnp.sin(angle)
    return (
        jnp.concatenate([cosine] * 4, axis=1),
        jnp.concatenate([-sine, sine, -sine, sine], axis=1),
    )


def body(
    inputs,
    piece_starts,
    routes,
    attn_gain,
    query_weight,
    key_weight,
    value_weight,
    out_weight,
    ffn_gain,
    router_weight,
    expert_gate,
    expert_up,
    expert_down,
    shared_gate,
    shared_up,
    shared_down,
    cotangent,
):
    _, tokens, width = inputs.shape
    shards = lax.axis_size("shard")
    rep, shard = lax.axis_index("rep"), lax.axis_index("shard")
    core = rep % 2
    ringed = shards == SLOTS
    rows = width // shards
    units = shared_gate.shape[1]
    x, cot, chosen = inputs[0], cotangent[0], routes[0]
    small = jnp.concatenate([router_weight.T, attn_gain[None], ffn_gain[None]], axis=0)
    small = jnp.pad(small, ((0, 10), (0, 0)))
    small = lax.dynamic_update_slice(jnp.zeros((16, width), BF), small, (0, shard * rows))
    blank = jnp.zeros((16, width), BF)
    if ringed:
        half_one = jnp.concatenate([query_weight, key_weight, small], axis=0)
        half_two = jnp.concatenate([value_weight, out_weight, blank], axis=0)
        piece = jnp.where(core == 0, half_one, half_two)
    else:
        wq, wk, wv, wo = [
            lax.all_gather(w, "shard", axis=0, tiled=True)
            for w in (query_weight, key_weight, value_weight, out_weight)
        ]
        ext = lax.psum(small.astype(F32), "shard")

    shared_pack = jnp.stack([shared_gate, shared_up, shared_down.T])
    my_half = lax.dynamic_slice_in_dim(shared_pack, core * (units // 2), units // 2, 2)
    expert_pack = jnp.stack([expert_gate[rep], expert_up[rep], expert_down[rep].T])

    cosine, sine = rope_tables(tokens, width // HEADS)
    token_f = shape((tokens, width))
    square = shape((width, width))
    packed = [shape((CAP, width))] * 4
    outs = [shape((8, tokens), F32), shape((tokens, 128), F32)] + [token_f] * 3
    work = 2 * tokens * width * (CAP * 4 + 3 * width)
    if ringed:
        rank, slot, q, k, v, *heads = call(
            head_kernel,
            outs + [square] * 4 + [shape((16, width), F32)] + packed,
            [VMEM] * 7,
            [VMEM] * 10 + [VMEM] + [ANY] * 3,
            [
                pltpu.VMEM((2, SLOTS, 2 * rows + 16, width), BF),
                pltpu.VMEM((3, CAP, width), BF),
                pltpu.SemaphoreType.DMA((31,)),
                pltpu.SemaphoreType.DMA((31,)),
                pltpu.SemaphoreType.DMA,
            ],
            flops=work,
            moved=24 * 2**20,
            group=0,
        )(chosen, chosen.T, cot, x, piece, cosine, sine)
        wq, wk, wv, wo, ext, *cot_in = heads
    else:
        rank, slot, q, k, v, *cot_out = call(
            plain_head_kernel, outs + packed, [VMEM] * 10, [VMEM] * 9, flops=work,
            moved=24 * 2**20,
        )(chosen, chosen.T, cot, x, cosine, sine, wq, wk, wv, ext)
        cot_in = [cot_out[0]] + [to_rep(cot_out[o], o) for o in (1, 2, 3)]

    outs = [token_f, shape((tokens, width), F32), shape((tokens, width), F32), token_f]
    outs += [shape((tokens, 128), F32)] + packed
    work = 2 * tokens * width * (8 * tokens + width + 4 * CAP)
    bias = pltpu.VMEM((tokens, tokens), F32)
    if ringed:
        attended, lse, middle, normed, probs, *x_out, shared_bank, expert_bank = call(
            forward_kernel,
            outs + [shape((2, SLOTS) + my_half.shape), shape((SLOTS,) + expert_pack.shape)],
            [SMEM] + [VMEM] * 7 + [ANY] * 2,
            [VMEM] * 9 + [ANY] * 2,
            [bias, pltpu.SemaphoreType.DMA((59,)), pltpu.SemaphoreType.DMA((59,))],
            flops=work,
            moved=30 * 2**20,
            group=1,
        )(piece_starts, q, k, v, x, wo, ext, rank, my_half, expert_pack)
    else:
        attended, lse, middle, normed, probs, *x_out = call(
            plain_forward_kernel, outs, [SMEM] + [VMEM] * 7, [VMEM] * 9, [bias], flops=work,
            moved=30 * 2**20,
        )(piece_starts, q, k, v, x, wo, ext, rank)

    rows_out = shape((CAP, width))
    rows_back = shape((CAP + 16, width))
    if ringed:
        half_grads = shape((SLOTS,) + my_half.shape)
        shared_out, shared_dx, grads_own, grads_other, y1, y2, y3, expert_bank = call(
            shared_kernel,
            [token_f] * 2 + [half_grads] * 2 + packed[:3] + [shape(expert_bank.shape)],
            [VMEM] * 2 + [ANY] * 7,
            [VMEM] * 2 + [ANY] * 6,
            [pltpu.SemaphoreType.DMA((9,)), pltpu.SemaphoreType.DMA((9,))]
            + unit_scratch(1, tokens, 0, width, 4, False),
            flops=18 * tokens * width * CHUNK * CHUNKS,
            moved=30 * 2**20,
            group=2,
            alias={8: 7},
        )(normed, cot, my_half, shared_bank, *x_out[1:], expert_pack, expert_bank)
        x_in = [x_out[0], y1, y2, y3]
        bank = shape(expert_bank.shape)
        half_x = (4,) + my_half.shape
        far_a, far_b, da, db, before, shared_mate, shared_x, expert_bank = call(
            far_kernel,
            [rows_out] * 2 + [rows_back] * 2 + [bank, half_grads, shape(half_x), bank],
            [VMEM] * 5 + [ANY] * 4,
            [VMEM] * 4 + [ANY] * 4,
            [
                pltpu.VMEM(half_x, BF),
                pltpu.VMEM(half_x, BF),
                pltpu.SemaphoreType.DMA((8,)),
                pltpu.SemaphoreType.DMA((6,)),
                pltpu.SemaphoreType.DMA((6,)),
            ]
            + unit_scratch(2, CAP, 16, width, 2, False),
            flops=36 * CAP * width * CHUNK * CHUNKS,
            moved=30 * 2**20,
            group=3,
            alias={8: 7},
        )(ext, *x_in[2:], *cot_in[2:], expert_pack, grads_own, grads_other, expert_bank)
        bank_x, bank_z = (4,) + expert_pack.shape, (3,) + expert_pack.shape
        half_z = (3,) + my_half.shape
        near_a, near_b, d0, shared_total, grads, d2, d3, d1, expert_x, _ = call(
            near_kernel,
            [rows_out] * 2 + [rows_back, shape(my_half.shape), bank] + [rows_back] * 3
            + [shape(bank_x), shape(half_z)],
            [VMEM] * 5 + [ANY] * 8,
            [VMEM] * 4 + [ANY] * 6,
            [
                pltpu.VMEM((CAP + 16, width), BF),
                pltpu.VMEM(half_x, BF),
                pltpu.VMEM((2,) + my_half.shape, BF),
                pltpu.SemaphoreType.DMA((3,)),
                pltpu.SemaphoreType.DMA((12,)),
                pltpu.SemaphoreType.DMA((12,)),
            ]
            + unit_scratch(2, CAP, 16, width, 2, True),
            flops=36 * CAP * width * CHUNK * CHUNKS,
            moved=30 * 2**20,
            group=4,
        )(
            ext, *x_in[:2], *cot_in[:2], expert_pack, expert_bank, before, da, db,
            grads_own, shared_mate, shared_x,
        )
        d_rows = [d0, d1, d2, d3]
    else:

        def slotted(part):
            every = lax.all_gather(part, "shard")
            every = every.reshape(SLOTS, shards // SLOTS, 3, width, part.shape[2])
            return every.transpose(0, 2, 3, 1, 4).reshape(SLOTS, 3, width, -1)

        shared_bank = slotted(my_half)
        shared_bank = jnp.concatenate([shared_bank, to_rep(shared_bank, 1)], axis=0)
        expert_bank = slotted(expert_pack)
        x_in = [x_out[0]] + [to_rep(x_out[o], o) for o in (1, 2, 3)]
        (shared_out,), (shared_dx,), shared_grads = plain_bank(
            ext, [normed], [cot], shared_bank, None, False
        )
        grads_own, grads_other = shared_grads[:SLOTS], shared_grads[SLOTS:]
        (far_a, far_b), (da, db), before = plain_bank(
            ext, x_in[2:], cot_in[2:], expert_bank, None, True
        )
        (near_a, near_b), (d0, d1), grads = plain_bank(
            ext, x_in[:2], cot_in[:2], expert_bank, before, True
        )
        d_rows = [d0, to_rep(d1, 1), to_rep(da, 2), to_rep(db, 3)]
    wide = shape((tokens, width), F32)
    outs = [wide, square, shape((16, width), F32)] + [token_f] * 3
    operands = (piece_starts, slot, *d_rows, shared_dx, probs, middle, normed, cot, ext, attended)
    operands += (wo, q, k, v, lse, cosine, sine)
    specs = [SMEM] + [VMEM] * 19
    scratch = [
        pltpu.VMEM((tokens, width), BF),
        pltpu.VMEM((tokens, width), BF),
        pltpu.VMEM((128, width), F32),
        pltpu.VMEM((8, width), F32),
        bias,
        pltpu.VMEM((tokens, 128), F32),
        pltpu.VMEM((tokens, 128), F32),
    ]
    work = 2 * tokens * width * (2 * width + 4 * CAP) + 40 * tokens * tokens * width
    if ringed:
        d_middle, grad_wo, grad_ext, dq, dk, dv, expert_total, *back = call(
            back_kernel,
            outs
            + [shape(expert_pack.shape)]
            + [rows_out] * 3
            + [shape(bank_z), shape(bank_z), shape(bank_x)],
            specs + [ANY] * 5,
            [VMEM] * 7 + [ANY] * 6,
            scratch
            + [
                pltpu.VMEM(bank_x, BF),
                pltpu.VMEM((1,) + expert_pack.shape, BF),
                pltpu.SemaphoreType.DMA((2,)),
                pltpu.SemaphoreType.DMA((11,)),
                pltpu.SemaphoreType.DMA((11,)),
            ],
            flops=work,
            moved=40 * 2**20,
            group=5,
            alias={24: 12},
        )(*operands, near_b, far_a, far_b, grads, expert_x)
        operands = (x, ext, dq, dk, dv, wq, wk, wv, d_middle, grad_wo, grad_ext)
        operands += (slot, near_a, *back[:3], shared_out, probs, middle)
        strip = (2, width // SLOTS, width)
        grad_in, outputs, weights, small, shared_pair, e1, e2, e3 = call(
            tail_kernel,
            [wide, token_f, shape((4, rows, width), F32), shape((16, width), F32)]
            + [shape((2,) + my_half.shape)]
            + [shape(expert_pack.shape)] * 3,
            [VMEM] * 19 + [ANY, VMEM],
            [VMEM] * 5 + [ANY] * 3,
            [
                pltpu.VMEM((tokens, width), BF),
                pltpu.VMEM((8, width), F32),
                pltpu.VMEM((4, width, width), BF),
                pltpu.VMEM((2, width, width), BF),
                pltpu.VMEM((4,) + strip, BF),
                pltpu.VMEM((3,) + strip, BF),
                pltpu.VMEM(strip, BF),
                pltpu.VMEM((2,) + strip, BF),
                pltpu.VMEM(strip, BF),
                pltpu.VMEM((4, 16, width), BF),
                pltpu.VMEM((6, 16, width), BF),
                pltpu.VMEM(my_half.shape, BF),
                pltpu.VMEM(my_half.shape, BF),
                pltpu.SemaphoreType.DMA((29,)),
                pltpu.SemaphoreType.DMA((29,)),
            ],
            flops=2 * tokens * width * (6 * width + 4 * CAP),
            moved=40 * 2**20,
            group=6,
        )(*operands, expert_total, shared_total)
        banks = [shape((4, width, units), F32)] * 2 + [shape((4, units, width), F32)]
        banks += [shape((width, units), F32)] * 2 + [shape((units, width), F32)]
        finals = call(finish_kernel, banks, [VMEM] * 5, [VMEM] * 6, moved=18 * 2**20)(
            expert_total, e1, e2, e3, shared_pair
        )
        grad_q, grad_k, grad_v, grad_o = (weights[i] for i in range(4))
    else:
        d_middle, grad_wo, grad_ext, dq, dk, dv = call(
            plain_back_kernel, outs, specs, [VMEM] * 6, scratch, flops=work, moved=40 * 2**20
        )(*operands)
        out_rows = [near_a, to_rep(near_b, 1), to_rep(far_a, 2), to_rep(far_b, 3)]
        grad_in, outputs, gw, gain = call(
            plain_tail_kernel,
            [wide, token_f, shape((3, width, width)), shape((8, width), F32)],
            [VMEM] * 17,
            [VMEM] * 4,
            [pltpu.VMEM((tokens, width), BF), pltpu.VMEM((8, width), F32)],
            flops=2 * tokens * width * (6 * width + 4 * CAP),
            moved=40 * 2**20,
        )(
            x, ext, dq, dk, dv, wq, wk, wv, d_middle, slot, *out_rows, shared_out, probs, middle
        )

        def over_rep(total):
            return lax.psum(total.astype(BF), "rep").astype(F32)

        def unslot(every, part_units):
            every = every.reshape(SLOTS, 3, width, shards // SLOTS, part_units)
            every = every.transpose(0, 3, 1, 2, 4).reshape(shards, 3, width, part_units)
            return lax.psum_scatter(every, "shard", scatter_dimension=0)

        grad_q, grad_k, grad_v, grad_o = (
            over_rep(lax.psum_scatter(w, "shard", tiled=True))
            for w in (gw[0], gw[1], gw[2], grad_wo)
        )
        small = grad_ext.at[4].add(jnp.sum(gain, axis=0))
        small = lax.psum(small, ("rep", "shard"))
        shared_sum = grads_own.astype(F32) + to_rep(grads_other, 1).astype(F32)
        total = unslot(shared_sum.astype(BF), units // 2).astype(F32)
        total = (total + to_rep(total.astype(BF), 2).astype(F32)).astype(BF)
        mate = to_rep(total, 1)
        shared_full = jnp.concatenate(
            [jnp.where(core == 0, total, mate), jnp.where(core == 0, mate, total)], axis=2
        ).astype(F32)
        expert_total = unslot(grads, units).astype(BF)
        parts = jnp.stack([expert_total] + [to_rep(expert_total, o) for o in (1, 2, 3)])
        full = jnp.take(parts, jnp.arange(4) ^ rep, axis=0).astype(F32)
        finals = (full[:, 0], full[:, 1], full[:, 2].transpose(0, 2, 1))
        finals += (shared_full[0], shared_full[1], shared_full[2].T)
    tiny = lax.dynamic_slice(small, (0, shard * rows), (16, rows))
    return (
        outputs[None],
        grad_in[None],
        tiny[4],
        grad_q,
        grad_k,
        grad_v,
        grad_o,
        tiny[5],
        tiny[:4].T,
        *finals,
    )


def solution(mesh):
    in_specs = (
        P(("rep", "shard"), None, None),
        P(("rep", "shard"), None),
        P(("rep", "shard"), None, None),
        P("shard"),
        P("shard", None),
        P("shard", None),
        P("shard", None),
        P("shard", None),
        P("shard"),
        P("shard", None),
        P(None, None, "shard"),
        P(None, None, "shard"),
        P(None, "shard", None),
        P(None, "shard"),
        P(None, "shard"),
        P("shard", None),
        P(("rep", "shard"), None, None),
    )
    out_specs = (
        P(("rep", "shard"), None, None),
        P(("rep", "shard"), None, None),
        P("shard"),
        P("shard", None),
        P("shard", None),
        P("shard", None),
        P("shard", None),
        P("shard"),
        P("shard", None),
        P(None, None, "shard"),
        P(None, None, "shard"),
        P(None, "shard", None),
        P(None, "shard"),
        P(None, "shard"),
        P("shard", None),
    )
    return jax.shard_map(body, mesh=mesh, in_specs=in_specs, out_specs=out_specs, check_vma=False)
```

```python
import functools

import jax
import jax.numpy as jnp
from jax import lax
from jax.experimental import pallas as pl
from jax.experimental.pallas import tpu as pltpu
from jax.sharding import PartitionSpec as P

HEADS = 12
PIECE = 256
CAP = 576
EPSILON = 1e-06
MASKED = -1e30
F32, BF = jnp.float32, jnp.bfloat16
AXES = ("rep", "shard")
TILE = 256
SLOTS = 8
VMEM_LIMIT = 62 * 2**20
ANY = pl.BlockSpec(memory_space=pl.ANY)
SMEM = pl.BlockSpec(memory_space=pltpu.SMEM)
VMEM = pl.BlockSpec(memory_space=pltpu.VMEM)


def dot(a, b, i, j):
    return lax.dot_general(a, b, (((i,), (j,)), ((), ())), preferred_element_type=F32)


def nn(a, b):
    return dot(a, b, 1, 0)


def nt(a, b):
    return dot(a, b, 1, 1)


def tn(a, b):
    return dot(a, b, 0, 0)


def iota(shape, dim):
    return lax.broadcasted_iota(jnp.int32, shape, dim)


def ones_where(cond):
    return jnp.where(cond, 1.0, 0.0).astype(BF)


def call(
    kernel, out_shape, in_specs, out_specs, scratch=(), flops=0, moved=0, grid=None, group=None,
    alias=None,
):
    extra = {} if grid is None else {"grid": grid}
    params = {} if group is None else {"collective_id": group, "has_side_effects": True}
    return pl.pallas_call(
        kernel,
        out_shape=out_shape,
        in_specs=in_specs,
        out_specs=out_specs,
        scratch_shapes=list(scratch),
        input_output_aliases=alias or {},
        compiler_params=pltpu.CompilerParams(vmem_limit_bytes=VMEM_LIMIT, **params),
        cost_estimate=pl.CostEstimate(flops=flops, bytes_accessed=moved, transcendentals=0),
        **extra,
    )


def shape(dims, dtype=BF):
    return jax.ShapeDtypeStruct(dims, dtype)


def permute(x, move):
    reps, shards = lax.axis_size("rep"), lax.axis_size("shard")
    pairs = []
    for r in range(reps):
        for s in range(shards):
            to_r, to_s = move(r, s)
            pairs.append((r * shards + s, to_r * shards + to_s))
    return lax.ppermute(x, AXES, pairs)


def to_rep(x, offset):
    return permute(x, lambda r, s: (r ^ offset, s))


def spin(block, cosine, sine):
    lane = iota(block.shape, 1)
    partner = jnp.where(lane % 64 < 32, pltpu.roll(block, 96, 1), pltpu.roll(block, 32, 1))
    return block * cosine + partner * sine


def sibling(rep, o):
    return 2 * lax.rem(lax.div(rep, 2) + o // 2, 2) + lax.rem(lax.rem(rep, 2) + o % 2, 2)


def route_slots(rep, routes, routes_t, rank_out, slot_out):
    tokens = routes.shape[0]
    first, second = routes_t[0:1, :], routes_t[1:2, :]
    expert = iota((8, tokens), 0)
    chosen = (expert == first) | (expert == second)
    upper = ones_where(iota((tokens, tokens), 0) <= iota((tokens, tokens), 1))
    rank = nn(ones_where(chosen), upper) - 1.0
    rank_out[...] = jnp.where(chosen, rank, -1.0)
    lane = iota((tokens, 128), 1)
    one, two = routes[:, 0:1], routes[:, 1:2]
    lower = ones_where(iota((tokens, tokens), 0) >= iota((tokens, tokens), 1))
    place = nn(lower, ones_where((lane == one) | (lane == two))) - 1.0
    for o in range(1, 4):
        place = place + jnp.where(lane == sibling(rep, o), float(o * CAP), 0.0)
    slot_one = jnp.sum(jnp.where(lane == one, place, 0.0), axis=1, keepdims=True)
    slot_two = jnp.sum(jnp.where(lane == two, place, 0.0), axis=1, keepdims=True)
    slot_out[...] = jnp.where(lane < 64, slot_one, slot_two)


def pack_row(rep, rank, source, o, out):
    row = rank[pl.ds(sibling(rep, o), 1), :]
    pick = ones_where(iota((CAP, source.shape[0]), 0).astype(F32) == row)
    out[...] = nn(pick, source[...]).astype(BF)


def pack_rows(rep, rank, source, packed):
    for o, out in enumerate(packed):
        pack_row(rep, rank, source, o, out)


def qkv_rows(x, ext, cosine, sine, wq, wk, wv, q, k, v):
    tokens, width = x.shape
    gain = ext[4:5, :]

    def tile(t, carry):
        at = pl.ds(pl.multiple_of(t * TILE, TILE), TILE)
        rows_in = x[at, :].astype(F32)
        scale = lax.rsqrt(jnp.mean(rows_in * rows_in, axis=1, keepdims=True) + EPSILON)
        normed = (rows_in * scale * gain).astype(BF)
        cos_t, sin_t = cosine[at, :], sine[at, :]
        for weight, out, factor in ((wq, q, 0.125), (wk, k, 1.0)):
            full = nn(normed, weight[...])
            for b in range(width // 128):
                turned = spin(full[:, b * 128 : (b + 1) * 128], cos_t, sin_t)
                out[at, b * 128 : (b + 1) * 128] = turned.astype(BF) * jnp.asarray(factor, BF)
        v[at, :] = nn(normed, wv[...]).astype(BF)
        return carry

    lax.fori_loop(0, tokens // TILE, tile, 0)


def when(cond, body):
    if cond is True:
        body()
    elif cond is not False:
        pl.when(cond)(body)


def both(one, two):
    if one is True or two is False:
        return two
    if two is True or one is False:
        return one
    return one & two


class Net:
    def __init__(self, send, recv):
        self.rep, self.shard = lax.axis_index("rep"), lax.axis_index("shard")
        self.core, self.z = lax.rem(self.rep, 2), lax.div(self.shard, 2)
        self.x = lax.rem(self.shard, 2)
        self.mate = self.rep + 1 - 2 * self.core
        self.across = self.shard + 1 - 2 * self.x
        first = lax.max(self.z - 1, 1 - self.z)
        third = 3 * (1 - lax.div(self.z, 2))
        self.levels = [self.z, first, 6 - self.z - first - third, third]
        self.up = lax.min(self.shard + 2, 6 + self.x)
        self.down = lax.max(self.shard - 2, self.x)
        self.cousins = [self.rep] + [sibling(self.rep, o) for o in (1, 2, 3)]
        self.send, self.recv = send, recv
        self.count, self.open = 0, {}

    def event(self):
        self.count += 1
        return self.count - 1

    def place(self, n, side):
        return self.levels[n] * 2 + (self.x if side == 0 else 1 - self.x)

    def cycle(self, d):
        return lax.rem(self.z + d, 4) * 2 + self.x

    def copy(self, event, source, target, rep, shard):
        return pltpu.make_async_remote_copy(
            src_ref=source,
            dst_ref=target,
            send_sem=self.send.at[event],
            recv_sem=self.recv.at[event],
            device_id=(rep, shard),
            device_id_type=pl.DeviceIdType.MESH,
        )

    def put(self, event, source, target, rep, shard, cond=True):
        when(cond, self.copy(event, source, target, rep, shard).start)
        self.open[event] = (cond, source)

    def got(self, event, like, cond=True):
        when(cond, self.copy(event, like, like, self.mate, self.shard).wait_recv)

    def settle(self, event):
        cond, source = self.open.pop(event)
        when(cond, self.copy(event, source, source, self.mate, self.shard).wait_send)

    def close(self):
        for event, (cond, source) in self.open.items():
            when(cond, self.copy(event, source, source, self.mate, self.shard).wait_send)

    def meet(self, z_ways, others):
        barrier = pltpu.get_barrier_semaphore()

        def greet(rep, shard):
            pl.semaphore_signal(
                barrier, inc=1, device_id=(rep, shard), device_id_type=pl.DeviceIdType.MESH
            )

        count = len(others)
        for rep, shard in others:
            greet(rep, shard)
        if z_ways == "line":
            when(self.z < 3, lambda: greet(self.rep, self.up))
            when(self.z > 0, lambda: greet(self.rep, self.down))
            count = count + lax.min(self.z, 1) + lax.min(3 - self.z, 1)
        if z_ways == "all":
            for d in (1, 2, 3):
                greet(self.rep, self.cycle(d))
            count = count + 3
        pl.semaphore_wait(barrier, count)


class Line:
    def __init__(self, net, bank, ways=4):
        self.net, self.bank = net, bank
        self.events = {(way, k): net.event() for way in range(ways) for k in range(-3, 4)}
        self.spots = {0: (net.shard, True)}
        for k in (1, 2, 3):
            self.spots[k] = (lax.min(net.shard + 2 * k, 6 + net.x), net.z < 4 - k)
            self.spots[-k] = (lax.max(net.shard - 2 * k, net.x), net.z >= k)
        self.flips = {k: spot + 1 - 2 * net.x for k, (spot, _) in self.spots.items()}
        self.onward = {k: both(self.spots[k][1], net.z < 3) for k in self.spots}
        self.back = {k: both(self.spots[k][1], net.z > 0) for k in self.spots}

    def spread(self, k, source):
        net, (spot, here) = self.net, self.spots[k]
        target = self.bank.at[net.core, spot]
        if -3 < k <= 0:
            event = self.events[0, k - 1]
            net.put(event, source, target, net.rep, net.up, self.onward[k])
        if 0 <= k < 3:
            event = self.events[0, k + 1]
            net.put(event, source, target, net.rep, net.down, self.back[k])
        net.put(self.events[1, k], source, target, net.rep, net.across, here)
        net.put(self.events[2, k], source, target, net.mate, net.shard, here)

    def along(self, k):
        spot, here = self.spots[k]
        piece = self.bank.at[self.net.core, spot]
        self.net.got(self.events[0, k], piece, here)
        self.spread(k, piece)

    def over(self, k):
        net, here = self.net, self.spots[k][1]
        piece = self.bank.at[net.core, self.flips[k]]
        net.got(self.events[1, k], piece, here)
        net.put(self.events[3, k], piece, piece, net.mate, net.shard, here)

    def finish(self):
        other = 1 - self.net.core
        for k in (0, 1, -1, 2, -2, 3, -3):
            spot, here = self.spots[k]
            self.net.got(self.events[2, k], self.bank.at[other, spot], here)
            self.net.got(self.events[3, k], self.bank.at[other, self.flips[k]], here)


class Spread:
    def __init__(self, net, piece, bank):
        self.net, self.piece, self.bank = net, piece, bank
        self.line = Line(net, bank, 8)
        self.events, self.spots, self.flips = self.line.events, self.line.spots, self.line.flips
        self.half = piece.shape[1] // 2
        y = lax.div(net.rep, 2)
        self.rows = [pl.ds(pl.multiple_of(n * self.half, 128), self.half) for n in (y, 1 - y)]
        self.far = net.cousins[2]

    def view(self, core, spot, rows):
        return self.bank.at[core, spot, :, self.rows[rows], :]

    def begin(self):
        net = self.net
        source = self.piece.at[:, self.rows[0], :]
        target = self.view(net.core, net.shard, 0)
        net.put(self.events[0, -1], source, target, net.rep, net.up, self.line.onward[0])
        net.put(self.events[0, 1], source, target, net.rep, net.down, self.line.back[0])
        net.put(self.events[1, 0], source, target, net.rep, net.across)
        whole = self.bank.at[net.core, net.shard]
        net.put(self.events[2, 0], self.piece, whole, net.mate, net.shard)

    def hand(self, way, k, here, piece):
        net = self.net
        net.put(self.events[way + 4, k], piece, piece, self.far, net.shard, here)
        net.put(self.events[way + 2, k], piece, piece, net.mate, net.shard, here)

    def along(self, k):
        net, (spot, here) = self.net, self.spots[k]
        piece = self.view(net.core, spot, 0)
        net.got(self.events[0, k], piece, here)
        if -3 < k < 0:
            net.put(self.events[0, k - 1], piece, piece, net.rep, net.up, self.line.onward[k])
        if 0 < k < 3:
            net.put(self.events[0, k + 1], piece, piece, net.rep, net.down, self.line.back[k])
        net.put(self.events[1, k], piece, piece, net.rep, net.across, here)
        self.hand(0, k, here, piece)

    def over(self, k):
        net, here = self.net, self.spots[k][1]
        piece = self.view(net.core, self.flips[k], 0)
        net.got(self.events[1, k], piece, here)
        self.hand(1, k, here, piece)

    def relay(self, way, k):
        net, here = self.net, self.spots[k][1]
        spot = self.spots[k][0] if way == 0 else self.flips[k]
        piece = self.view(net.core, spot, 1)
        net.got(self.events[way + 4, k], piece, here)
        net.put(self.events[way + 6, k], piece, piece, net.mate, net.shard, here)

    def finish(self):
        net, other = self.net, 1 - self.net.core
        net.got(self.events[2, 0], self.bank.at[other, net.shard])
        for k in (0, 1, -1, 2, -2, 3, -3):
            spot, here = self.spots[k]
            if k:
                net.got(self.events[2, k], self.view(other, spot, 0), here)
                net.got(self.events[6, k], self.view(other, spot, 1), here)
            net.got(self.events[3, k], self.view(other, self.flips[k], 0), here)
            net.got(self.events[7, k], self.view(other, self.flips[k], 1), here)


def exchange(net, sources, targets):
    events = [net.event() for _ in range(3)]
    for o in (2, 3, 1):
        net.put(events[o - 1], sources[o - 1], targets[o - 1], net.cousins[o], net.shard)
    return [(events[o], targets[o]) for o in range(3)]


def head_kernel(
    routes, routes_t, cot, x, piece, cosine, sine,
    rank, slot, q, k, v, wq, wk, wv, wo, ext, c0, c1, c2, c3,
    bank, packed, send, recv, own_sem,
):
    width = x.shape[1]
    half = width // SLOTS
    net = Net(send, recv)
    line = Line(net, bank)
    peers = [(net.cousins[o], net.shard) for o in (1, 2, 3)]
    net.meet("line", peers + [(net.rep, net.across)])
    line.spread(0, piece)
    own = pltpu.make_async_copy(piece, bank.at[net.core, net.shard], own_sem)
    own.start()
    route_slots(net.rep, routes, routes_t, rank, slot)
    events = [net.event() for _ in range(3)]
    for o, far in ((2, c2), (3, c3), (1, c1)):
        pack_row(net.rep, rank, cot, o, packed.at[o - 1])
        net.put(events[o - 1], packed.at[o - 1], far, net.cousins[o], net.shard)
    arrivals = [(events[0], c1), (events[1], c2), (events[2], c3)]
    pack_row(net.rep, rank, cot, 0, c0)
    line.along(1)
    line.along(-1)
    line.over(0)
    line.along(2)
    line.along(-2)
    line.over(1)
    line.over(-1)
    line.along(3)
    line.along(-3)
    for step in (2, -2, 3, -3):
        line.over(step)
    own.wait()
    line.finish()
    gathered = bank[0, 0, 2 * half : 2 * half + 16, :].astype(F32)
    for j in range(1, SLOTS):
        gathered = gathered + bank[0, j, 2 * half : 2 * half + 16, :].astype(F32)
    ext[...] = gathered
    for j in range(SLOTS):
        at = slice(j * half, (j + 1) * half)
        wq[at, :] = bank[0, j, 0:half, :]
        wk[at, :] = bank[0, j, half : 2 * half, :]
        wv[at, :] = bank[1, j, 0:half, :]
        wo[at, :] = bank[1, j, half : 2 * half, :]
    qkv_rows(x, ext, cosine, sine, wq, wk, wv, q, k, v)
    for event, like in arrivals:
        net.got(event, like)
    net.close()


def plain_head_kernel(
    routes, routes_t, cot, x, cosine, sine, wq, wk, wv, ext,
    rank, slot, q, k, v, c0, c1, c2, c3,
):
    rep = lax.axis_index("rep")
    route_slots(rep, routes, routes_t, rank, slot)
    pack_rows(rep, rank, cot, (c0, c1, c2, c3))
    qkv_rows(x, ext, cosine, sine, wq, wk, wv, q, k, v)


def fill_bias(starts, bias):
    tokens = bias.shape[0]

    def tile(t, carry):
        at = pl.ds(pl.multiple_of(t * TILE, TILE), TILE)
        query = iota((TILE, tokens), 0) + t * TILE
        key = iota((TILE, tokens), 1)
        allowed = key <= query
        for n in range(2):
            begin = starts[0, n]
            inside = (query >= begin) & (query < begin + PIECE)
            allowed = allowed | (inside & (key >= begin) & (key < begin + PIECE))
        bias[at, :] = jnp.where(allowed, 0.0, MASKED)
        return carry

    lax.fori_loop(0, tokens // TILE, tile, 0)


def keep_half(block, h):
    low = iota(block.shape, 1) < 64
    return jnp.where(low if h == 0 else ~low, block.astype(F32), 0.0).astype(BF)


def biased(scores, bias, begin, free, end):
    tail = scores[:, free:] + bias[begin : begin + TILE, free:end]
    return tail if free == 0 else jnp.concatenate([scores[:, :free], tail], axis=1)


def attend_pairs(q, k, v, out, lse, bias, step):
    tokens, width = q.shape

    def pair(i, carry):
        step(i)
        cols = pl.ds(pl.multiple_of(i * 128, 128), 128)
        keys = k[:, cols]
        low = iota((tokens, 128), 1) < 64
        values = v[:, cols].astype(F32)
        value_one = [
            jnp.where(low, values, 1.0).astype(BF),
            jnp.where(low, 1.0, values).astype(BF),
        ]
        low = iota((TILE, 128), 1) < 64
        for t in range(tokens // TILE):
            begin = t * TILE
            end = min(tokens, begin + TILE + PIECE)
            block = q[begin : begin + TILE, cols]
            results, totals = [], []
            for h in range(2):
                scores = nt(keep_half(block, h), keys[:end])
                scores = biased(scores, bias, begin, begin, end)
                row_max = jnp.max(scores, axis=1, keepdims=True)
                probs = jnp.exp(scores - row_max).astype(BF)
                mixed = nn(probs, value_one[h][:end])
                total = pltpu.roll(mixed, 64, 1)
                results.append(mixed / total)
                totals.append(row_max + jnp.log(total))
            out[begin : begin + TILE, cols] = jnp.where(low, results[0], results[1]).astype(BF)
            lse[begin : begin + TILE, cols] = jnp.where(low, totals[0], totals[1])
        return carry

    lax.fori_loop(0, width // 128, pair, 0)


def router_rows(ext):
    rows = jnp.where(iota(ext.shape, 0) < 4, ext[...], 0.0)
    return jnp.concatenate([rows, jnp.zeros((112, ext.shape[1]), F32)], axis=0).astype(BF)


def route_probs(normed, router):
    logits = nt(normed, router)
    logits = jnp.where(iota(logits.shape, 1) < 4, logits, MASKED)
    raised = jnp.exp(logits - jnp.max(logits, axis=1, keepdims=True))
    return raised / jnp.sum(raised, axis=1, keepdims=True)


def middle_rows(rep, x, attended, wo, ext, rank, middle, normed, probs, packed):
    tokens = x.shape[0]
    gain = ext[5:6, :]
    router = router_rows(ext)

    def tile(t, carry):
        at = pl.ds(pl.multiple_of(t * TILE, TILE), TILE)
        rows = x[at, :].astype(F32) + nn(attended[at, :], wo[...])
        scale = lax.rsqrt(jnp.mean(rows * rows, axis=1, keepdims=True) + EPSILON)
        middle[at, :] = rows
        unit = (rows * scale * gain).astype(BF)
        normed[at, :] = unit
        probs[at, :] = route_probs(unit, router)
        return carry

    lax.fori_loop(0, tokens // TILE, tile, 0)
    pack_rows(rep, rank, normed, packed)


def forward_kernel(
    starts, q, k, v, x, wo, ext, rank, shared_piece, expert_piece,
    attended, lse, middle, normed, probs, x0, x1, x2, x3, shared_bank, expert_bank,
    bias, send, recv,
):
    net = Net(send, recv)
    spread = Spread(net, shared_piece, shared_bank)
    events = [net.event() for _ in range(3)]
    mine = expert_bank.at[net.shard]
    more_up, more_down = net.z < 3, net.z > 0
    net.meet("line", [(net.mate, net.shard), (net.rep, net.across), (spread.far, net.shard)])
    spread.begin()
    fill_bias(starts, bias)

    def step(i):
        @pl.when(i == 1)
        def _():
            spread.along(1)
            spread.along(-1)
            spread.over(0)

        @pl.when(i == 3)
        def _():
            spread.along(2)
            spread.along(-2)
            spread.over(1)
            spread.over(-1)
            spread.relay(1, 0)
            spread.relay(0, 1)
            spread.relay(0, -1)

        @pl.when(i == 5)
        def _():
            spread.along(3)
            spread.along(-3)
            net.put(events[0], expert_piece, mine, net.rep, net.up, more_up)
            net.put(events[1], expert_piece, mine, net.rep, net.down, more_down)
            net.put(events[2], expert_piece, mine, net.rep, net.across)
            spread.over(2)
            spread.over(-2)

    attend_pairs(q, k, v, attended, lse, bias, step)
    spread.over(3)
    spread.over(-3)
    middle_rows(net.rep, x, attended, wo, ext, rank, middle, normed, probs, (x0, x1, x2, x3))
    for way, k_step in ((1, 1), (1, -1), (0, 2), (0, -2), (1, 2), (1, -2)):
        spread.relay(way, k_step)
    for way, k_step in ((0, 3), (0, -3), (1, 3), (1, -3)):
        spread.relay(way, k_step)
    spread.finish()
    net.got(events[0], mine, net.z > 0)
    net.got(events[1], mine, net.z < 3)
    net.got(events[2], mine)
    net.close()


def plain_forward_kernel(
    starts, q, k, v, x, wo, ext, rank,
    attended, lse, middle, normed, probs, x0, x1, x2, x3, bias,
):
    fill_bias(starts, bias)
    attend_pairs(q, k, v, attended, lse, bias, lambda i: None)
    rep = lax.axis_index("rep")
    middle_rows(rep, x, attended, wo, ext, rank, middle, normed, probs, (x0, x1, x2, x3))


CHUNK, CHUNKS = 512, 4


def unit_bank(
    expert, ext, xs, cs, source, target, before, unit, outs, dxs, scratch, ready=None,
    emit=None, reclaim=None,
):
    out_acc, dx_acc, gate, wbuf, dw_acc, dw_out, in_sems, out_sems = scratch[:8]
    routed = expert is not None
    blocks, rows = len(xs), xs[0].shape[0]
    per = CHUNK // unit

    def loads(of, buffer, sems, k, b):
        return [
            pltpu.make_async_copy(
                of(k * per + i), buffer.at[b, :, :, pl.ds(i * unit, unit)], sems.at[b, i]
            )
            for i in range(per)
        ]

    def stores(k, b):
        return [
            pltpu.make_async_copy(
                dw_out.at[b, :, :, pl.ds(i * unit, unit)],
                target(k * per + i),
                out_sems.at[b, i],
            )
            for i in range(per)
        ]

    def start_loads(k, b):
        if ready is not None:
            ready(k)
        for copy in loads(source, wbuf, in_sems, k, b):
            copy.start()
        if before is not None:
            for copy in loads(before, scratch[8], scratch[9], k, b):
                copy.start()

    start_loads(0, 0)
    if routed:
        router = router_rows(ext)
        for n in range(blocks):
            probs = route_probs(xs[n][...], router)
            lane = iota(probs.shape, 1)
            gate[n] = jnp.sum(jnp.where(lane == expert, probs, 0.0), axis=1, keepdims=True)

    def chunk(k, carry):
        b = lax.rem(k, 2)
        for copy in loads(source, wbuf, in_sems, 0, b):
            copy.wait()
        for n in range(blocks):
            x, c = xs[n][...], cs[n][...]
            wg, wu, wd = wbuf[b, 0], wbuf[b, 1], wbuf[b, 2]
            gate_h, up_h, back_h = nn(x, wg), nn(x, wu), nn(c, wd)
            sigma = 1.0 / (1.0 + jnp.exp(-gate_h))
            silu = gate_h * sigma
            hidden = silu * up_h
            if routed:
                share = gate[n]
                scaled = back_h * share
                weighted = (hidden * share).astype(BF)
            else:
                scaled, weighted = back_h, hidden.astype(BF)
            d_up = (scaled * silu).astype(BF)
            d_gate = (scaled * up_h * (sigma + silu * (1.0 - sigma))).astype(BF)
            product = nt(hidden.astype(BF), wd)
            d_rows = nt(d_gate, wg) + nt(d_up, wu)
            parts = (tn(x, d_gate), tn(x, d_up), tn(c, weighted))
            if routed:
                pairs = (hidden * back_h).astype(BF)
                d_share = nt(jnp.ones((16, CHUNK), BF), pairs)

            @pl.when(k == 0)
            def _():
                out_acc[n] = product
                dx_acc[n, 0:rows, :] = d_rows
                if routed:
                    dx_acc[n, rows : rows + 16, :] = jnp.zeros((16, d_rows.shape[1]), F32)
                    dx_acc[n, rows : rows + 16, 0:rows] = d_share

            @pl.when(k != 0)
            def _():
                out_acc[n] += product
                dx_acc[n, 0:rows, :] += d_rows
                if routed:
                    dx_acc[n, rows : rows + 16, 0:rows] += d_share

            for i in range(3):
                if n == 0:
                    dw_acc[i] = parts[i]
                else:
                    dw_acc[i] += parts[i]

        for nxt in range(1, CHUNKS):

            @pl.when(k + 1 == nxt)
            def _():
                start_loads(nxt, nxt % 2)

        @pl.when(k >= 2)
        def _():
            for copy in stores(0, b):
                copy.wait()

        if reclaim is not None:
            for now in (2, 3):
                when(k == now, functools.partial(reclaim, now))
        if before is not None:
            for copy in loads(before, scratch[8], scratch[9], 0, b):
                copy.wait()
            for i in range(3):
                dw_out[b, i] = (dw_acc[i] + scratch[8][b, i].astype(F32)).astype(BF)
        else:
            for i in range(3):
                dw_out[b, i] = dw_acc[i].astype(BF)
        for now in range(CHUNKS):

            @pl.when(k == now)
            def _():
                for copy in stores(now, now % 2):
                    copy.start()
                if emit is not None:
                    emit(now)

        return carry

    lax.fori_loop(0, CHUNKS, chunk, 0)
    for n in range(blocks):
        outs[n][...] = out_acc[n].astype(BF)
        dxs[n][...] = dx_acc[n].astype(BF)
    for b in range(2):
        for copy in stores(0, b):
            copy.wait()


def unit_scratch(blocks, rows, extra, width, per, chained):
    scratch = [
        pltpu.VMEM((blocks, rows, width), F32),
        pltpu.VMEM((blocks, rows + extra, width), F32),
        pltpu.VMEM((blocks, rows, 1), F32),
        pltpu.VMEM((2, 3, width, CHUNK), BF),
        pltpu.VMEM((3, width, CHUNK), F32),
        pltpu.VMEM((2, 3, width, CHUNK), BF),
        pltpu.SemaphoreType.DMA((2, per)),
        pltpu.SemaphoreType.DMA((2, per)),
    ]
    if chained:
        scratch += [
            pltpu.VMEM((2, 3, width, CHUNK), BF),
            pltpu.SemaphoreType.DMA((2, per)),
        ]
    return scratch


def shared_kernel(
    x, c, piece, bank, x1, x2, x3, expert_piece, expert_in,
    out, dx, grads_own, grads_other, y1, y2, y3, experts,
    send, recv, *scratch,
):
    net = Net(send, recv)
    events = [net.event() for _ in range(6)]
    peers = [(net.cousins[o], net.shard) for o in (1, 2, 3)]
    net.meet("line", peers + [(net.rep, net.across)])
    arrivals = exchange(net, (x1, x2, x3), (y1, y2, y3))
    low, high = experts.at[net.down], experts.at[net.up]
    net.put(events[0], low, low, net.rep, net.up, (net.z > 0) & (net.z < 3))
    net.put(events[1], high, high, net.rep, net.down, (net.z > 0) & (net.z < 3))
    near, next_near = experts.at[net.place(1, 0)], experts.at[net.place(2, 0)]
    net.put(events[2], near, near, net.rep, net.across)
    below = experts.at[lax.max(net.shard - 4, net.x)]
    above = experts.at[lax.min(net.shard + 4, 6 + net.x)]

    def spot(n):
        return net.place(n % 4, n // 4 % 2)

    spots = [spot(n) for n in range(8)]
    halves = [net.core, 1 - net.core]

    def source(n):
        return piece if n == 0 else bank.at[halves[n // 8], spots[n % 8]]

    def target(n):
        return (grads_own, grads_other)[n // 8].at[spots[n % 8]]

    from_below, from_above = net.z > 1, net.z < 2
    last_up, last_down = net.z == 2, net.z == 1

    def ready(k):
        if k == 2:
            net.got(events[0], below, from_below)
            net.got(events[1], above, from_above)
            net.put(events[3], next_near, next_near, net.rep, net.across)
            net.put(events[4], below, below, net.rep, net.up, last_up)
            net.put(events[5], above, above, net.rep, net.down, last_down)

    unit_bank(None, None, [x], [c], source, target, None, 128, [out], [dx], scratch, ready)
    for event, like in arrivals:
        net.got(event, like)
    net.got(events[2], near)
    net.got(events[3], near)
    net.got(events[4], near, net.z == 3)
    net.got(events[5], near, net.z == 0)
    net.close()


def far_kernel(
    ext, xa, xb, ca, cb, expert_piece, shared_own, shared_other, expert_in,
    oa, ob, da, db, grads, shared_mate, shared_keep, shared_y, experts,
    part_a, part_b, part_sems, send, recv, *scratch,
):
    net = Net(send, recv)
    events = [net.event() for _ in range(10)]
    far = net.cousins[2]
    net.meet("none", [(net.rep, net.across), (net.mate, net.shard), (far, net.shard)])
    last = experts.at[net.place(3, 0)]
    net.put(events[0], last, last, net.rep, net.across)
    net.put(events[1], shared_other, shared_mate, net.mate, net.shard)
    own = pltpu.make_async_copy(shared_own, part_a, part_sems.at[0])
    mate = pltpu.make_async_copy(shared_mate, part_b, part_sems.at[1])
    own.start()
    spots = [net.place(n // 2, n % 2) for n in range(8)]
    y, quarter = lax.div(net.rep, 2), part_a.shape[2] // 2
    rows = [pl.ds(pl.multiple_of(n * quarter, 128), quarter) for n in (y, 1 - y)]
    keep = pltpu.make_async_copy(part_a.at[:, :, rows[0], :], shared_keep, part_sems.at[2])
    away = [part_a.at[j, :, rows[1], :] for j in range(SLOTS)]

    def source(n):
        return expert_piece if n == 0 else experts.at[spots[n]]

    def target(n):
        return grads.at[spots[n]]

    def ready(k):
        if k == 1:
            net.got(events[1], shared_mate)
            mate.start()
            own.wait()
            mate.wait()

            def add(j, carry):
                part_a[j] = (part_a[j].astype(F32) + part_b[j].astype(F32)).astype(BF)
                return carry

            lax.fori_loop(0, SLOTS, add, 0)
            for j in range(SLOTS):
                net.put(events[2 + j], away[j], shared_y.at[j], far, net.shard)
            keep.start()
        if k == 3:
            net.got(events[0], last)

    unit_bank(
        net.rep, ext, [xa, xb], [ca, cb], source, target, None, 256, [oa, ob], [da, db],
        scratch, ready,
    )
    keep.wait()
    for j in range(SLOTS):
        net.got(events[2 + j], shared_y.at[j])
    net.close()


def near_kernel(
    ext, xa, xb, ca, cb, expert_piece, experts, before, far_a, far_b,
    shared_keep, shared_y,
    oa, ob, da, shared_total, grads, back_a, back_b, back_c, expert_x,
    db, part_a, part_b, from_x, from_z, sems, send, recv, *scratch,
):
    net = Net(send, recv)
    events = [net.event() for _ in range(4)]
    x_events = [net.event() for _ in range(4)]
    z_events = [net.event() for _ in range(3)]
    peers = [(net.cousins[o], net.shard) for o in (1, 2, 3)]
    one = pltpu.make_async_copy(shared_keep, part_a, sems.at[0])
    two = pltpu.make_async_copy(shared_y, part_b, sems.at[1])
    one.start()
    two.start()
    net.meet("all", peers + [(net.rep, net.across)])
    net.put(events[0], far_a, back_a, net.cousins[2], net.shard)
    net.put(events[1], far_b, back_b, net.cousins[3], net.shard)
    one.wait()
    two.wait()

    def add(j, carry):
        part_a[j] = (part_a[j].astype(F32) + part_b[j].astype(F32)).astype(BF)
        return carry

    lax.fori_loop(0, SLOTS, add, 0)
    mine = [net.cycle(d) for d in range(4)]
    theirs = [spot + 1 - 2 * net.x for spot in mine]
    for d in (2, 1, 3, 0):
        net.put(x_events[d], part_a.at[theirs[d]], from_x.at[d], net.rep, net.across)
    pieces, lands = [part_a.at[spot] for spot in mine], [from_x.at[d] for d in range(4)]
    ends = [from_z.at[d] for d in range(3)]
    spots = [net.place(3 - n // 2, n % 2) for n in range(8)]
    own_slot = 6
    half = scratch[5].at[0, :, :, pl.ds(256, 256)]
    target = expert_x.at[net.levels[3]]

    def source(n):
        return expert_piece if n == own_slot else experts.at[spots[n]]

    def ready(k):
        if k == 2:
            for d in (2, 1, 3, 0):
                net.got(x_events[d], lands[d])
                total = part_a[mine[d]].astype(F32) + from_x[d].astype(F32)
                part_a[mine[d]] = total.astype(BF)
                if d:
                    net.put(z_events[d - 1], pieces[d], ends[d - 1], net.rep, mine[d])

    def emit(now):
        if now == 0:
            net.put(events[3], half, target, net.rep, net.across)

    def reclaim(now):
        if now == 2:
            net.copy(events[3], half, half, net.mate, net.shard).wait_send()

    unit_bank(
        net.rep, ext, [xa, xb], [ca, cb], source,
        lambda n: grads.at[spots[n]], lambda n: before.at[spots[n]],
        256, [oa, ob], [da, db], scratch, ready, emit, reclaim,
    )
    net.open.pop(events[3])
    net.put(events[2], db, back_c, net.mate, net.shard)
    total = part_a[mine[0]].astype(F32)
    for d in (1, 2, 3):
        net.got(z_events[d - 1], ends[d - 1])
        total = total + from_z[d - 1].astype(F32)
    shared_total[...] = total.astype(BF)
    net.got(events[0], back_a)
    net.got(events[1], back_b)
    net.got(events[2], back_c)
    net.got(events[3], target)
    net.close()


def plain_bank_kernel(blocks, unit, routed, chained, ext, *refs):
    refs = list(refs)

    def take(n):
        taken = refs[:n]
        del refs[:n]
        return taken

    xs, cs = take(blocks), take(blocks)
    bank = take(1)[0]
    before = take(1)[0] if chained else None
    outs, dxs = take(blocks), take(blocks)
    grads = take(1)[0]
    unit_bank(
        lax.axis_index("rep") if routed else None,
        ext, xs, cs,
        lambda n: bank.at[n],
        lambda n: grads.at[n],
        (lambda n: before.at[n]) if chained else None,
        unit, outs, dxs, refs,
    )


def plain_bank(ext, xs, cs, bank, before, routed):
    blocks, (rows, width) = len(xs), xs[0].shape
    chained = before is not None
    extra, unit = (16 if routed else 0), bank.shape[3]
    operands = [ext, *xs, *cs, bank] + ([before] if chained else [])
    outs = [shape((rows, width))] * blocks + [shape((rows + extra, width))] * blocks
    results = call(
        functools.partial(plain_bank_kernel, blocks, unit, routed, chained),
        outs + [shape(bank.shape)],
        [VMEM] * (1 + 2 * blocks) + [ANY] * (2 if chained else 1),
        [VMEM] * (2 * blocks) + [ANY],
        unit_scratch(blocks, rows, extra, width, CHUNK // unit, chained),
        flops=18 * blocks * rows * width * 4 * CHUNK,
        moved=30 * 2**20,
    )(*operands)
    return results[:blocks], results[blocks : 2 * blocks], results[2 * blocks]


def combine_rows(
    slot, d0, d1, d2, d3, d_shared, probs, middle, normed, cot, ext, attended, wo,
    d_middle, d_attended, grad_wo, grad_ext, branch, router_acc, gain_acc,
):
    tokens, width = middle.shape
    rep = lax.axis_index("rep")
    gain = ext[5:6, :]
    router = router_rows(ext)
    router_acc[...] = jnp.zeros_like(router_acc)
    gain_acc[...] = jnp.zeros_like(gain_acc)

    def tile(t, carry):
        at = pl.ds(pl.multiple_of(t * TILE, TILE), TILE)
        slot_one, slot_two = slot[at, 0:1], slot[at, 64:65]
        d_normed = d_shared[at, :].astype(F32)
        lane = iota((TILE, 128), 1)
        d_gates = jnp.zeros((TILE, 128), F32)
        for o, d in enumerate((d0, d1, d2, d3)):
            place = (iota((TILE, CAP), 1) + o * CAP).astype(F32)
            hit = (place == slot_one) | (place == slot_two)
            d_normed = d_normed + nn(ones_where(hit), d[0:CAP, :])
            share = d[CAP : CAP + 16, 0:CAP].astype(F32)[0:1, :]
            d_share = jnp.sum(jnp.where(hit, share, 0.0), axis=1, keepdims=True)
            d_gates = d_gates + jnp.where(lane == sibling(rep, o), d_share, 0.0)
        p = probs[at, :]
        inner = jnp.sum(d_gates * p, axis=1, keepdims=True)
        d_logits = (p * (d_gates - inner)).astype(BF)
        d_normed = d_normed + nn(d_logits, router)
        router_acc[...] += tn(d_logits, normed[at, :])
        rows = middle[at, :]
        scale = lax.rsqrt(jnp.mean(rows * rows, axis=1, keepdims=True) + EPSILON)
        unit = rows * scale
        gain_acc[...] += jnp.sum((d_normed * unit).reshape(TILE // 8, 8, width), axis=0)
        w = d_normed * gain
        inner = jnp.mean(w * unit, axis=1, keepdims=True)
        total = cot[at, :].astype(F32) + scale * (w - unit * inner)
        d_middle[at, :] = total
        rounded = total.astype(BF)
        branch[at, :] = rounded
        d_attended[at, :] = nt(rounded, wo[...]).astype(BF)
        return carry

    lax.fori_loop(0, tokens // TILE, tile, 0)
    grad_wo[...] = tn(attended[...], branch[...]).astype(BF)
    row = iota((16, width), 0)
    total = jnp.sum(gain_acc[...], axis=0, keepdims=True)
    grad_ext[...] = jnp.where(row < 4, router_acc[0:16, :], jnp.where(row == 5, total, 0.0))


def output_rows(slot, o0, o1, o2, o3, shared, probs, middle, out, first, last):
    rep = lax.axis_index("rep")

    def tile(t, carry):
        at = pl.ds(pl.multiple_of(t * TILE, TILE), TILE)
        slot_one, slot_two = slot[at, 0:1], slot[at, 64:65]
        total = middle[at, :] + shared[at, :].astype(F32)
        p = probs[at, :]
        lane = iota((TILE, 128), 1)
        for o, rows in enumerate((o0, o1, o2, o3)):
            place = (iota((TILE, CAP), 1) + o * CAP).astype(F32)
            hit = (place == slot_one) | (place == slot_two)
            share = jnp.sum(jnp.where(lane == sibling(rep, o), p, 0.0), axis=1, keepdims=True)
            total = total + nn(jnp.where(hit, share, 0.0).astype(BF), rows[...])
        out[at, :] = total.astype(BF)
        return carry

    lax.fori_loop(first, last, tile, 0)


def back_pairs(
    q, k, v, d_out, out, lse, cosine, sine, dq, dk, dv, bias, dk_acc, dv_acc, step
):
    tokens, width = q.shape

    def pair(i, carry):
        step(i)
        cols = pl.ds(pl.multiple_of(i * 128, 128), 128)
        keys, values = k[:, cols], v[:, cols]
        half_keys = [keep_half(keys, 0), keep_half(keys, 1)]
        dk_acc[...] = jnp.zeros_like(dk_acc)
        dv_acc[...] = jnp.zeros_like(dv_acc)
        low = iota((TILE, 128), 1) < 64
        for t in range(tokens // TILE):
            begin = t * TILE
            end = min(tokens, begin + TILE + PIECE)
            at = slice(begin, begin + TILE)
            block, grad = q[at, cols], d_out[at, cols]
            product = grad.astype(F32) * out[at, cols].astype(F32)
            block_lse = lse[at, cols]
            d_block = None
            for h in range(2):
                block_h, grad_h = keep_half(block, h), keep_half(grad, h)
                scores = nt(block_h, keys[:end])
                scores = biased(scores, bias, begin, begin, end)
                probs = jnp.exp(scores - block_lse[:, 64 * h : 64 * h + 1])
                d_probs = nt(grad_h, values[:end])
                inner = jnp.sum(
                    jnp.where(low if h == 0 else ~low, product, 0.0), axis=1, keepdims=True
                )
                d_scores = (probs * (d_probs - inner)).astype(BF)
                part = nn(d_scores, half_keys[h][:end])
                d_block = part if d_block is None else d_block + part
                dk_acc[0:end, :] += tn(d_scores, block_h)
                dv_acc[0:end, :] += tn(probs.astype(BF), grad_h)
            dq[at, cols] = spin(d_block * 0.125, cosine[at, :], -sine[at, :]).astype(BF)
        dk[:, cols] = spin(dk_acc[...], cosine[...], -sine[...]).astype(BF)
        dv[:, cols] = dv_acc[...].astype(BF)
        return carry

    lax.fori_loop(0, width // 128, pair, 0)


def fetch(sources, targets, sems):
    copies = [pltpu.make_async_copy(a, b, sems.at[i]) for i, (a, b) in enumerate(zip(sources, targets))]
    for copy in copies:
        copy.start()
    for copy in copies:
        copy.wait()


class Chain:
    def __init__(self, net, own, from_x, up_in, down_in, held, spare, sems):
        self.net, self.own, self.from_x = net, own, from_x
        self.up_in, self.down_in = up_in, down_in
        self.held, self.spare, self.sems = held, spare, sems
        self.events = {(way, d): net.event() for way in range(2) for d in (1, 2, 3)}
        self.spots = [net.place(n, 0) for n in range(4)]
        self.sends, self.gets = {}, {}
        z = net.z
        for d in (1, 2, 3):
            self.sends[0, d] = (held.at[lax.min(z + d, 3)], z < 4 - d)
            self.sends[1, d] = (held.at[lax.max(z - d, 0)], z > d - 1)
            self.gets[0, d] = (lax.min(z + d - 1, 3), (z > 0) & (z < 5 - d))
            self.gets[1, d] = (lax.max(z - d + 1, 0), (z < 3) & (z > d - 2))

    def level(self, n):
        to = self.net.levels[n]
        far = self.from_x.at[to]
        fetch([self.own.at[self.spots[n]], far], [self.held.at[to], self.spare.at[0]], self.sems)
        self.held[to] = (self.held[to].astype(F32) + self.spare[0].astype(F32)).astype(BF)

    def send(self, d):
        net = self.net
        for way, to, into in ((0, net.up, self.up_in), (1, net.down, self.down_in)):
            source, here = self.sends[way, d]
            net.put(self.events[way, d], source, into.at[d - 1], net.rep, to, here)

    def take(self, d):
        for way, into in ((0, self.up_in), (1, self.down_in)):
            to, here = self.gets[way, d]

            def add():
                self.net.copy(
                    self.events[way, d], into.at[d - 1], into.at[d - 1],
                    self.net.mate, self.net.shard,
                ).wait_recv()
                fetch([into.at[d - 1]], [self.spare.at[0]], self.sems)
                total = self.held[to].astype(F32) + self.spare[0].astype(F32)
                self.held[to] = total.astype(BF)

            when(here, add)


def back_kernel(
    starts, slot, d0, d1, d2, d3, d_shared, probs, middle, normed, cot, ext, attended, wo,
    cosine, sine,
    q_in, k_in, v_in, lse_in, o1, o2, o3, grads, expert_x_in,
    d_middle, grad_wo, grad_ext, dq, dk, dv, expert_total,
    r1, r2, r3, up_in, down_in, expert_x,
    d_attended, branch, router_acc, gain_acc, bias, dk_acc, dv_acc,
    q, k, v, lse, held, spare, sems, load_sems, send, recv,
):
    net = Net(send, recv)
    x_events = [net.event() for _ in range(3)]
    chain = Chain(net, grads, expert_x, up_in, down_in, held, spare, sems)
    peers = [(net.cousins[o], net.shard) for o in (1, 2, 3)]
    net.meet("line", peers + [(net.rep, net.across)])
    targets = [expert_x.at[net.levels[n]] for n in range(3)]
    pairs = ((q_in, q), (k_in, k), (v_in, v), (lse_in, lse))
    loads = [pltpu.make_async_copy(a, b, load_sems.at[i]) for i, (a, b) in enumerate(pairs)]
    for n in (2, 1, 0):
        source = grads.at[net.place(n, 1)]
        net.put(x_events[n], source, targets[n], net.rep, net.across)
    arrivals = exchange(net, (o1, o2, o3), (r1, r2, r3))
    chain.level(3)
    chain.send(3)
    for copy in loads:
        copy.start()
    combine_rows(
        slot, d0, d1, d2, d3, d_shared, probs, middle, normed, cot, ext, attended, wo,
        d_middle, d_attended, grad_wo, grad_ext, branch, router_acc, gain_acc,
    )
    fill_bias(starts, bias)
    net.got(x_events[2], targets[2])
    chain.level(2)
    chain.take(3)
    chain.send(2)
    for copy in loads:
        copy.wait()

    def step(i):
        @pl.when(i == 1)
        def _():
            net.got(x_events[1], targets[1])
            chain.level(1)

        @pl.when(i == 4)
        def _():
            chain.take(2)
            chain.send(1)

    back_pairs(
        q, k, v, d_attended, attended, lse, cosine, sine, dq, dk, dv, bias, dk_acc, dv_acc, step
    )
    net.got(x_events[0], targets[0])
    chain.level(0)
    for event, like in arrivals:
        net.got(event, like)
    chain.take(1)
    expert_total[...] = held[net.z]
    net.close()


def plain_back_kernel(
    starts, slot, d0, d1, d2, d3, d_shared, probs, middle, normed, cot, ext, attended, wo,
    q, k, v, lse, cosine, sine,
    d_middle, grad_wo, grad_ext, dq, dk, dv,
    d_attended, branch, router_acc, gain_acc, bias, dk_acc, dv_acc,
):
    combine_rows(
        slot, d0, d1, d2, d3, d_shared, probs, middle, normed, cot, ext, attended, wo,
        d_middle, d_attended, grad_wo, grad_ext, branch, router_acc, gain_acc,
    )
    fill_bias(starts, bias)
    back_pairs(
        q, k, v, d_attended, attended, lse, cosine, sine, dq, dk, dv, bias, dk_acc, dv_acc,
        lambda i: None,
    )


def norm_rows(x, ext, normed_all):
    gain = ext[4:5, :]

    def tile(t, carry):
        at = pl.ds(pl.multiple_of(t * TILE, TILE), TILE)
        rows = x[at, :].astype(F32)
        scale = lax.rsqrt(jnp.mean(rows * rows, axis=1, keepdims=True) + EPSILON)
        normed_all[at, :] = (rows * scale * gain).astype(BF)
        return carry

    lax.fori_loop(0, x.shape[0] // TILE, tile, 0)


def input_grad(x, ext, dq, dk, dv, wq, wk, wv, d_middle, grad_in, gain_acc):
    tokens, width = x.shape
    gain = ext[4:5, :]
    gain_acc[...] = jnp.zeros_like(gain_acc)

    def tile(t, carry):
        at = pl.ds(pl.multiple_of(t * TILE, TILE), TILE)
        rows = x[at, :].astype(F32)
        scale = lax.rsqrt(jnp.mean(rows * rows, axis=1, keepdims=True) + EPSILON)
        unit = rows * scale
        d_normed = nt(dq[at, :], wq[...]) + nt(dk[at, :], wk[...]) + nt(dv[at, :], wv[...])
        gain_acc[...] += jnp.sum((d_normed * unit).reshape(TILE // 8, 8, width), axis=0)
        w = d_normed * gain
        inner = jnp.mean(w * unit, axis=1, keepdims=True)
        grad_in[at, :] = d_middle[at, :] + scale * (w - unit * inner)
        return carry

    lax.fori_loop(0, tokens // TILE, tile, 0)


def tail_kernel(
    x, ext, dq, dk, dv, wq, wk, wv, grad_wo, grad_ext,
    d_middle_in, slot_in, o0_in, o1_in, o2_in, o3_in, shared_in, probs_in, middle_in,
    expert_total, shared_total,
    grad_in, outputs, weights, small, shared_far, shared_mate, shared_cross, e1, e2, e3,
    normed_all, gain_acc, gw, from_mate, from_x, from_z, from_y, result, from_core,
    tiny, tiny_in, d_middle, slot, o0, o1, o2, o3, shared_out, probs, middle, load_sems,
    send, recv,
):
    width = x.shape[1]
    half = width // SLOTS
    net = Net(send, recv)
    e_events = [net.event() for _ in range(3)]
    s_events = [net.event() for _ in range(3)]
    m_events = [net.event() for _ in range(2)]
    x_events = [[net.event() for _ in range(2)] for _ in range(4)]
    z_events = [[net.event() for _ in range(2)] for _ in range(3)]
    y_event, c_event = net.event(), net.event()
    t_events = [net.event() for _ in range(6)]
    net.meet(
        "all", [(net.mate, net.shard), (net.cousins[2], net.shard), (net.rep, net.across)]
    )
    far = net.cousins[2]
    net.put(s_events[0], shared_total, shared_far, far, net.shard)
    net.put(s_events[1], shared_total, shared_mate, net.mate, net.shard)
    net.put(e_events[1], expert_total, e2, far, net.shard)
    net.put(e_events[0], expert_total, e1, net.mate, net.shard)
    pairs = (
        (d_middle_in, d_middle), (slot_in, slot), (o0_in, o0), (o1_in, o1), (o2_in, o2),
        (o3_in, o3), (shared_in, shared_out), (probs_in, probs), (middle_in, middle),
    )
    loads = [pltpu.make_async_copy(a, b, load_sems.at[i]) for i, (a, b) in enumerate(pairs)]
    for copy in loads:
        copy.start()
    norm_rows(x, ext, normed_all)
    spots = [lax.rem(i + 2 * net.core, 4) for i in range(4)]
    gw[spots[0]] = tn(normed_all[...], dq[...]).astype(BF)
    gw[spots[1]] = tn(normed_all[...], dk[...]).astype(BF)
    gw[spots[2]] = tn(normed_all[...], dv[...]).astype(BF)
    gw[spots[3]] = grad_wo[...]
    for i in range(2):
        net.put(m_events[i], gw.at[2 + i], from_mate.at[i], net.mate, net.shard)

    def rows_of(spot):
        return pl.ds(pl.multiple_of(spot * half, 32), half)

    mine = [rows_of(net.cycle(d)) for d in range(4)]
    theirs = [rows_of(net.cycle(d) + 1 - 2 * net.x) for d in range(4)]
    for i in range(2):
        net.got(m_events[i], from_mate.at[i])
        gw[i] = (gw[i].astype(F32) + from_mate[i].astype(F32)).astype(BF)
    for d in (2, 1, 3, 0):
        for i in range(2):
            net.put(
                x_events[d][i], gw.at[i, theirs[d]], from_x.at[d, i], net.rep, net.across
            )
    for copy in loads:
        copy.wait()
    input_grad(x, ext, dq, dk, dv, wq, wk, wv, d_middle, grad_in, gain_acc)
    row = iota((16, width), 0)
    total = jnp.sum(gain_acc[...], axis=0, keepdims=True)
    tiny[0] = (grad_ext[...] + jnp.where(row == 4, total, 0.0)).astype(BF)
    net.put(t_events[0], tiny.at[0], tiny_in.at[0], net.mate, net.shard)

    def add_across(d):
        for i in range(2):
            net.got(x_events[d][i], from_x.at[d, i])
            summed = gw[i, mine[d], :].astype(F32) + from_x[d, i].astype(F32)
            gw[i, mine[d], :] = summed.astype(BF)
            if d:
                net.put(
                    z_events[d - 1][i], gw.at[i, mine[d]], from_z.at[d - 1, i],
                    net.rep, net.cycle(d),
                )

    def tiny_add(n, target_rep, target_shard):
        net.got(t_events[n], tiny_in.at[n])
        tiny[n + 1] = (tiny[n].astype(F32) + tiny_in[n].astype(F32)).astype(BF)
        if target_rep is not None:
            source, target = tiny.at[n + 1], tiny_in.at[n + 1]
            net.put(t_events[n + 1], source, target, target_rep, target_shard)

    add_across(2)
    tiny_add(0, net.rep, net.across)
    output_rows(slot, o0, o1, o2, o3, shared_out, probs, middle, outputs, 0, 2)
    add_across(1)
    tiny_add(1, far, net.shard)
    net.got(s_events[0], shared_far)
    net.put(s_events[2], shared_far, shared_cross, net.mate, net.shard)
    output_rows(slot, o0, o1, o2, o3, shared_out, probs, middle, outputs, 2, 4)
    tiny_add(2, None, None)
    for d in (1, 2, 3):
        net.put(t_events[2 + d], tiny.at[3], tiny_in.at[2 + d], net.rep, net.cycle(d))
    add_across(3)
    add_across(0)
    for i in range(2):
        total = gw[i, mine[0], :].astype(F32)
        for d in (1, 2, 3):
            net.got(z_events[d - 1][i], from_z.at[d - 1, i])
            total = total + from_z[d - 1, i].astype(F32)
        result[0, i] = total.astype(BF)
    net.put(y_event, result.at[0], from_y, far, net.shard)
    total = tiny[3].astype(F32)
    for d in (1, 2, 3):
        net.got(t_events[2 + d], tiny_in.at[2 + d])
        total = total + tiny_in[2 + d].astype(F32)
    small[...] = total.astype(BF).astype(F32)
    net.got(e_events[1], e2)
    net.put(e_events[2], e2, e3, net.mate, net.shard)
    net.got(y_event, from_y)
    result[1] = (result[0].astype(F32) + from_y[...].astype(F32)).astype(BF)
    net.put(c_event, result.at[1], from_core, net.mate, net.shard)
    for i in range(2):
        weights[spots[i]] = result[1, i].astype(F32)
    net.got(c_event, from_core)
    for i in range(2):
        weights[spots[2 + i]] = from_core[i].astype(F32)
    net.got(e_events[0], e1)
    net.got(s_events[1], shared_mate)
    net.got(s_events[2], shared_cross)
    net.got(e_events[2], e3)
    net.close()


def plain_tail_kernel(
    x, ext, dq, dk, dv, wq, wk, wv, d_middle,
    slot, o0, o1, o2, o3, shared_out, probs, middle,
    grad_in, outputs, gw, gain, normed_all, gain_acc,
):
    norm_rows(x, ext, normed_all)
    for i, d in enumerate((dq, dk, dv)):
        gw[i] = tn(normed_all[...], d[...]).astype(BF)
    input_grad(x, ext, dq, dk, dv, wq, wk, wv, d_middle, grad_in, gain_acc)
    gain[...] = gain_acc[...]
    output_rows(
        slot, o0, o1, o2, o3, shared_out, probs, middle, outputs, 0, x.shape[0] // TILE
    )


def finish_kernel(e0, e1, e2, e3, q0, q1, q2, q3, gate, up, down, s_gate, s_up, s_down):
    rep = lax.axis_index("rep")
    for o, part in enumerate((e0, e1, e2, e3)):
        at = sibling(rep, o)
        gate[at] = part[0].astype(F32)
        up[at] = part[1].astype(F32)
        down[at] = part[2].astype(F32).T
    quarter, span = q0.shape[1:]
    for o, part in enumerate((q0, q1, q2, q3)):
        for other in range(4):

            @pl.when(sibling(rep, o) == other)
            def _():
                rows = slice(other // 2 * quarter, (other // 2 + 1) * quarter)
                cols = slice(other % 2 * span, (other % 2 + 1) * span)
                s_gate[rows, cols] = part[0].astype(F32)
                s_up[rows, cols] = part[1].astype(F32)
                s_down[cols, rows] = part[2].astype(F32).T


def rope_tables(length, head_dim):
    positions = jnp.arange(length, dtype=F32)
    inverse_freq = 10000.0 ** (-2.0 * jnp.arange(head_dim // 2, dtype=F32) / head_dim)
    angle = positions[:, None] * inverse_freq[None, :]
    cosine, sine = jnp.cos(angle), jnp.sin(angle)
    return (
        jnp.concatenate([cosine] * 4, axis=1),
        jnp.concatenate([-sine, sine, -sine, sine], axis=1),
    )


def body(
    inputs,
    piece_starts,
    routes,
    attn_gain,
    query_weight,
    key_weight,
    value_weight,
    out_weight,
    ffn_gain,
    router_weight,
    expert_gate,
    expert_up,
    expert_down,
    shared_gate,
    shared_up,
    shared_down,
    cotangent,
):
    _, tokens, width = inputs.shape
    shards = lax.axis_size("shard")
    rep, shard = lax.axis_index("rep"), lax.axis_index("shard")
    core = rep % 2
    ringed = shards == SLOTS
    rows = width // shards
    units = shared_gate.shape[1]
    x, cot, chosen = inputs[0], cotangent[0], routes[0]
    small = jnp.concatenate([router_weight.T, attn_gain[None], ffn_gain[None]], axis=0)
    small = jnp.pad(small, ((0, 10), (0, 0)))
    small = lax.dynamic_update_slice(jnp.zeros((16, width), BF), small, (0, shard * rows))
    blank = jnp.zeros((16, width), BF)
    if ringed:
        half_one = jnp.concatenate([query_weight, key_weight, small], axis=0)
        half_two = jnp.concatenate([value_weight, out_weight, blank], axis=0)
        piece = jnp.where(core == 0, half_one, half_two)
    else:
        wq, wk, wv, wo = [
            lax.all_gather(w, "shard", axis=0, tiled=True)
            for w in (query_weight, key_weight, value_weight, out_weight)
        ]
        ext = lax.psum(small.astype(F32), "shard")

    shared_pack = jnp.stack([shared_gate, shared_up, shared_down.T])
    my_half = lax.dynamic_slice_in_dim(shared_pack, core * (units // 2), units // 2, 2)
    expert_pack = jnp.stack([expert_gate[rep], expert_up[rep], expert_down[rep].T])

    cosine, sine = rope_tables(tokens, width // HEADS)
    token_f = shape((tokens, width))
    square = shape((width, width))
    packed = [shape((CAP, width))] * 4
    outs = [shape((8, tokens), F32), shape((tokens, 128), F32)] + [token_f] * 3
    work = 2 * tokens * width * (CAP * 4 + 3 * width)
    if ringed:
        rank, slot, q, k, v, *heads = call(
            head_kernel,
            outs + [square] * 4 + [shape((16, width), F32)] + packed,
            [VMEM] * 7,
            [VMEM] * 10 + [VMEM] + [ANY] * 3,
            [
                pltpu.VMEM((2, SLOTS, 2 * rows + 16, width), BF),
                pltpu.VMEM((3, CAP, width), BF),
                pltpu.SemaphoreType.DMA((31,)),
                pltpu.SemaphoreType.DMA((31,)),
                pltpu.SemaphoreType.DMA,
            ],
            flops=work,
            moved=24 * 2**20,
            group=0,
        )(chosen, chosen.T, cot, x, piece, cosine, sine)
        wq, wk, wv, wo, ext, *cot_in = heads
    else:
        rank, slot, q, k, v, *cot_out = call(
            plain_head_kernel, outs + packed, [VMEM] * 10, [VMEM] * 9, flops=work,
            moved=24 * 2**20,
        )(chosen, chosen.T, cot, x, cosine, sine, wq, wk, wv, ext)
        cot_in = [cot_out[0]] + [to_rep(cot_out[o], o) for o in (1, 2, 3)]

    outs = [token_f, shape((tokens, width), F32), shape((tokens, width), F32), token_f]
    outs += [shape((tokens, 128), F32)] + packed
    work = 2 * tokens * width * (8 * tokens + width + 4 * CAP)
    bias = pltpu.VMEM((tokens, tokens), F32)
    if ringed:
        attended, lse, middle, normed, probs, *x_out, shared_bank, expert_bank = call(
            forward_kernel,
            outs + [shape((2, SLOTS) + my_half.shape), shape((SLOTS,) + expert_pack.shape)],
            [SMEM] + [VMEM] * 7 + [ANY] * 2,
            [VMEM] * 9 + [ANY] * 2,
            [bias, pltpu.SemaphoreType.DMA((59,)), pltpu.SemaphoreType.DMA((59,))],
            flops=work,
            moved=30 * 2**20,
            group=1,
        )(piece_starts, q, k, v, x, wo, ext, rank, my_half, expert_pack)
    else:
        attended, lse, middle, normed, probs, *x_out = call(
            plain_forward_kernel, outs, [SMEM] + [VMEM] * 7, [VMEM] * 9, [bias], flops=work,
            moved=30 * 2**20,
        )(piece_starts, q, k, v, x, wo, ext, rank)

    rows_out = shape((CAP, width))
    rows_back = shape((CAP + 16, width))
    if ringed:
        half_grads = shape((SLOTS,) + my_half.shape)
        shared_out, shared_dx, grads_own, grads_other, y1, y2, y3, expert_bank = call(
            shared_kernel,
            [token_f] * 2 + [half_grads] * 2 + packed[:3] + [shape(expert_bank.shape)],
            [VMEM] * 2 + [ANY] * 7,
            [VMEM] * 2 + [ANY] * 6,
            [pltpu.SemaphoreType.DMA((9,)), pltpu.SemaphoreType.DMA((9,))]
            + unit_scratch(1, tokens, 0, width, 4, False),
            flops=18 * tokens * width * CHUNK * CHUNKS,
            moved=30 * 2**20,
            group=2,
            alias={8: 7},
        )(normed, cot, my_half, shared_bank, *x_out[1:], expert_pack, expert_bank)
        x_in = [x_out[0], y1, y2, y3]
        bank = shape(expert_bank.shape)
        quarter = (3, width // 2, units // 2)
        quarters = (SLOTS,) + quarter
        far_a, far_b, da, db, before, _, shared_keep, shared_y, expert_bank = call(
            far_kernel,
            [rows_out] * 2 + [rows_back] * 2 + [bank, half_grads]
            + [shape(quarters), shape(quarters), bank],
            [VMEM] * 5 + [ANY] * 4,
            [VMEM] * 4 + [ANY] * 5,
            [
                pltpu.VMEM(half_grads.shape, BF),
                pltpu.VMEM(half_grads.shape, BF),
                pltpu.SemaphoreType.DMA((3,)),
                pltpu.SemaphoreType.DMA((10,)),
                pltpu.SemaphoreType.DMA((10,)),
            ]
            + unit_scratch(2, CAP, 16, width, 2, False),
            flops=36 * CAP * width * CHUNK * CHUNKS,
            moved=30 * 2**20,
            group=3,
            alias={8: 8},
        )(ext, *x_in[2:], *cot_in[2:], expert_pack, grads_own, grads_other, expert_bank)
        bank_x, bank_z = (4,) + expert_pack.shape, (3,) + expert_pack.shape
        near_a, near_b, d0, shared_total, grads, d2, d3, d1, expert_x = call(
            near_kernel,
            [rows_out] * 2 + [rows_back, shape(quarter), bank] + [rows_back] * 3 + [shape(bank_x)],
            [VMEM] * 5 + [ANY] * 7,
            [VMEM] * 4 + [ANY] * 5,
            [
                pltpu.VMEM((CAP + 16, width), BF),
                pltpu.VMEM(quarters, BF),
                pltpu.VMEM(quarters, BF),
                pltpu.VMEM((4,) + quarter, BF),
                pltpu.VMEM((3,) + quarter, BF),
                pltpu.SemaphoreType.DMA((2,)),
                pltpu.SemaphoreType.DMA((11,)),
                pltpu.SemaphoreType.DMA((11,)),
            ]
            + unit_scratch(2, CAP, 16, width, 2, True),
            flops=36 * CAP * width * CHUNK * CHUNKS,
            moved=30 * 2**20,
            group=4,
        )(
            ext, *x_in[:2], *cot_in[:2], expert_pack, expert_bank, before, da, db,
            shared_keep, shared_y,
        )
        d_rows = [d0, d1, d2, d3]
    else:

        def slotted(part):
            every = lax.all_gather(part, "shard")
            every = every.reshape(SLOTS, shards // SLOTS, 3, width, part.shape[2])
            return every.transpose(0, 2, 3, 1, 4).reshape(SLOTS, 3, width, -1)

        shared_bank = slotted(my_half)
        shared_bank = jnp.concatenate([shared_bank, to_rep(shared_bank, 1)], axis=0)
        expert_bank = slotted(expert_pack)
        x_in = [x_out[0]] + [to_rep(x_out[o], o) for o in (1, 2, 3)]
        (shared_out,), (shared_dx,), shared_grads = plain_bank(
            ext, [normed], [cot], shared_bank, None, False
        )
        grads_own, grads_other = shared_grads[:SLOTS], shared_grads[SLOTS:]
        (far_a, far_b), (da, db), before = plain_bank(
            ext, x_in[2:], cot_in[2:], expert_bank, None, True
        )
        (near_a, near_b), (d0, d1), grads = plain_bank(
            ext, x_in[:2], cot_in[:2], expert_bank, before, True
        )
        d_rows = [d0, to_rep(d1, 1), to_rep(da, 2), to_rep(db, 3)]
    wide = shape((tokens, width), F32)
    outs = [wide, square, shape((16, width), F32)] + [token_f] * 3
    operands = (piece_starts, slot, *d_rows, shared_dx, probs, middle, normed, cot, ext, attended)
    operands += (wo,)
    specs = [SMEM] + [VMEM] * 15
    scratch = [
        pltpu.VMEM((tokens, width), BF),
        pltpu.VMEM((tokens, width), BF),
        pltpu.VMEM((128, width), F32),
        pltpu.VMEM((8, width), F32),
        bias,
        pltpu.VMEM((tokens, 128), F32),
        pltpu.VMEM((tokens, 128), F32),
    ]
    work = 2 * tokens * width * (2 * width + 4 * CAP) + 40 * tokens * tokens * width
    if ringed:
        d_middle, grad_wo, grad_ext, dq, dk, dv, expert_total, *back = call(
            back_kernel,
            outs
            + [shape(expert_pack.shape)]
            + [rows_out] * 3
            + [shape(bank_z), shape(bank_z), shape(bank_x)],
            specs + [ANY] * 9,
            [VMEM] * 7 + [ANY] * 6,
            scratch
            + [
                pltpu.VMEM((tokens, width), BF),
                pltpu.VMEM((tokens, width), BF),
                pltpu.VMEM((tokens, width), BF),
                pltpu.VMEM((tokens, width), F32),
                pltpu.VMEM(bank_x, BF),
                pltpu.VMEM((1,) + expert_pack.shape, BF),
                pltpu.SemaphoreType.DMA((2,)),
                pltpu.SemaphoreType.DMA((4,)),
                pltpu.SemaphoreType.DMA((12,)),
                pltpu.SemaphoreType.DMA((12,)),
            ],
            flops=work,
            moved=40 * 2**20,
            group=5,
            alias={24: 12},
        )(*operands, cosine, sine, q, k, v, lse, near_b, far_a, far_b, grads, expert_x)
        operands = (x, ext, dq, dk, dv, wq, wk, wv, grad_wo, grad_ext)
        operands += (d_middle, slot, near_a, *back[:3], shared_out, probs, middle)
        strip = (2, width // SLOTS, width)
        grad_in, outputs, weights, small, *rest = call(
            tail_kernel,
            [wide, token_f, shape((4, rows, width), F32), shape((16, width), F32)]
            + [shape(quarter)] * 3
            + [shape(expert_pack.shape)] * 3,
            [VMEM] * 10 + [ANY] * 11,
            [VMEM] * 4 + [ANY] * 6,
            [
                pltpu.VMEM((tokens, width), BF),
                pltpu.VMEM((8, width), F32),
                pltpu.VMEM((4, width, width), BF),
                pltpu.VMEM((2, width, width), BF),
                pltpu.VMEM((4,) + strip, BF),
                pltpu.VMEM((3,) + strip, BF),
                pltpu.VMEM(strip, BF),
                pltpu.VMEM((2,) + strip, BF),
                pltpu.VMEM(strip, BF),
                pltpu.VMEM((4, 16, width), BF),
                pltpu.VMEM((6, 16, width), BF),
                pltpu.VMEM((tokens, width), F32),
                pltpu.VMEM((tokens, 128), F32),
                pltpu.VMEM((CAP, width), BF),
                pltpu.VMEM((CAP, width), BF),
                pltpu.VMEM((CAP, width), BF),
                pltpu.VMEM((CAP, width), BF),
                pltpu.VMEM((tokens, width), BF),
                pltpu.VMEM((tokens, 128), F32),
                pltpu.VMEM((tokens, width), F32),
                pltpu.SemaphoreType.DMA((9,)),
                pltpu.SemaphoreType.DMA((30,)),
                pltpu.SemaphoreType.DMA((30,)),
            ],
            flops=2 * tokens * width * (6 * width + 4 * CAP),
            moved=40 * 2**20,
            group=6,
        )(*operands, expert_total, shared_total)
        banks = [shape((4, width, units), F32)] * 2 + [shape((4, units, width), F32)]
        banks += [shape((width, units), F32)] * 2 + [shape((units, width), F32)]
        shared_far, shared_mate, shared_cross, *experts = rest
        finals = call(finish_kernel, banks, [VMEM] * 8, [VMEM] * 6, moved=18 * 2**20)(
            expert_total, *experts, shared_total, shared_mate, shared_far, shared_cross
        )
        grad_q, grad_k, grad_v, grad_o = (weights[i] for i in range(4))
    else:
        d_middle, grad_wo, grad_ext, dq, dk, dv = call(
            plain_back_kernel, outs, specs + [VMEM] * 4, [VMEM] * 6, scratch, flops=work,
            moved=40 * 2**20,
        )(*operands, q, k, v, lse, cosine, sine)
        out_rows = [near_a, to_rep(near_b, 1), to_rep(far_a, 2), to_rep(far_b, 3)]
        grad_in, outputs, gw, gain = call(
            plain_tail_kernel,
            [wide, token_f, shape((3, width, width)), shape((8, width), F32)],
            [VMEM] * 17,
            [VMEM] * 4,
            [pltpu.VMEM((tokens, width), BF), pltpu.VMEM((8, width), F32)],
            flops=2 * tokens * width * (6 * width + 4 * CAP),
            moved=40 * 2**20,
        )(
            x, ext, dq, dk, dv, wq, wk, wv, d_middle, slot, *out_rows, shared_out, probs, middle
        )

        def over_rep(total):
            return lax.psum(total.astype(BF), "rep").astype(F32)

        def unslot(every, part_units):
            every = every.reshape(SLOTS, 3, width, shards // SLOTS, part_units)
            every = every.transpose(0, 3, 1, 2, 4).reshape(shards, 3, width, part_units)
            return lax.psum_scatter(every, "shard", scatter_dimension=0)

        grad_q, grad_k, grad_v, grad_o = (
            over_rep(lax.psum_scatter(w, "shard", tiled=True))
            for w in (gw[0], gw[1], gw[2], grad_wo)
        )
        small = grad_ext.at[4].add(jnp.sum(gain, axis=0))
        small = lax.psum(small, ("rep", "shard"))
        shared_sum = grads_own.astype(F32) + to_rep(grads_other, 1).astype(F32)
        total = unslot(shared_sum.astype(BF), units // 2).astype(F32)
        total = (total + to_rep(total.astype(BF), 2).astype(F32)).astype(BF)
        mate = to_rep(total, 1)
        shared_full = jnp.concatenate(
            [jnp.where(core == 0, total, mate), jnp.where(core == 0, mate, total)], axis=2
        ).astype(F32)
        expert_total = unslot(grads, units).astype(BF)
        parts = jnp.stack([expert_total] + [to_rep(expert_total, o) for o in (1, 2, 3)])
        full = jnp.take(parts, jnp.arange(4) ^ rep, axis=0).astype(F32)
        finals = (full[:, 0], full[:, 1], full[:, 2].transpose(0, 2, 1))
        finals += (shared_full[0], shared_full[1], shared_full[2].T)
    tiny = lax.dynamic_slice(small, (0, shard * rows), (16, rows))
    return (
        outputs[None],
        grad_in[None],
        tiny[4],
        grad_q,
        grad_k,
        grad_v,
        grad_o,
        tiny[5],
        tiny[:4].T,
        *finals,
    )


def solution(mesh):
    in_specs = (
        P(("rep", "shard"), None, None),
        P(("rep", "shard"), None),
        P(("rep", "shard"), None, None),
        P("shard"),
        P("shard", None),
        P("shard", None),
        P("shard", None),
        P("shard", None),
        P("shard"),
        P("shard", None),
        P(None, None, "shard"),
        P(None, None, "shard"),
        P(None, "shard", None),
        P(None, "shard"),
        P(None, "shard"),
        P("shard", None),
        P(("rep", "shard"), None, None),
    )
    out_specs = (
        P(("rep", "shard"), None, None),
        P(("rep", "shard"), None, None),
        P("shard"),
        P("shard", None),
        P("shard", None),
        P("shard", None),
        P("shard", None),
        P("shard"),
        P("shard", None),
        P(None, None, "shard"),
        P(None, None, "shard"),
        P(None, "shard", None),
        P(None, "shard"),
        P(None, "shard"),
        P("shard", None),
    )
    return jax.shard_map(body, mesh=mesh, in_specs=in_specs, out_specs=out_specs, check_vma=False)
```

```python
import functools

import jax
import jax.numpy as jnp
from jax import lax
from jax.experimental import pallas as pl
from jax.experimental.pallas import tpu as pltpu
from jax.sharding import PartitionSpec as P

HEADS = 12
PIECE = 256
CAP = 576
EPSILON = 1e-06
MASKED = -1e30
F32, BF = jnp.float32, jnp.bfloat16
AXES = ("rep", "shard")
TILE = 256
SLOTS = 8
VMEM_LIMIT = 62 * 2**20
ANY = pl.BlockSpec(memory_space=pl.ANY)
SMEM = pl.BlockSpec(memory_space=pltpu.SMEM)
VMEM = pl.BlockSpec(memory_space=pltpu.VMEM)


def dot(a, b, i, j):
    return lax.dot_general(a, b, (((i,), (j,)), ((), ())), preferred_element_type=F32)


def nn(a, b):
    return dot(a, b, 1, 0)


def nt(a, b):
    return dot(a, b, 1, 1)


def tn(a, b):
    return dot(a, b, 0, 0)


def iota(shape, dim):
    return lax.broadcasted_iota(jnp.int32, shape, dim)


def ones_where(cond):
    return jnp.where(cond, 1.0, 0.0).astype(BF)


def call(
    kernel, out_shape, in_specs, out_specs, scratch=(), flops=0, moved=0, grid=None, group=None,
    alias=None,
):
    extra = {} if grid is None else {"grid": grid}
    params = {} if group is None else {"collective_id": group, "has_side_effects": True}
    return pl.pallas_call(
        kernel,
        out_shape=out_shape,
        in_specs=in_specs,
        out_specs=out_specs,
        scratch_shapes=list(scratch),
        input_output_aliases=alias or {},
        compiler_params=pltpu.CompilerParams(vmem_limit_bytes=VMEM_LIMIT, **params),
        cost_estimate=pl.CostEstimate(flops=flops, bytes_accessed=moved, transcendentals=0),
        **extra,
    )


def shape(dims, dtype=BF):
    return jax.ShapeDtypeStruct(dims, dtype)


def permute(x, move):
    reps, shards = lax.axis_size("rep"), lax.axis_size("shard")
    pairs = []
    for r in range(reps):
        for s in range(shards):
            to_r, to_s = move(r, s)
            pairs.append((r * shards + s, to_r * shards + to_s))
    return lax.ppermute(x, AXES, pairs)


def to_rep(x, offset):
    return permute(x, lambda r, s: (r ^ offset, s))


def spin(block, cosine, sine):
    lane = iota(block.shape, 1)
    partner = jnp.where(lane % 64 < 32, pltpu.roll(block, 96, 1), pltpu.roll(block, 32, 1))
    return block * cosine + partner * sine


def sibling(rep, o):
    return 2 * lax.rem(lax.div(rep, 2) + o // 2, 2) + lax.rem(lax.rem(rep, 2) + o % 2, 2)


def route_slots(rep, routes, routes_t, rank_out, slot_out):
    tokens = routes.shape[0]
    first, second = routes_t[0:1, :], routes_t[1:2, :]
    expert = iota((8, tokens), 0)
    chosen = (expert == first) | (expert == second)
    upper = ones_where(iota((tokens, tokens), 0) <= iota((tokens, tokens), 1))
    rank = nn(ones_where(chosen), upper) - 1.0
    rank_out[...] = jnp.where(chosen, rank, -1.0)
    lane = iota((tokens, 128), 1)
    one, two = routes[:, 0:1], routes[:, 1:2]
    lower = ones_where(iota((tokens, tokens), 0) >= iota((tokens, tokens), 1))
    place = nn(lower, ones_where((lane == one) | (lane == two))) - 1.0
    for o in range(1, 4):
        place = place + jnp.where(lane == sibling(rep, o), float(o * CAP), 0.0)
    slot_one = jnp.sum(jnp.where(lane == one, place, 0.0), axis=1, keepdims=True)
    slot_two = jnp.sum(jnp.where(lane == two, place, 0.0), axis=1, keepdims=True)
    slot_out[...] = jnp.where(lane < 64, slot_one, slot_two)


def pack_row(rep, rank, source, o, out):
    row = rank[pl.ds(sibling(rep, o), 1), :]
    pick = ones_where(iota((CAP, source.shape[0]), 0).astype(F32) == row)
    out[...] = nn(pick, source[...]).astype(BF)


def pack_rows(rep, rank, source, packed):
    for o, out in enumerate(packed):
        pack_row(rep, rank, source, o, out)


def qkv_rows(x, ext, cosine, sine, wq, wk, wv, q, k, v):
    tokens, width = x.shape
    gain = ext[4:5, :]

    def tile(t, carry):
        at = pl.ds(pl.multiple_of(t * TILE, TILE), TILE)
        rows_in = x[at, :].astype(F32)
        scale = lax.rsqrt(jnp.mean(rows_in * rows_in, axis=1, keepdims=True) + EPSILON)
        normed = (rows_in * scale * gain).astype(BF)
        cos_t, sin_t = cosine[at, :], sine[at, :]
        for weight, out, factor in ((wq, q, 0.125), (wk, k, 1.0)):
            full = nn(normed, weight[...])
            for b in range(width // 128):
                turned = spin(full[:, b * 128 : (b + 1) * 128], cos_t, sin_t)
                out[at, b * 128 : (b + 1) * 128] = turned.astype(BF) * jnp.asarray(factor, BF)
        v[at, :] = nn(normed, wv[...]).astype(BF)
        return carry

    lax.fori_loop(0, tokens // TILE, tile, 0)


def when(cond, body):
    if cond is True:
        body()
    elif cond is not False:
        pl.when(cond)(body)


def both(one, two):
    if one is True or two is False:
        return two
    if two is True or one is False:
        return one
    return one & two


class Net:
    def __init__(self, send, recv):
        self.rep, self.shard = lax.axis_index("rep"), lax.axis_index("shard")
        self.core, self.z = lax.rem(self.rep, 2), lax.div(self.shard, 2)
        self.x = lax.rem(self.shard, 2)
        self.mate = self.rep + 1 - 2 * self.core
        self.across = self.shard + 1 - 2 * self.x
        first = lax.max(self.z - 1, 1 - self.z)
        third = 3 * (1 - lax.div(self.z, 2))
        self.levels = [self.z, first, 6 - self.z - first - third, third]
        self.up = lax.min(self.shard + 2, 6 + self.x)
        self.down = lax.max(self.shard - 2, self.x)
        self.cousins = [self.rep] + [sibling(self.rep, o) for o in (1, 2, 3)]
        self.send, self.recv = send, recv
        self.count, self.open = 0, {}

    def event(self):
        self.count += 1
        return self.count - 1

    def place(self, n, side):
        return self.levels[n] * 2 + (self.x if side == 0 else 1 - self.x)

    def cycle(self, d):
        return lax.rem(self.z + d, 4) * 2 + self.x

    def copy(self, event, source, target, rep, shard):
        return pltpu.make_async_remote_copy(
            src_ref=source,
            dst_ref=target,
            send_sem=self.send.at[event],
            recv_sem=self.recv.at[event],
            device_id=(rep, shard),
            device_id_type=pl.DeviceIdType.MESH,
        )

    def put(self, event, source, target, rep, shard, cond=True):
        when(cond, self.copy(event, source, target, rep, shard).start)
        self.open[event] = (cond, source)

    def got(self, event, like, cond=True):
        when(cond, self.copy(event, like, like, self.mate, self.shard).wait_recv)

    def settle(self, event):
        cond, source = self.open.pop(event)
        when(cond, self.copy(event, source, source, self.mate, self.shard).wait_send)

    def close(self):
        for event, (cond, source) in self.open.items():
            when(cond, self.copy(event, source, source, self.mate, self.shard).wait_send)

    def meet(self, z_ways, others):
        barrier = pltpu.get_barrier_semaphore()

        def greet(rep, shard):
            pl.semaphore_signal(
                barrier, inc=1, device_id=(rep, shard), device_id_type=pl.DeviceIdType.MESH
            )

        count = len(others)
        for rep, shard in others:
            greet(rep, shard)
        if z_ways == "line":
            when(self.z < 3, lambda: greet(self.rep, self.up))
            when(self.z > 0, lambda: greet(self.rep, self.down))
            count = count + lax.min(self.z, 1) + lax.min(3 - self.z, 1)
        if z_ways == "all":
            for d in (1, 2, 3):
                greet(self.rep, self.cycle(d))
            count = count + 3
        pl.semaphore_wait(barrier, count)


class Line:
    def __init__(self, net, bank, ways=4):
        self.net, self.bank = net, bank
        self.events = {(way, k): net.event() for way in range(ways) for k in range(-3, 4)}
        self.spots = {0: (net.shard, True)}
        for k in (1, 2, 3):
            self.spots[k] = (lax.min(net.shard + 2 * k, 6 + net.x), net.z < 4 - k)
            self.spots[-k] = (lax.max(net.shard - 2 * k, net.x), net.z >= k)
        self.flips = {k: spot + 1 - 2 * net.x for k, (spot, _) in self.spots.items()}
        self.onward = {k: both(self.spots[k][1], net.z < 3) for k in self.spots}
        self.back = {k: both(self.spots[k][1], net.z > 0) for k in self.spots}

    def spread(self, k, source):
        net, (spot, here) = self.net, self.spots[k]
        target = self.bank.at[net.core, spot]
        if -3 < k <= 0:
            event = self.events[0, k - 1]
            net.put(event, source, target, net.rep, net.up, self.onward[k])
        if 0 <= k < 3:
            event = self.events[0, k + 1]
            net.put(event, source, target, net.rep, net.down, self.back[k])
        net.put(self.events[1, k], source, target, net.rep, net.across, here)
        net.put(self.events[2, k], source, target, net.mate, net.shard, here)

    def along(self, k):
        spot, here = self.spots[k]
        piece = self.bank.at[self.net.core, spot]
        self.net.got(self.events[0, k], piece, here)
        self.spread(k, piece)

    def over(self, k):
        net, here = self.net, self.spots[k][1]
        piece = self.bank.at[net.core, self.flips[k]]
        net.got(self.events[1, k], piece, here)
        net.put(self.events[3, k], piece, piece, net.mate, net.shard, here)

    def finish(self):
        other = 1 - self.net.core
        for k in (0, 1, -1, 2, -2, 3, -3):
            spot, here = self.spots[k]
            self.net.got(self.events[2, k], self.bank.at[other, spot], here)
            self.net.got(self.events[3, k], self.bank.at[other, self.flips[k]], here)


class Spread:
    def __init__(self, net, piece, bank):
        self.net, self.piece, self.bank = net, piece, bank
        self.line = Line(net, bank, 8)
        self.events, self.spots, self.flips = self.line.events, self.line.spots, self.line.flips
        self.half = piece.shape[1] // 2
        y = lax.div(net.rep, 2)
        self.rows = [pl.ds(pl.multiple_of(n * self.half, 128), self.half) for n in (y, 1 - y)]
        self.far = net.cousins[2]

    def view(self, core, spot, rows):
        return self.bank.at[core, spot, :, self.rows[rows], :]

    def begin(self):
        net = self.net
        source = self.piece.at[:, self.rows[0], :]
        target = self.view(net.core, net.shard, 0)
        net.put(self.events[0, -1], source, target, net.rep, net.up, self.line.onward[0])
        net.put(self.events[0, 1], source, target, net.rep, net.down, self.line.back[0])
        net.put(self.events[1, 0], source, target, net.rep, net.across)
        whole = self.bank.at[net.core, net.shard]
        net.put(self.events[2, 0], self.piece, whole, net.mate, net.shard)

    def hand(self, way, k, here, piece):
        net = self.net
        net.put(self.events[way + 4, k], piece, piece, self.far, net.shard, here)
        net.put(self.events[way + 2, k], piece, piece, net.mate, net.shard, here)

    def along(self, k):
        net, (spot, here) = self.net, self.spots[k]
        piece = self.view(net.core, spot, 0)
        net.got(self.events[0, k], piece, here)
        if -3 < k < 0:
            net.put(self.events[0, k - 1], piece, piece, net.rep, net.up, self.line.onward[k])
        if 0 < k < 3:
            net.put(self.events[0, k + 1], piece, piece, net.rep, net.down, self.line.back[k])
        net.put(self.events[1, k], piece, piece, net.rep, net.across, here)
        self.hand(0, k, here, piece)

    def over(self, k):
        net, here = self.net, self.spots[k][1]
        piece = self.view(net.core, self.flips[k], 0)
        net.got(self.events[1, k], piece, here)
        self.hand(1, k, here, piece)

    def relay(self, way, k):
        net, here = self.net, self.spots[k][1]
        spot = self.spots[k][0] if way == 0 else self.flips[k]
        piece = self.view(net.core, spot, 1)
        net.got(self.events[way + 4, k], piece, here)
        net.put(self.events[way + 6, k], piece, piece, net.mate, net.shard, here)

    def finish(self):
        net, other = self.net, 1 - self.net.core
        net.got(self.events[2, 0], self.bank.at[other, net.shard])
        for k in (0, 1, -1, 2, -2, 3, -3):
            spot, here = self.spots[k]
            if k:
                net.got(self.events[2, k], self.view(other, spot, 0), here)
                net.got(self.events[6, k], self.view(other, spot, 1), here)
            net.got(self.events[3, k], self.view(other, self.flips[k], 0), here)
            net.got(self.events[7, k], self.view(other, self.flips[k], 1), here)


def exchange(net, sources, targets):
    events = [net.event() for _ in range(3)]
    for o in (2, 3, 1):
        net.put(events[o - 1], sources[o - 1], targets[o - 1], net.cousins[o], net.shard)
    return [(events[o], targets[o]) for o in range(3)]


def head_kernel(
    routes, routes_t, cot, x, piece, cosine, sine, expert_piece,
    rank, slot, q, k, v, wq, wk, wv, wo, ext, c0, c1, c2, c3, experts,
    bank, packed, send, recv, own_sem,
):
    width = x.shape[1]
    half = width // SLOTS
    net = Net(send, recv)
    line = Line(net, bank)
    e_events = [net.event() for _ in range(3)]
    mine, most = experts.at[net.shard], experts.at[net.shard, pl.ds(0, 2)]
    peers = [(net.cousins[o], net.shard) for o in (1, 2, 3)]
    net.meet("line", peers + [(net.rep, net.across)])
    line.spread(0, piece)
    own = pltpu.make_async_copy(piece, bank.at[net.core, net.shard], own_sem)
    own.start()
    route_slots(net.rep, routes, routes_t, rank, slot)
    events = [net.event() for _ in range(3)]
    for o, far in ((2, c2), (3, c3), (1, c1)):
        pack_row(net.rep, rank, cot, o, packed.at[o - 1])
        net.put(events[o - 1], packed.at[o - 1], far, net.cousins[o], net.shard)
    arrivals = [(events[0], c1), (events[1], c2), (events[2], c3)]
    pack_row(net.rep, rank, cot, 0, c0)
    line.along(1)
    line.along(-1)
    line.over(0)
    line.along(2)
    line.along(-2)
    net.put(e_events[0], expert_piece, mine, net.rep, net.up, net.z < 3)
    net.put(e_events[1], expert_piece, mine, net.rep, net.down, net.z > 0)
    line.over(1)
    line.over(-1)
    line.along(3)
    line.along(-3)
    net.put(e_events[2], expert_piece.at[pl.ds(0, 2)], most, net.rep, net.across)
    for step in (2, -2, 3, -3):
        line.over(step)
    own.wait()
    line.finish()
    gathered = bank[0, 0, 2 * half : 2 * half + 16, :].astype(F32)
    for j in range(1, SLOTS):
        gathered = gathered + bank[0, j, 2 * half : 2 * half + 16, :].astype(F32)
    ext[...] = gathered
    for j in range(SLOTS):
        at = slice(j * half, (j + 1) * half)
        wq[at, :] = bank[0, j, 0:half, :]
        wk[at, :] = bank[0, j, half : 2 * half, :]
        wv[at, :] = bank[1, j, 0:half, :]
        wo[at, :] = bank[1, j, half : 2 * half, :]
    qkv_rows(x, ext, cosine, sine, wq, wk, wv, q, k, v)
    for event, like in arrivals:
        net.got(event, like)
    net.got(e_events[0], mine, net.z > 0)
    net.got(e_events[1], mine, net.z < 3)
    net.got(e_events[2], most)
    net.close()


def plain_head_kernel(
    routes, routes_t, cot, x, cosine, sine, wq, wk, wv, ext,
    rank, slot, q, k, v, c0, c1, c2, c3,
):
    rep = lax.axis_index("rep")
    route_slots(rep, routes, routes_t, rank, slot)
    pack_rows(rep, rank, cot, (c0, c1, c2, c3))
    qkv_rows(x, ext, cosine, sine, wq, wk, wv, q, k, v)


def fill_bias(starts, bias):
    tokens = bias.shape[0]

    def tile(t, carry):
        at = pl.ds(pl.multiple_of(t * TILE, TILE), TILE)
        query = iota((TILE, tokens), 0) + t * TILE
        key = iota((TILE, tokens), 1)
        allowed = key <= query
        for n in range(2):
            begin = starts[0, n]
            inside = (query >= begin) & (query < begin + PIECE)
            allowed = allowed | (inside & (key >= begin) & (key < begin + PIECE))
        bias[at, :] = jnp.where(allowed, 0.0, MASKED)
        return carry

    lax.fori_loop(0, tokens // TILE, tile, 0)


def keep_half(block, h):
    low = iota(block.shape, 1) < 64
    return jnp.where(low if h == 0 else ~low, block.astype(F32), 0.0).astype(BF)


def biased(scores, bias, begin, free, end):
    tail = scores[:, free:] + bias[begin : begin + TILE, free:end]
    return tail if free == 0 else jnp.concatenate([scores[:, :free], tail], axis=1)


def attend_pairs(q, k, v, out, lse, bias, step):
    tokens, width = q.shape

    def pair(i, carry):
        step(i)
        cols = pl.ds(pl.multiple_of(i * 128, 128), 128)
        keys = k[:, cols]
        low = iota((tokens, 128), 1) < 64
        values = v[:, cols].astype(F32)
        value_one = [
            jnp.where(low, values, 1.0).astype(BF),
            jnp.where(low, 1.0, values).astype(BF),
        ]
        low = iota((TILE, 128), 1) < 64
        for t in range(tokens // TILE):
            begin = t * TILE
            end = min(tokens, begin + TILE + PIECE)
            block = q[begin : begin + TILE, cols]
            results, totals = [], []
            for h in range(2):
                scores = nt(keep_half(block, h), keys[:end])
                scores = biased(scores, bias, begin, begin, end)
                row_max = jnp.max(scores, axis=1, keepdims=True)
                probs = jnp.exp(scores - row_max).astype(BF)
                mixed = nn(probs, value_one[h][:end])
                total = pltpu.roll(mixed, 64, 1)
                results.append(mixed / total)
                totals.append(row_max + jnp.log(total))
            out[begin : begin + TILE, cols] = jnp.where(low, results[0], results[1]).astype(BF)
            lse[begin : begin + TILE, cols] = jnp.where(low, totals[0], totals[1])
        return carry

    lax.fori_loop(0, width // 128, pair, 0)


def router_rows(ext):
    rows = jnp.where(iota(ext.shape, 0) < 4, ext[...], 0.0)
    return jnp.concatenate([rows, jnp.zeros((112, ext.shape[1]), F32)], axis=0).astype(BF)


def route_probs(normed, router):
    logits = nt(normed, router)
    logits = jnp.where(iota(logits.shape, 1) < 4, logits, MASKED)
    raised = jnp.exp(logits - jnp.max(logits, axis=1, keepdims=True))
    return raised / jnp.sum(raised, axis=1, keepdims=True)


def middle_rows(rep, x, attended, wo, ext, rank, middle, normed, probs, packed):
    tokens = x.shape[0]
    gain = ext[5:6, :]
    router = router_rows(ext)

    def tile(t, carry):
        at = pl.ds(pl.multiple_of(t * TILE, TILE), TILE)
        rows = x[at, :].astype(F32) + nn(attended[at, :], wo[...])
        scale = lax.rsqrt(jnp.mean(rows * rows, axis=1, keepdims=True) + EPSILON)
        middle[at, :] = rows
        unit = (rows * scale * gain).astype(BF)
        normed[at, :] = unit
        probs[at, :] = route_probs(unit, router)
        return carry

    lax.fori_loop(0, tokens // TILE, tile, 0)
    pack_rows(rep, rank, normed, packed)


def forward_kernel(
    starts, q, k, v, x, wo, ext, rank, shared_piece, expert_piece, expert_in,
    attended, lse, middle, normed, probs, x0, x1, x2, x3, shared_bank, experts,
    bias, send, recv,
):
    net = Net(send, recv)
    spread = Spread(net, shared_piece, shared_bank)
    events = [net.event() for _ in range(4)]
    inner = (net.z > 0) & (net.z < 3)
    low, high = experts.at[net.down], experts.at[net.up]
    rest, last = experts.at[net.shard, pl.ds(2, 1)], expert_piece.at[pl.ds(2, 1)]
    near = experts.at[net.place(1, 0), pl.ds(0, 2)]
    net.meet("line", [(net.mate, net.shard), (net.rep, net.across), (spread.far, net.shard)])
    spread.begin()
    fill_bias(starts, bias)

    def step(i):
        @pl.when(i == 1)
        def _():
            spread.along(1)
            spread.along(-1)
            spread.over(0)

        @pl.when(i == 3)
        def _():
            spread.along(2)
            spread.along(-2)
            spread.over(1)
            spread.over(-1)
            spread.relay(1, 0)
            spread.relay(0, 1)
            spread.relay(0, -1)

        @pl.when(i == 5)
        def _():
            spread.along(3)
            spread.along(-3)
            net.put(events[0], low, low, net.rep, net.up, inner)
            net.put(events[1], high, high, net.rep, net.down, inner)
            net.put(events[2], last, rest, net.rep, net.across)
            net.put(events[3], near, near, net.rep, net.across)
            spread.over(2)
            spread.over(-2)

    attend_pairs(q, k, v, attended, lse, bias, step)
    spread.over(3)
    spread.over(-3)
    middle_rows(net.rep, x, attended, wo, ext, rank, middle, normed, probs, (x0, x1, x2, x3))
    for way, k_step in ((1, 1), (1, -1), (0, 2), (0, -2), (1, 2), (1, -2)):
        spread.relay(way, k_step)
    for way, k_step in ((0, 3), (0, -3), (1, 3), (1, -3)):
        spread.relay(way, k_step)
    spread.finish()
    net.got(events[0], low, net.z > 1)
    net.got(events[1], low, net.z < 2)
    net.got(events[2], rest)
    net.got(events[3], near)
    net.close()


def plain_forward_kernel(
    starts, q, k, v, x, wo, ext, rank,
    attended, lse, middle, normed, probs, x0, x1, x2, x3, bias,
):
    fill_bias(starts, bias)
    attend_pairs(q, k, v, attended, lse, bias, lambda i: None)
    rep = lax.axis_index("rep")
    middle_rows(rep, x, attended, wo, ext, rank, middle, normed, probs, (x0, x1, x2, x3))


CHUNK, CHUNKS = 512, 4


def unit_bank(
    expert, ext, xs, cs, source, target, before, unit, outs, dxs, scratch, ready=None,
    emit=None, reclaim=None,
):
    out_acc, dx_acc, gate, wbuf, dw_acc, dw_out, in_sems, out_sems = scratch[:8]
    routed = expert is not None
    blocks, rows = len(xs), xs[0].shape[0]
    per = CHUNK // unit

    def loads(of, buffer, sems, k, b):
        return [
            pltpu.make_async_copy(
                of(k * per + i), buffer.at[b, :, :, pl.ds(i * unit, unit)], sems.at[b, i]
            )
            for i in range(per)
        ]

    def stores(k, b):
        return [
            pltpu.make_async_copy(
                dw_out.at[b, :, :, pl.ds(i * unit, unit)],
                target(k * per + i),
                out_sems.at[b, i],
            )
            for i in range(per)
        ]

    def start_loads(k, b):
        if ready is not None:
            ready(k)
        for copy in loads(source, wbuf, in_sems, k, b):
            copy.start()
        if before is not None:
            for copy in loads(before, scratch[8], scratch[9], k, b):
                copy.start()

    start_loads(0, 0)
    if routed:
        router = router_rows(ext)
        for n in range(blocks):
            probs = route_probs(xs[n][...], router)
            lane = iota(probs.shape, 1)
            gate[n] = jnp.sum(jnp.where(lane == expert, probs, 0.0), axis=1, keepdims=True)

    def chunk(k, carry):
        b = lax.rem(k, 2)
        for copy in loads(source, wbuf, in_sems, 0, b):
            copy.wait()
        for n in range(blocks):
            x, c = xs[n][...], cs[n][...]
            wg, wu, wd = wbuf[b, 0], wbuf[b, 1], wbuf[b, 2]
            gate_h, up_h, back_h = nn(x, wg), nn(x, wu), nn(c, wd)
            sigma = 1.0 / (1.0 + jnp.exp(-gate_h))
            silu = gate_h * sigma
            hidden = silu * up_h
            if routed:
                share = gate[n]
                scaled = back_h * share
                weighted = (hidden * share).astype(BF)
            else:
                scaled, weighted = back_h, hidden.astype(BF)
            d_up = (scaled * silu).astype(BF)
            d_gate = (scaled * up_h * (sigma + silu * (1.0 - sigma))).astype(BF)
            product = nt(hidden.astype(BF), wd)
            d_rows = nt(d_gate, wg) + nt(d_up, wu)
            parts = (tn(x, d_gate), tn(x, d_up), tn(c, weighted))
            if routed:
                pairs = (hidden * back_h).astype(BF)
                d_share = nt(jnp.ones((16, CHUNK), BF), pairs)

            @pl.when(k == 0)
            def _():
                out_acc[n] = product
                dx_acc[n, 0:rows, :] = d_rows
                if routed:
                    dx_acc[n, rows : rows + 16, :] = jnp.zeros((16, d_rows.shape[1]), F32)
                    dx_acc[n, rows : rows + 16, 0:rows] = d_share

            @pl.when(k != 0)
            def _():
                out_acc[n] += product
                dx_acc[n, 0:rows, :] += d_rows
                if routed:
                    dx_acc[n, rows : rows + 16, 0:rows] += d_share

            for i in range(3):
                if n == 0:
                    dw_acc[i] = parts[i]
                else:
                    dw_acc[i] += parts[i]

        for nxt in range(1, CHUNKS):

            @pl.when(k + 1 == nxt)
            def _():
                start_loads(nxt, nxt % 2)

        @pl.when(k >= 2)
        def _():
            for copy in stores(0, b):
                copy.wait()

        if reclaim is not None:
            for now in (2, 3):
                when(k == now, functools.partial(reclaim, now))
        if before is not None:
            for copy in loads(before, scratch[8], scratch[9], 0, b):
                copy.wait()
            for i in range(3):
                dw_out[b, i] = (dw_acc[i] + scratch[8][b, i].astype(F32)).astype(BF)
        else:
            for i in range(3):
                dw_out[b, i] = dw_acc[i].astype(BF)
        for now in range(CHUNKS):

            @pl.when(k == now)
            def _():
                for copy in stores(now, now % 2):
                    copy.start()
                if emit is not None:
                    emit(now)

        return carry

    lax.fori_loop(0, CHUNKS, chunk, 0)
    for n in range(blocks):
        outs[n][...] = out_acc[n].astype(BF)
        dxs[n][...] = dx_acc[n].astype(BF)
    for b in range(2):
        for copy in stores(0, b):
            copy.wait()


def unit_scratch(blocks, rows, extra, width, per, chained):
    scratch = [
        pltpu.VMEM((blocks, rows, width), F32),
        pltpu.VMEM((blocks, rows + extra, width), F32),
        pltpu.VMEM((blocks, rows, 1), F32),
        pltpu.VMEM((2, 3, width, CHUNK), BF),
        pltpu.VMEM((3, width, CHUNK), F32),
        pltpu.VMEM((2, 3, width, CHUNK), BF),
        pltpu.SemaphoreType.DMA((2, per)),
        pltpu.SemaphoreType.DMA((2, per)),
    ]
    if chained:
        scratch += [
            pltpu.VMEM((2, 3, width, CHUNK), BF),
            pltpu.SemaphoreType.DMA((2, per)),
        ]
    return scratch


def shared_kernel(
    x, c, piece, bank, x1, x2, x3, expert_in,
    out, dx, grads_own, grads_other, shared_mate, y1, y2, y3, experts,
    send, recv, *scratch,
):
    net = Net(send, recv)
    events = [net.event() for _ in range(4)]
    core_events = [net.event() for _ in range(8)]
    peers = [(net.cousins[o], net.shard) for o in (1, 2, 3)]
    net.meet("line", peers + [(net.rep, net.across)])
    arrivals = exchange(net, (x1, x2, x3), (y1, y2, y3))
    near, second = experts.at[net.place(1, 0), pl.ds(2, 1)], experts.at[net.place(2, 0)]
    net.put(events[0], near, near, net.rep, net.across)
    net.put(events[1], second, second, net.rep, net.across)
    below = experts.at[lax.max(net.shard - 4, net.x)]
    above = experts.at[lax.min(net.shard + 4, 6 + net.x)]
    net.put(events[2], below, below, net.rep, net.up, net.z == 2)
    net.put(events[3], above, above, net.rep, net.down, net.z == 1)
    spots = [net.place(n % 4, n // 4 % 2) for n in range(8)]
    halves = [net.core, 1 - net.core]
    done = scratch[5]
    slices = [done.at[n // 4, :, :, pl.ds(n % 4 * 128, 128)] for n in range(8)]
    places = [shared_mate.at[spot] for spot in spots]

    def source(n):
        return piece if n == 0 else bank.at[halves[n // 8], spots[n % 8]]

    def target(n):
        return (grads_own, grads_other)[n // 8].at[spots[n % 8]]

    def emit(now):
        if now >= 2:
            for n in range(4 * now - 8, 4 * now - 4):
                net.put(core_events[n], slices[n], places[n], net.mate, net.shard)

    unit_bank(
        None, None, [x], [c], source, target, None, 128, [out], [dx], scratch, None, emit
    )
    for event, like in arrivals:
        net.got(event, like)
    net.got(events[0], near)
    net.got(events[1], second)
    net.got(events[2], second, net.z == 3)
    net.got(events[3], second, net.z == 0)
    for n in range(8):
        net.got(core_events[n], places[n])
    net.close()


def far_kernel(
    ext, xa, xb, ca, cb, expert_piece, shared_own, shared_mate, expert_in,
    oa, ob, da, db, grads, shared_keep, shared_y, experts,
    part_a, part_b, part_sems, send, recv, *scratch,
):
    net = Net(send, recv)
    events = [net.event() for _ in range(9)]
    far = net.cousins[2]
    parts = copies_of(((shared_own, part_a), (shared_mate, part_b)), part_sems)
    for copy in parts:
        copy.start()
    net.meet("none", [(net.rep, net.across), (far, net.shard)])
    last = experts.at[net.place(3, 0)]
    net.put(events[0], last, last, net.rep, net.across)
    spots = [net.place(n // 2, n % 2) for n in range(8)]
    y, quarter = lax.div(net.rep, 2), part_a.shape[2] // 2
    rows = [pl.ds(pl.multiple_of(n * quarter, 128), quarter) for n in (y, 1 - y)]
    keep = pltpu.make_async_copy(part_a.at[:, :, rows[0], :], shared_keep, part_sems.at[2])
    away = [part_a.at[j, :, rows[1], :] for j in range(SLOTS)]

    def source(n):
        return expert_piece if n == 0 else experts.at[spots[n]]

    def target(n):
        return grads.at[spots[n]]

    def ready(k):
        if k == 3:
            net.got(events[0], last)

    for copy in parts:
        copy.wait()

    def add(j, carry):
        part_a[j] = part_a[j] + part_b[j]
        return carry

    lax.fori_loop(0, SLOTS, add, 0)
    for j in range(SLOTS):
        net.put(events[1 + j], away[j], shared_y.at[j], far, net.shard)
    keep.start()
    unit_bank(
        net.rep, ext, [xa, xb], [ca, cb], source, target, None, 256, [oa, ob], [da, db],
        scratch, ready,
    )
    keep.wait()
    for j in range(SLOTS):
        net.got(events[1 + j], shared_y.at[j])
    net.close()


def near_kernel(
    ext, xa, xb, ca, cb, expert_piece, experts, before, far_a, far_b,
    shared_keep, shared_y,
    oa, ob, da, shared_total, grads, back_a, back_b, back_c, expert_x,
    db, part_a, part_b, from_x, from_z, sems, send, recv, *scratch,
):
    net = Net(send, recv)
    events = [net.event() for _ in range(4)]
    x_events = [net.event() for _ in range(4)]
    z_events = [net.event() for _ in range(3)]
    peers = [(net.cousins[o], net.shard) for o in (1, 2, 3)]
    one = pltpu.make_async_copy(shared_keep, part_a, sems.at[0])
    two = pltpu.make_async_copy(shared_y, part_b, sems.at[1])
    one.start()
    two.start()
    net.meet("all", peers + [(net.rep, net.across)])
    net.put(events[0], far_a, back_a, net.cousins[2], net.shard)
    net.put(events[1], far_b, back_b, net.cousins[3], net.shard)
    one.wait()
    two.wait()

    def add(j, carry):
        part_a[j] = part_a[j] + part_b[j]
        return carry

    lax.fori_loop(0, SLOTS, add, 0)
    mine = [net.cycle(d) for d in range(4)]
    theirs = [spot + 1 - 2 * net.x for spot in mine]
    for d in (2, 1, 3, 0):
        net.put(x_events[d], part_a.at[theirs[d]], from_x.at[d], net.rep, net.across)
    pieces, lands = [part_a.at[spot] for spot in mine], [from_x.at[d] for d in range(4)]
    ends = [from_z.at[d] for d in range(3)]
    spots = [net.place(3 - n // 2, n % 2) for n in range(8)]
    own_slot = 6
    half = scratch[5].at[0, :, :, pl.ds(256, 256)]
    target = expert_x.at[net.levels[3]]

    def source(n):
        return expert_piece if n == own_slot else experts.at[spots[n]]

    def ready(k):
        if k == 2:
            for d in (2, 1, 3, 0):
                net.got(x_events[d], lands[d])
                part_a[mine[d]] = part_a[mine[d]] + from_x[d]
                if d:
                    net.put(z_events[d - 1], pieces[d], ends[d - 1], net.rep, mine[d])

    def emit(now):
        if now == 0:
            net.put(events[3], half, target, net.rep, net.across)

    def reclaim(now):
        if now == 2:
            net.copy(events[3], half, half, net.mate, net.shard).wait_send()

    unit_bank(
        net.rep, ext, [xa, xb], [ca, cb], source,
        lambda n: grads.at[spots[n]], lambda n: before.at[spots[n]],
        256, [oa, ob], [da, db], scratch, ready, emit, reclaim,
    )
    net.open.pop(events[3])
    net.put(events[2], db, back_c, net.mate, net.shard)
    total = part_a[mine[0]].astype(F32)
    for d in (1, 2, 3):
        net.got(z_events[d - 1], ends[d - 1])
        total = total + from_z[d - 1].astype(F32)
    shared_total[...] = total.astype(BF)
    net.got(events[0], back_a)
    net.got(events[1], back_b)
    net.got(events[2], back_c)
    net.got(events[3], target)
    net.close()


def plain_bank_kernel(blocks, unit, routed, chained, ext, *refs):
    refs = list(refs)

    def take(n):
        taken = refs[:n]
        del refs[:n]
        return taken

    xs, cs = take(blocks), take(blocks)
    bank = take(1)[0]
    before = take(1)[0] if chained else None
    outs, dxs = take(blocks), take(blocks)
    grads = take(1)[0]
    unit_bank(
        lax.axis_index("rep") if routed else None,
        ext, xs, cs,
        lambda n: bank.at[n],
        lambda n: grads.at[n],
        (lambda n: before.at[n]) if chained else None,
        unit, outs, dxs, refs,
    )


def plain_bank(ext, xs, cs, bank, before, routed):
    blocks, (rows, width) = len(xs), xs[0].shape
    chained = before is not None
    extra, unit = (16 if routed else 0), bank.shape[3]
    operands = [ext, *xs, *cs, bank] + ([before] if chained else [])
    outs = [shape((rows, width))] * blocks + [shape((rows + extra, width))] * blocks
    results = call(
        functools.partial(plain_bank_kernel, blocks, unit, routed, chained),
        outs + [shape(bank.shape)],
        [VMEM] * (1 + 2 * blocks) + [ANY] * (2 if chained else 1),
        [VMEM] * (2 * blocks) + [ANY],
        unit_scratch(blocks, rows, extra, width, CHUNK // unit, chained),
        flops=18 * blocks * rows * width * 4 * CHUNK,
        moved=30 * 2**20,
    )(*operands)
    return results[:blocks], results[blocks : 2 * blocks], results[2 * blocks]


def combine_rows(
    slot, d0, d1, d2, d3, d_shared, probs, middle, normed, cot, ext, attended, wo,
    d_middle, d_attended, grad_wo, grad_ext, branch, router_acc, gain_acc,
):
    tokens, width = middle.shape
    rep = lax.axis_index("rep")
    gain = ext[5:6, :]
    router = router_rows(ext)
    router_acc[...] = jnp.zeros_like(router_acc)
    gain_acc[...] = jnp.zeros_like(gain_acc)

    def tile(t, carry):
        at = pl.ds(pl.multiple_of(t * TILE, TILE), TILE)
        slot_one, slot_two = slot[at, 0:1], slot[at, 64:65]
        d_normed = d_shared[at, :].astype(F32)
        lane = iota((TILE, 128), 1)
        d_gates = jnp.zeros((TILE, 128), F32)
        for o, d in enumerate((d0, d1, d2, d3)):
            place = (iota((TILE, CAP), 1) + o * CAP).astype(F32)
            hit = (place == slot_one) | (place == slot_two)
            d_normed = d_normed + nn(ones_where(hit), d[0:CAP, :])
            share = d[CAP : CAP + 16, 0:CAP].astype(F32)[0:1, :]
            d_share = jnp.sum(jnp.where(hit, share, 0.0), axis=1, keepdims=True)
            d_gates = d_gates + jnp.where(lane == sibling(rep, o), d_share, 0.0)
        p = probs[at, :]
        inner = jnp.sum(d_gates * p, axis=1, keepdims=True)
        d_logits = (p * (d_gates - inner)).astype(BF)
        d_normed = d_normed + nn(d_logits, router)
        router_acc[...] += tn(d_logits, normed[at, :])
        rows = middle[at, :]
        scale = lax.rsqrt(jnp.mean(rows * rows, axis=1, keepdims=True) + EPSILON)
        unit = rows * scale
        gain_acc[...] += jnp.sum((d_normed * unit).reshape(TILE // 8, 8, width), axis=0)
        w = d_normed * gain
        inner = jnp.mean(w * unit, axis=1, keepdims=True)
        total = cot[at, :].astype(F32) + scale * (w - unit * inner)
        d_middle[at, :] = total
        rounded = total.astype(BF)
        branch[at, :] = rounded
        d_attended[at, :] = nt(rounded, wo[...]).astype(BF)
        return carry

    lax.fori_loop(0, tokens // TILE, tile, 0)
    grad_wo[...] = tn(attended[...], branch[...]).astype(BF)
    row = iota((16, width), 0)
    total = jnp.sum(gain_acc[...], axis=0, keepdims=True)
    grad_ext[...] = jnp.where(row < 4, router_acc[0:16, :], jnp.where(row == 5, total, 0.0))


def output_rows(slot, o0, o1, o2, o3, shared, probs, middle, out, first, last):
    rep = lax.axis_index("rep")

    def tile(t, carry):
        at = pl.ds(pl.multiple_of(t * TILE, TILE), TILE)
        slot_one, slot_two = slot[at, 0:1], slot[at, 64:65]
        total = middle[at, :] + shared[at, :].astype(F32)
        p = probs[at, :]
        lane = iota((TILE, 128), 1)
        for o, rows in enumerate((o0, o1, o2, o3)):
            place = (iota((TILE, CAP), 1) + o * CAP).astype(F32)
            hit = (place == slot_one) | (place == slot_two)
            share = jnp.sum(jnp.where(lane == sibling(rep, o), p, 0.0), axis=1, keepdims=True)
            total = total + nn(jnp.where(hit, share, 0.0).astype(BF), rows[...])
        out[at, :] = total.astype(BF)
        return carry

    lax.fori_loop(first, last, tile, 0)


def back_pairs(
    q, k, v, d_out, out, lse, cosine, sine, dq, dk, dv, bias, dk_acc, dv_acc, step
):
    tokens, width = q.shape

    def pair(i, carry):
        step(i)
        cols = pl.ds(pl.multiple_of(i * 128, 128), 128)
        keys, values = k[:, cols], v[:, cols]
        half_keys = [keep_half(keys, 0), keep_half(keys, 1)]
        dk_acc[...] = jnp.zeros_like(dk_acc)
        dv_acc[...] = jnp.zeros_like(dv_acc)
        low = iota((TILE, 128), 1) < 64
        for t in range(tokens // TILE):
            begin = t * TILE
            end = min(tokens, begin + TILE + PIECE)
            at = slice(begin, begin + TILE)
            block, grad = q[at, cols], d_out[at, cols]
            product = grad.astype(F32) * out[at, cols].astype(F32)
            block_lse = lse[at, cols]
            d_block = None
            for h in range(2):
                block_h, grad_h = keep_half(block, h), keep_half(grad, h)
                scores = nt(block_h, keys[:end])
                scores = biased(scores, bias, begin, begin, end)
                probs = jnp.exp(scores - block_lse[:, 64 * h : 64 * h + 1])
                d_probs = nt(grad_h, values[:end])
                inner = jnp.sum(
                    jnp.where(low if h == 0 else ~low, product, 0.0), axis=1, keepdims=True
                )
                d_scores = (probs * (d_probs - inner)).astype(BF)
                part = nn(d_scores, half_keys[h][:end])
                d_block = part if d_block is None else d_block + part
                dk_acc[0:end, :] += tn(d_scores, block_h)
                dv_acc[0:end, :] += tn(probs.astype(BF), grad_h)
            dq[at, cols] = spin(d_block * 0.125, cosine[at, :], -sine[at, :]).astype(BF)
        dk[:, cols] = spin(dk_acc[...], cosine[...], -sine[...]).astype(BF)
        dv[:, cols] = dv_acc[...].astype(BF)
        return carry

    lax.fori_loop(0, width // 128, pair, 0)


def copies_of(pairs, sems):
    return [pltpu.make_async_copy(a, b, sems.at[i]) for i, (a, b) in enumerate(pairs)]


def fetch(sources, targets, sems):
    copies = copies_of(zip(sources, targets), sems)
    for copy in copies:
        copy.start()
    for copy in copies:
        copy.wait()


class Chain:
    def __init__(self, net, own, from_x, up_in, down_in, held, spare, sems):
        self.net, self.own, self.from_x = net, own, from_x
        self.up_in, self.down_in = up_in, down_in
        self.held, self.spare, self.sems = held, spare, sems
        self.events = {(way, d): net.event() for way in range(2) for d in (1, 2, 3)}
        self.spots = [net.place(n, 0) for n in range(4)]
        self.sends, self.gets = {}, {}
        z = net.z
        for d in (1, 2, 3):
            self.sends[0, d] = (held.at[lax.min(z + d, 3)], z < 4 - d)
            self.sends[1, d] = (held.at[lax.max(z - d, 0)], z > d - 1)
            self.gets[0, d] = (lax.min(z + d - 1, 3), (z > 0) & (z < 5 - d))
            self.gets[1, d] = (lax.max(z - d + 1, 0), (z < 3) & (z > d - 2))

    def level(self, n):
        to = self.net.levels[n]
        far = self.from_x.at[to]
        fetch([self.own.at[self.spots[n]], far], [self.held.at[to], self.spare.at[0]], self.sems)
        self.held[to] = self.held[to] + self.spare[0]

    def send(self, d):
        net = self.net
        for way, to, into in ((0, net.up, self.up_in), (1, net.down, self.down_in)):
            source, here = self.sends[way, d]
            net.put(self.events[way, d], source, into.at[d - 1], net.rep, to, here)

    def take(self, d):
        for way, into in ((0, self.up_in), (1, self.down_in)):
            to, here = self.gets[way, d]

            def add():
                self.net.copy(
                    self.events[way, d], into.at[d - 1], into.at[d - 1],
                    self.net.mate, self.net.shard,
                ).wait_recv()
                fetch([into.at[d - 1]], [self.spare.at[0]], self.sems)
                self.held[to] = self.held[to] + self.spare[0]

            when(here, add)


BACK_ROWS = 19


def back_kernel(starts, *refs):
    raw, refs = refs[:BACK_ROWS], refs[BACK_ROWS:]
    o1, o2, o3, grads, expert_x_in = refs[:5]
    d_middle, grad_wo, grad_ext, dq, dk, dv, expert_total = refs[5:12]
    r1, r2, r3, up_in, down_in, expert_x = refs[12:18]
    d_attended, branch, router_acc, gain_acc, bias, dk_acc, dv_acc = refs[18:25]
    local = refs[25 : 25 + BACK_ROWS]
    held, spare, sems, load_sems, send, recv = refs[25 + BACK_ROWS :]
    slot, d0, d1, d2, d3, d_shared, probs, middle, normed, cot, ext, attended, wo = local[:13]
    cosine, sine, q, k, v, lse = local[13:]
    loads = copies_of(zip(raw, local), load_sems)
    for copy in loads:
        copy.start()
    net = Net(send, recv)
    x_events = [net.event() for _ in range(3)]
    chain = Chain(net, grads, expert_x, up_in, down_in, held, spare, sems)
    peers = [(net.cousins[o], net.shard) for o in (1, 2, 3)]
    net.meet("line", peers + [(net.rep, net.across)])
    targets = [expert_x.at[net.levels[n]] for n in range(3)]
    for n in (2, 1, 0):
        source = grads.at[net.place(n, 1)]
        net.put(x_events[n], source, targets[n], net.rep, net.across)
    arrivals = exchange(net, (o1, o2, o3), (r1, r2, r3))
    chain.level(3)
    chain.send(3)
    fill_bias(starts, bias)
    for copy in loads:
        copy.wait()
    combine_rows(
        slot, d0, d1, d2, d3, d_shared, probs, middle, normed, cot, ext, attended, wo,
        d_middle, d_attended, grad_wo, grad_ext, branch, router_acc, gain_acc,
    )
    net.got(x_events[2], targets[2])
    chain.level(2)
    chain.take(3)
    chain.send(2)

    def step(i):
        @pl.when(i == 1)
        def _():
            net.got(x_events[1], targets[1])
            chain.level(1)

        @pl.when(i == 4)
        def _():
            chain.take(2)
            chain.send(1)

    back_pairs(
        q, k, v, d_attended, attended, lse, cosine, sine, dq, dk, dv, bias, dk_acc, dv_acc, step
    )
    net.got(x_events[0], targets[0])
    chain.level(0)
    for event, like in arrivals:
        net.got(event, like)
    chain.take(1)
    expert_total[...] = held[net.z]
    net.close()


def plain_back_kernel(
    starts, slot, d0, d1, d2, d3, d_shared, probs, middle, normed, cot, ext, attended, wo,
    q, k, v, lse, cosine, sine,
    d_middle, grad_wo, grad_ext, dq, dk, dv,
    d_attended, branch, router_acc, gain_acc, bias, dk_acc, dv_acc,
):
    combine_rows(
        slot, d0, d1, d2, d3, d_shared, probs, middle, normed, cot, ext, attended, wo,
        d_middle, d_attended, grad_wo, grad_ext, branch, router_acc, gain_acc,
    )
    fill_bias(starts, bias)
    back_pairs(
        q, k, v, d_attended, attended, lse, cosine, sine, dq, dk, dv, bias, dk_acc, dv_acc,
        lambda i: None,
    )


def norm_rows(x, ext, normed_all):
    gain = ext[4:5, :]

    def tile(t, carry):
        at = pl.ds(pl.multiple_of(t * TILE, TILE), TILE)
        rows = x[at, :].astype(F32)
        scale = lax.rsqrt(jnp.mean(rows * rows, axis=1, keepdims=True) + EPSILON)
        normed_all[at, :] = (rows * scale * gain).astype(BF)
        return carry

    lax.fori_loop(0, x.shape[0] // TILE, tile, 0)


def input_grad(x, ext, dq, dk, dv, wq, wk, wv, d_middle, grad_in, gain_acc):
    tokens, width = x.shape
    gain = ext[4:5, :]
    gain_acc[...] = jnp.zeros_like(gain_acc)

    def tile(t, carry):
        at = pl.ds(pl.multiple_of(t * TILE, TILE), TILE)
        rows = x[at, :].astype(F32)
        scale = lax.rsqrt(jnp.mean(rows * rows, axis=1, keepdims=True) + EPSILON)
        unit = rows * scale
        d_normed = nt(dq[at, :], wq[...]) + nt(dk[at, :], wk[...]) + nt(dv[at, :], wv[...])
        gain_acc[...] += jnp.sum((d_normed * unit).reshape(TILE // 8, 8, width), axis=0)
        w = d_normed * gain
        inner = jnp.mean(w * unit, axis=1, keepdims=True)
        grad_in[at, :] = d_middle[at, :] + scale * (w - unit * inner)
        return carry

    lax.fori_loop(0, tokens // TILE, tile, 0)


def tail_kernel(
    x, ext, dq, dk, dv, wq, wk, wv, grad_wo, grad_ext,
    d_middle_in, slot_in, o0_in, o1_in, o2_in, o3_in, shared_in, probs_in, middle_in,
    expert_total, shared_total,
    grad_in, outputs, weights, small, shared_far, shared_mate, shared_cross, e1, e2, e3,
    normed_all, gain_acc, gw, from_mate, from_x, from_z, from_y, result, from_core,
    tiny, tiny_in, d_middle, slot, o0, o1, o2, o3, shared_out, probs, middle, load_sems,
    send, recv,
):
    width = x.shape[1]
    half = width // SLOTS
    net = Net(send, recv)
    e_events = [net.event() for _ in range(3)]
    s_events = [net.event() for _ in range(3)]
    m_events = [net.event() for _ in range(2)]
    x_events = [[net.event() for _ in range(2)] for _ in range(4)]
    z_events = [[net.event() for _ in range(2)] for _ in range(3)]
    y_event, c_event = net.event(), net.event()
    t_events = [net.event() for _ in range(6)]
    net.meet(
        "all", [(net.mate, net.shard), (net.cousins[2], net.shard), (net.rep, net.across)]
    )
    far = net.cousins[2]
    net.put(s_events[0], shared_total, shared_far, far, net.shard)
    net.put(s_events[1], shared_total, shared_mate, net.mate, net.shard)
    net.put(e_events[1], expert_total, e2, far, net.shard)
    net.put(e_events[0], expert_total, e1, net.mate, net.shard)
    pairs = (
        (d_middle_in, d_middle), (slot_in, slot), (o0_in, o0), (o1_in, o1), (o2_in, o2),
        (o3_in, o3), (shared_in, shared_out), (probs_in, probs), (middle_in, middle),
    )
    loads = [pltpu.make_async_copy(a, b, load_sems.at[i]) for i, (a, b) in enumerate(pairs)]
    for copy in loads:
        copy.start()
    norm_rows(x, ext, normed_all)
    spots = [lax.rem(i + 2 * net.core, 4) for i in range(4)]

    def rows_of(spot):
        return pl.ds(pl.multiple_of(spot * half, 32), half)

    mine = [rows_of(net.cycle(d)) for d in range(4)]
    theirs = [rows_of(net.cycle(d) + 1 - 2 * net.x) for d in range(4)]

    def hand(i):
        net.put(m_events[i], gw.at[2 + i], from_mate.at[i], net.mate, net.shard)

    def cross(i):
        net.got(m_events[i], from_mate.at[i])
        gw[i] = gw[i] + from_mate[i]
        for d in (2, 1, 3, 0):
            source = gw.at[i, theirs[d]]
            net.put(x_events[d][i], source, from_x.at[d, i], net.rep, net.across)

    gw[spots[0]] = tn(normed_all[...], dq[...]).astype(BF)
    gw[spots[2]] = tn(normed_all[...], dv[...]).astype(BF)
    hand(0)
    gw[spots[1]] = tn(normed_all[...], dk[...]).astype(BF)
    gw[spots[3]] = grad_wo[...]
    hand(1)
    cross(0)
    cross(1)
    for copy in loads:
        copy.wait()
    input_grad(x, ext, dq, dk, dv, wq, wk, wv, d_middle, grad_in, gain_acc)
    row = iota((16, width), 0)
    total = jnp.sum(gain_acc[...], axis=0, keepdims=True)
    tiny[0] = (grad_ext[...] + jnp.where(row == 4, total, 0.0)).astype(BF)
    net.put(t_events[0], tiny.at[0], tiny_in.at[0], net.mate, net.shard)

    def add_across(d):
        for i in range(2):
            net.got(x_events[d][i], from_x.at[d, i])
            gw[i, mine[d], :] = gw[i, mine[d], :] + from_x[d, i]
            if d:
                net.put(
                    z_events[d - 1][i], gw.at[i, mine[d]], from_z.at[d - 1, i],
                    net.rep, net.cycle(d),
                )

    def tiny_add(n, target_rep, target_shard):
        net.got(t_events[n], tiny_in.at[n])
        tiny[n + 1] = (tiny[n].astype(F32) + tiny_in[n].astype(F32)).astype(BF)
        if target_rep is not None:
            source, target = tiny.at[n + 1], tiny_in.at[n + 1]
            net.put(t_events[n + 1], source, target, target_rep, target_shard)

    add_across(2)
    tiny_add(0, net.rep, net.across)
    output_rows(slot, o0, o1, o2, o3, shared_out, probs, middle, outputs, 0, 2)
    add_across(1)
    tiny_add(1, far, net.shard)
    net.got(s_events[0], shared_far)
    net.put(s_events[2], shared_far, shared_cross, net.mate, net.shard)
    output_rows(slot, o0, o1, o2, o3, shared_out, probs, middle, outputs, 2, 4)
    tiny_add(2, None, None)
    for d in (1, 2, 3):
        net.put(t_events[2 + d], tiny.at[3], tiny_in.at[2 + d], net.rep, net.cycle(d))
    add_across(3)
    add_across(0)
    for i in range(2):
        total = gw[i, mine[0], :].astype(F32)
        for d in (1, 2, 3):
            net.got(z_events[d - 1][i], from_z.at[d - 1, i])
            total = total + from_z[d - 1, i].astype(F32)
        result[0, i] = total.astype(BF)
    net.put(y_event, result.at[0], from_y, far, net.shard)
    total = tiny[3].astype(F32)
    for d in (1, 2, 3):
        net.got(t_events[2 + d], tiny_in.at[2 + d])
        total = total + tiny_in[2 + d].astype(F32)
    small[...] = total.astype(BF).astype(F32)
    net.got(e_events[1], e2)
    net.put(e_events[2], e2, e3, net.mate, net.shard)
    net.got(y_event, from_y)
    result[1] = (result[0].astype(F32) + from_y[...].astype(F32)).astype(BF)
    net.put(c_event, result.at[1], from_core, net.mate, net.shard)
    for i in range(2):
        weights[spots[i]] = result[1, i].astype(F32)
    net.got(c_event, from_core)
    for i in range(2):
        weights[spots[2 + i]] = from_core[i].astype(F32)
    net.got(e_events[0], e1)
    net.got(s_events[1], shared_mate)
    net.got(s_events[2], shared_cross)
    net.got(e_events[2], e3)
    net.close()


def plain_tail_kernel(
    x, ext, dq, dk, dv, wq, wk, wv, d_middle,
    slot, o0, o1, o2, o3, shared_out, probs, middle,
    grad_in, outputs, gw, gain, normed_all, gain_acc,
):
    norm_rows(x, ext, normed_all)
    for i, d in enumerate((dq, dk, dv)):
        gw[i] = tn(normed_all[...], d[...]).astype(BF)
    input_grad(x, ext, dq, dk, dv, wq, wk, wv, d_middle, grad_in, gain_acc)
    gain[...] = gain_acc[...]
    output_rows(
        slot, o0, o1, o2, o3, shared_out, probs, middle, outputs, 0, x.shape[0] // TILE
    )


def finish_kernel(
    e0, e1, e2, e3, q0, q1, q2, q3, weights,
    gate, up, down, s_gate, s_up, s_down, grad_q, grad_k, grad_v, grad_o,
    part, ready_gate, ready_up, ready_down, in_sems, out_sems,
):
    rep = lax.axis_index("rep")
    loads = copies_of([(e, part.at[o]) for o, e in enumerate((e0, e1, e2, e3))], in_sems)
    for copy in loads:
        copy.start()
    stores = []
    for o in range(4):
        at = sibling(rep, o)
        pairs = ((ready_gate, gate), (ready_up, up), (ready_down, down))
        stores.append(copies_of([(a.at[o], b.at[at]) for a, b in pairs], out_sems.at[o]))
        loads[o].wait()
        ready_gate[o] = part[o, 0].astype(F32)
        ready_up[o] = part[o, 1].astype(F32)
        ready_down[o] = part[o, 2].astype(F32).T
        for copy in stores[o]:
            copy.start()
    quarter, span = q0.shape[1:]
    for o, piece in enumerate((q0, q1, q2, q3)):
        for other in range(4):

            @pl.when(sibling(rep, o) == other)
            def _():
                rows = slice(other // 2 * quarter, (other // 2 + 1) * quarter)
                cols = slice(other % 2 * span, (other % 2 + 1) * span)
                s_gate[rows, cols] = piece[0].astype(F32)
                s_up[rows, cols] = piece[1].astype(F32)
                s_down[cols, rows] = piece[2].astype(F32).T

    for i, out in enumerate((grad_q, grad_k, grad_v, grad_o)):
        out[...] = weights[i]
    for copies in stores:
        for copy in copies:
            copy.wait()


def rope_tables(length, head_dim):
    positions = jnp.arange(length, dtype=F32)
    inverse_freq = 10000.0 ** (-2.0 * jnp.arange(head_dim // 2, dtype=F32) / head_dim)
    angle = positions[:, None] * inverse_freq[None, :]
    cosine, sine = jnp.cos(angle), jnp.sin(angle)
    return (
        jnp.concatenate([cosine] * 4, axis=1),
        jnp.concatenate([-sine, sine, -sine, sine], axis=1),
    )


def body(
    inputs,
    piece_starts,
    routes,
    attn_gain,
    query_weight,
    key_weight,
    value_weight,
    out_weight,
    ffn_gain,
    router_weight,
    expert_gate,
    expert_up,
    expert_down,
    shared_gate,
    shared_up,
    shared_down,
    cotangent,
):
    _, tokens, width = inputs.shape
    shards = lax.axis_size("shard")
    rep, shard = lax.axis_index("rep"), lax.axis_index("shard")
    core = rep % 2
    ringed = shards == SLOTS
    rows = width // shards
    units = shared_gate.shape[1]
    x, cot, chosen = inputs[0], cotangent[0], routes[0]
    small = jnp.concatenate([router_weight.T, attn_gain[None], ffn_gain[None]], axis=0)
    small = jnp.pad(small, ((0, 10), (0, 0)))
    small = lax.dynamic_update_slice(jnp.zeros((16, width), BF), small, (0, shard * rows))
    blank = jnp.zeros((16, width), BF)
    if ringed:
        half_one = jnp.concatenate([query_weight, key_weight, small], axis=0)
        half_two = jnp.concatenate([value_weight, out_weight, blank], axis=0)
        piece = jnp.where(core == 0, half_one, half_two)
    else:
        wq, wk, wv, wo = [
            lax.all_gather(w, "shard", axis=0, tiled=True)
            for w in (query_weight, key_weight, value_weight, out_weight)
        ]
        ext = lax.psum(small.astype(F32), "shard")

    shared_pack = jnp.stack([shared_gate, shared_up, shared_down.T])
    my_half = lax.dynamic_slice_in_dim(shared_pack, core * (units // 2), units // 2, 2)
    expert_pack = jnp.stack([expert_gate[rep], expert_up[rep], expert_down[rep].T])

    cosine, sine = rope_tables(tokens, width // HEADS)
    token_f = shape((tokens, width))
    square = shape((width, width))
    packed = [shape((CAP, width))] * 4
    outs = [shape((8, tokens), F32), shape((tokens, 128), F32)] + [token_f] * 3
    work = 2 * tokens * width * (CAP * 4 + 3 * width)
    if ringed:
        rank, slot, q, k, v, *heads = call(
            head_kernel,
            outs + [square] * 4 + [shape((16, width), F32)] + packed
            + [shape((SLOTS,) + expert_pack.shape)],
            [VMEM] * 7 + [ANY],
            [VMEM] * 10 + [VMEM] + [ANY] * 4,
            [
                pltpu.VMEM((2, SLOTS, 2 * rows + 16, width), BF),
                pltpu.VMEM((3, CAP, width), BF),
                pltpu.SemaphoreType.DMA((34,)),
                pltpu.SemaphoreType.DMA((34,)),
                pltpu.SemaphoreType.DMA,
            ],
            flops=work,
            moved=24 * 2**20,
            group=0,
        )(chosen, chosen.T, cot, x, piece, cosine, sine, expert_pack)
        wq, wk, wv, wo, ext, *cot_in, expert_bank = heads
    else:
        rank, slot, q, k, v, *cot_out = call(
            plain_head_kernel, outs + packed, [VMEM] * 10, [VMEM] * 9, flops=work,
            moved=24 * 2**20,
        )(chosen, chosen.T, cot, x, cosine, sine, wq, wk, wv, ext)
        cot_in = [cot_out[0]] + [to_rep(cot_out[o], o) for o in (1, 2, 3)]

    outs = [token_f, shape((tokens, width), F32), shape((tokens, width), F32), token_f]
    outs += [shape((tokens, 128), F32)] + packed
    work = 2 * tokens * width * (8 * tokens + width + 4 * CAP)
    bias = pltpu.VMEM((tokens, tokens), F32)
    if ringed:
        attended, lse, middle, normed, probs, *x_out, shared_bank, expert_bank = call(
            forward_kernel,
            outs + [shape((2, SLOTS) + my_half.shape), shape((SLOTS,) + expert_pack.shape)],
            [SMEM] + [VMEM] * 7 + [ANY] * 3,
            [VMEM] * 9 + [ANY] * 2,
            [bias, pltpu.SemaphoreType.DMA((60,)), pltpu.SemaphoreType.DMA((60,))],
            flops=work,
            moved=30 * 2**20,
            group=1,
            alias={10: 10},
        )(piece_starts, q, k, v, x, wo, ext, rank, my_half, expert_pack, expert_bank)
    else:
        attended, lse, middle, normed, probs, *x_out = call(
            plain_forward_kernel, outs, [SMEM] + [VMEM] * 7, [VMEM] * 9, [bias], flops=work,
            moved=30 * 2**20,
        )(piece_starts, q, k, v, x, wo, ext, rank)

    rows_out = shape((CAP, width))
    rows_back = shape((CAP + 16, width))
    if ringed:
        half_grads = shape((SLOTS,) + my_half.shape)
        shared_out, shared_dx, grads_own, _, shared_mate, y1, y2, y3, expert_bank = call(
            shared_kernel,
            [token_f] * 2 + [half_grads] * 3 + packed[:3] + [shape(expert_bank.shape)],
            [VMEM] * 2 + [ANY] * 6,
            [VMEM] * 2 + [ANY] * 7,
            [pltpu.SemaphoreType.DMA((15,)), pltpu.SemaphoreType.DMA((15,))]
            + unit_scratch(1, tokens, 0, width, 4, False),
            flops=18 * tokens * width * CHUNK * CHUNKS,
            moved=30 * 2**20,
            group=2,
            alias={7: 8},
        )(normed, cot, my_half, shared_bank, *x_out[1:], expert_bank)
        x_in = [x_out[0], y1, y2, y3]
        bank = shape(expert_bank.shape)
        quarter = (3, width // 2, units // 2)
        quarters = (SLOTS,) + quarter
        far_a, far_b, da, db, before, shared_keep, shared_y, expert_bank = call(
            far_kernel,
            [rows_out] * 2 + [rows_back] * 2 + [bank, shape(quarters), shape(quarters), bank],
            [VMEM] * 5 + [ANY] * 4,
            [VMEM] * 4 + [ANY] * 4,
            [
                pltpu.VMEM(half_grads.shape, BF),
                pltpu.VMEM(half_grads.shape, BF),
                pltpu.SemaphoreType.DMA((3,)),
                pltpu.SemaphoreType.DMA((9,)),
                pltpu.SemaphoreType.DMA((9,)),
            ]
            + unit_scratch(2, CAP, 16, width, 2, False),
            flops=36 * CAP * width * CHUNK * CHUNKS,
            moved=30 * 2**20,
            group=3,
            alias={8: 7},
        )(ext, *x_in[2:], *cot_in[2:], expert_pack, grads_own, shared_mate, expert_bank)
        bank_x, bank_z = (4,) + expert_pack.shape, (3,) + expert_pack.shape
        near_a, near_b, d0, shared_total, grads, d2, d3, d1, expert_x = call(
            near_kernel,
            [rows_out] * 2 + [rows_back, shape(quarter), bank] + [rows_back] * 3 + [shape(bank_x)],
            [VMEM] * 5 + [ANY] * 7,
            [VMEM] * 4 + [ANY] * 5,
            [
                pltpu.VMEM((CAP + 16, width), BF),
                pltpu.VMEM(quarters, BF),
                pltpu.VMEM(quarters, BF),
                pltpu.VMEM((4,) + quarter, BF),
                pltpu.VMEM((3,) + quarter, BF),
                pltpu.SemaphoreType.DMA((2,)),
                pltpu.SemaphoreType.DMA((11,)),
                pltpu.SemaphoreType.DMA((11,)),
            ]
            + unit_scratch(2, CAP, 16, width, 2, True),
            flops=36 * CAP * width * CHUNK * CHUNKS,
            moved=30 * 2**20,
            group=4,
        )(
            ext, *x_in[:2], *cot_in[:2], expert_pack, expert_bank, before, da, db,
            shared_keep, shared_y,
        )
        d_rows = [d0, d1, d2, d3]
    else:

        def slotted(part):
            every = lax.all_gather(part, "shard")
            every = every.reshape(SLOTS, shards // SLOTS, 3, width, part.shape[2])
            return every.transpose(0, 2, 3, 1, 4).reshape(SLOTS, 3, width, -1)

        shared_bank = slotted(my_half)
        shared_bank = jnp.concatenate([shared_bank, to_rep(shared_bank, 1)], axis=0)
        expert_bank = slotted(expert_pack)
        x_in = [x_out[0]] + [to_rep(x_out[o], o) for o in (1, 2, 3)]
        (shared_out,), (shared_dx,), shared_grads = plain_bank(
            ext, [normed], [cot], shared_bank, None, False
        )
        grads_own, grads_other = shared_grads[:SLOTS], shared_grads[SLOTS:]
        (far_a, far_b), (da, db), before = plain_bank(
            ext, x_in[2:], cot_in[2:], expert_bank, None, True
        )
        (near_a, near_b), (d0, d1), grads = plain_bank(
            ext, x_in[:2], cot_in[:2], expert_bank, before, True
        )
        d_rows = [d0, to_rep(d1, 1), to_rep(da, 2), to_rep(db, 3)]
    wide = shape((tokens, width), F32)
    outs = [wide, square, shape((16, width), F32)] + [token_f] * 3
    operands = (piece_starts, slot, *d_rows, shared_dx, probs, middle, normed, cot, ext, attended)
    operands += (wo,)
    specs = [SMEM] + [VMEM] * 15
    scratch = [
        pltpu.VMEM((tokens, width), BF),
        pltpu.VMEM((tokens, width), BF),
        pltpu.VMEM((128, width), F32),
        pltpu.VMEM((8, width), F32),
        bias,
        pltpu.VMEM((tokens, 128), F32),
        pltpu.VMEM((tokens, 128), F32),
    ]
    work = 2 * tokens * width * (2 * width + 4 * CAP) + 40 * tokens * tokens * width
    if ringed:
        late = (*operands[1:], cosine, sine, q, k, v, lse)
        d_middle, grad_wo, grad_ext, dq, dk, dv, expert_total, *back = call(
            back_kernel,
            outs
            + [shape(expert_pack.shape)]
            + [rows_out] * 3
            + [shape(bank_z), shape(bank_z), shape(bank_x)],
            [SMEM] + [ANY] * (len(late) + 5),
            [VMEM] * 7 + [ANY] * 6,
            scratch
            + [pltpu.VMEM(a.shape, a.dtype) for a in late]
            + [
                pltpu.VMEM(bank_x, BF),
                pltpu.VMEM((1,) + expert_pack.shape, BF),
                pltpu.SemaphoreType.DMA((2,)),
                pltpu.SemaphoreType.DMA((len(late),)),
                pltpu.SemaphoreType.DMA((12,)),
                pltpu.SemaphoreType.DMA((12,)),
            ],
            flops=work,
            moved=40 * 2**20,
            group=5,
            alias={24: 12},
        )(piece_starts, *late, near_b, far_a, far_b, grads, expert_x)
        operands = (x, ext, dq, dk, dv, wq, wk, wv, grad_wo, grad_ext)
        operands += (d_middle, slot, near_a, *back[:3], shared_out, probs, middle)
        strip = (2, width // SLOTS, width)
        grad_in, outputs, weights, small, *rest = call(
            tail_kernel,
            [wide, token_f, shape((4, rows, width), F32), shape((16, width), F32)]
            + [shape(quarter)] * 3
            + [shape(expert_pack.shape)] * 3,
            [VMEM] * 10 + [ANY] * 11,
            [VMEM] * 4 + [ANY] * 6,
            [
                pltpu.VMEM((tokens, width), BF),
                pltpu.VMEM((8, width), F32),
                pltpu.VMEM((4, width, width), BF),
                pltpu.VMEM((2, width, width), BF),
                pltpu.VMEM((4,) + strip, BF),
                pltpu.VMEM((3,) + strip, BF),
                pltpu.VMEM(strip, BF),
                pltpu.VMEM((2,) + strip, BF),
                pltpu.VMEM(strip, BF),
                pltpu.VMEM((4, 16, width), BF),
                pltpu.VMEM((6, 16, width), BF),
                pltpu.VMEM((tokens, width), F32),
                pltpu.VMEM((tokens, 128), F32),
                pltpu.VMEM((CAP, width), BF),
                pltpu.VMEM((CAP, width), BF),
                pltpu.VMEM((CAP, width), BF),
                pltpu.VMEM((CAP, width), BF),
                pltpu.VMEM((tokens, width), BF),
                pltpu.VMEM((tokens, 128), F32),
                pltpu.VMEM((tokens, width), F32),
                pltpu.SemaphoreType.DMA((9,)),
                pltpu.SemaphoreType.DMA((30,)),
                pltpu.SemaphoreType.DMA((30,)),
            ],
            flops=2 * tokens * width * (6 * width + 4 * CAP),
            moved=40 * 2**20,
            group=6,
        )(*operands, expert_total, shared_total)
        banks = [shape((4, width, units), F32)] * 2 + [shape((4, units, width), F32)]
        banks += [shape((width, units), F32)] * 2 + [shape((units, width), F32)]
        shared_far, shared_mate, shared_cross, *experts = rest
        *finals, grad_q, grad_k, grad_v, grad_o = call(
            finish_kernel,
            banks + [shape((rows, width), F32)] * 4,
            [ANY] * 4 + [VMEM] * 5,
            [ANY] * 3 + [VMEM] * 7,
            [pltpu.VMEM((4,) + expert_pack.shape, BF)]
            + [pltpu.VMEM(b.shape, F32) for b in banks[:3]]
            + [pltpu.SemaphoreType.DMA((4,)), pltpu.SemaphoreType.DMA((4, 3))],
            moved=18 * 2**20,
        )(
            expert_total, *experts, shared_total, shared_mate, shared_far, shared_cross, weights
        )
    else:
        d_middle, grad_wo, grad_ext, dq, dk, dv = call(
            plain_back_kernel, outs, specs + [VMEM] * 4, [VMEM] * 6, scratch, flops=work,
            moved=40 * 2**20,
        )(*operands, q, k, v, lse, cosine, sine)
        out_rows = [near_a, to_rep(near_b, 1), to_rep(far_a, 2), to_rep(far_b, 3)]
        grad_in, outputs, gw, gain = call(
            plain_tail_kernel,
            [wide, token_f, shape((3, width, width)), shape((8, width), F32)],
            [VMEM] * 17,
            [VMEM] * 4,
            [pltpu.VMEM((tokens, width), BF), pltpu.VMEM((8, width), F32)],
            flops=2 * tokens * width * (6 * width + 4 * CAP),
            moved=40 * 2**20,
        )(
            x, ext, dq, dk, dv, wq, wk, wv, d_middle, slot, *out_rows, shared_out, probs, middle
        )

        def over_rep(total):
            return lax.psum(total.astype(BF), "rep").astype(F32)

        def unslot(every, part_units):
            every = every.reshape(SLOTS, 3, width, shards // SLOTS, part_units)
            every = every.transpose(0, 3, 1, 2, 4).reshape(shards, 3, width, part_units)
            return lax.psum_scatter(every, "shard", scatter_dimension=0)

        grad_q, grad_k, grad_v, grad_o = (
            over_rep(lax.psum_scatter(w, "shard", tiled=True))
            for w in (gw[0], gw[1], gw[2], grad_wo)
        )
        small = grad_ext.at[4].add(jnp.sum(gain, axis=0))
        small = lax.psum(small, ("rep", "shard"))
        shared_sum = grads_own.astype(F32) + to_rep(grads_other, 1).astype(F32)
        total = unslot(shared_sum.astype(BF), units // 2).astype(F32)
        total = (total + to_rep(total.astype(BF), 2).astype(F32)).astype(BF)
        mate = to_rep(total, 1)
        shared_full = jnp.concatenate(
            [jnp.where(core == 0, total, mate), jnp.where(core == 0, mate, total)], axis=2
        ).astype(F32)
        expert_total = unslot(grads, units).astype(BF)
        parts = jnp.stack([expert_total] + [to_rep(expert_total, o) for o in (1, 2, 3)])
        full = jnp.take(parts, jnp.arange(4) ^ rep, axis=0).astype(F32)
        finals = (full[:, 0], full[:, 1], full[:, 2].transpose(0, 2, 1))
        finals += (shared_full[0], shared_full[1], shared_full[2].T)
    tiny = lax.dynamic_slice(small, (0, shard * rows), (16, rows))
    return (
        outputs[None],
        grad_in[None],
        tiny[4],
        grad_q,
        grad_k,
        grad_v,
        grad_o,
        tiny[5],
        tiny[:4].T,
        *finals,
    )


def solution(mesh):
    in_specs = (
        P(("rep", "shard"), None, None),
        P(("rep", "shard"), None),
        P(("rep", "shard"), None, None),
        P("shard"),
        P("shard", None),
        P("shard", None),
        P("shard", None),
        P("shard", None),
        P("shard"),
        P("shard", None),
        P(None, None, "shard"),
        P(None, None, "shard"),
        P(None, "shard", None),
        P(None, "shard"),
        P(None, "shard"),
        P("shard", None),
        P(("rep", "shard"), None, None),
    )
    out_specs = (
        P(("rep", "shard"), None, None),
        P(("rep", "shard"), None, None),
        P("shard"),
        P("shard", None),
        P("shard", None),
        P("shard", None),
        P("shard", None),
        P("shard"),
        P("shard", None),
        P(None, None, "shard"),
        P(None, None, "shard"),
        P(None, "shard", None),
        P(None, "shard"),
        P(None, "shard"),
        P("shard", None),
    )
    return jax.shard_map(body, mesh=mesh, in_specs=in_specs, out_specs=out_specs, check_vma=False)
```

```python
import functools

import jax
import jax.numpy as jnp
from jax import lax
from jax.experimental import pallas as pl
from jax.experimental.pallas import tpu as pltpu
from jax.sharding import PartitionSpec as P

HEADS = 12
PIECE = 256
CAP = 576
EPSILON = 1e-06
MASKED = -1e30
F32, BF = jnp.float32, jnp.bfloat16
AXES = ("rep", "shard")
TILE = 256
SLOTS = 8
VMEM_LIMIT = 62 * 2**20
ANY = pl.BlockSpec(memory_space=pl.ANY)
SMEM = pl.BlockSpec(memory_space=pltpu.SMEM)
VMEM = pl.BlockSpec(memory_space=pltpu.VMEM)


def dot(a, b, i, j):
    return lax.dot_general(a, b, (((i,), (j,)), ((), ())), preferred_element_type=F32)


def nn(a, b):
    return dot(a, b, 1, 0)


def nt(a, b):
    return dot(a, b, 1, 1)


def tn(a, b):
    return dot(a, b, 0, 0)


def iota(shape, dim):
    return lax.broadcasted_iota(jnp.int32, shape, dim)


def ones_where(cond):
    return jnp.where(cond, 1.0, 0.0).astype(BF)


def call(
    kernel, out_shape, in_specs, out_specs, scratch=(), flops=0, moved=0, grid=None, group=None,
    alias=None,
):
    extra = {} if grid is None else {"grid": grid}
    params = {} if group is None else {"collective_id": group, "has_side_effects": True}
    return pl.pallas_call(
        kernel,
        out_shape=out_shape,
        in_specs=in_specs,
        out_specs=out_specs,
        scratch_shapes=list(scratch),
        input_output_aliases=alias or {},
        compiler_params=pltpu.CompilerParams(vmem_limit_bytes=VMEM_LIMIT, **params),
        cost_estimate=pl.CostEstimate(flops=flops, bytes_accessed=moved, transcendentals=0),
        **extra,
    )


def shape(dims, dtype=BF):
    return jax.ShapeDtypeStruct(dims, dtype)


def permute(x, move):
    reps, shards = lax.axis_size("rep"), lax.axis_size("shard")
    pairs = []
    for r in range(reps):
        for s in range(shards):
            to_r, to_s = move(r, s)
            pairs.append((r * shards + s, to_r * shards + to_s))
    return lax.ppermute(x, AXES, pairs)


def to_rep(x, offset):
    return permute(x, lambda r, s: (r ^ offset, s))


def spin(block, cosine, sine):
    lane = iota(block.shape, 1)
    partner = jnp.where(lane % 64 < 32, pltpu.roll(block, 96, 1), pltpu.roll(block, 32, 1))
    return block * cosine + partner * sine


def sibling(rep, o):
    return 2 * lax.rem(lax.div(rep, 2) + o // 2, 2) + lax.rem(lax.rem(rep, 2) + o % 2, 2)


def route_slots(rep, routes, routes_t, rank_out, slot_out):
    tokens = routes.shape[0]
    first, second = routes_t[0:1, :], routes_t[1:2, :]
    expert = iota((8, tokens), 0)
    chosen = (expert == first) | (expert == second)
    upper = ones_where(iota((tokens, tokens), 0) <= iota((tokens, tokens), 1))
    rank = nn(ones_where(chosen), upper) - 1.0
    rank_out[...] = jnp.where(chosen, rank, -1.0)
    lane = iota((tokens, 128), 1)
    one, two = routes[:, 0:1], routes[:, 1:2]
    lower = ones_where(iota((tokens, tokens), 0) >= iota((tokens, tokens), 1))
    place = nn(lower, ones_where((lane == one) | (lane == two))) - 1.0
    for o in range(1, 4):
        place = place + jnp.where(lane == sibling(rep, o), float(o * CAP), 0.0)
    slot_one = jnp.sum(jnp.where(lane == one, place, 0.0), axis=1, keepdims=True)
    slot_two = jnp.sum(jnp.where(lane == two, place, 0.0), axis=1, keepdims=True)
    slot_out[...] = jnp.where(lane < 64, slot_one, slot_two)


def pack_row(rep, rank, source, o, out):
    row = rank[pl.ds(sibling(rep, o), 1), :]
    pick = ones_where(iota((CAP, source.shape[0]), 0).astype(F32) == row)
    out[...] = nn(pick, source[...]).astype(BF)


def pack_rows(rep, rank, source, packed):
    for o, out in enumerate(packed):
        pack_row(rep, rank, source, o, out)


def qkv_rows(x, ext, cosine, sine, wq, wk, wv, q, k, v):
    tokens, width = x.shape
    gain = ext[4:5, :]

    def tile(t, carry):
        at = pl.ds(pl.multiple_of(t * TILE, TILE), TILE)
        rows_in = x[at, :].astype(F32)
        scale = lax.rsqrt(jnp.mean(rows_in * rows_in, axis=1, keepdims=True) + EPSILON)
        normed = (rows_in * scale * gain).astype(BF)
        cos_t, sin_t = cosine[at, :], sine[at, :]
        for weight, out, factor in ((wq, q, 0.125), (wk, k, 1.0)):
            full = nn(normed, weight[...])
            for b in range(width // 128):
                turned = spin(full[:, b * 128 : (b + 1) * 128], cos_t, sin_t)
                out[at, b * 128 : (b + 1) * 128] = turned.astype(BF) * jnp.asarray(factor, BF)
        v[at, :] = nn(normed, wv[...]).astype(BF)
        return carry

    lax.fori_loop(0, tokens // TILE, tile, 0)


def when(cond, body):
    if cond is True:
        body()
    elif cond is not False:
        pl.when(cond)(body)


def both(one, two):
    if one is True or two is False:
        return two
    if two is True or one is False:
        return one
    return one & two


class Net:
    def __init__(self, send, recv):
        self.rep, self.shard = lax.axis_index("rep"), lax.axis_index("shard")
        self.core, self.z = lax.rem(self.rep, 2), lax.div(self.shard, 2)
        self.x = lax.rem(self.shard, 2)
        self.mate = self.rep + 1 - 2 * self.core
        self.across = self.shard + 1 - 2 * self.x
        first = lax.max(self.z - 1, 1 - self.z)
        third = 3 * (1 - lax.div(self.z, 2))
        self.levels = [self.z, first, 6 - self.z - first - third, third]
        self.up = lax.min(self.shard + 2, 6 + self.x)
        self.down = lax.max(self.shard - 2, self.x)
        self.cousins = [self.rep] + [sibling(self.rep, o) for o in (1, 2, 3)]
        self.send, self.recv = send, recv
        self.count, self.open = 0, {}

    def event(self):
        self.count += 1
        return self.count - 1

    def place(self, n, side):
        return self.levels[n] * 2 + (self.x if side == 0 else 1 - self.x)

    def cycle(self, d):
        return lax.rem(self.z + d, 4) * 2 + self.x

    def copy(self, event, source, target, rep, shard):
        return pltpu.make_async_remote_copy(
            src_ref=source,
            dst_ref=target,
            send_sem=self.send.at[event],
            recv_sem=self.recv.at[event],
            device_id=(rep, shard),
            device_id_type=pl.DeviceIdType.MESH,
        )

    def put(self, event, source, target, rep, shard, cond=True):
        when(cond, self.copy(event, source, target, rep, shard).start)
        self.open[event] = (cond, source)

    def got(self, event, like, cond=True):
        when(cond, self.copy(event, like, like, self.mate, self.shard).wait_recv)

    def settle(self, event):
        cond, source = self.open.pop(event)
        when(cond, self.copy(event, source, source, self.mate, self.shard).wait_send)

    def close(self):
        for event, (cond, source) in self.open.items():
            when(cond, self.copy(event, source, source, self.mate, self.shard).wait_send)

    def meet(self, z_ways, others):
        barrier = pltpu.get_barrier_semaphore()

        def greet(rep, shard):
            pl.semaphore_signal(
                barrier, inc=1, device_id=(rep, shard), device_id_type=pl.DeviceIdType.MESH
            )

        count = len(others)
        for rep, shard in others:
            greet(rep, shard)
        if z_ways == "line":
            when(self.z < 3, lambda: greet(self.rep, self.up))
            when(self.z > 0, lambda: greet(self.rep, self.down))
            count = count + lax.min(self.z, 1) + lax.min(3 - self.z, 1)
        if z_ways == "all":
            for d in (1, 2, 3):
                greet(self.rep, self.cycle(d))
            count = count + 3
        pl.semaphore_wait(barrier, count)


class Line:
    def __init__(self, net, bank, ways=4):
        self.net, self.bank = net, bank
        self.events = {(way, k): net.event() for way in range(ways) for k in range(-3, 4)}
        self.spots = {0: (net.shard, True)}
        for k in (1, 2, 3):
            self.spots[k] = (lax.min(net.shard + 2 * k, 6 + net.x), net.z < 4 - k)
            self.spots[-k] = (lax.max(net.shard - 2 * k, net.x), net.z >= k)
        self.flips = {k: spot + 1 - 2 * net.x for k, (spot, _) in self.spots.items()}
        self.onward = {k: both(self.spots[k][1], net.z < 3) for k in self.spots}
        self.back = {k: both(self.spots[k][1], net.z > 0) for k in self.spots}

    def spread(self, k, source):
        net, (spot, here) = self.net, self.spots[k]
        target = self.bank.at[net.core, spot]
        if -3 < k <= 0:
            event = self.events[0, k - 1]
            net.put(event, source, target, net.rep, net.up, self.onward[k])
        if 0 <= k < 3:
            event = self.events[0, k + 1]
            net.put(event, source, target, net.rep, net.down, self.back[k])
        net.put(self.events[1, k], source, target, net.rep, net.across, here)
        net.put(self.events[2, k], source, target, net.mate, net.shard, here)

    def along(self, k):
        spot, here = self.spots[k]
        piece = self.bank.at[self.net.core, spot]
        self.net.got(self.events[0, k], piece, here)
        self.spread(k, piece)

    def over(self, k):
        net, here = self.net, self.spots[k][1]
        piece = self.bank.at[net.core, self.flips[k]]
        net.got(self.events[1, k], piece, here)
        net.put(self.events[3, k], piece, piece, net.mate, net.shard, here)

    def finish(self):
        other = 1 - self.net.core
        for k in (0, 1, -1, 2, -2, 3, -3):
            spot, here = self.spots[k]
            self.net.got(self.events[2, k], self.bank.at[other, spot], here)
            self.net.got(self.events[3, k], self.bank.at[other, self.flips[k]], here)


class Spread:
    def __init__(self, net, piece, bank):
        self.net, self.piece, self.bank = net, piece, bank
        self.line = Line(net, bank, 8)
        self.events, self.spots, self.flips = self.line.events, self.line.spots, self.line.flips
        self.half = piece.shape[1] // 2
        y = lax.div(net.rep, 2)
        self.rows = [pl.ds(pl.multiple_of(n * self.half, 128), self.half) for n in (y, 1 - y)]
        self.far = net.cousins[2]

    def view(self, core, spot, rows):
        return self.bank.at[core, spot, :, self.rows[rows], :]

    def begin(self):
        net = self.net
        source = self.piece.at[:, self.rows[0], :]
        target = self.view(net.core, net.shard, 0)
        net.put(self.events[0, -1], source, target, net.rep, net.up, self.line.onward[0])
        net.put(self.events[0, 1], source, target, net.rep, net.down, self.line.back[0])
        net.put(self.events[1, 0], source, target, net.rep, net.across)
        whole = self.bank.at[net.core, net.shard]
        net.put(self.events[2, 0], self.piece, whole, net.mate, net.shard)

    def hand(self, way, k, here, piece):
        net = self.net
        net.put(self.events[way + 4, k], piece, piece, self.far, net.shard, here)
        net.put(self.events[way + 2, k], piece, piece, net.mate, net.shard, here)

    def along(self, k):
        net, (spot, here) = self.net, self.spots[k]
        piece = self.view(net.core, spot, 0)
        net.got(self.events[0, k], piece, here)
        if -3 < k < 0:
            net.put(self.events[0, k - 1], piece, piece, net.rep, net.up, self.line.onward[k])
        if 0 < k < 3:
            net.put(self.events[0, k + 1], piece, piece, net.rep, net.down, self.line.back[k])
        net.put(self.events[1, k], piece, piece, net.rep, net.across, here)
        self.hand(0, k, here, piece)

    def over(self, k):
        net, here = self.net, self.spots[k][1]
        piece = self.view(net.core, self.flips[k], 0)
        net.got(self.events[1, k], piece, here)
        self.hand(1, k, here, piece)

    def relay(self, way, k):
        net, here = self.net, self.spots[k][1]
        spot = self.spots[k][0] if way == 0 else self.flips[k]
        piece = self.view(net.core, spot, 1)
        net.got(self.events[way + 4, k], piece, here)
        net.put(self.events[way + 6, k], piece, piece, net.mate, net.shard, here)

    def finish(self):
        net, other = self.net, 1 - self.net.core
        net.got(self.events[2, 0], self.bank.at[other, net.shard])
        for k in (0, 1, -1, 2, -2, 3, -3):
            spot, here = self.spots[k]
            if k:
                net.got(self.events[2, k], self.view(other, spot, 0), here)
                net.got(self.events[6, k], self.view(other, spot, 1), here)
            net.got(self.events[3, k], self.view(other, self.flips[k], 0), here)
            net.got(self.events[7, k], self.view(other, self.flips[k], 1), here)


def exchange(net, sources, targets):
    events = [net.event() for _ in range(3)]
    for o in (2, 3, 1):
        net.put(events[o - 1], sources[o - 1], targets[o - 1], net.cousins[o], net.shard)
    return [(events[o], targets[o]) for o in range(3)]


def head_kernel(
    routes, routes_t, cot, x, wq_in, wk_in, wv_in, wo_in, small, cosine, sine, expert_piece,
    *refs,
):
    width = x.shape[1]
    half = width // SLOTS
    outs, (c1, c2, c3, experts) = refs[:11], refs[11:15]
    bank, packed, piece, out_sems, send, recv, own_sem = refs[15:22]
    rank, slot, q, k, v, wq, wk, wv, wo, ext, c0 = refs[22:]
    stores = copies_of(zip(refs[22:], outs), out_sems)
    net = Net(send, recv)
    for core, (low, high) in enumerate(((wq_in, wk_in), (wv_in, wo_in))):

        @pl.when(net.core == core)
        def _():
            piece[0:half, :] = low[...]
            piece[half : 2 * half, :] = high[...]

    piece[2 * half : 2 * half + 16, :] = small[...]
    line = Line(net, bank)
    e_events = [net.event() for _ in range(3)]
    mine, most = experts.at[net.shard], experts.at[net.shard, pl.ds(0, 2)]
    peers = [(net.cousins[o], net.shard) for o in (1, 2, 3)]
    net.meet("line", peers + [(net.rep, net.across)])
    line.spread(0, piece)
    own = pltpu.make_async_copy(piece, bank.at[net.core, net.shard], own_sem)
    own.start()
    route_slots(net.rep, routes, routes_t, rank, slot)
    events = [net.event() for _ in range(3)]
    for o, far in ((2, c2), (3, c3), (1, c1)):
        pack_row(net.rep, rank, cot, o, packed.at[o - 1])
        net.put(events[o - 1], packed.at[o - 1], far, net.cousins[o], net.shard)
    arrivals = [(events[0], c1), (events[1], c2), (events[2], c3)]
    pack_row(net.rep, rank, cot, 0, c0)
    line.along(1)
    line.along(-1)
    line.over(0)
    line.along(2)
    line.along(-2)
    net.put(e_events[0], expert_piece, mine, net.rep, net.up, net.z < 3)
    net.put(e_events[1], expert_piece, mine, net.rep, net.down, net.z > 0)
    line.over(1)
    line.over(-1)
    line.along(3)
    line.along(-3)
    net.put(e_events[2], expert_piece.at[pl.ds(0, 2)], most, net.rep, net.across)
    for step in (2, -2, 3, -3):
        line.over(step)
    own.wait()
    line.finish()
    gathered = bank[0, 0, 2 * half : 2 * half + 16, :].astype(F32)
    for j in range(1, SLOTS):
        gathered = gathered + bank[0, j, 2 * half : 2 * half + 16, :].astype(F32)
    ext[...] = gathered
    for j in range(SLOTS):
        at = slice(j * half, (j + 1) * half)
        wq[at, :] = bank[0, j, 0:half, :]
        wk[at, :] = bank[0, j, half : 2 * half, :]
        wv[at, :] = bank[1, j, 0:half, :]
        wo[at, :] = bank[1, j, half : 2 * half, :]
    qkv_rows(x, ext, cosine, sine, wq, wk, wv, q, k, v)
    for copy in stores:
        copy.start()
    for event, like in arrivals:
        net.got(event, like)
    net.got(e_events[0], mine, net.z > 0)
    net.got(e_events[1], mine, net.z < 3)
    net.got(e_events[2], most)
    for copy in stores:
        copy.wait()
    net.close()


def plain_head_kernel(
    routes, routes_t, cot, x, cosine, sine, wq, wk, wv, ext,
    rank, slot, q, k, v, c0, c1, c2, c3,
):
    rep = lax.axis_index("rep")
    route_slots(rep, routes, routes_t, rank, slot)
    pack_rows(rep, rank, cot, (c0, c1, c2, c3))
    qkv_rows(x, ext, cosine, sine, wq, wk, wv, q, k, v)


def fill_bias(starts, bias):
    tokens = bias.shape[0]

    def tile(t, carry):
        at = pl.ds(pl.multiple_of(t * TILE, TILE), TILE)
        query = iota((TILE, tokens), 0) + t * TILE
        key = iota((TILE, tokens), 1)
        allowed = key <= query
        for n in range(2):
            begin = starts[0, n]
            inside = (query >= begin) & (query < begin + PIECE)
            allowed = allowed | (inside & (key >= begin) & (key < begin + PIECE))
        bias[at, :] = jnp.where(allowed, 0.0, MASKED)
        return carry

    lax.fori_loop(0, tokens // TILE, tile, 0)


def keep_half(block, h):
    low = iota(block.shape, 1) < 64
    return jnp.where(low if h == 0 else ~low, block.astype(F32), 0.0).astype(BF)


def biased(scores, bias, begin, free, end):
    tail = scores[:, free:] + bias[begin : begin + TILE, free:end]
    return tail if free == 0 else jnp.concatenate([scores[:, :free], tail], axis=1)


def attend_pairs(q, k, v, out, lse, bias, step):
    tokens, width = q.shape

    def pair(i, carry):
        step(i)
        cols = pl.ds(pl.multiple_of(i * 128, 128), 128)
        keys = k[:, cols]
        low = iota((tokens, 128), 1) < 64
        values = v[:, cols].astype(F32)
        value_one = [
            jnp.where(low, values, 1.0).astype(BF),
            jnp.where(low, 1.0, values).astype(BF),
        ]
        low = iota((TILE, 128), 1) < 64
        for t in range(tokens // TILE):
            begin = t * TILE
            end = min(tokens, begin + TILE + PIECE)
            block = q[begin : begin + TILE, cols]
            results, totals = [], []
            for h in range(2):
                scores = nt(keep_half(block, h), keys[:end])
                scores = biased(scores, bias, begin, begin, end)
                row_max = jnp.max(scores, axis=1, keepdims=True)
                probs = jnp.exp(scores - row_max).astype(BF)
                mixed = nn(probs, value_one[h][:end])
                total = pltpu.roll(mixed, 64, 1)
                results.append(mixed / total)
                totals.append(row_max + jnp.log(total))
            out[begin : begin + TILE, cols] = jnp.where(low, results[0], results[1]).astype(BF)
            lse[begin : begin + TILE, cols] = jnp.where(low, totals[0], totals[1])
        return carry

    lax.fori_loop(0, width // 128, pair, 0)


def router_rows(ext):
    rows = jnp.where(iota(ext.shape, 0) < 4, ext[...], 0.0)
    return jnp.concatenate([rows, jnp.zeros((112, ext.shape[1]), F32)], axis=0).astype(BF)


def route_probs(normed, router):
    logits = nt(normed, router)
    logits = jnp.where(iota(logits.shape, 1) < 4, logits, MASKED)
    raised = jnp.exp(logits - jnp.max(logits, axis=1, keepdims=True))
    return raised / jnp.sum(raised, axis=1, keepdims=True)


def middle_rows(rep, x, attended, wo, ext, rank, middle, normed, probs, packed):
    tokens = x.shape[0]
    gain = ext[5:6, :]
    router = router_rows(ext)

    def tile(t, carry):
        at = pl.ds(pl.multiple_of(t * TILE, TILE), TILE)
        rows = x[at, :].astype(F32) + nn(attended[at, :], wo[...])
        scale = lax.rsqrt(jnp.mean(rows * rows, axis=1, keepdims=True) + EPSILON)
        middle[at, :] = rows
        unit = (rows * scale * gain).astype(BF)
        normed[at, :] = unit
        probs[at, :] = route_probs(unit, router)
        return carry

    lax.fori_loop(0, tokens // TILE, tile, 0)
    pack_rows(rep, rank, normed, packed)


def forward_kernel(
    starts, q, k, v, x, wo, ext, rank, shared_piece, expert_piece, expert_in,
    *refs,
):
    outs, shared_bank, experts = refs[:9], refs[9], refs[10]
    bias, out_sems, send, recv = refs[11:15]
    attended, lse, middle, normed, probs, x0, x1, x2, x3 = refs[15:]
    stores = copies_of(zip(refs[15:], outs), out_sems)
    net = Net(send, recv)
    spread = Spread(net, shared_piece, shared_bank)
    events = [net.event() for _ in range(4)]
    inner = (net.z > 0) & (net.z < 3)
    low, high = experts.at[net.down], experts.at[net.up]
    rest, last = experts.at[net.shard, pl.ds(2, 1)], expert_piece.at[pl.ds(2, 1)]
    near = experts.at[net.place(1, 0), pl.ds(0, 2)]
    net.meet("line", [(net.mate, net.shard), (net.rep, net.across), (spread.far, net.shard)])
    spread.begin()
    fill_bias(starts, bias)

    def step(i):
        @pl.when(i == 1)
        def _():
            spread.along(1)
            spread.along(-1)
            spread.over(0)

        @pl.when(i == 3)
        def _():
            spread.along(2)
            spread.along(-2)
            spread.over(1)
            spread.over(-1)

        @pl.when(i == 5)
        def _():
            spread.along(3)
            spread.along(-3)
            net.put(events[0], low, low, net.rep, net.up, inner)
            net.put(events[1], high, high, net.rep, net.down, inner)
            net.put(events[2], last, rest, net.rep, net.across)
            net.put(events[3], near, near, net.rep, net.across)
            spread.over(2)
            spread.over(-2)

    attend_pairs(q, k, v, attended, lse, bias, step)
    for copy in stores[:2]:
        copy.start()
    spread.over(3)
    spread.over(-3)
    for way, k_step in ((1, 0), (0, 1), (0, -1)):
        spread.relay(way, k_step)
    middle_rows(net.rep, x, attended, wo, ext, rank, middle, normed, probs, (x0, x1, x2, x3))
    for copy in stores[2:]:
        copy.start()
    for way, k_step in ((1, 1), (1, -1), (0, 2), (0, -2), (1, 2), (1, -2)):
        spread.relay(way, k_step)
    for way, k_step in ((0, 3), (0, -3), (1, 3), (1, -3)):
        spread.relay(way, k_step)
    spread.finish()
    net.got(events[0], low, net.z > 1)
    net.got(events[1], low, net.z < 2)
    net.got(events[2], rest)
    net.got(events[3], near)
    for copy in stores:
        copy.wait()
    net.close()


def plain_forward_kernel(
    starts, q, k, v, x, wo, ext, rank,
    attended, lse, middle, normed, probs, x0, x1, x2, x3, bias,
):
    fill_bias(starts, bias)
    attend_pairs(q, k, v, attended, lse, bias, lambda i: None)
    rep = lax.axis_index("rep")
    middle_rows(rep, x, attended, wo, ext, rank, middle, normed, probs, (x0, x1, x2, x3))


CHUNK, CHUNKS = 512, 4


def unit_bank(
    expert, ext, xs, cs, source, target, before, unit, outs, dxs, scratch, ready=None,
    emit=None,
):
    out_acc, dx_acc, gate, wbuf, dw_acc, dw_out, in_sems, out_sems = scratch[:8]
    routed = expert is not None
    blocks, rows = len(xs), xs[0].shape[0]
    per = CHUNK // unit

    def loads(of, buffer, sems, k, b):
        return [
            pltpu.make_async_copy(
                of(k * per + i), buffer.at[b, :, :, pl.ds(i * unit, unit)], sems.at[b, i]
            )
            for i in range(per)
        ]

    def stores(k, b):
        return [
            pltpu.make_async_copy(
                dw_out.at[b, :, :, pl.ds(i * unit, unit)],
                target(k * per + i),
                out_sems.at[b, i],
            )
            for i in range(per)
        ]

    def start_loads(k, b):
        if ready is not None:
            ready(k)
        for copy in loads(source, wbuf, in_sems, k, b):
            copy.start()
        if before is not None:
            for copy in loads(before, scratch[8], scratch[9], k, b):
                copy.start()

    start_loads(0, 0)
    if routed:
        router = router_rows(ext)
        for n in range(blocks):
            probs = route_probs(xs[n][...], router)
            lane = iota(probs.shape, 1)
            gate[n] = jnp.sum(jnp.where(lane == expert, probs, 0.0), axis=1, keepdims=True)

    def chunk(k, carry):
        b = lax.rem(k, 2)
        for copy in loads(source, wbuf, in_sems, 0, b):
            copy.wait()
        for n in range(blocks):
            x, c = xs[n][...], cs[n][...]
            wg, wu, wd = wbuf[b, 0], wbuf[b, 1], wbuf[b, 2]
            gate_h, up_h, back_h = nn(x, wg), nn(x, wu), nn(c, wd)
            sigma = 1.0 / (1.0 + jnp.exp(-gate_h))
            silu = gate_h * sigma
            hidden = silu * up_h
            if routed:
                share = gate[n]
                scaled = back_h * share
                weighted = (hidden * share).astype(BF)
            else:
                scaled, weighted = back_h, hidden.astype(BF)
            d_up = (scaled * silu).astype(BF)
            d_gate = (scaled * up_h * (sigma + silu * (1.0 - sigma))).astype(BF)
            product = nt(hidden.astype(BF), wd)
            d_rows = nt(d_gate, wg) + nt(d_up, wu)
            parts = (tn(x, d_gate), tn(x, d_up), tn(c, weighted))
            if routed:
                pairs = (hidden * back_h).astype(BF)
                d_share = nt(jnp.ones((16, CHUNK), BF), pairs)

            @pl.when(k == 0)
            def _():
                out_acc[n] = product
                dx_acc[n, 0:rows, :] = d_rows
                if routed:
                    dx_acc[n, rows : rows + 16, :] = jnp.zeros((16, d_rows.shape[1]), F32)
                    dx_acc[n, rows : rows + 16, 0:rows] = d_share

            @pl.when(k != 0)
            def _():
                out_acc[n] += product
                dx_acc[n, 0:rows, :] += d_rows
                if routed:
                    dx_acc[n, rows : rows + 16, 0:rows] += d_share

            for i in range(3):
                if n == 0:
                    dw_acc[i] = parts[i]
                else:
                    dw_acc[i] += parts[i]

        for nxt in range(1, CHUNKS):

            @pl.when(k + 1 == nxt)
            def _():
                start_loads(nxt, nxt % 2)

        @pl.when(k >= 2)
        def _():
            for copy in stores(0, b):
                copy.wait()

        if before is not None:
            for copy in loads(before, scratch[8], scratch[9], 0, b):
                copy.wait()
            for i in range(3):
                dw_out[b, i] = (dw_acc[i] + scratch[8][b, i].astype(F32)).astype(BF)
        else:
            for i in range(3):
                dw_out[b, i] = dw_acc[i].astype(BF)
        for now in range(CHUNKS):

            @pl.when(k == now)
            def _():
                for copy in stores(now, now % 2):
                    copy.start()
                if emit is not None:
                    emit(now)

        return carry

    lax.fori_loop(0, CHUNKS, chunk, 0)
    for n in range(blocks):
        outs[n][...] = out_acc[n].astype(BF)
        dxs[n][...] = dx_acc[n].astype(BF)
    for b in range(2):
        for copy in stores(0, b):
            copy.wait()


def unit_scratch(blocks, rows, extra, width, per, chained):
    scratch = [
        pltpu.VMEM((blocks, rows, width), F32),
        pltpu.VMEM((blocks, rows + extra, width), F32),
        pltpu.VMEM((blocks, rows, 1), F32),
        pltpu.VMEM((2, 3, width, CHUNK), BF),
        pltpu.VMEM((3, width, CHUNK), F32),
        pltpu.VMEM((2, 3, width, CHUNK), BF),
        pltpu.SemaphoreType.DMA((2, per)),
        pltpu.SemaphoreType.DMA((2, per)),
    ]
    if chained:
        scratch += [
            pltpu.VMEM((2, 3, width, CHUNK), BF),
            pltpu.SemaphoreType.DMA((2, per)),
        ]
    return scratch


def shared_kernel(
    x, c, piece, bank, x1, x2, x3, expert_in,
    out, dx, grads_own, grads_other, shared_mate, y1, y2, y3, experts,
    send, recv, *scratch,
):
    net = Net(send, recv)
    events = [net.event() for _ in range(4)]
    core_events = [net.event() for _ in range(8)]
    peers = [(net.cousins[o], net.shard) for o in (1, 2, 3)]
    net.meet("line", peers + [(net.rep, net.across)])
    arrivals = exchange(net, (x1, x2, x3), (y1, y2, y3))
    near, second = experts.at[net.place(1, 0), pl.ds(2, 1)], experts.at[net.place(2, 0)]
    net.put(events[0], near, near, net.rep, net.across)
    net.put(events[1], second, second, net.rep, net.across)
    below = experts.at[lax.max(net.shard - 4, net.x)]
    above = experts.at[lax.min(net.shard + 4, 6 + net.x)]
    net.put(events[2], below, below, net.rep, net.up, net.z == 2)
    net.put(events[3], above, above, net.rep, net.down, net.z == 1)
    spots = [net.place(n % 4, n // 4 % 2) for n in range(8)]
    halves = [net.core, 1 - net.core]
    done = scratch[5]
    slices = [done.at[n // 4, :, :, pl.ds(n % 4 * 128, 128)] for n in range(8)]
    places = [shared_mate.at[spot] for spot in spots]

    def source(n):
        return piece if n == 0 else bank.at[halves[n // 8], spots[n % 8]]

    def target(n):
        return (grads_own, grads_other)[n // 8].at[spots[n % 8]]

    def emit(now):
        if now >= 2:
            for n in range(4 * now - 8, 4 * now - 4):
                net.put(core_events[n], slices[n], places[n], net.mate, net.shard)

    unit_bank(
        None, None, [x], [c], source, target, None, 128, [out], [dx], scratch, None, emit
    )
    for event, like in arrivals:
        net.got(event, like)
    net.got(events[0], near)
    net.got(events[1], second)
    net.got(events[2], second, net.z == 3)
    net.got(events[3], second, net.z == 0)
    for n in range(8):
        net.got(core_events[n], places[n])
    net.close()


def far_kernel(
    ext, xa, xb, ca, cb, expert_piece, shared_own, shared_mate, expert_in,
    oa, ob, da, db, grads, shared_keep, shared_y, experts,
    part_a, part_b, part_sems, send, recv, *scratch,
):
    net = Net(send, recv)
    events = [net.event() for _ in range(9)]
    far = net.cousins[2]
    parts = copies_of(((shared_own, part_a), (shared_mate, part_b)), part_sems)
    for copy in parts:
        copy.start()
    net.meet("none", [(net.rep, net.across), (far, net.shard)])
    last = experts.at[net.place(3, 0)]
    net.put(events[0], last, last, net.rep, net.across)
    spots = [net.place(n // 2, n % 2) for n in range(8)]
    y, quarter = lax.div(net.rep, 2), part_a.shape[2] // 2
    rows = [pl.ds(pl.multiple_of(n * quarter, 128), quarter) for n in (y, 1 - y)]
    keep = pltpu.make_async_copy(part_a.at[:, :, rows[0], :], shared_keep, part_sems.at[2])
    away = [part_a.at[j, :, rows[1], :] for j in range(SLOTS)]

    def source(n):
        return expert_piece if n == 0 else experts.at[spots[n]]

    def target(n):
        return grads.at[spots[n]]

    def ready(k):
        if k == 3:
            net.got(events[0], last)

    for copy in parts:
        copy.wait()

    def add(j, carry):
        part_a[j] = part_a[j] + part_b[j]
        return carry

    lax.fori_loop(0, SLOTS, add, 0)
    for j in range(SLOTS):
        net.put(events[1 + j], away[j], shared_y.at[j], far, net.shard)
    keep.start()
    unit_bank(
        net.rep, ext, [xa, xb], [ca, cb], source, target, None, 256, [oa, ob], [da, db],
        scratch, ready,
    )
    keep.wait()
    for j in range(SLOTS):
        net.got(events[1 + j], shared_y.at[j])
    net.close()


def near_kernel(
    ext, xa, xb, ca, cb, expert_piece, experts, before, far_a, far_b,
    shared_keep, shared_y,
    oa, ob, da, shared_total, grads, back_a, back_b, back_c, expert_x,
    db, part_a, part_b, from_x, from_z, third, sems, send, recv, *scratch,
):
    net = Net(send, recv)
    events = [net.event() for _ in range(4)]
    x_events = [net.event() for _ in range(4)]
    z_events = [net.event() for _ in range(3)]
    peers = [(net.cousins[o], net.shard) for o in (1, 2, 3)]
    one = pltpu.make_async_copy(shared_keep, part_a, sems.at[0])
    two = pltpu.make_async_copy(shared_y, part_b, sems.at[1])
    one.start()
    two.start()
    net.meet("all", peers + [(net.rep, net.across)])
    net.put(events[0], far_a, back_a, net.cousins[2], net.shard)
    net.put(events[1], far_b, back_b, net.cousins[3], net.shard)
    one.wait()
    two.wait()

    def add(j, carry):
        part_a[j] = part_a[j] + part_b[j]
        return carry

    lax.fori_loop(0, SLOTS, add, 0)
    mine = [net.cycle(d) for d in range(4)]
    theirs = [spot + 1 - 2 * net.x for spot in mine]
    for d in (2, 1, 3, 0):
        net.put(x_events[d], part_a.at[theirs[d]], from_x.at[d], net.rep, net.across)
    pieces, lands = [part_a.at[spot] for spot in mine], [from_x.at[d] for d in range(4)]
    ends = [from_z.at[d] for d in range(3)]
    spots = [net.place(3 - n // 2, n % 2) for n in range(8)]
    own_slot = 6
    done, target = scratch[5], expert_x.at[net.levels[3]]

    def source(n):
        return expert_piece if n == own_slot else experts.at[spots[n]]

    def ready(k):
        if k == 2:
            for d in (2, 1, 3, 0):
                net.got(x_events[d], lands[d])
                part_a[mine[d]] = part_a[mine[d]] + from_x[d]
                if d:
                    net.put(z_events[d - 1], pieces[d], ends[d - 1], net.rep, mine[d])

    def emit(now):
        if now == 0:
            third[...] = done[0, :, :, 256:512]
            net.put(events[3], third, target, net.rep, net.across)

    unit_bank(
        net.rep, ext, [xa, xb], [ca, cb], source,
        lambda n: grads.at[spots[n]], lambda n: before.at[spots[n]],
        256, [oa, ob], [da, db], scratch, ready, emit,
    )
    net.put(events[2], db, back_c, net.mate, net.shard)
    total = part_a[mine[0]].astype(F32)
    for d in (1, 2, 3):
        net.got(z_events[d - 1], ends[d - 1])
        total = total + from_z[d - 1].astype(F32)
    shared_total[...] = total.astype(BF)
    net.got(events[0], back_a)
    net.got(events[1], back_b)
    net.got(events[2], back_c)
    net.got(events[3], target)
    net.close()


def plain_bank_kernel(blocks, unit, routed, chained, ext, *refs):
    refs = list(refs)

    def take(n):
        taken = refs[:n]
        del refs[:n]
        return taken

    xs, cs = take(blocks), take(blocks)
    bank = take(1)[0]
    before = take(1)[0] if chained else None
    outs, dxs = take(blocks), take(blocks)
    grads = take(1)[0]
    unit_bank(
        lax.axis_index("rep") if routed else None,
        ext, xs, cs,
        lambda n: bank.at[n],
        lambda n: grads.at[n],
        (lambda n: before.at[n]) if chained else None,
        unit, outs, dxs, refs,
    )


def plain_bank(ext, xs, cs, bank, before, routed):
    blocks, (rows, width) = len(xs), xs[0].shape
    chained = before is not None
    extra, unit = (16 if routed else 0), bank.shape[3]
    operands = [ext, *xs, *cs, bank] + ([before] if chained else [])
    outs = [shape((rows, width))] * blocks + [shape((rows + extra, width))] * blocks
    results = call(
        functools.partial(plain_bank_kernel, blocks, unit, routed, chained),
        outs + [shape(bank.shape)],
        [VMEM] * (1 + 2 * blocks) + [ANY] * (2 if chained else 1),
        [VMEM] * (2 * blocks) + [ANY],
        unit_scratch(blocks, rows, extra, width, CHUNK // unit, chained),
        flops=18 * blocks * rows * width * 4 * CHUNK,
        moved=30 * 2**20,
    )(*operands)
    return results[:blocks], results[blocks : 2 * blocks], results[2 * blocks]


def combine_rows(
    slot, d0, d1, d2, d3, d_shared, probs, middle, normed, cot, ext, attended, wo,
    d_middle, d_attended, grad_wo, grad_ext, branch, router_acc, gain_acc,
):
    tokens, width = middle.shape
    rep = lax.axis_index("rep")
    gain = ext[5:6, :]
    router = router_rows(ext)
    router_acc[...] = jnp.zeros_like(router_acc)
    gain_acc[...] = jnp.zeros_like(gain_acc)

    def tile(t, carry):
        at = pl.ds(pl.multiple_of(t * TILE, TILE), TILE)
        slot_one, slot_two = slot[at, 0:1], slot[at, 64:65]
        d_normed = d_shared[at, :].astype(F32)
        lane = iota((TILE, 128), 1)
        d_gates = jnp.zeros((TILE, 128), F32)
        for o, d in enumerate((d0, d1, d2, d3)):
            place = (iota((TILE, CAP), 1) + o * CAP).astype(F32)
            hit = (place == slot_one) | (place == slot_two)
            d_normed = d_normed + nn(ones_where(hit), d[0:CAP, :])
            share = d[CAP : CAP + 16, 0:CAP].astype(F32)[0:1, :]
            d_share = jnp.sum(jnp.where(hit, share, 0.0), axis=1, keepdims=True)
            d_gates = d_gates + jnp.where(lane == sibling(rep, o), d_share, 0.0)
        p = probs[at, :]
        inner = jnp.sum(d_gates * p, axis=1, keepdims=True)
        d_logits = (p * (d_gates - inner)).astype(BF)
        d_normed = d_normed + nn(d_logits, router)
        router_acc[...] += tn(d_logits, normed[at, :])
        rows = middle[at, :]
        scale = lax.rsqrt(jnp.mean(rows * rows, axis=1, keepdims=True) + EPSILON)
        unit = rows * scale
        gain_acc[...] += jnp.sum((d_normed * unit).reshape(TILE // 8, 8, width), axis=0)
        w = d_normed * gain
        inner = jnp.mean(w * unit, axis=1, keepdims=True)
        total = cot[at, :].astype(F32) + scale * (w - unit * inner)
        d_middle[at, :] = total
        rounded = total.astype(BF)
        branch[at, :] = rounded
        d_attended[at, :] = nt(rounded, wo[...]).astype(BF)
        return carry

    lax.fori_loop(0, tokens // TILE, tile, 0)
    grad_wo[...] = tn(attended[...], branch[...]).astype(BF)
    row = iota((16, width), 0)
    total = jnp.sum(gain_acc[...], axis=0, keepdims=True)
    grad_ext[...] = jnp.where(row < 4, router_acc[0:16, :], jnp.where(row == 5, total, 0.0))


def output_rows(slot, o0, o1, o2, o3, shared, probs, middle, out, first, last):
    rep = lax.axis_index("rep")

    def tile(t, carry):
        at = pl.ds(pl.multiple_of(t * TILE, TILE), TILE)
        slot_one, slot_two = slot[at, 0:1], slot[at, 64:65]
        total = middle[at, :] + shared[at, :].astype(F32)
        p = probs[at, :]
        lane = iota((TILE, 128), 1)
        for o, rows in enumerate((o0, o1, o2, o3)):
            place = (iota((TILE, CAP), 1) + o * CAP).astype(F32)
            hit = (place == slot_one) | (place == slot_two)
            share = jnp.sum(jnp.where(lane == sibling(rep, o), p, 0.0), axis=1, keepdims=True)
            total = total + nn(jnp.where(hit, share, 0.0).astype(BF), rows[...])
        out[at, :] = total.astype(BF)
        return carry

    lax.fori_loop(first, last, tile, 0)


def back_pairs(
    q, k, v, d_out, out, lse, cosine, sine, dq, dk, dv, bias, dk_acc, dv_acc, step
):
    tokens, width = q.shape

    def pair(i, carry):
        step(i)
        cols = pl.ds(pl.multiple_of(i * 128, 128), 128)
        keys, values = k[:, cols], v[:, cols]
        half_keys = [keep_half(keys, 0), keep_half(keys, 1)]
        dk_acc[...] = jnp.zeros_like(dk_acc)
        dv_acc[...] = jnp.zeros_like(dv_acc)
        low = iota((TILE, 128), 1) < 64
        for t in range(tokens // TILE):
            begin = t * TILE
            end = min(tokens, begin + TILE + PIECE)
            at = slice(begin, begin + TILE)
            block, grad = q[at, cols], d_out[at, cols]
            product = grad.astype(F32) * out[at, cols].astype(F32)
            block_lse = lse[at, cols]
            d_block = None
            for h in range(2):
                block_h, grad_h = keep_half(block, h), keep_half(grad, h)
                scores = nt(block_h, keys[:end])
                scores = biased(scores, bias, begin, begin, end)
                probs = jnp.exp(scores - block_lse[:, 64 * h : 64 * h + 1])
                d_probs = nt(grad_h, values[:end])
                inner = jnp.sum(
                    jnp.where(low if h == 0 else ~low, product, 0.0), axis=1, keepdims=True
                )
                d_scores = (probs * (d_probs - inner)).astype(BF)
                part = nn(d_scores, half_keys[h][:end])
                d_block = part if d_block is None else d_block + part
                dk_acc[0:end, :] += tn(d_scores, block_h)
                dv_acc[0:end, :] += tn(probs.astype(BF), grad_h)
            dq[at, cols] = spin(d_block * 0.125, cosine[at, :], -sine[at, :]).astype(BF)
        dk[:, cols] = spin(dk_acc[...], cosine[...], -sine[...]).astype(BF)
        dv[:, cols] = dv_acc[...].astype(BF)
        return carry

    lax.fori_loop(0, width // 128, pair, 0)


def copies_of(pairs, sems):
    return [pltpu.make_async_copy(a, b, sems.at[i]) for i, (a, b) in enumerate(pairs)]


def fetch(sources, targets, sems):
    copies = copies_of(zip(sources, targets), sems)
    for copy in copies:
        copy.start()
    for copy in copies:
        copy.wait()


class Chain:
    def __init__(self, net, own, from_x, up_in, down_in, held, spare, sems):
        self.net, self.own, self.from_x = net, own, from_x
        self.up_in, self.down_in = up_in, down_in
        self.held, self.spare, self.sems = held, spare, sems
        self.events = {(way, d): net.event() for way in range(2) for d in (1, 2, 3)}
        self.spots = [net.place(n, 0) for n in range(4)]
        self.sends, self.gets = {}, {}
        z = net.z
        for d in (1, 2, 3):
            self.sends[0, d] = (held.at[lax.min(z + d, 3)], z < 4 - d)
            self.sends[1, d] = (held.at[lax.max(z - d, 0)], z > d - 1)
            self.gets[0, d] = (lax.min(z + d - 1, 3), (z > 0) & (z < 5 - d))
            self.gets[1, d] = (lax.max(z - d + 1, 0), (z < 3) & (z > d - 2))

    def level(self, n):
        to = self.net.levels[n]
        far = self.from_x.at[to]
        fetch([self.own.at[self.spots[n]], far], [self.held.at[to], self.spare.at[0]], self.sems)
        self.held[to] = self.held[to] + self.spare[0]

    def send(self, d):
        net = self.net
        for way, to, into in ((0, net.up, self.up_in), (1, net.down, self.down_in)):
            source, here = self.sends[way, d]
            net.put(self.events[way, d], source, into.at[d - 1], net.rep, to, here)

    def take(self, d):
        for way, into in ((0, self.up_in), (1, self.down_in)):
            to, here = self.gets[way, d]

            def add():
                self.net.copy(
                    self.events[way, d], into.at[d - 1], into.at[d - 1],
                    self.net.mate, self.net.shard,
                ).wait_recv()
                fetch([into.at[d - 1]], [self.spare.at[0]], self.sems)
                self.held[to] = self.held[to] + self.spare[0]

            when(here, add)


BACK_ROWS = 19


def back_kernel(starts, *refs):
    raw, refs = refs[:BACK_ROWS], refs[BACK_ROWS:]
    o1, o2, o3, grads, expert_x_in = refs[:5]
    outs, expert_total = refs[5:11], refs[11]
    r1, r2, r3, up_in, down_in, expert_x = refs[12:18]
    d_attended, branch, router_acc, gain_acc, bias, dk_acc, dv_acc = refs[18:25]
    local = refs[25 : 25 + BACK_ROWS]
    held, spare, sems, load_sems, out_sems, send, recv = refs[25 + BACK_ROWS : 32 + BACK_ROWS]
    d_middle, grad_wo, grad_ext, dq, dk, dv = refs[32 + BACK_ROWS :]
    stores = copies_of(zip((d_middle, grad_wo, grad_ext, dq, dk, dv), outs), out_sems)
    slot, d0, d1, d2, d3, d_shared, probs, middle, normed, cot, ext, attended, wo = local[:13]
    cosine, sine, q, k, v, lse = local[13:]
    loads = copies_of(zip(raw, local), load_sems)
    for copy in loads:
        copy.start()
    net = Net(send, recv)
    x_events = [net.event() for _ in range(3)]
    chain = Chain(net, grads, expert_x, up_in, down_in, held, spare, sems)
    peers = [(net.cousins[o], net.shard) for o in (1, 2, 3)]
    net.meet("line", peers + [(net.rep, net.across)])
    targets = [expert_x.at[net.levels[n]] for n in range(3)]
    for n in (2, 1, 0):
        source = grads.at[net.place(n, 1)]
        net.put(x_events[n], source, targets[n], net.rep, net.across)
    arrivals = exchange(net, (o1, o2, o3), (r1, r2, r3))
    chain.level(3)
    chain.send(3)
    fill_bias(starts, bias)
    for copy in loads:
        copy.wait()
    combine_rows(
        slot, d0, d1, d2, d3, d_shared, probs, middle, normed, cot, ext, attended, wo,
        d_middle, d_attended, grad_wo, grad_ext, branch, router_acc, gain_acc,
    )
    for copy in stores[:3]:
        copy.start()
    net.got(x_events[2], targets[2])
    chain.level(2)
    chain.take(3)
    chain.send(2)

    def step(i):
        @pl.when(i == 3)
        def _():
            net.got(x_events[1], targets[1])
            chain.level(1)

        @pl.when(i == 4)
        def _():
            chain.take(2)
            chain.send(1)

    back_pairs(
        q, k, v, d_attended, attended, lse, cosine, sine, dq, dk, dv, bias, dk_acc, dv_acc, step
    )
    for copy in stores[3:]:
        copy.start()
    net.got(x_events[0], targets[0])
    chain.level(0)
    for event, like in arrivals:
        net.got(event, like)
    chain.take(1)
    expert_total[...] = held[net.z]
    for copy in stores:
        copy.wait()
    net.close()


def plain_back_kernel(
    starts, slot, d0, d1, d2, d3, d_shared, probs, middle, normed, cot, ext, attended, wo,
    q, k, v, lse, cosine, sine,
    d_middle, grad_wo, grad_ext, dq, dk, dv,
    d_attended, branch, router_acc, gain_acc, bias, dk_acc, dv_acc,
):
    combine_rows(
        slot, d0, d1, d2, d3, d_shared, probs, middle, normed, cot, ext, attended, wo,
        d_middle, d_attended, grad_wo, grad_ext, branch, router_acc, gain_acc,
    )
    fill_bias(starts, bias)
    back_pairs(
        q, k, v, d_attended, attended, lse, cosine, sine, dq, dk, dv, bias, dk_acc, dv_acc,
        lambda i: None,
    )


def norm_rows(x, ext, normed_all):
    gain = ext[4:5, :]

    def tile(t, carry):
        at = pl.ds(pl.multiple_of(t * TILE, TILE), TILE)
        rows = x[at, :].astype(F32)
        scale = lax.rsqrt(jnp.mean(rows * rows, axis=1, keepdims=True) + EPSILON)
        normed_all[at, :] = (rows * scale * gain).astype(BF)
        return carry

    lax.fori_loop(0, x.shape[0] // TILE, tile, 0)


def input_grad(x, ext, dq, dk, dv, wq, wk, wv, d_middle, grad_in, gain_acc, first, last):
    width = x.shape[1]
    gain = ext[4:5, :]

    def tile(t, carry):
        at = pl.ds(pl.multiple_of(t * TILE, TILE), TILE)
        rows = x[at, :].astype(F32)
        scale = lax.rsqrt(jnp.mean(rows * rows, axis=1, keepdims=True) + EPSILON)
        unit = rows * scale
        d_normed = nt(dq[at, :], wq[...]) + nt(dk[at, :], wk[...]) + nt(dv[at, :], wv[...])
        gain_acc[...] += jnp.sum((d_normed * unit).reshape(TILE // 8, 8, width), axis=0)
        w = d_normed * gain
        inner = jnp.mean(w * unit, axis=1, keepdims=True)
        grad_in[at, :] = d_middle[at, :] + scale * (w - unit * inner)
        return carry

    lax.fori_loop(first, last, tile, 0)


def tail_kernel(
    x, ext, dq, dk, dv, wq, wk, wv, grad_wo, grad_ext,
    d_middle_in, slot_in, o0_in, o1_in, o2_in, o3_in, shared_in, probs_in, middle_in,
    expert_total, shared_total,
    grad_in, outputs, weights, small, shared_far, shared_mate, shared_cross, e1, e2, e3,
    normed_all, gain_acc, gw, from_mate, from_x, from_z, from_y, result, from_core,
    tiny, tiny_in, d_middle, slot, o0, o1, o2, o3, shared_out, probs, middle, load_sems,
    send, recv,
):
    width = x.shape[1]
    half = width // SLOTS
    net = Net(send, recv)
    e_events = [net.event() for _ in range(3)]
    s_events = [net.event() for _ in range(3)]
    m_events = [net.event() for _ in range(2)]
    x_events = [[net.event() for _ in range(2)] for _ in range(4)]
    z_events = [[net.event() for _ in range(2)] for _ in range(3)]
    y_events = [net.event() for _ in range(2)]
    c_events = [net.event() for _ in range(2)]
    t_events = [net.event() for _ in range(6)]
    net.meet(
        "all", [(net.mate, net.shard), (net.cousins[2], net.shard), (net.rep, net.across)]
    )
    far = net.cousins[2]
    net.put(s_events[0], shared_total, shared_far, far, net.shard)
    net.put(s_events[1], shared_total, shared_mate, net.mate, net.shard)
    net.put(e_events[1], expert_total, e2, far, net.shard)
    net.put(e_events[0], expert_total, e1, net.mate, net.shard)
    pairs = (
        (d_middle_in, d_middle), (slot_in, slot), (o0_in, o0), (o1_in, o1), (o2_in, o2),
        (o3_in, o3), (shared_in, shared_out), (probs_in, probs), (middle_in, middle),
    )
    loads = [pltpu.make_async_copy(a, b, load_sems.at[i]) for i, (a, b) in enumerate(pairs)]
    for copy in loads:
        copy.start()
    norm_rows(x, ext, normed_all)
    spots = [lax.rem(i + 2 * net.core, 4) for i in range(4)]

    def rows_of(spot):
        return pl.ds(pl.multiple_of(spot * half, 32), half)

    mine = [rows_of(net.cycle(d)) for d in range(4)]
    theirs = [rows_of(net.cycle(d) + 1 - 2 * net.x) for d in range(4)]

    def hand(i):
        net.put(m_events[i], gw.at[2 + i], from_mate.at[i], net.mate, net.shard)

    def cross(i):
        net.got(m_events[i], from_mate.at[i])
        gw[i] = gw[i] + from_mate[i]
        for d in (2, 1, 3, 0):
            source = gw.at[i, theirs[d]]
            net.put(x_events[d][i], source, from_x.at[d, i], net.rep, net.across)

    gw[spots[0]] = tn(normed_all[...], dq[...]).astype(BF)
    gw[spots[2]] = tn(normed_all[...], dv[...]).astype(BF)
    hand(0)
    gw[spots[1]] = tn(normed_all[...], dk[...]).astype(BF)
    gw[spots[3]] = grad_wo[...]
    hand(1)
    cross(0)
    cross(1)
    gain_acc[...] = jnp.zeros_like(gain_acc)
    for copy in loads:
        copy.wait()
    count = x.shape[0] // TILE

    def inputs(first, last):
        input_grad(x, ext, dq, dk, dv, wq, wk, wv, d_middle, grad_in, gain_acc, first, last)

    def results(first, last):
        output_rows(
            slot, o0, o1, o2, o3, shared_out, probs, middle, outputs, first, last
        )

    def add_across(d, i):
        net.got(x_events[d][i], from_x.at[d, i])
        gw[i, mine[d], :] = gw[i, mine[d], :] + from_x[d, i]
        if d:
            net.put(
                z_events[d - 1][i], gw.at[i, mine[d]], from_z.at[d - 1, i],
                net.rep, net.cycle(d),
            )

    def add_along(i):
        total = gw[i, mine[0], :].astype(F32)
        for d in (1, 2, 3):
            net.got(z_events[d - 1][i], from_z.at[d - 1, i])
            total = total + from_z[d - 1, i].astype(F32)
        result[0, i] = total.astype(BF)
        net.put(y_events[i], result.at[0, i], from_y.at[i], far, net.shard)

    def tiny_add(n, target_rep, target_shard):
        net.got(t_events[n], tiny_in.at[n])
        tiny[n + 1] = (tiny[n].astype(F32) + tiny_in[n].astype(F32)).astype(BF)
        if target_rep is not None:
            source, target = tiny.at[n + 1], tiny_in.at[n + 1]
            net.put(t_events[n + 1], source, target, target_rep, target_shard)

    inputs(0, 2)
    add_across(2, 0)
    add_across(1, 0)
    inputs(2, 3)
    add_across(3, 0)
    inputs(3, count)
    add_across(0, 0)
    row = iota((16, width), 0)
    total = jnp.sum(gain_acc[...], axis=0, keepdims=True)
    tiny[0] = (grad_ext[...] + jnp.where(row == 4, total, 0.0)).astype(BF)
    net.put(t_events[0], tiny.at[0], tiny_in.at[0], net.mate, net.shard)
    results(0, 1)
    add_across(2, 1)
    tiny_add(0, net.rep, net.across)
    results(1, 2)
    add_across(1, 1)
    tiny_add(1, far, net.shard)
    add_along(0)
    results(2, 3)
    add_across(3, 1)
    tiny_add(2, None, None)
    for d in (1, 2, 3):
        net.put(t_events[2 + d], tiny.at[3], tiny_in.at[2 + d], net.rep, net.cycle(d))
    net.got(s_events[0], shared_far)
    net.put(s_events[2], shared_far, shared_cross, net.mate, net.shard)
    results(3, count)
    add_across(0, 1)
    net.got(e_events[1], e2)
    net.put(e_events[2], e2, e3, net.mate, net.shard)
    total = tiny[3].astype(F32)
    for d in (1, 2, 3):
        net.got(t_events[2 + d], tiny_in.at[2 + d])
        total = total + tiny_in[2 + d].astype(F32)
    small[...] = total.astype(BF).astype(F32)
    add_along(1)
    for i in range(2):
        net.got(y_events[i], from_y.at[i])
        result[1, i] = (result[0, i].astype(F32) + from_y[i].astype(F32)).astype(BF)
        net.put(c_events[i], result.at[1, i], from_core.at[i], net.mate, net.shard)
        weights[spots[i]] = result[1, i].astype(F32)
    for i in range(2):
        net.got(c_events[i], from_core.at[i])
        weights[spots[2 + i]] = from_core[i].astype(F32)
    net.got(e_events[0], e1)
    net.got(s_events[1], shared_mate)
    net.got(s_events[2], shared_cross)
    net.got(e_events[2], e3)
    net.close()


def plain_tail_kernel(
    x, ext, dq, dk, dv, wq, wk, wv, d_middle,
    slot, o0, o1, o2, o3, shared_out, probs, middle,
    grad_in, outputs, gw, gain, normed_all, gain_acc,
):
    norm_rows(x, ext, normed_all)
    for i, d in enumerate((dq, dk, dv)):
        gw[i] = tn(normed_all[...], d[...]).astype(BF)
    gain_acc[...] = jnp.zeros_like(gain_acc)
    count = x.shape[0] // TILE
    input_grad(x, ext, dq, dk, dv, wq, wk, wv, d_middle, grad_in, gain_acc, 0, count)
    gain[...] = gain_acc[...]
    output_rows(
        slot, o0, o1, o2, o3, shared_out, probs, middle, outputs, 0, x.shape[0] // TILE
    )


def finish_kernel(
    e0, e1, e2, e3, q0, q1, q2, q3, weights,
    gate, up, down, s_gate, s_up, s_down, grad_q, grad_k, grad_v, grad_o,
    part, ready_gate, ready_up, ready_down, in_sems, out_sems,
):
    rep = lax.axis_index("rep")
    loads = copies_of([(e, part.at[o]) for o, e in enumerate((e0, e1, e2, e3))], in_sems)
    for copy in loads:
        copy.start()
    stores = []
    for o in range(4):
        at = sibling(rep, o)
        pairs = ((ready_gate, gate), (ready_up, up), (ready_down, down))
        stores.append(copies_of([(a.at[o], b.at[at]) for a, b in pairs], out_sems.at[o]))
        loads[o].wait()
        ready_gate[o] = part[o, 0].astype(F32)
        ready_up[o] = part[o, 1].astype(F32)
        ready_down[o] = part[o, 2].astype(F32).T
        for copy in stores[o]:
            copy.start()
    quarter, span = q0.shape[1:]
    for o, piece in enumerate((q0, q1, q2, q3)):
        for other in range(4):

            @pl.when(sibling(rep, o) == other)
            def _():
                rows = slice(other // 2 * quarter, (other // 2 + 1) * quarter)
                cols = slice(other % 2 * span, (other % 2 + 1) * span)
                s_gate[rows, cols] = piece[0].astype(F32)
                s_up[rows, cols] = piece[1].astype(F32)
                s_down[cols, rows] = piece[2].astype(F32).T

    for i, out in enumerate((grad_q, grad_k, grad_v, grad_o)):
        out[...] = weights[i]
    for copies in stores:
        for copy in copies:
            copy.wait()


def rope_tables(length, head_dim):
    positions = jnp.arange(length, dtype=F32)
    inverse_freq = 10000.0 ** (-2.0 * jnp.arange(head_dim // 2, dtype=F32) / head_dim)
    angle = positions[:, None] * inverse_freq[None, :]
    cosine, sine = jnp.cos(angle), jnp.sin(angle)
    return (
        jnp.concatenate([cosine] * 4, axis=1),
        jnp.concatenate([-sine, sine, -sine, sine], axis=1),
    )


def body(
    inputs,
    piece_starts,
    routes,
    attn_gain,
    query_weight,
    key_weight,
    value_weight,
    out_weight,
    ffn_gain,
    router_weight,
    expert_gate,
    expert_up,
    expert_down,
    shared_gate,
    shared_up,
    shared_down,
    cotangent,
):
    _, tokens, width = inputs.shape
    shards = lax.axis_size("shard")
    rep, shard = lax.axis_index("rep"), lax.axis_index("shard")
    core = rep % 2
    ringed = shards == SLOTS
    rows = width // shards
    units = shared_gate.shape[1]
    x, cot, chosen = inputs[0], cotangent[0], routes[0]
    small = jnp.concatenate([router_weight.T, attn_gain[None], ffn_gain[None]], axis=0)
    small = jnp.pad(small, ((0, 10), (0, 0)))
    small = lax.dynamic_update_slice(jnp.zeros((16, width), BF), small, (0, shard * rows))
    if not ringed:
        wq, wk, wv, wo = [
            lax.all_gather(w, "shard", axis=0, tiled=True)
            for w in (query_weight, key_weight, value_weight, out_weight)
        ]
        ext = lax.psum(small.astype(F32), "shard")

    shared_pack = jnp.stack([shared_gate, shared_up, shared_down.T])
    my_half = lax.dynamic_slice_in_dim(shared_pack, core * (units // 2), units // 2, 2)
    expert_pack = jnp.stack([expert_gate[rep], expert_up[rep], expert_down[rep].T])

    cosine, sine = rope_tables(tokens, width // HEADS)
    token_f = shape((tokens, width))
    square = shape((width, width))
    packed = [shape((CAP, width))] * 4
    outs = [shape((8, tokens), F32), shape((tokens, 128), F32)] + [token_f] * 3
    work = 2 * tokens * width * (CAP * 4 + 3 * width)
    if ringed:
        firsts = outs + [square] * 4 + [shape((16, width), F32), packed[0]]
        rank, slot, q, k, v, *heads = call(
            head_kernel,
            firsts + packed[1:] + [shape((SLOTS,) + expert_pack.shape)],
            [VMEM] * 11 + [ANY],
            [ANY] * 15,
            [
                pltpu.VMEM((2, SLOTS, 2 * rows + 16, width), BF),
                pltpu.VMEM((3, CAP, width), BF),
                pltpu.VMEM((2 * rows + 16, width), BF),
                pltpu.SemaphoreType.DMA((11,)),
                pltpu.SemaphoreType.DMA((34,)),
                pltpu.SemaphoreType.DMA((34,)),
                pltpu.SemaphoreType.DMA,
            ]
            + [pltpu.VMEM(a.shape, a.dtype) for a in firsts],
            flops=work,
            moved=24 * 2**20,
            group=0,
        )(
            chosen, chosen.T, cot, x, query_weight, key_weight, value_weight, out_weight, small,
            cosine, sine, expert_pack,
        )
        wq, wk, wv, wo, ext, *cot_in, expert_bank = heads
    else:
        rank, slot, q, k, v, *cot_out = call(
            plain_head_kernel, outs + packed, [VMEM] * 10, [VMEM] * 9, flops=work,
            moved=24 * 2**20,
        )(chosen, chosen.T, cot, x, cosine, sine, wq, wk, wv, ext)
        cot_in = [cot_out[0]] + [to_rep(cot_out[o], o) for o in (1, 2, 3)]

    outs = [token_f, shape((tokens, width), F32), shape((tokens, width), F32), token_f]
    outs += [shape((tokens, 128), F32)] + packed
    work = 2 * tokens * width * (8 * tokens + width + 4 * CAP)
    bias = pltpu.VMEM((tokens, tokens), F32)
    if ringed:
        attended, lse, middle, normed, probs, *x_out, shared_bank, expert_bank = call(
            forward_kernel,
            outs + [shape((2, SLOTS) + my_half.shape), shape((SLOTS,) + expert_pack.shape)],
            [SMEM] + [VMEM] * 7 + [ANY] * 3,
            [ANY] * 11,
            [
                bias,
                pltpu.SemaphoreType.DMA((9,)),
                pltpu.SemaphoreType.DMA((60,)),
                pltpu.SemaphoreType.DMA((60,)),
            ]
            + [pltpu.VMEM(a.shape, a.dtype) for a in outs],
            flops=work,
            moved=30 * 2**20,
            group=1,
            alias={10: 10},
        )(piece_starts, q, k, v, x, wo, ext, rank, my_half, expert_pack, expert_bank)
    else:
        attended, lse, middle, normed, probs, *x_out = call(
            plain_forward_kernel, outs, [SMEM] + [VMEM] * 7, [VMEM] * 9, [bias], flops=work,
            moved=30 * 2**20,
        )(piece_starts, q, k, v, x, wo, ext, rank)

    rows_out = shape((CAP, width))
    rows_back = shape((CAP + 16, width))
    if ringed:
        half_grads = shape((SLOTS,) + my_half.shape)
        shared_out, shared_dx, grads_own, _, shared_mate, y1, y2, y3, expert_bank = call(
            shared_kernel,
            [token_f] * 2 + [half_grads] * 3 + packed[:3] + [shape(expert_bank.shape)],
            [VMEM] * 2 + [ANY] * 6,
            [VMEM] * 2 + [ANY] * 7,
            [pltpu.SemaphoreType.DMA((15,)), pltpu.SemaphoreType.DMA((15,))]
            + unit_scratch(1, tokens, 0, width, 4, False),
            flops=18 * tokens * width * CHUNK * CHUNKS,
            moved=30 * 2**20,
            group=2,
            alias={7: 8},
        )(normed, cot, my_half, shared_bank, *x_out[1:], expert_bank)
        x_in = [x_out[0], y1, y2, y3]
        bank = shape(expert_bank.shape)
        quarter = (3, width // 2, units // 2)
        quarters = (SLOTS,) + quarter
        far_a, far_b, da, db, before, shared_keep, shared_y, expert_bank = call(
            far_kernel,
            [rows_out] * 2 + [rows_back] * 2 + [bank, shape(quarters), shape(quarters), bank],
            [VMEM] * 5 + [ANY] * 4,
            [VMEM] * 4 + [ANY] * 4,
            [
                pltpu.VMEM(half_grads.shape, BF),
                pltpu.VMEM(half_grads.shape, BF),
                pltpu.SemaphoreType.DMA((3,)),
                pltpu.SemaphoreType.DMA((9,)),
                pltpu.SemaphoreType.DMA((9,)),
            ]
            + unit_scratch(2, CAP, 16, width, 2, False),
            flops=36 * CAP * width * CHUNK * CHUNKS,
            moved=30 * 2**20,
            group=3,
            alias={8: 7},
        )(ext, *x_in[2:], *cot_in[2:], expert_pack, grads_own, shared_mate, expert_bank)
        bank_x, bank_z = (4,) + expert_pack.shape, (3,) + expert_pack.shape
        near_a, near_b, d0, shared_total, grads, d2, d3, d1, expert_x = call(
            near_kernel,
            [rows_out] * 2 + [rows_back, shape(quarter), bank] + [rows_back] * 3 + [shape(bank_x)],
            [VMEM] * 5 + [ANY] * 7,
            [VMEM] * 4 + [ANY] * 5,
            [
                pltpu.VMEM((CAP + 16, width), BF),
                pltpu.VMEM(quarters, BF),
                pltpu.VMEM(quarters, BF),
                pltpu.VMEM((4,) + quarter, BF),
                pltpu.VMEM((3,) + quarter, BF),
                pltpu.VMEM(expert_pack.shape, BF),
                pltpu.SemaphoreType.DMA((2,)),
                pltpu.SemaphoreType.DMA((11,)),
                pltpu.SemaphoreType.DMA((11,)),
            ]
            + unit_scratch(2, CAP, 16, width, 2, True),
            flops=36 * CAP * width * CHUNK * CHUNKS,
            moved=30 * 2**20,
            group=4,
        )(
            ext, *x_in[:2], *cot_in[:2], expert_pack, expert_bank, before, da, db,
            shared_keep, shared_y,
        )
        d_rows = [d0, d1, d2, d3]
    else:

        def slotted(part):
            every = lax.all_gather(part, "shard")
            every = every.reshape(SLOTS, shards // SLOTS, 3, width, part.shape[2])
            return every.transpose(0, 2, 3, 1, 4).reshape(SLOTS, 3, width, -1)

        shared_bank = slotted(my_half)
        shared_bank = jnp.concatenate([shared_bank, to_rep(shared_bank, 1)], axis=0)
        expert_bank = slotted(expert_pack)
        x_in = [x_out[0]] + [to_rep(x_out[o], o) for o in (1, 2, 3)]
        (shared_out,), (shared_dx,), shared_grads = plain_bank(
            ext, [normed], [cot], shared_bank, None, False
        )
        grads_own, grads_other = shared_grads[:SLOTS], shared_grads[SLOTS:]
        (far_a, far_b), (da, db), before = plain_bank(
            ext, x_in[2:], cot_in[2:], expert_bank, None, True
        )
        (near_a, near_b), (d0, d1), grads = plain_bank(
            ext, x_in[:2], cot_in[:2], expert_bank, before, True
        )
        d_rows = [d0, to_rep(d1, 1), to_rep(da, 2), to_rep(db, 3)]
    wide = shape((tokens, width), F32)
    outs = [wide, square, shape((16, width), F32)] + [token_f] * 3
    operands = (piece_starts, slot, *d_rows, shared_dx, probs, middle, normed, cot, ext, attended)
    operands += (wo,)
    specs = [SMEM] + [VMEM] * 15
    scratch = [
        pltpu.VMEM((tokens, width), BF),
        pltpu.VMEM((tokens, width), BF),
        pltpu.VMEM((128, width), F32),
        pltpu.VMEM((8, width), F32),
        bias,
        pltpu.VMEM((tokens, 128), F32),
        pltpu.VMEM((tokens, 128), F32),
    ]
    work = 2 * tokens * width * (2 * width + 4 * CAP) + 40 * tokens * tokens * width
    if ringed:
        late = (*operands[1:], cosine, sine, q, k, v, lse)
        d_middle, grad_wo, grad_ext, dq, dk, dv, expert_total, *back = call(
            back_kernel,
            outs
            + [shape(expert_pack.shape)]
            + [rows_out] * 3
            + [shape(bank_z), shape(bank_z), shape(bank_x)],
            [SMEM] + [ANY] * (len(late) + 5),
            [ANY] * 6 + [VMEM] + [ANY] * 6,
            scratch
            + [pltpu.VMEM(a.shape, a.dtype) for a in late]
            + [
                pltpu.VMEM(bank_x, BF),
                pltpu.VMEM((1,) + expert_pack.shape, BF),
                pltpu.SemaphoreType.DMA((2,)),
                pltpu.SemaphoreType.DMA((len(late),)),
                pltpu.SemaphoreType.DMA((6,)),
                pltpu.SemaphoreType.DMA((12,)),
                pltpu.SemaphoreType.DMA((12,)),
            ]
            + [pltpu.VMEM(a.shape, a.dtype) for a in outs],
            flops=work,
            moved=40 * 2**20,
            group=5,
            alias={24: 12},
        )(piece_starts, *late, near_b, far_a, far_b, grads, expert_x)
        operands = (x, ext, dq, dk, dv, wq, wk, wv, grad_wo, grad_ext)
        operands += (d_middle, slot, near_a, *back[:3], shared_out, probs, middle)
        strip = (2, width // SLOTS, width)
        grad_in, outputs, weights, small, *rest = call(
            tail_kernel,
            [wide, token_f, shape((4, rows, width), F32), shape((16, width), F32)]
            + [shape(quarter)] * 3
            + [shape(expert_pack.shape)] * 3,
            [VMEM] * 10 + [ANY] * 11,
            [VMEM] * 4 + [ANY] * 6,
            [
                pltpu.VMEM((tokens, width), BF),
                pltpu.VMEM((8, width), F32),
                pltpu.VMEM((4, width, width), BF),
                pltpu.VMEM((2, width, width), BF),
                pltpu.VMEM((4,) + strip, BF),
                pltpu.VMEM((3,) + strip, BF),
                pltpu.VMEM(strip, BF),
                pltpu.VMEM((2,) + strip, BF),
                pltpu.VMEM(strip, BF),
                pltpu.VMEM((4, 16, width), BF),
                pltpu.VMEM((6, 16, width), BF),
                pltpu.VMEM((tokens, width), F32),
                pltpu.VMEM((tokens, 128), F32),
                pltpu.VMEM((CAP, width), BF),
                pltpu.VMEM((CAP, width), BF),
                pltpu.VMEM((CAP, width), BF),
                pltpu.VMEM((CAP, width), BF),
                pltpu.VMEM((tokens, width), BF),
                pltpu.VMEM((tokens, 128), F32),
                pltpu.VMEM((tokens, width), F32),
                pltpu.SemaphoreType.DMA((9,)),
                pltpu.SemaphoreType.DMA((32,)),
                pltpu.SemaphoreType.DMA((32,)),
            ],
            flops=2 * tokens * width * (6 * width + 4 * CAP),
            moved=40 * 2**20,
            group=6,
        )(*operands, expert_total, shared_total)
        banks = [shape((4, width, units), F32)] * 2 + [shape((4, units, width), F32)]
        banks += [shape((width, units), F32)] * 2 + [shape((units, width), F32)]
        shared_far, shared_mate, shared_cross, *experts = rest
        *finals, grad_q, grad_k, grad_v, grad_o = call(
            finish_kernel,
            banks + [shape((rows, width), F32)] * 4,
            [ANY] * 4 + [VMEM] * 5,
            [ANY] * 3 + [VMEM] * 7,
            [pltpu.VMEM((4,) + expert_pack.shape, BF)]
            + [pltpu.VMEM(b.shape, F32) for b in banks[:3]]
            + [pltpu.SemaphoreType.DMA((4,)), pltpu.SemaphoreType.DMA((4, 3))],
            moved=18 * 2**20,
        )(
            expert_total, *experts, shared_total, shared_mate, shared_far, shared_cross, weights
        )
    else:
        d_middle, grad_wo, grad_ext, dq, dk, dv = call(
            plain_back_kernel, outs, specs + [VMEM] * 4, [VMEM] * 6, scratch, flops=work,
            moved=40 * 2**20,
        )(*operands, q, k, v, lse, cosine, sine)
        out_rows = [near_a, to_rep(near_b, 1), to_rep(far_a, 2), to_rep(far_b, 3)]
        grad_in, outputs, gw, gain = call(
            plain_tail_kernel,
            [wide, token_f, shape((3, width, width)), shape((8, width), F32)],
            [VMEM] * 17,
            [VMEM] * 4,
            [pltpu.VMEM((tokens, width), BF), pltpu.VMEM((8, width), F32)],
            flops=2 * tokens * width * (6 * width + 4 * CAP),
            moved=40 * 2**20,
        )(
            x, ext, dq, dk, dv, wq, wk, wv, d_middle, slot, *out_rows, shared_out, probs, middle
        )

        def over_rep(total):
            return lax.psum(total.astype(BF), "rep").astype(F32)

        def unslot(every, part_units):
            every = every.reshape(SLOTS, 3, width, shards // SLOTS, part_units)
            every = every.transpose(0, 3, 1, 2, 4).reshape(shards, 3, width, part_units)
            return lax.psum_scatter(every, "shard", scatter_dimension=0)

        grad_q, grad_k, grad_v, grad_o = (
            over_rep(lax.psum_scatter(w, "shard", tiled=True))
            for w in (gw[0], gw[1], gw[2], grad_wo)
        )
        small = grad_ext.at[4].add(jnp.sum(gain, axis=0))
        small = lax.psum(small, ("rep", "shard"))
        shared_sum = grads_own.astype(F32) + to_rep(grads_other, 1).astype(F32)
        total = unslot(shared_sum.astype(BF), units // 2).astype(F32)
        total = (total + to_rep(total.astype(BF), 2).astype(F32)).astype(BF)
        mate = to_rep(total, 1)
        shared_full = jnp.concatenate(
            [jnp.where(core == 0, total, mate), jnp.where(core == 0, mate, total)], axis=2
        ).astype(F32)
        expert_total = unslot(grads, units).astype(BF)
        parts = jnp.stack([expert_total] + [to_rep(expert_total, o) for o in (1, 2, 3)])
        full = jnp.take(parts, jnp.arange(4) ^ rep, axis=0).astype(F32)
        finals = (full[:, 0], full[:, 1], full[:, 2].transpose(0, 2, 1))
        finals += (shared_full[0], shared_full[1], shared_full[2].T)
    tiny = lax.dynamic_slice(small, (0, shard * rows), (16, rows))
    return (
        outputs[None],
        grad_in[None],
        tiny[4],
        grad_q,
        grad_k,
        grad_v,
        grad_o,
        tiny[5],
        tiny[:4].T,
        *finals,
    )


def solution(mesh):
    in_specs = (
        P(("rep", "shard"), None, None),
        P(("rep", "shard"), None),
        P(("rep", "shard"), None, None),
        P("shard"),
        P("shard", None),
        P("shard", None),
        P("shard", None),
        P("shard", None),
        P("shard"),
        P("shard", None),
        P(None, None, "shard"),
        P(None, None, "shard"),
        P(None, "shard", None),
        P(None, "shard"),
        P(None, "shard"),
        P("shard", None),
        P(("rep", "shard"), None, None),
    )
    out_specs = (
        P(("rep", "shard"), None, None),
        P(("rep", "shard"), None, None),
        P("shard"),
        P("shard", None),
        P("shard", None),
        P("shard", None),
        P("shard", None),
        P("shard"),
        P("shard", None),
        P(None, None, "shard"),
        P(None, None, "shard"),
        P(None, "shard", None),
        P(None, "shard"),
        P(None, "shard"),
        P("shard", None),
    )
    return jax.shard_map(body, mesh=mesh, in_specs=in_specs, out_specs=out_specs, check_vma=False)
```

```python
import functools

import jax
import jax.numpy as jnp
import numpy as np
from jax import lax
from jax.experimental import pallas as pl
from jax.experimental.pallas import tpu as pltpu
from jax.sharding import PartitionSpec as P

HEADS = 12
PIECE = 256
CAP = 576
EPSILON = 1e-06
MASKED = -1e30
F32, BF = jnp.float32, jnp.bfloat16
AXES = ("rep", "shard")
TILE = 256
SLOTS = 8
VMEM_LIMIT = 62 * 2**20
ANY = pl.BlockSpec(memory_space=pl.ANY)
SMEM = pl.BlockSpec(memory_space=pltpu.SMEM)
VMEM = pl.BlockSpec(memory_space=pltpu.VMEM)


def dot(a, b, i, j):
    return lax.dot_general(a, b, (((i,), (j,)), ((), ())), preferred_element_type=F32)


def nn(a, b):
    return dot(a, b, 1, 0)


def nt(a, b):
    return dot(a, b, 1, 1)


def tn(a, b):
    return dot(a, b, 0, 0)


def iota(shape, dim):
    return lax.broadcasted_iota(jnp.int32, shape, dim)


def ones_where(cond):
    return jnp.where(cond, 1.0, 0.0).astype(BF)


def call(
    kernel, out_shape, in_specs, out_specs, scratch=(), flops=0, moved=0, grid=None, group=None,
    alias=None,
):
    extra = {} if grid is None else {"grid": grid}
    params = {} if group is None else {"collective_id": group, "has_side_effects": True}
    return pl.pallas_call(
        kernel,
        out_shape=out_shape,
        in_specs=in_specs,
        out_specs=out_specs,
        scratch_shapes=list(scratch),
        input_output_aliases=alias or {},
        compiler_params=pltpu.CompilerParams(vmem_limit_bytes=VMEM_LIMIT, **params),
        cost_estimate=pl.CostEstimate(flops=flops, bytes_accessed=moved, transcendentals=0),
        **extra,
    )


def shape(dims, dtype=BF):
    return jax.ShapeDtypeStruct(dims, dtype)


def permute(x, move):
    reps, shards = lax.axis_size("rep"), lax.axis_size("shard")
    pairs = []
    for r in range(reps):
        for s in range(shards):
            to_r, to_s = move(r, s)
            pairs.append((r * shards + s, to_r * shards + to_s))
    return lax.ppermute(x, AXES, pairs)


def to_rep(x, offset):
    return permute(x, lambda r, s: (r ^ offset, s))


def spin(block, cosine, sine):
    lane = iota(block.shape, 1)
    partner = jnp.where(lane % 64 < 32, pltpu.roll(block, 96, 1), pltpu.roll(block, 32, 1))
    return block * cosine + partner * sine


def sibling(rep, o):
    return 2 * lax.rem(lax.div(rep, 2) + o // 2, 2) + lax.rem(lax.rem(rep, 2) + o % 2, 2)


def route_slots(rep, routes, routes_t, rank_out, slot_out):
    tokens = routes.shape[0]
    first, second = routes_t[0:1, :], routes_t[1:2, :]
    expert = iota((8, tokens), 0)
    chosen = (expert == first) | (expert == second)
    upper = ones_where(iota((tokens, tokens), 0) <= iota((tokens, tokens), 1))
    rank = nn(ones_where(chosen), upper) - 1.0
    rank_out[...] = jnp.where(chosen, rank, -1.0)
    lane = iota((tokens, 128), 1)
    one, two = routes[:, 0:1], routes[:, 1:2]
    lower = ones_where(iota((tokens, tokens), 0) >= iota((tokens, tokens), 1))
    place = nn(lower, ones_where((lane == one) | (lane == two))) - 1.0
    for o in range(1, 4):
        place = place + jnp.where(lane == sibling(rep, o), float(o * CAP), 0.0)
    slot_one = jnp.sum(jnp.where(lane == one, place, 0.0), axis=1, keepdims=True)
    slot_two = jnp.sum(jnp.where(lane == two, place, 0.0), axis=1, keepdims=True)
    slot_out[...] = jnp.where(lane < 64, slot_one, slot_two)


def pack_row(rep, rank, source, o, out):
    row = rank[pl.ds(sibling(rep, o), 1), :]
    pick = ones_where(iota((CAP, source.shape[0]), 0).astype(F32) == row)
    out[...] = nn(pick, source[...]).astype(BF)


def pack_rows(rep, rank, source, packed):
    for o, out in enumerate(packed):
        pack_row(rep, rank, source, o, out)


def qkv_rows(x, ext, cosine, sine, wq, wk, wv, q, k, v):
    tokens, width = x.shape
    gain = ext[4:5, :]

    def tile(t, carry):
        at = pl.ds(pl.multiple_of(t * TILE, TILE), TILE)
        rows_in = x[at, :].astype(F32)
        scale = lax.rsqrt(jnp.mean(rows_in * rows_in, axis=1, keepdims=True) + EPSILON)
        normed = (rows_in * scale * gain).astype(BF)
        cos_t, sin_t = cosine[at, :], sine[at, :]
        for weight, out, factor in ((wq, q, 0.125), (wk, k, 1.0)):
            full = nn(normed, weight[...])
            for b in range(width // 128):
                turned = spin(full[:, b * 128 : (b + 1) * 128], cos_t, sin_t)
                out[at, b * 128 : (b + 1) * 128] = turned.astype(BF) * jnp.asarray(factor, BF)
        v[at, :] = nn(normed, wv[...]).astype(BF)
        return carry

    lax.fori_loop(0, tokens // TILE, tile, 0)


def when(cond, body):
    if cond is True:
        body()
    elif cond is not False:
        pl.when(cond)(body)


def both(one, two):
    if one is True or two is False:
        return two
    if two is True or one is False:
        return one
    return one & two


class Net:
    def __init__(self, send, recv):
        self.rep, self.shard = lax.axis_index("rep"), lax.axis_index("shard")
        self.core, self.z = lax.rem(self.rep, 2), lax.div(self.shard, 2)
        self.x = lax.rem(self.shard, 2)
        self.mate = self.rep + 1 - 2 * self.core
        self.across = self.shard + 1 - 2 * self.x
        first = lax.max(self.z - 1, 1 - self.z)
        third = 3 * (1 - lax.div(self.z, 2))
        self.levels = [self.z, first, 6 - self.z - first - third, third]
        self.up = lax.min(self.shard + 2, 6 + self.x)
        self.down = lax.max(self.shard - 2, self.x)
        self.cousins = [self.rep] + [sibling(self.rep, o) for o in (1, 2, 3)]
        self.send, self.recv = send, recv
        self.count, self.open = 0, {}

    def event(self):
        self.count += 1
        return self.count - 1

    def place(self, n, side):
        return self.levels[n] * 2 + (self.x if side == 0 else 1 - self.x)

    def cycle(self, d):
        return lax.rem(self.z + d, 4) * 2 + self.x

    def copy(self, event, source, target, rep, shard):
        return pltpu.make_async_remote_copy(
            src_ref=source,
            dst_ref=target,
            send_sem=self.send.at[event],
            recv_sem=self.recv.at[event],
            device_id=(rep, shard),
            device_id_type=pl.DeviceIdType.MESH,
        )

    def put(self, event, source, target, rep, shard, cond=True):
        when(cond, self.copy(event, source, target, rep, shard).start)
        self.open[event] = (cond, source)

    def got(self, event, like, cond=True):
        when(cond, self.copy(event, like, like, self.mate, self.shard).wait_recv)

    def settle(self, event):
        cond, source = self.open.pop(event)
        when(cond, self.copy(event, source, source, self.mate, self.shard).wait_send)

    def close(self):
        for event, (cond, source) in self.open.items():
            when(cond, self.copy(event, source, source, self.mate, self.shard).wait_send)

    def meet(self, z_ways, others):
        barrier = pltpu.get_barrier_semaphore()

        def greet(rep, shard):
            pl.semaphore_signal(
                barrier, inc=1, device_id=(rep, shard), device_id_type=pl.DeviceIdType.MESH
            )

        count = len(others)
        for rep, shard in others:
            greet(rep, shard)
        if z_ways == "line":
            when(self.z < 3, lambda: greet(self.rep, self.up))
            when(self.z > 0, lambda: greet(self.rep, self.down))
            count = count + lax.min(self.z, 1) + lax.min(3 - self.z, 1)
        if z_ways == "all":
            for d in (1, 2, 3):
                greet(self.rep, self.cycle(d))
            count = count + 3
        pl.semaphore_wait(barrier, count)


class Line:
    def __init__(self, net, bank, ways=4):
        self.net, self.bank = net, bank
        self.events = {(way, k): net.event() for way in range(ways) for k in range(-3, 4)}
        self.spots = {0: (net.shard, True)}
        for k in (1, 2, 3):
            self.spots[k] = (lax.min(net.shard + 2 * k, 6 + net.x), net.z < 4 - k)
            self.spots[-k] = (lax.max(net.shard - 2 * k, net.x), net.z >= k)
        self.flips = {k: spot + 1 - 2 * net.x for k, (spot, _) in self.spots.items()}
        self.onward = {k: both(self.spots[k][1], net.z < 3) for k in self.spots}
        self.back = {k: both(self.spots[k][1], net.z > 0) for k in self.spots}

    def spread(self, k, source):
        net, (spot, here) = self.net, self.spots[k]
        target = self.bank.at[net.core, spot]
        if -3 < k <= 0:
            event = self.events[0, k - 1]
            net.put(event, source, target, net.rep, net.up, self.onward[k])
        if 0 <= k < 3:
            event = self.events[0, k + 1]
            net.put(event, source, target, net.rep, net.down, self.back[k])
        net.put(self.events[1, k], source, target, net.rep, net.across, here)
        net.put(self.events[2, k], source, target, net.mate, net.shard, here)

    def along(self, k):
        spot, here = self.spots[k]
        piece = self.bank.at[self.net.core, spot]
        self.net.got(self.events[0, k], piece, here)
        self.spread(k, piece)

    def over(self, k):
        net, here = self.net, self.spots[k][1]
        piece = self.bank.at[net.core, self.flips[k]]
        net.got(self.events[1, k], piece, here)
        net.put(self.events[3, k], piece, piece, net.mate, net.shard, here)

    def finish(self):
        other = 1 - self.net.core
        for k in (0, 1, -1, 2, -2, 3, -3):
            spot, here = self.spots[k]
            self.net.got(self.events[2, k], self.bank.at[other, spot], here)
            self.net.got(self.events[3, k], self.bank.at[other, self.flips[k]], here)


class Spread:
    def __init__(self, net, piece, bank):
        self.net, self.piece, self.bank = net, piece, bank
        self.line = Line(net, bank, 8)
        self.events, self.spots, self.flips = self.line.events, self.line.spots, self.line.flips
        self.half = piece.shape[1] // 2
        y = lax.div(net.rep, 2)
        self.rows = [pl.ds(pl.multiple_of(n * self.half, 128), self.half) for n in (y, 1 - y)]
        self.far = net.cousins[2]

    def view(self, core, spot, rows):
        return self.bank.at[core, spot, :, self.rows[rows], :]

    def begin(self):
        net = self.net
        source = self.piece.at[:, self.rows[0], :]
        target = self.view(net.core, net.shard, 0)
        net.put(self.events[0, -1], source, target, net.rep, net.up, self.line.onward[0])
        net.put(self.events[0, 1], source, target, net.rep, net.down, self.line.back[0])
        net.put(self.events[1, 0], source, target, net.rep, net.across)
        whole = self.bank.at[net.core, net.shard]
        net.put(self.events[2, 0], self.piece, whole, net.mate, net.shard)

    def hand(self, way, k, here, piece):
        net = self.net
        net.put(self.events[way + 4, k], piece, piece, self.far, net.shard, here)
        net.put(self.events[way + 2, k], piece, piece, net.mate, net.shard, here)

    def along(self, k):
        net, (spot, here) = self.net, self.spots[k]
        piece = self.view(net.core, spot, 0)
        net.got(self.events[0, k], piece, here)
        if -3 < k < 0:
            net.put(self.events[0, k - 1], piece, piece, net.rep, net.up, self.line.onward[k])
        if 0 < k < 3:
            net.put(self.events[0, k + 1], piece, piece, net.rep, net.down, self.line.back[k])
        net.put(self.events[1, k], piece, piece, net.rep, net.across, here)
        self.hand(0, k, here, piece)

    def over(self, k):
        net, here = self.net, self.spots[k][1]
        piece = self.view(net.core, self.flips[k], 0)
        net.got(self.events[1, k], piece, here)
        self.hand(1, k, here, piece)

    def relay(self, way, k):
        net, here = self.net, self.spots[k][1]
        spot = self.spots[k][0] if way == 0 else self.flips[k]
        piece = self.view(net.core, spot, 1)
        net.got(self.events[way + 4, k], piece, here)
        net.put(self.events[way + 6, k], piece, piece, net.mate, net.shard, here)

    def finish(self):
        net, other = self.net, 1 - self.net.core
        net.got(self.events[2, 0], self.bank.at[other, net.shard])
        for k in (0, 1, -1, 2, -2, 3, -3):
            spot, here = self.spots[k]
            if k:
                net.got(self.events[2, k], self.view(other, spot, 0), here)
                net.got(self.events[6, k], self.view(other, spot, 1), here)
            net.got(self.events[3, k], self.view(other, self.flips[k], 0), here)
            net.got(self.events[7, k], self.view(other, self.flips[k], 1), here)


def exchange(net, sources, targets):
    events = [net.event() for _ in range(3)]
    for o in (2, 3, 1):
        net.put(events[o - 1], sources[o - 1], targets[o - 1], net.cousins[o], net.shard)
    return [(events[o], targets[o]) for o in range(3)]


def head_kernel(
    routes, routes_t, cot, x, wq_in, wk_in, wv_in, wo_in, small, cosine, sine,
    e_gate, e_up, e_down, s_gate, s_up, s_down,
    *refs,
):
    width = x.shape[1]
    half = width // SLOTS
    outs, (c1, c2, c3, experts) = refs[:13], refs[13:17]
    bank, packed, piece, e_raw, s_raw, pack_sems, out_sems, send, recv, own_sem = refs[17:27]
    rank, slot, q, k, v, wq, wk, wv, wo, ext, c0, expert_piece, shared_piece = refs[27:]
    stores = copies_of(zip(refs[27:], outs), out_sems)
    net = Net(send, recv)
    units = s_raw.shape[0]
    cut = pl.ds(pl.multiple_of(net.core * units, 128), units)
    packs = copies_of(
        (
            (e_gate.at[net.rep], expert_piece.at[0]),
            (e_up.at[net.rep], expert_piece.at[1]),
            (e_down.at[net.rep], e_raw),
            (s_gate.at[:, cut], shared_piece.at[0]),
            (s_up.at[:, cut], shared_piece.at[1]),
            (s_down.at[cut, :], s_raw),
        ),
        pack_sems,
    )
    for copy in packs:
        copy.start()
    for core, (low, high) in enumerate(((wq_in, wk_in), (wv_in, wo_in))):

        @pl.when(net.core == core)
        def _():
            piece[0:half, :] = low[...]
            piece[half : 2 * half, :] = high[...]

    piece[2 * half : 2 * half + 16, :] = small[...]
    line = Line(net, bank)
    e_events = [net.event() for _ in range(3)]
    mine, most = experts.at[net.shard], experts.at[net.shard, pl.ds(0, 2)]
    peers = [(net.cousins[o], net.shard) for o in (1, 2, 3)]
    net.meet("line", peers + [(net.rep, net.across)])
    line.spread(0, piece)
    own = pltpu.make_async_copy(piece, bank.at[net.core, net.shard], own_sem)
    own.start()
    route_slots(net.rep, routes, routes_t, rank, slot)
    events = [net.event() for _ in range(3)]
    for o, far in ((2, c2), (3, c3), (1, c1)):
        pack_row(net.rep, rank, cot, o, packed.at[o - 1])
        net.put(events[o - 1], packed.at[o - 1], far, net.cousins[o], net.shard)
    arrivals = [(events[0], c1), (events[1], c2), (events[2], c3)]
    pack_row(net.rep, rank, cot, 0, c0)
    for copy in packs:
        copy.wait()
    expert_piece[2] = e_raw[...].astype(F32).T.astype(BF)
    shared_piece[2] = s_raw[...].astype(F32).T.astype(BF)
    line.along(1)
    line.along(-1)
    line.over(0)
    line.along(2)
    line.along(-2)
    net.put(e_events[0], expert_piece, mine, net.rep, net.up, net.z < 3)
    net.put(e_events[1], expert_piece, mine, net.rep, net.down, net.z > 0)
    line.over(1)
    line.over(-1)
    line.along(3)
    line.along(-3)
    net.put(e_events[2], expert_piece.at[pl.ds(0, 2)], most, net.rep, net.across)
    for step in (2, -2, 3, -3):
        line.over(step)
    own.wait()
    line.finish()
    gathered = bank[0, 0, 2 * half : 2 * half + 16, :].astype(F32)
    for j in range(1, SLOTS):
        gathered = gathered + bank[0, j, 2 * half : 2 * half + 16, :].astype(F32)
    ext[...] = gathered
    for j in range(SLOTS):
        at = slice(j * half, (j + 1) * half)
        wq[at, :] = bank[0, j, 0:half, :]
        wk[at, :] = bank[0, j, half : 2 * half, :]
        wv[at, :] = bank[1, j, 0:half, :]
        wo[at, :] = bank[1, j, half : 2 * half, :]
    qkv_rows(x, ext, cosine, sine, wq, wk, wv, q, k, v)
    for copy in stores:
        copy.start()
    for event, like in arrivals:
        net.got(event, like)
    net.got(e_events[0], mine, net.z > 0)
    net.got(e_events[1], mine, net.z < 3)
    net.got(e_events[2], most)
    for copy in stores:
        copy.wait()
    net.close()


def plain_head_kernel(
    routes, routes_t, cot, x, cosine, sine, wq, wk, wv, ext,
    rank, slot, q, k, v, c0, c1, c2, c3,
):
    rep = lax.axis_index("rep")
    route_slots(rep, routes, routes_t, rank, slot)
    pack_rows(rep, rank, cot, (c0, c1, c2, c3))
    qkv_rows(x, ext, cosine, sine, wq, wk, wv, q, k, v)


def fill_bias(starts, bias):
    tokens = bias.shape[0]

    def tile(t, carry):
        at = pl.ds(pl.multiple_of(t * TILE, TILE), TILE)
        query = iota((TILE, tokens), 0) + t * TILE
        key = iota((TILE, tokens), 1)
        allowed = key <= query
        for n in range(2):
            begin = starts[0, n]
            inside = (query >= begin) & (query < begin + PIECE)
            allowed = allowed | (inside & (key >= begin) & (key < begin + PIECE))
        bias[at, :] = jnp.where(allowed, 0.0, MASKED)
        return carry

    lax.fori_loop(0, tokens // TILE, tile, 0)


def keep_half(block, h):
    low = iota(block.shape, 1) < 64
    return jnp.where(low if h == 0 else ~low, block.astype(F32), 0.0).astype(BF)


def biased(scores, bias, begin, free, end):
    tail = scores[:, free:] + bias[begin : begin + TILE, free:end]
    return tail if free == 0 else jnp.concatenate([scores[:, :free], tail], axis=1)


def attend_pairs(q, k, v, out, lse, bias, step):
    tokens, width = q.shape

    def pair(i, carry):
        step(i)
        cols = pl.ds(pl.multiple_of(i * 128, 128), 128)
        keys = k[:, cols]
        low = iota((tokens, 128), 1) < 64
        values = v[:, cols].astype(F32)
        value_one = [
            jnp.where(low, values, 1.0).astype(BF),
            jnp.where(low, 1.0, values).astype(BF),
        ]
        low = iota((TILE, 128), 1) < 64
        for t in range(tokens // TILE):
            begin = t * TILE
            end = min(tokens, begin + TILE + PIECE)
            block = q[begin : begin + TILE, cols]
            results, totals = [], []
            for h in range(2):
                scores = nt(keep_half(block, h), keys[:end])
                scores = biased(scores, bias, begin, begin, end)
                row_max = jnp.max(scores, axis=1, keepdims=True)
                probs = jnp.exp(scores - row_max).astype(BF)
                mixed = nn(probs, value_one[h][:end])
                total = pltpu.roll(mixed, 64, 1)
                results.append(mixed / total)
                totals.append(row_max + jnp.log(total))
            out[begin : begin + TILE, cols] = jnp.where(low, results[0], results[1]).astype(BF)
            lse[begin : begin + TILE, cols] = jnp.where(low, totals[0], totals[1])
        return carry

    lax.fori_loop(0, width // 128, pair, 0)


def router_rows(ext):
    rows = jnp.where(iota(ext.shape, 0) < 4, ext[...], 0.0)
    return jnp.concatenate([rows, jnp.zeros((112, ext.shape[1]), F32)], axis=0).astype(BF)


def route_probs(normed, router):
    logits = nt(normed, router)
    logits = jnp.where(iota(logits.shape, 1) < 4, logits, MASKED)
    raised = jnp.exp(logits - jnp.max(logits, axis=1, keepdims=True))
    return raised / jnp.sum(raised, axis=1, keepdims=True)


def middle_rows(rep, x, attended, wo, ext, rank, middle, normed, probs, packed):
    tokens = x.shape[0]
    gain = ext[5:6, :]
    router = router_rows(ext)

    def tile(t, carry):
        at = pl.ds(pl.multiple_of(t * TILE, TILE), TILE)
        rows = x[at, :].astype(F32) + nn(attended[at, :], wo[...])
        scale = lax.rsqrt(jnp.mean(rows * rows, axis=1, keepdims=True) + EPSILON)
        middle[at, :] = rows
        unit = (rows * scale * gain).astype(BF)
        normed[at, :] = unit
        probs[at, :] = route_probs(unit, router)
        return carry

    lax.fori_loop(0, tokens // TILE, tile, 0)
    pack_rows(rep, rank, normed, packed)


def forward_kernel(
    starts, q, k, v, x, wo, ext, rank, shared_piece, expert_piece, expert_in,
    *refs,
):
    outs, shared_bank, experts = refs[:9], refs[9], refs[10]
    bias, out_sems, send, recv = refs[11:15]
    attended, lse, middle, normed, probs, x0, x1, x2, x3 = refs[15:]
    stores = copies_of(zip(refs[15:], outs), out_sems)
    net = Net(send, recv)
    spread = Spread(net, shared_piece, shared_bank)
    events = [net.event() for _ in range(4)]
    inner = (net.z > 0) & (net.z < 3)
    low, high = experts.at[net.down], experts.at[net.up]
    rest, last = experts.at[net.shard, pl.ds(2, 1)], expert_piece.at[pl.ds(2, 1)]
    near = experts.at[net.place(1, 0), pl.ds(0, 2)]
    net.meet("line", [(net.mate, net.shard), (net.rep, net.across), (spread.far, net.shard)])
    spread.begin()
    fill_bias(starts, bias)

    def step(i):
        @pl.when(i == 1)
        def _():
            spread.along(1)
            spread.along(-1)
            spread.over(0)

        @pl.when(i == 3)
        def _():
            spread.along(2)
            spread.along(-2)
            spread.over(1)
            spread.over(-1)

        @pl.when(i == 5)
        def _():
            spread.along(3)
            spread.along(-3)
            net.put(events[0], low, low, net.rep, net.up, inner)
            net.put(events[1], high, high, net.rep, net.down, inner)
            net.put(events[2], last, rest, net.rep, net.across)
            net.put(events[3], near, near, net.rep, net.across)
            spread.over(2)
            spread.over(-2)

    attend_pairs(q, k, v, attended, lse, bias, step)
    for copy in stores[:2]:
        copy.start()
    spread.over(3)
    spread.over(-3)
    for way, k_step in ((1, 0), (0, 1), (0, -1)):
        spread.relay(way, k_step)
    middle_rows(net.rep, x, attended, wo, ext, rank, middle, normed, probs, (x0, x1, x2, x3))
    for copy in stores[2:]:
        copy.start()
    for way, k_step in ((1, 1), (1, -1), (0, 2), (0, -2), (1, 2), (1, -2)):
        spread.relay(way, k_step)
    for way, k_step in ((0, 3), (0, -3), (1, 3), (1, -3)):
        spread.relay(way, k_step)
    spread.finish()
    net.got(events[0], low, net.z > 1)
    net.got(events[1], low, net.z < 2)
    net.got(events[2], rest)
    net.got(events[3], near)
    for copy in stores:
        copy.wait()
    net.close()


def plain_forward_kernel(
    starts, q, k, v, x, wo, ext, rank,
    attended, lse, middle, normed, probs, x0, x1, x2, x3, bias,
):
    fill_bias(starts, bias)
    attend_pairs(q, k, v, attended, lse, bias, lambda i: None)
    rep = lax.axis_index("rep")
    middle_rows(rep, x, attended, wo, ext, rank, middle, normed, probs, (x0, x1, x2, x3))


CHUNK, CHUNKS = 512, 4


def unit_bank(
    expert, ext, xs, cs, source, target, before, unit, outs, dxs, scratch, ready=None,
    emit=None,
):
    out_acc, dx_acc, gate, wbuf, stage, dw_out, in_sems, out_sems, xc = scratch[:9]
    routed = expert is not None
    blocks, rows = len(xs), xs[0].shape[0]
    per = CHUNK // unit

    def loads(of, buffer, sems, k, b):
        return [
            pltpu.make_async_copy(
                of(k * per + i), buffer.at[b, :, :, pl.ds(i * unit, unit)], sems.at[b, i]
            )
            for i in range(per)
        ]

    def stores(k, b):
        return [
            pltpu.make_async_copy(
                dw_out.at[b, :, :, pl.ds(i * unit, unit)],
                target(k * per + i),
                out_sems.at[b, i],
            )
            for i in range(per)
        ]

    def start_loads(k, b):
        if ready is not None:
            ready(k)
        for copy in loads(source, wbuf, in_sems, k, b):
            copy.start()
        if before is not None:
            for copy in loads(before, scratch[9], scratch[10], k, b):
                copy.start()

    start_loads(0, 0)
    for n in range(blocks):
        xc[0, n * rows : (n + 1) * rows, :] = xs[n][...]
        xc[1, n * rows : (n + 1) * rows, :] = cs[n][...]
    if routed:
        router = router_rows(ext)
        for n in range(blocks):
            probs = route_probs(xs[n][...], router)
            lane = iota(probs.shape, 1)
            gate[n] = jnp.sum(jnp.where(lane == expert, probs, 0.0), axis=1, keepdims=True)

    def chunk(k, carry):
        b = lax.rem(k, 2)
        for copy in loads(source, wbuf, in_sems, 0, b):
            copy.wait()
        for n in range(blocks):
            x, c = xs[n][...], cs[n][...]
            wg, wu, wd = wbuf[b, 0], wbuf[b, 1], wbuf[b, 2]
            gate_h, up_h, back_h = nn(x, wg), nn(x, wu), nn(c, wd)
            sigma = 0.5 * jnp.tanh(0.5 * gate_h) + 0.5
            silu = gate_h * sigma
            hidden = silu * up_h
            if routed:
                share = gate[n]
                scaled = back_h * share
                weighted = (hidden * share).astype(BF)
            else:
                scaled, weighted = back_h, hidden.astype(BF)
            d_up = (scaled * silu).astype(BF)
            d_gate = (scaled * up_h * (sigma + silu * (1.0 - sigma))).astype(BF)
            product = nt(hidden.astype(BF), wd)
            d_rows = nt(d_gate, wg) + nt(d_up, wu)
            at = slice(n * rows, (n + 1) * rows)
            stage[0, at, :] = d_gate
            stage[1, at, :] = d_up
            stage[2, at, :] = weighted
            if routed:
                pairs = (hidden * back_h).astype(BF)
                d_share = nt(jnp.ones((16, CHUNK), BF), pairs)

            @pl.when(k == 0)
            def _():
                out_acc[n] = product
                dx_acc[n, 0:rows, :] = d_rows
                if routed:
                    dx_acc[n, rows : rows + 16, :] = jnp.zeros((16, d_rows.shape[1]), F32)
                    dx_acc[n, rows : rows + 16, 0:rows] = d_share

            @pl.when(k != 0)
            def _():
                out_acc[n] += product
                dx_acc[n, 0:rows, :] += d_rows
                if routed:
                    dx_acc[n, rows : rows + 16, 0:rows] += d_share

        for nxt in range(1, CHUNKS):

            @pl.when(k + 1 == nxt)
            def _():
                start_loads(nxt, nxt % 2)

        @pl.when(k >= 2)
        def _():
            for copy in stores(0, b):
                copy.wait()

        if before is not None:
            for copy in loads(before, scratch[9], scratch[10], 0, b):
                copy.wait()
        for i in range(3):
            part = tn(xc[i // 2], stage[i])
            if before is not None:
                part = part + scratch[9][b, i].astype(F32)
            dw_out[b, i] = part.astype(BF)
        for now in range(CHUNKS):

            @pl.when(k == now)
            def _():
                for copy in stores(now, now % 2):
                    copy.start()
                if emit is not None:
                    emit(now)

        return carry

    lax.fori_loop(0, CHUNKS, chunk, 0)
    for n in range(blocks):
        outs[n][...] = out_acc[n].astype(BF)
        dxs[n][...] = dx_acc[n].astype(BF)
    for b in range(2):
        for copy in stores(0, b):
            copy.wait()


def unit_scratch(blocks, rows, extra, width, per, chained):
    scratch = [
        pltpu.VMEM((blocks, rows, width), F32),
        pltpu.VMEM((blocks, rows + extra, width), F32),
        pltpu.VMEM((blocks, rows, 1), F32),
        pltpu.VMEM((2, 3, width, CHUNK), BF),
        pltpu.VMEM((3, blocks * rows, CHUNK), BF),
        pltpu.VMEM((2, 3, width, CHUNK), BF),
        pltpu.SemaphoreType.DMA((2, per)),
        pltpu.SemaphoreType.DMA((2, per)),
        pltpu.VMEM((2, blocks * rows, width), BF),
    ]
    if chained:
        scratch += [
            pltpu.VMEM((2, 3, width, CHUNK), BF),
            pltpu.SemaphoreType.DMA((2, per)),
        ]
    return scratch


def shared_kernel(
    x, c, piece, bank, x1, x2, x3, expert_in,
    out, dx, grads_own, grads_other, shared_mate, y1, y2, y3, experts,
    send, recv, *scratch,
):
    net = Net(send, recv)
    events = [net.event() for _ in range(4)]
    core_events = [net.event() for _ in range(8)]
    peers = [(net.cousins[o], net.shard) for o in (1, 2, 3)]
    net.meet("line", peers + [(net.rep, net.across)])
    arrivals = exchange(net, (x1, x2, x3), (y1, y2, y3))
    near, second = experts.at[net.place(1, 0), pl.ds(2, 1)], experts.at[net.place(2, 0)]
    net.put(events[0], near, near, net.rep, net.across)
    net.put(events[1], second, second, net.rep, net.across)
    below = experts.at[lax.max(net.shard - 4, net.x)]
    above = experts.at[lax.min(net.shard + 4, 6 + net.x)]
    net.put(events[2], below, below, net.rep, net.up, net.z == 2)
    net.put(events[3], above, above, net.rep, net.down, net.z == 1)
    spots = [net.place(n % 4, n // 4 % 2) for n in range(8)]
    halves = [net.core, 1 - net.core]
    done = scratch[5]
    slices = [done.at[n // 4, :, :, pl.ds(n % 4 * 128, 128)] for n in range(8)]
    places = [shared_mate.at[spot] for spot in spots]

    def source(n):
        return piece if n == 0 else bank.at[halves[n // 8], spots[n % 8]]

    def target(n):
        return (grads_own, grads_other)[n // 8].at[spots[n % 8]]

    def emit(now):
        if now >= 2:
            for n in range(4 * now - 8, 4 * now - 4):
                net.put(core_events[n], slices[n], places[n], net.mate, net.shard)

    unit_bank(
        None, None, [x], [c], source, target, None, 128, [out], [dx], scratch, None, emit
    )
    for event, like in arrivals:
        net.got(event, like)
    net.got(events[0], near)
    net.got(events[1], second)
    net.got(events[2], second, net.z == 3)
    net.got(events[3], second, net.z == 0)
    for n in range(8):
        net.got(core_events[n], places[n])
    net.close()


def far_kernel(
    ext, xa, xb, ca, cb, expert_piece, shared_own, shared_mate, expert_in,
    oa, ob, da, db, grads, shared_keep, shared_y, experts,
    part_a, part_b, part_sems, send, recv, *scratch,
):
    net = Net(send, recv)
    events = [net.event() for _ in range(9)]
    far = net.cousins[2]
    parts = copies_of(((shared_own, part_a), (shared_mate, part_b)), part_sems)
    for copy in parts:
        copy.start()
    net.meet("none", [(net.rep, net.across), (far, net.shard)])
    last = experts.at[net.place(3, 0)]
    net.put(events[0], last, last, net.rep, net.across)
    spots = [net.place(n // 2, n % 2) for n in range(8)]
    y, quarter = lax.div(net.rep, 2), part_a.shape[2] // 2
    rows = [pl.ds(pl.multiple_of(n * quarter, 128), quarter) for n in (y, 1 - y)]
    keep = pltpu.make_async_copy(part_a.at[:, :, rows[0], :], shared_keep, part_sems.at[2])
    away = [part_a.at[j, :, rows[1], :] for j in range(SLOTS)]

    def source(n):
        return expert_piece if n == 0 else experts.at[spots[n]]

    def target(n):
        return grads.at[spots[n]]

    def ready(k):
        if k == 3:
            net.got(events[0], last)

    for copy in parts:
        copy.wait()

    def add(j, carry):
        part_a[j] = part_a[j] + part_b[j]
        return carry

    lax.fori_loop(0, SLOTS, add, 0)
    for j in range(SLOTS):
        net.put(events[1 + j], away[j], shared_y.at[j], far, net.shard)
    keep.start()
    unit_bank(
        net.rep, ext, [xa, xb], [ca, cb], source, target, None, 256, [oa, ob], [da, db],
        scratch, ready,
    )
    keep.wait()
    for j in range(SLOTS):
        net.got(events[1 + j], shared_y.at[j])
    net.close()


def near_kernel(
    ext, xa, xb, ca, cb, expert_piece, experts, before, far_a, far_b,
    shared_keep, shared_y,
    oa, ob, da, shared_total, grads, back_a, back_b, back_c, expert_x,
    db, part_a, part_b, from_x, from_z, third, sems, send, recv, *scratch,
):
    net = Net(send, recv)
    events = [net.event() for _ in range(4)]
    x_events = [net.event() for _ in range(4)]
    z_events = [net.event() for _ in range(3)]
    peers = [(net.cousins[o], net.shard) for o in (1, 2, 3)]
    one = pltpu.make_async_copy(shared_keep, part_a, sems.at[0])
    two = pltpu.make_async_copy(shared_y, part_b, sems.at[1])
    one.start()
    two.start()
    net.meet("all", peers + [(net.rep, net.across)])
    net.put(events[0], far_a, back_a, net.cousins[2], net.shard)
    net.put(events[1], far_b, back_b, net.cousins[3], net.shard)
    one.wait()
    two.wait()

    def add(j, carry):
        part_a[j] = part_a[j] + part_b[j]
        return carry

    lax.fori_loop(0, SLOTS, add, 0)
    mine = [net.cycle(d) for d in range(4)]
    theirs = [spot + 1 - 2 * net.x for spot in mine]
    for d in (2, 1, 3, 0):
        net.put(x_events[d], part_a.at[theirs[d]], from_x.at[d], net.rep, net.across)
    pieces, lands = [part_a.at[spot] for spot in mine], [from_x.at[d] for d in range(4)]
    ends = [from_z.at[d] for d in range(3)]
    spots = [net.place(3 - n // 2, n % 2) for n in range(8)]
    own_slot = 6
    done, target = scratch[5], expert_x.at[net.levels[3]]

    def source(n):
        return expert_piece if n == own_slot else experts.at[spots[n]]

    def ready(k):
        if k == 2:
            for d in (2, 1, 3, 0):
                net.got(x_events[d], lands[d])
                part_a[mine[d]] = part_a[mine[d]] + from_x[d]
                if d:
                    net.put(z_events[d - 1], pieces[d], ends[d - 1], net.rep, mine[d])

    def emit(now):
        if now == 0:
            third[...] = done[0, :, :, 256:512]
            net.put(events[3], third, target, net.rep, net.across)

    unit_bank(
        net.rep, ext, [xa, xb], [ca, cb], source,
        lambda n: grads.at[spots[n]], lambda n: before.at[spots[n]],
        256, [oa, ob], [da, db], scratch, ready, emit,
    )
    net.put(events[2], db, back_c, net.mate, net.shard)
    total = part_a[mine[0]].astype(F32)
    for d in (1, 2, 3):
        net.got(z_events[d - 1], ends[d - 1])
        total = total + from_z[d - 1].astype(F32)
    shared_total[...] = total.astype(BF)
    net.got(events[0], back_a)
    net.got(events[1], back_b)
    net.got(events[2], back_c)
    net.got(events[3], target)
    net.close()


def plain_bank_kernel(blocks, unit, routed, chained, ext, *refs):
    refs = list(refs)

    def take(n):
        taken = refs[:n]
        del refs[:n]
        return taken

    xs, cs = take(blocks), take(blocks)
    bank = take(1)[0]
    before = take(1)[0] if chained else None
    outs, dxs = take(blocks), take(blocks)
    grads = take(1)[0]
    unit_bank(
        lax.axis_index("rep") if routed else None,
        ext, xs, cs,
        lambda n: bank.at[n],
        lambda n: grads.at[n],
        (lambda n: before.at[n]) if chained else None,
        unit, outs, dxs, refs,
    )


def plain_bank(ext, xs, cs, bank, before, routed):
    blocks, (rows, width) = len(xs), xs[0].shape
    chained = before is not None
    extra, unit = (16 if routed else 0), bank.shape[3]
    operands = [ext, *xs, *cs, bank] + ([before] if chained else [])
    outs = [shape((rows, width))] * blocks + [shape((rows + extra, width))] * blocks
    results = call(
        functools.partial(plain_bank_kernel, blocks, unit, routed, chained),
        outs + [shape(bank.shape)],
        [VMEM] * (1 + 2 * blocks) + [ANY] * (2 if chained else 1),
        [VMEM] * (2 * blocks) + [ANY],
        unit_scratch(blocks, rows, extra, width, CHUNK // unit, chained),
        flops=18 * blocks * rows * width * 4 * CHUNK,
        moved=30 * 2**20,
    )(*operands)
    return results[:blocks], results[blocks : 2 * blocks], results[2 * blocks]


def combine_rows(
    slot, d0, d1, d2, d3, d_shared, probs, middle, normed, cot, ext, attended, wo,
    d_middle, d_attended, grad_wo, grad_ext, branch, router_acc, gain_acc,
):
    tokens, width = middle.shape
    rep = lax.axis_index("rep")
    gain = ext[5:6, :]
    router = router_rows(ext)
    router_acc[...] = jnp.zeros_like(router_acc)
    gain_acc[...] = jnp.zeros_like(gain_acc)

    def tile(t, carry):
        at = pl.ds(pl.multiple_of(t * TILE, TILE), TILE)
        slot_one, slot_two = slot[at, 0:1], slot[at, 64:65]
        d_normed = d_shared[at, :].astype(F32)
        lane = iota((TILE, 128), 1)
        d_gates = jnp.zeros((TILE, 128), F32)
        for o, d in enumerate((d0, d1, d2, d3)):
            place = (iota((TILE, CAP), 1) + o * CAP).astype(F32)
            hit = (place == slot_one) | (place == slot_two)
            d_normed = d_normed + nn(ones_where(hit), d[0:CAP, :])
            share = d[CAP : CAP + 16, 0:CAP].astype(F32)[0:1, :]
            d_share = jnp.sum(jnp.where(hit, share, 0.0), axis=1, keepdims=True)
            d_gates = d_gates + jnp.where(lane == sibling(rep, o), d_share, 0.0)
        p = probs[at, :]
        inner = jnp.sum(d_gates * p, axis=1, keepdims=True)
        d_logits = (p * (d_gates - inner)).astype(BF)
        d_normed = d_normed + nn(d_logits, router)
        router_acc[...] += tn(d_logits, normed[at, :])
        rows = middle[at, :]
        scale = lax.rsqrt(jnp.mean(rows * rows, axis=1, keepdims=True) + EPSILON)
        unit = rows * scale
        gain_acc[...] += jnp.sum((d_normed * unit).reshape(TILE // 8, 8, width), axis=0)
        w = d_normed * gain
        inner = jnp.mean(w * unit, axis=1, keepdims=True)
        total = cot[at, :].astype(F32) + scale * (w - unit * inner)
        d_middle[at, :] = total
        rounded = total.astype(BF)
        branch[at, :] = rounded
        d_attended[at, :] = nt(rounded, wo[...]).astype(BF)
        return carry

    lax.fori_loop(0, tokens // TILE, tile, 0)
    grad_wo[...] = tn(attended[...], branch[...]).astype(BF)
    row = iota((16, width), 0)
    total = jnp.sum(gain_acc[...], axis=0, keepdims=True)
    grad_ext[...] = jnp.where(row < 4, router_acc[0:16, :], jnp.where(row == 5, total, 0.0))


def output_rows(slot, o0, o1, o2, o3, shared, probs, middle, out, first, last):
    rep = lax.axis_index("rep")

    def tile(t, carry):
        at = pl.ds(pl.multiple_of(t * TILE, TILE), TILE)
        slot_one, slot_two = slot[at, 0:1], slot[at, 64:65]
        total = middle[at, :] + shared[at, :].astype(F32)
        p = probs[at, :]
        lane = iota((TILE, 128), 1)
        for o, rows in enumerate((o0, o1, o2, o3)):
            place = (iota((TILE, CAP), 1) + o * CAP).astype(F32)
            hit = (place == slot_one) | (place == slot_two)
            share = jnp.sum(jnp.where(lane == sibling(rep, o), p, 0.0), axis=1, keepdims=True)
            total = total + nn(jnp.where(hit, share, 0.0).astype(BF), rows[...])
        out[at, :] = total.astype(BF)
        return carry

    lax.fori_loop(first, last, tile, 0)


def back_pairs(
    q, k, v, d_out, out, lse, cosine, sine, dq, dk, dv, bias, dk_acc, dv_acc, step
):
    tokens, width = q.shape

    def pair(i, carry):
        step(i)
        cols = pl.ds(pl.multiple_of(i * 128, 128), 128)
        keys, values = k[:, cols], v[:, cols]
        half_keys = [keep_half(keys, 0), keep_half(keys, 1)]
        dk_acc[...] = jnp.zeros_like(dk_acc)
        dv_acc[...] = jnp.zeros_like(dv_acc)
        low = iota((TILE, 128), 1) < 64
        for t in range(tokens // TILE):
            begin = t * TILE
            end = min(tokens, begin + TILE + PIECE)
            at = slice(begin, begin + TILE)
            block, grad = q[at, cols], d_out[at, cols]
            product = grad.astype(F32) * out[at, cols].astype(F32)
            block_lse = lse[at, cols]
            d_block = None
            for h in range(2):
                block_h, grad_h = keep_half(block, h), keep_half(grad, h)
                scores = nt(block_h, keys[:end])
                scores = biased(scores, bias, begin, begin, end)
                probs = jnp.exp(scores - block_lse[:, 64 * h : 64 * h + 1])
                d_probs = nt(grad_h, values[:end])
                inner = jnp.sum(
                    jnp.where(low if h == 0 else ~low, product, 0.0), axis=1, keepdims=True
                )
                d_scores = (probs * (d_probs - inner)).astype(BF)
                part = nn(d_scores, half_keys[h][:end])
                d_block = part if d_block is None else d_block + part
                dk_acc[0:end, :] += tn(d_scores, block_h)
                dv_acc[0:end, :] += tn(probs.astype(BF), grad_h)
            dq[at, cols] = spin(d_block * 0.125, cosine[at, :], -sine[at, :]).astype(BF)
        dk[:, cols] = spin(dk_acc[...], cosine[...], -sine[...]).astype(BF)
        dv[:, cols] = dv_acc[...].astype(BF)
        return carry

    lax.fori_loop(0, width // 128, pair, 0)


def copies_of(pairs, sems):
    return [pltpu.make_async_copy(a, b, sems.at[i]) for i, (a, b) in enumerate(pairs)]


def fetch(sources, targets, sems):
    copies = copies_of(zip(sources, targets), sems)
    for copy in copies:
        copy.start()
    for copy in copies:
        copy.wait()


class Chain:
    def __init__(self, net, own, from_x, up_in, down_in, held, spare, sems):
        self.net, self.own, self.from_x = net, own, from_x
        self.up_in, self.down_in = up_in, down_in
        self.held, self.spare, self.sems = held, spare, sems
        self.events = {(way, d): net.event() for way in range(2) for d in (1, 2, 3)}
        self.spots = [net.place(n, 0) for n in range(4)]
        self.sends, self.gets = {}, {}
        z = net.z
        for d in (1, 2, 3):
            self.sends[0, d] = (held.at[lax.min(z + d, 3)], z < 4 - d)
            self.sends[1, d] = (held.at[lax.max(z - d, 0)], z > d - 1)
            self.gets[0, d] = (lax.min(z + d - 1, 3), (z > 0) & (z < 5 - d))
            self.gets[1, d] = (lax.max(z - d + 1, 0), (z < 3) & (z > d - 2))

    def level(self, n):
        to = self.net.levels[n]
        far = self.from_x.at[to]
        fetch([self.own.at[self.spots[n]], far], [self.held.at[to], self.spare.at[0]], self.sems)
        self.held[to] = self.held[to] + self.spare[0]

    def send(self, d):
        net = self.net
        for way, to, into in ((0, net.up, self.up_in), (1, net.down, self.down_in)):
            source, here = self.sends[way, d]
            net.put(self.events[way, d], source, into.at[d - 1], net.rep, to, here)

    def take(self, d):
        for way, into in ((0, self.up_in), (1, self.down_in)):
            to, here = self.gets[way, d]

            def add():
                self.net.copy(
                    self.events[way, d], into.at[d - 1], into.at[d - 1],
                    self.net.mate, self.net.shard,
                ).wait_recv()
                fetch([into.at[d - 1]], [self.spare.at[0]], self.sems)
                self.held[to] = self.held[to] + self.spare[0]

            when(here, add)


BACK_ROWS = 19


def back_kernel(starts, *refs):
    raw, refs = refs[:BACK_ROWS], refs[BACK_ROWS:]
    o1, o2, o3, grads, expert_x_in = refs[:5]
    outs, expert_total = refs[5:11], refs[11]
    r1, r2, r3, up_in, down_in, expert_x = refs[12:18]
    d_attended, branch, router_acc, gain_acc, bias, dk_acc, dv_acc = refs[18:25]
    local = refs[25 : 25 + BACK_ROWS]
    held, spare, sems, load_sems, out_sems, send, recv = refs[25 + BACK_ROWS : 32 + BACK_ROWS]
    d_middle, grad_wo, grad_ext, dq, dk, dv = refs[32 + BACK_ROWS :]
    stores = copies_of(zip((d_middle, grad_wo, grad_ext, dq, dk, dv), outs), out_sems)
    slot, d0, d1, d2, d3, d_shared, probs, middle, normed, cot, ext, attended, wo = local[:13]
    cosine, sine, q, k, v, lse = local[13:]
    loads = copies_of(zip(raw, local), load_sems)
    for copy in loads:
        copy.start()
    net = Net(send, recv)
    x_events = [net.event() for _ in range(3)]
    chain = Chain(net, grads, expert_x, up_in, down_in, held, spare, sems)
    peers = [(net.cousins[o], net.shard) for o in (1, 2, 3)]
    net.meet("line", peers + [(net.rep, net.across)])
    targets = [expert_x.at[net.levels[n]] for n in range(3)]
    for n in (2, 1, 0):
        source = grads.at[net.place(n, 1)]
        net.put(x_events[n], source, targets[n], net.rep, net.across)
    arrivals = exchange(net, (o1, o2, o3), (r1, r2, r3))
    chain.level(3)
    chain.send(3)
    fill_bias(starts, bias)
    for copy in loads:
        copy.wait()
    combine_rows(
        slot, d0, d1, d2, d3, d_shared, probs, middle, normed, cot, ext, attended, wo,
        d_middle, d_attended, grad_wo, grad_ext, branch, router_acc, gain_acc,
    )
    for copy in stores[:3]:
        copy.start()
    net.got(x_events[2], targets[2])
    chain.level(2)
    chain.take(3)
    chain.send(2)

    def step(i):
        @pl.when(i == 3)
        def _():
            net.got(x_events[1], targets[1])
            chain.level(1)

        @pl.when(i == 4)
        def _():
            chain.take(2)
            chain.send(1)

    back_pairs(
        q, k, v, d_attended, attended, lse, cosine, sine, dq, dk, dv, bias, dk_acc, dv_acc, step
    )
    for copy in stores[3:]:
        copy.start()
    net.got(x_events[0], targets[0])
    chain.level(0)
    for event, like in arrivals:
        net.got(event, like)
    chain.take(1)
    expert_total[...] = held[net.z]
    for copy in stores:
        copy.wait()
    net.close()


def plain_back_kernel(
    starts, slot, d0, d1, d2, d3, d_shared, probs, middle, normed, cot, ext, attended, wo,
    q, k, v, lse, cosine, sine,
    d_middle, grad_wo, grad_ext, dq, dk, dv,
    d_attended, branch, router_acc, gain_acc, bias, dk_acc, dv_acc,
):
    combine_rows(
        slot, d0, d1, d2, d3, d_shared, probs, middle, normed, cot, ext, attended, wo,
        d_middle, d_attended, grad_wo, grad_ext, branch, router_acc, gain_acc,
    )
    fill_bias(starts, bias)
    back_pairs(
        q, k, v, d_attended, attended, lse, cosine, sine, dq, dk, dv, bias, dk_acc, dv_acc,
        lambda i: None,
    )


def norm_rows(x, ext, normed_all):
    gain = ext[4:5, :]

    def tile(t, carry):
        at = pl.ds(pl.multiple_of(t * TILE, TILE), TILE)
        rows = x[at, :].astype(F32)
        scale = lax.rsqrt(jnp.mean(rows * rows, axis=1, keepdims=True) + EPSILON)
        normed_all[at, :] = (rows * scale * gain).astype(BF)
        return carry

    lax.fori_loop(0, x.shape[0] // TILE, tile, 0)


def input_grad(x, ext, dq, dk, dv, wq, wk, wv, d_middle, grad_in, gain_acc, first, last):
    width = x.shape[1]
    gain = ext[4:5, :]

    def tile(t, carry):
        at = pl.ds(pl.multiple_of(t * TILE, TILE), TILE)
        rows = x[at, :].astype(F32)
        scale = lax.rsqrt(jnp.mean(rows * rows, axis=1, keepdims=True) + EPSILON)
        unit = rows * scale
        d_normed = nt(dq[at, :], wq[...]) + nt(dk[at, :], wk[...]) + nt(dv[at, :], wv[...])
        gain_acc[...] += jnp.sum((d_normed * unit).reshape(TILE // 8, 8, width), axis=0)
        w = d_normed * gain
        inner = jnp.mean(w * unit, axis=1, keepdims=True)
        grad_in[at, :] = d_middle[at, :] + scale * (w - unit * inner)
        return carry

    lax.fori_loop(first, last, tile, 0)


def tail_kernel(
    x, ext, dq, dk, dv, wq, wk, wv, grad_wo, grad_ext,
    d_middle_in, slot_in, o0_in, o1_in, o2_in, o3_in, shared_in, probs_in, middle_in,
    expert_total, shared_total,
    grad_in, outputs, weights, small, shared_far, shared_mate, shared_cross, e1, e2, e3,
    normed_all, gain_acc, gw, from_mate, from_x, from_z, from_y, result, from_core,
    tiny, tiny_in, d_middle, slot, o0, o1, o2, o3, shared_out, probs, middle, load_sems,
    send, recv,
):
    width = x.shape[1]
    half = width // SLOTS
    net = Net(send, recv)
    e_events = [net.event() for _ in range(3)]
    s_events = [net.event() for _ in range(3)]
    m_events = [net.event() for _ in range(2)]
    x_events = [[net.event() for _ in range(2)] for _ in range(4)]
    z_events = [[net.event() for _ in range(2)] for _ in range(3)]
    y_events = [net.event() for _ in range(2)]
    c_events = [net.event() for _ in range(2)]
    t_events = [net.event() for _ in range(6)]
    net.meet(
        "all", [(net.mate, net.shard), (net.cousins[2], net.shard), (net.rep, net.across)]
    )
    far = net.cousins[2]
    net.put(s_events[0], shared_total, shared_far, far, net.shard)
    net.put(s_events[1], shared_total, shared_mate, net.mate, net.shard)
    net.put(e_events[1], expert_total, e2, far, net.shard)
    net.put(e_events[0], expert_total, e1, net.mate, net.shard)
    pairs = (
        (d_middle_in, d_middle), (slot_in, slot), (o0_in, o0), (o1_in, o1), (o2_in, o2),
        (o3_in, o3), (shared_in, shared_out), (probs_in, probs), (middle_in, middle),
    )
    loads = [pltpu.make_async_copy(a, b, load_sems.at[i]) for i, (a, b) in enumerate(pairs)]
    for copy in loads:
        copy.start()
    norm_rows(x, ext, normed_all)
    spots = [lax.rem(i + 2 * net.core, 4) for i in range(4)]

    def rows_of(spot):
        return pl.ds(pl.multiple_of(spot * half, 32), half)

    mine = [rows_of(net.cycle(d)) for d in range(4)]
    theirs = [rows_of(net.cycle(d) + 1 - 2 * net.x) for d in range(4)]

    def hand(i):
        net.put(m_events[i], gw.at[2 + i], from_mate.at[i], net.mate, net.shard)

    def cross(i):
        net.got(m_events[i], from_mate.at[i])
        gw[i] = gw[i] + from_mate[i]
        for d in (2, 1, 3, 0):
            source = gw.at[i, theirs[d]]
            net.put(x_events[d][i], source, from_x.at[d, i], net.rep, net.across)

    gw[spots[0]] = tn(normed_all[...], dq[...]).astype(BF)
    gw[spots[2]] = tn(normed_all[...], dv[...]).astype(BF)
    hand(0)
    gw[spots[1]] = tn(normed_all[...], dk[...]).astype(BF)
    gw[spots[3]] = grad_wo[...]
    hand(1)
    cross(0)
    cross(1)
    gain_acc[...] = jnp.zeros_like(gain_acc)
    for copy in loads:
        copy.wait()
    count = x.shape[0] // TILE

    def inputs(first, last):
        input_grad(x, ext, dq, dk, dv, wq, wk, wv, d_middle, grad_in, gain_acc, first, last)

    def results(first, last):
        output_rows(
            slot, o0, o1, o2, o3, shared_out, probs, middle, outputs, first, last
        )

    def add_across(d, i):
        net.got(x_events[d][i], from_x.at[d, i])
        gw[i, mine[d], :] = gw[i, mine[d], :] + from_x[d, i]
        if d:
            net.put(
                z_events[d - 1][i], gw.at[i, mine[d]], from_z.at[d - 1, i],
                net.rep, net.cycle(d),
            )

    def add_along(i):
        total = gw[i, mine[0], :].astype(F32)
        for d in (1, 2, 3):
            net.got(z_events[d - 1][i], from_z.at[d - 1, i])
            total = total + from_z[d - 1, i].astype(F32)
        result[0, i] = total.astype(BF)
        net.put(y_events[i], result.at[0, i], from_y.at[i], far, net.shard)

    def tiny_add(n, target_rep, target_shard):
        net.got(t_events[n], tiny_in.at[n])
        tiny[n + 1] = (tiny[n].astype(F32) + tiny_in[n].astype(F32)).astype(BF)
        if target_rep is not None:
            source, target = tiny.at[n + 1], tiny_in.at[n + 1]
            net.put(t_events[n + 1], source, target, target_rep, target_shard)

    inputs(0, 2)
    add_across(2, 0)
    add_across(1, 0)
    inputs(2, 3)
    add_across(3, 0)
    inputs(3, count)
    add_across(0, 0)
    row = iota((16, width), 0)
    total = jnp.sum(gain_acc[...], axis=0, keepdims=True)
    tiny[0] = (grad_ext[...] + jnp.where(row == 4, total, 0.0)).astype(BF)
    net.put(t_events[0], tiny.at[0], tiny_in.at[0], net.mate, net.shard)
    results(0, 1)
    add_across(2, 1)
    tiny_add(0, net.rep, net.across)
    results(1, 2)
    add_across(1, 1)
    tiny_add(1, far, net.shard)
    add_along(0)
    results(2, 3)
    add_across(3, 1)
    tiny_add(2, None, None)
    for d in (1, 2, 3):
        net.put(t_events[2 + d], tiny.at[3], tiny_in.at[2 + d], net.rep, net.cycle(d))
    net.got(s_events[0], shared_far)
    net.put(s_events[2], shared_far, shared_cross, net.mate, net.shard)
    results(3, count)
    add_across(0, 1)
    net.got(e_events[1], e2)
    net.put(e_events[2], e2, e3, net.mate, net.shard)
    total = tiny[3].astype(F32)
    for d in (1, 2, 3):
        net.got(t_events[2 + d], tiny_in.at[2 + d])
        total = total + tiny_in[2 + d].astype(F32)
    small[...] = total.astype(BF).astype(F32)
    add_along(1)
    for i in range(2):
        net.got(y_events[i], from_y.at[i])
        result[1, i] = (result[0, i].astype(F32) + from_y[i].astype(F32)).astype(BF)
        net.put(c_events[i], result.at[1, i], from_core.at[i], net.mate, net.shard)
        weights[spots[i]] = result[1, i].astype(F32)
    for i in range(2):
        net.got(c_events[i], from_core.at[i])
        weights[spots[2 + i]] = from_core[i].astype(F32)
    net.got(e_events[0], e1)
    net.got(s_events[1], shared_mate)
    net.got(s_events[2], shared_cross)
    net.got(e_events[2], e3)
    net.close()


def plain_tail_kernel(
    x, ext, dq, dk, dv, wq, wk, wv, d_middle,
    slot, o0, o1, o2, o3, shared_out, probs, middle,
    grad_in, outputs, gw, gain, normed_all, gain_acc,
):
    norm_rows(x, ext, normed_all)
    for i, d in enumerate((dq, dk, dv)):
        gw[i] = tn(normed_all[...], d[...]).astype(BF)
    gain_acc[...] = jnp.zeros_like(gain_acc)
    count = x.shape[0] // TILE
    input_grad(x, ext, dq, dk, dv, wq, wk, wv, d_middle, grad_in, gain_acc, 0, count)
    gain[...] = gain_acc[...]
    output_rows(
        slot, o0, o1, o2, o3, shared_out, probs, middle, outputs, 0, x.shape[0] // TILE
    )


def finish_kernel(
    e0, e1, e2, e3, wide, plain, q0, q1, q2, q3, weights, small,
    gate, up, down, wide_out, plain_out, s_gate, s_up, s_down,
    grad_q, grad_k, grad_v, grad_o, gain_one, gain_two, grad_router,
    part, wide_in, plain_in, ready_gate, ready_up, ready_down, in_sems, out_sems,
):
    rep, shard = lax.axis_index("rep"), lax.axis_index("shard")
    pairs = [(e, part.at[o]) for o, e in enumerate((e0, e1, e2, e3))]
    loads = copies_of(pairs + [(wide, wide_in), (plain, plain_in)], in_sems)
    for copy in loads:
        copy.start()
    stores = []
    for o in range(4):
        at = sibling(rep, o)
        pairs = [(ready_gate.at[o], gate.at[at]), (ready_up.at[o], up.at[at])]
        pairs.append((ready_down.at[o], down.at[at]))
        loads[o].wait()
        ready_gate[o] = part[o, 0].astype(F32)
        ready_up[o] = part[o, 1].astype(F32)
        ready_down[o] = part[o, 2].astype(F32).T
        made = [pltpu.make_async_copy(a, b, out_sems.at[3 * o + i]) for i, (a, b) in enumerate(pairs)]
        for copy in made:
            copy.start()
        stores += made
    passed = ((wide_in, wide_out), (plain_in, plain_out))
    for i, (a, b) in enumerate(passed):
        loads[4 + i].wait()
        copy = pltpu.make_async_copy(a, b, out_sems.at[12 + i])
        copy.start()
        stores.append(copy)
    quarter, span = q0.shape[1:]
    for o, piece in enumerate((q0, q1, q2, q3)):
        owner = sibling(rep, o)
        rows = pl.ds(pl.multiple_of(lax.div(owner, 2) * quarter, 128), quarter)
        cols = pl.ds(pl.multiple_of(lax.rem(owner, 2) * span, 128), span)
        s_gate[rows, cols] = piece[0].astype(F32)
        s_up[rows, cols] = piece[1].astype(F32)
        s_down[cols, rows] = piece[2].astype(F32).T
    for i, out in enumerate((grad_q, grad_k, grad_v, grad_o)):
        out[...] = weights[i]
    rows, width = weights.shape[1:]
    tiny = small[...].astype(BF)
    pick = ones_where(iota((width, rows), 0) == iota((width, rows), 1) + shard * rows)
    gains = nn(tiny, pick)
    gain_one[...] = gains[4:5, :]
    gain_two[...] = gains[5:6, :]
    grad_router[...] = dot(pick, tiny, 0, 1)[:, 0:4]
    for copy in stores:
        copy.wait()


def rope_tables(length, head_dim):
    positions = np.arange(length, dtype=np.float32)
    inverse_freq = np.float32(10000.0) ** (
        np.float32(-2.0) * np.arange(head_dim // 2, dtype=np.float32) / np.float32(head_dim)
    )
    angle = positions[:, None] * inverse_freq[None, :]
    cosine, sine = np.cos(angle), np.sin(angle)
    return (
        jnp.asarray(np.concatenate([cosine] * 4, axis=1)),
        jnp.asarray(np.concatenate([-sine, sine, -sine, sine], axis=1)),
    )


def body(
    inputs,
    piece_starts,
    routes,
    attn_gain,
    query_weight,
    key_weight,
    value_weight,
    out_weight,
    ffn_gain,
    router_weight,
    expert_gate,
    expert_up,
    expert_down,
    shared_gate,
    shared_up,
    shared_down,
    cotangent,
):
    _, tokens, width = inputs.shape
    shards = lax.axis_size("shard")
    rep, shard = lax.axis_index("rep"), lax.axis_index("shard")
    core = rep % 2
    ringed = shards == SLOTS
    rows = width // shards
    units = shared_gate.shape[1]
    x, cot, chosen = inputs[0], cotangent[0], routes[0]
    small = jnp.concatenate([router_weight.T, attn_gain[None], ffn_gain[None]], axis=0)
    small = jnp.pad(small, ((0, 10), (0, 0)))
    small = lax.dynamic_update_slice(jnp.zeros((16, width), BF), small, (0, shard * rows))
    if not ringed:
        wq, wk, wv, wo = [
            lax.all_gather(w, "shard", axis=0, tiled=True)
            for w in (query_weight, key_weight, value_weight, out_weight)
        ]
        ext = lax.psum(small.astype(F32), "shard")
        shared_pack = jnp.stack([shared_gate, shared_up, shared_down.T])
        my_half = lax.dynamic_slice_in_dim(shared_pack, core * (units // 2), units // 2, 2)
        expert_pack = jnp.stack([expert_gate[rep], expert_up[rep], expert_down[rep].T])

    cosine, sine = rope_tables(tokens, width // HEADS)
    token_f = shape((tokens, width))
    square = shape((width, width))
    packed = [shape((CAP, width))] * 4
    outs = [shape((8, tokens), F32), shape((tokens, 128), F32)] + [token_f] * 3
    work = 2 * tokens * width * (CAP * 4 + 3 * width)
    if ringed:
        expert_shape, half_shape = shape((3, width, units)), shape((3, width, units // 2))
        firsts = outs + [square] * 4 + [shape((16, width), F32), packed[0]]
        firsts += [expert_shape, half_shape]
        rank, slot, q, k, v, wq, wk, wv, wo, ext, cot_own, expert_pack, my_half, *heads = call(
            head_kernel,
            firsts + packed[1:] + [shape((SLOTS,) + expert_shape.shape)],
            [VMEM] * 11 + [ANY] * 6,
            [ANY] * 17,
            [
                pltpu.VMEM((2, SLOTS, 2 * rows + 16, width), BF),
                pltpu.VMEM((3, CAP, width), BF),
                pltpu.VMEM((2 * rows + 16, width), BF),
                pltpu.VMEM((units, width), BF),
                pltpu.VMEM((units // 2, width), BF),
                pltpu.SemaphoreType.DMA((6,)),
                pltpu.SemaphoreType.DMA((13,)),
                pltpu.SemaphoreType.DMA((34,)),
                pltpu.SemaphoreType.DMA((34,)),
                pltpu.SemaphoreType.DMA,
            ]
            + [pltpu.VMEM(a.shape, a.dtype) for a in firsts],
            flops=work,
            moved=24 * 2**20,
            group=0,
        )(
            chosen, chosen.T, cot, x, query_weight, key_weight, value_weight, out_weight, small,
            cosine, sine, expert_gate, expert_up, expert_down, shared_gate, shared_up, shared_down,
        )
        *cot_in, expert_bank = heads
        cot_in = [cot_own, *cot_in]
    else:
        rank, slot, q, k, v, *cot_out = call(
            plain_head_kernel, outs + packed, [VMEM] * 10, [VMEM] * 9, flops=work,
            moved=24 * 2**20,
        )(chosen, chosen.T, cot, x, cosine, sine, wq, wk, wv, ext)
        cot_in = [cot_out[0]] + [to_rep(cot_out[o], o) for o in (1, 2, 3)]

    outs = [token_f, shape((tokens, width), F32), shape((tokens, width), F32), token_f]
    outs += [shape((tokens, 128), F32)] + packed
    work = 2 * tokens * width * (8 * tokens + width + 4 * CAP)
    bias = pltpu.VMEM((tokens, tokens), F32)
    if ringed:
        attended, lse, middle, normed, probs, *x_out, shared_bank, expert_bank = call(
            forward_kernel,
            outs + [shape((2, SLOTS) + my_half.shape), shape((SLOTS,) + expert_pack.shape)],
            [SMEM] + [VMEM] * 7 + [ANY] * 3,
            [ANY] * 11,
            [
                bias,
                pltpu.SemaphoreType.DMA((9,)),
                pltpu.SemaphoreType.DMA((60,)),
                pltpu.SemaphoreType.DMA((60,)),
            ]
            + [pltpu.VMEM(a.shape, a.dtype) for a in outs],
            flops=work,
            moved=30 * 2**20,
            group=1,
            alias={10: 10},
        )(piece_starts, q, k, v, x, wo, ext, rank, my_half, expert_pack, expert_bank)
    else:
        attended, lse, middle, normed, probs, *x_out = call(
            plain_forward_kernel, outs, [SMEM] + [VMEM] * 7, [VMEM] * 9, [bias], flops=work,
            moved=30 * 2**20,
        )(piece_starts, q, k, v, x, wo, ext, rank)

    rows_out = shape((CAP, width))
    rows_back = shape((CAP + 16, width))
    if ringed:
        half_grads = shape((SLOTS,) + my_half.shape)
        shared_out, shared_dx, grads_own, _, shared_mate, y1, y2, y3, expert_bank = call(
            shared_kernel,
            [token_f] * 2 + [half_grads] * 3 + packed[:3] + [shape(expert_bank.shape)],
            [VMEM] * 2 + [ANY] * 6,
            [VMEM] * 2 + [ANY] * 7,
            [pltpu.SemaphoreType.DMA((15,)), pltpu.SemaphoreType.DMA((15,))]
            + unit_scratch(1, tokens, 0, width, 4, False),
            flops=18 * tokens * width * CHUNK * CHUNKS,
            moved=30 * 2**20,
            group=2,
            alias={7: 8},
        )(normed, cot, my_half, shared_bank, *x_out[1:], expert_bank)
        x_in = [x_out[0], y1, y2, y3]
        bank = shape(expert_bank.shape)
        quarter = (3, width // 2, units // 2)
        quarters = (SLOTS,) + quarter
        far_a, far_b, da, db, before, shared_keep, shared_y, expert_bank = call(
            far_kernel,
            [rows_out] * 2 + [rows_back] * 2 + [bank, shape(quarters), shape(quarters), bank],
            [VMEM] * 5 + [ANY] * 4,
            [VMEM] * 4 + [ANY] * 4,
            [
                pltpu.VMEM(half_grads.shape, BF),
                pltpu.VMEM(half_grads.shape, BF),
                pltpu.SemaphoreType.DMA((3,)),
                pltpu.SemaphoreType.DMA((9,)),
                pltpu.SemaphoreType.DMA((9,)),
            ]
            + unit_scratch(2, CAP, 16, width, 2, False),
            flops=36 * CAP * width * CHUNK * CHUNKS,
            moved=30 * 2**20,
            group=3,
            alias={8: 7},
        )(ext, *x_in[2:], *cot_in[2:], expert_pack, grads_own, shared_mate, expert_bank)
        bank_x, bank_z = (4,) + expert_pack.shape, (3,) + expert_pack.shape
        near_a, near_b, d0, shared_total, grads, d2, d3, d1, expert_x = call(
            near_kernel,
            [rows_out] * 2 + [rows_back, shape(quarter), bank] + [rows_back] * 3 + [shape(bank_x)],
            [VMEM] * 5 + [ANY] * 7,
            [VMEM] * 4 + [ANY] * 5,
            [
                pltpu.VMEM((CAP + 16, width), BF),
                pltpu.VMEM(quarters, BF),
                pltpu.VMEM(quarters, BF),
                pltpu.VMEM((4,) + quarter, BF),
                pltpu.VMEM((3,) + quarter, BF),
                pltpu.VMEM(expert_pack.shape, BF),
                pltpu.SemaphoreType.DMA((2,)),
                pltpu.SemaphoreType.DMA((11,)),
                pltpu.SemaphoreType.DMA((11,)),
            ]
            + unit_scratch(2, CAP, 16, width, 2, True),
            flops=36 * CAP * width * CHUNK * CHUNKS,
            moved=30 * 2**20,
            group=4,
        )(
            ext, *x_in[:2], *cot_in[:2], expert_pack, expert_bank, before, da, db,
            shared_keep, shared_y,
        )
        d_rows = [d0, d1, d2, d3]
    else:

        def slotted(part):
            every = lax.all_gather(part, "shard")
            every = every.reshape(SLOTS, shards // SLOTS, 3, width, part.shape[2])
            return every.transpose(0, 2, 3, 1, 4).reshape(SLOTS, 3, width, -1)

        shared_bank = slotted(my_half)
        shared_bank = jnp.concatenate([shared_bank, to_rep(shared_bank, 1)], axis=0)
        expert_bank = slotted(expert_pack)
        x_in = [x_out[0]] + [to_rep(x_out[o], o) for o in (1, 2, 3)]
        (shared_out,), (shared_dx,), shared_grads = plain_bank(
            ext, [normed], [cot], shared_bank, None, False
        )
        grads_own, grads_other = shared_grads[:SLOTS], shared_grads[SLOTS:]
        (far_a, far_b), (da, db), before = plain_bank(
            ext, x_in[2:], cot_in[2:], expert_bank, None, True
        )
        (near_a, near_b), (d0, d1), grads = plain_bank(
            ext, x_in[:2], cot_in[:2], expert_bank, before, True
        )
        d_rows = [d0, to_rep(d1, 1), to_rep(da, 2), to_rep(db, 3)]
    wide = shape((tokens, width), F32)
    outs = [wide, square, shape((16, width), F32)] + [token_f] * 3
    operands = (piece_starts, slot, *d_rows, shared_dx, probs, middle, normed, cot, ext, attended)
    operands += (wo,)
    specs = [SMEM] + [VMEM] * 15
    scratch = [
        pltpu.VMEM((tokens, width), BF),
        pltpu.VMEM((tokens, width), BF),
        pltpu.VMEM((128, width), F32),
        pltpu.VMEM((8, width), F32),
        bias,
        pltpu.VMEM((tokens, 128), F32),
        pltpu.VMEM((tokens, 128), F32),
    ]
    work = 2 * tokens * width * (2 * width + 4 * CAP) + 40 * tokens * tokens * width
    if ringed:
        late = (*operands[1:], cosine, sine, q, k, v, lse)
        d_middle, grad_wo, grad_ext, dq, dk, dv, expert_total, *back = call(
            back_kernel,
            outs
            + [shape(expert_pack.shape)]
            + [rows_out] * 3
            + [shape(bank_z), shape(bank_z), shape(bank_x)],
            [SMEM] + [ANY] * (len(late) + 5),
            [ANY] * 6 + [VMEM] + [ANY] * 6,
            scratch
            + [pltpu.VMEM(a.shape, a.dtype) for a in late]
            + [
                pltpu.VMEM(bank_x, BF),
                pltpu.VMEM((1,) + expert_pack.shape, BF),
                pltpu.SemaphoreType.DMA((2,)),
                pltpu.SemaphoreType.DMA((len(late),)),
                pltpu.SemaphoreType.DMA((6,)),
                pltpu.SemaphoreType.DMA((12,)),
                pltpu.SemaphoreType.DMA((12,)),
            ]
            + [pltpu.VMEM(a.shape, a.dtype) for a in outs],
            flops=work,
            moved=40 * 2**20,
            group=5,
            alias={24: 12},
        )(piece_starts, *late, near_b, far_a, far_b, grads, expert_x)
        operands = (x, ext, dq, dk, dv, wq, wk, wv, grad_wo, grad_ext)
        operands += (d_middle, slot, near_a, *back[:3], shared_out, probs, middle)
        strip = (2, width // SLOTS, width)
        grad_in, outputs, weights, small, *rest = call(
            tail_kernel,
            [wide, token_f, shape((4, rows, width), F32), shape((16, width), F32)]
            + [shape(quarter)] * 3
            + [shape(expert_pack.shape)] * 3,
            [VMEM] * 10 + [ANY] * 11,
            [VMEM] * 4 + [ANY] * 6,
            [
                pltpu.VMEM((tokens, width), BF),
                pltpu.VMEM((8, width), F32),
                pltpu.VMEM((4, width, width), BF),
                pltpu.VMEM((2, width, width), BF),
                pltpu.VMEM((4,) + strip, BF),
                pltpu.VMEM((3,) + strip, BF),
                pltpu.VMEM(strip, BF),
                pltpu.VMEM((2,) + strip, BF),
                pltpu.VMEM(strip, BF),
                pltpu.VMEM((4, 16, width), BF),
                pltpu.VMEM((6, 16, width), BF),
                pltpu.VMEM((tokens, width), F32),
                pltpu.VMEM((tokens, 128), F32),
                pltpu.VMEM((CAP, width), BF),
                pltpu.VMEM((CAP, width), BF),
                pltpu.VMEM((CAP, width), BF),
                pltpu.VMEM((CAP, width), BF),
                pltpu.VMEM((tokens, width), BF),
                pltpu.VMEM((tokens, 128), F32),
                pltpu.VMEM((tokens, width), F32),
                pltpu.SemaphoreType.DMA((9,)),
                pltpu.SemaphoreType.DMA((32,)),
                pltpu.SemaphoreType.DMA((32,)),
            ],
            flops=2 * tokens * width * (6 * width + 4 * CAP),
            moved=40 * 2**20,
            group=6,
        )(*operands, expert_total, shared_total)
        banks = [shape((4, width, units), F32)] * 2 + [shape((4, units, width), F32)]
        banks += [shape((width, units), F32)] * 2 + [shape((units, width), F32)]
        shared_far, shared_mate, shared_cross, *experts = rest
        *finals, grad_q, grad_k, grad_v, grad_o, gain_one, gain_two, grad_router = call(
            finish_kernel,
            banks[:3] + [wide, token_f] + banks[3:] + [shape((rows, width), F32)] * 4
            + [shape((1, rows), F32)] * 2 + [shape((rows, 4), F32)],
            [ANY] * 6 + [VMEM] * 6,
            [ANY] * 5 + [VMEM] * 10,
            [
                pltpu.VMEM((4,) + expert_pack.shape, BF),
                pltpu.VMEM((tokens, width), F32),
                pltpu.VMEM((tokens, width), BF),
            ]
            + [pltpu.VMEM(b.shape, F32) for b in banks[:3]]
            + [pltpu.SemaphoreType.DMA((6,)), pltpu.SemaphoreType.DMA((14,))],
            moved=26 * 2**20,
        )(
            expert_total, *experts, grad_in, outputs,
            shared_total, shared_mate, shared_far, shared_cross, weights, small,
        )
        grad_in, outputs = finals.pop(3), finals.pop(3)
        gain_one, gain_two = gain_one[0], gain_two[0]
    else:
        d_middle, grad_wo, grad_ext, dq, dk, dv = call(
            plain_back_kernel, outs, specs + [VMEM] * 4, [VMEM] * 6, scratch, flops=work,
            moved=40 * 2**20,
        )(*operands, q, k, v, lse, cosine, sine)
        out_rows = [near_a, to_rep(near_b, 1), to_rep(far_a, 2), to_rep(far_b, 3)]
        grad_in, outputs, gw, gain = call(
            plain_tail_kernel,
            [wide, token_f, shape((3, width, width)), shape((8, width), F32)],
            [VMEM] * 17,
            [VMEM] * 4,
            [pltpu.VMEM((tokens, width), BF), pltpu.VMEM((8, width), F32)],
            flops=2 * tokens * width * (6 * width + 4 * CAP),
            moved=40 * 2**20,
        )(
            x, ext, dq, dk, dv, wq, wk, wv, d_middle, slot, *out_rows, shared_out, probs, middle
        )

        def over_rep(total):
            return lax.psum(total.astype(BF), "rep").astype(F32)

        def unslot(every, part_units):
            every = every.reshape(SLOTS, 3, width, shards // SLOTS, part_units)
            every = every.transpose(0, 3, 1, 2, 4).reshape(shards, 3, width, part_units)
            return lax.psum_scatter(every, "shard", scatter_dimension=0)

        grad_q, grad_k, grad_v, grad_o = (
            over_rep(lax.psum_scatter(w, "shard", tiled=True))
            for w in (gw[0], gw[1], gw[2], grad_wo)
        )
        small = grad_ext.at[4].add(jnp.sum(gain, axis=0))
        small = lax.psum(small, ("rep", "shard"))
        shared_sum = grads_own.astype(F32) + to_rep(grads_other, 1).astype(F32)
        total = unslot(shared_sum.astype(BF), units // 2).astype(F32)
        total = (total + to_rep(total.astype(BF), 2).astype(F32)).astype(BF)
        mate = to_rep(total, 1)
        shared_full = jnp.concatenate(
            [jnp.where(core == 0, total, mate), jnp.where(core == 0, mate, total)], axis=2
        ).astype(F32)
        expert_total = unslot(grads, units).astype(BF)
        parts = jnp.stack([expert_total] + [to_rep(expert_total, o) for o in (1, 2, 3)])
        full = jnp.take(parts, jnp.arange(4) ^ rep, axis=0).astype(F32)
        finals = (full[:, 0], full[:, 1], full[:, 2].transpose(0, 2, 1))
        finals += (shared_full[0], shared_full[1], shared_full[2].T)
        tiny = lax.dynamic_slice(small, (0, shard * rows), (16, rows))
        gain_one, gain_two, grad_router = tiny[4], tiny[5], tiny[:4].T
    return (
        outputs[None],
        grad_in[None],
        gain_one,
        grad_q,
        grad_k,
        grad_v,
        grad_o,
        gain_two,
        grad_router,
        *finals,
    )


def solution(mesh):
    in_specs = (
        P(("rep", "shard"), None, None),
        P(("rep", "shard"), None),
        P(("rep", "shard"), None, None),
        P("shard"),
        P("shard", None),
        P("shard", None),
        P("shard", None),
        P("shard", None),
        P("shard"),
        P("shard", None),
        P(None, None, "shard"),
        P(None, None, "shard"),
        P(None, "shard", None),
        P(None, "shard"),
        P(None, "shard"),
        P("shard", None),
        P(("rep", "shard"), None, None),
    )
    out_specs = (
        P(("rep", "shard"), None, None),
        P(("rep", "shard"), None, None),
        P("shard"),
        P("shard", None),
        P("shard", None),
        P("shard", None),
        P("shard", None),
        P("shard"),
        P("shard", None),
        P(None, None, "shard"),
        P(None, None, "shard"),
        P(None, "shard", None),
        P(None, "shard"),
        P(None, "shard"),
        P("shard", None),
    )
    return jax.shard_map(body, mesh=mesh, in_specs=in_specs, out_specs=out_specs, check_vma=False)
```

```python
import functools

import jax
import jax.numpy as jnp
import numpy as np
from jax import lax
from jax.experimental import pallas as pl
from jax.experimental.pallas import tpu as pltpu
from jax.sharding import PartitionSpec as P

HEADS = 12
PIECE = 256
CAP = 576
EPSILON = 1e-06
MASKED = -1e30
F32, BF = jnp.float32, jnp.bfloat16
AXES = ("rep", "shard")
TILE = 256
SLOTS = 8
VMEM_LIMIT = 62 * 2**20
ANY = pl.BlockSpec(memory_space=pl.ANY)
SMEM = pl.BlockSpec(memory_space=pltpu.SMEM)
VMEM = pl.BlockSpec(memory_space=pltpu.VMEM)


def dot(a, b, i, j):
    return lax.dot_general(a, b, (((i,), (j,)), ((), ())), preferred_element_type=F32)


def nn(a, b):
    return dot(a, b, 1, 0)


def nt(a, b):
    return dot(a, b, 1, 1)


def tn(a, b):
    return dot(a, b, 0, 0)


def iota(shape, dim):
    return lax.broadcasted_iota(jnp.int32, shape, dim)


def ones_where(cond):
    return jnp.where(cond, 1.0, 0.0).astype(BF)


def call(
    kernel, out_shape, in_specs, out_specs, scratch=(), flops=0, moved=0, grid=None, group=None,
    alias=None,
):
    extra = {} if grid is None else {"grid": grid}
    params = {} if group is None else {"collective_id": group, "has_side_effects": True}
    return pl.pallas_call(
        kernel,
        out_shape=out_shape,
        in_specs=in_specs,
        out_specs=out_specs,
        scratch_shapes=list(scratch),
        input_output_aliases=alias or {},
        compiler_params=pltpu.CompilerParams(vmem_limit_bytes=VMEM_LIMIT, **params),
        cost_estimate=pl.CostEstimate(flops=flops, bytes_accessed=moved, transcendentals=0),
        **extra,
    )


def shape(dims, dtype=BF):
    return jax.ShapeDtypeStruct(dims, dtype)


def permute(x, move):
    reps, shards = lax.axis_size("rep"), lax.axis_size("shard")
    pairs = []
    for r in range(reps):
        for s in range(shards):
            to_r, to_s = move(r, s)
            pairs.append((r * shards + s, to_r * shards + to_s))
    return lax.ppermute(x, AXES, pairs)


def to_rep(x, offset):
    return permute(x, lambda r, s: (r ^ offset, s))


def spin(block, cosine, sine):
    lane = iota(block.shape, 1)
    partner = jnp.where(lane % 64 < 32, pltpu.roll(block, 96, 1), pltpu.roll(block, 32, 1))
    return block * cosine + partner * sine


def sibling(rep, o):
    return 2 * lax.rem(lax.div(rep, 2) + o // 2, 2) + lax.rem(lax.rem(rep, 2) + o % 2, 2)


def route_slots(rep, routes, routes_t, rank_out, slot_out):
    tokens = routes.shape[0]
    first, second = routes_t[0:1, :], routes_t[1:2, :]
    expert = iota((8, tokens), 0)
    chosen = (expert == first) | (expert == second)
    upper = ones_where(iota((tokens, tokens), 0) <= iota((tokens, tokens), 1))
    rank = nn(ones_where(chosen), upper) - 1.0
    rank_out[...] = jnp.where(chosen, rank, -1.0)
    lane = iota((tokens, 128), 1)
    one, two = routes[:, 0:1], routes[:, 1:2]
    lower = ones_where(iota((tokens, tokens), 0) >= iota((tokens, tokens), 1))
    place = nn(lower, ones_where((lane == one) | (lane == two))) - 1.0
    for o in range(1, 4):
        place = place + jnp.where(lane == sibling(rep, o), float(o * CAP), 0.0)
    slot_one = jnp.sum(jnp.where(lane == one, place, 0.0), axis=1, keepdims=True)
    slot_two = jnp.sum(jnp.where(lane == two, place, 0.0), axis=1, keepdims=True)
    slot_out[...] = jnp.where(lane < 64, slot_one, slot_two)


def pack_row(rep, rank, source, o, out):
    row = rank[pl.ds(sibling(rep, o), 1), :]
    pick = ones_where(iota((CAP, source.shape[0]), 0).astype(F32) == row)
    out[...] = nn(pick, source[...]).astype(BF)


def pack_rows(rep, rank, source, packed):
    for o, out in enumerate(packed):
        pack_row(rep, rank, source, o, out)


def qkv_rows(x, ext, cosine, sine, wq, wk, wv, q, k, v):
    tokens, width = x.shape
    gain = ext[4:5, :]

    def tile(t, carry):
        at = pl.ds(pl.multiple_of(t * TILE, TILE), TILE)
        rows_in = x[at, :].astype(F32)
        scale = lax.rsqrt(jnp.mean(rows_in * rows_in, axis=1, keepdims=True) + EPSILON)
        normed = (rows_in * scale * gain).astype(BF)
        cos_t, sin_t = cosine[at, :], sine[at, :]
        for weight, out, factor in ((wq, q, 0.125), (wk, k, 1.0)):
            full = nn(normed, weight[...])
            for b in range(width // 128):
                turned = spin(full[:, b * 128 : (b + 1) * 128], cos_t, sin_t)
                out[at, b * 128 : (b + 1) * 128] = turned.astype(BF) * jnp.asarray(factor, BF)
        v[at, :] = nn(normed, wv[...]).astype(BF)
        return carry

    lax.fori_loop(0, tokens // TILE, tile, 0)


def when(cond, body):
    if cond is True:
        body()
    elif cond is not False:
        pl.when(cond)(body)


def both(one, two):
    if one is True or two is False:
        return two
    if two is True or one is False:
        return one
    return one & two


class Net:
    def __init__(self, send, recv):
        self.rep, self.shard = lax.axis_index("rep"), lax.axis_index("shard")
        self.core, self.z = lax.rem(self.rep, 2), lax.div(self.shard, 2)
        self.x = lax.rem(self.shard, 2)
        self.mate = self.rep + 1 - 2 * self.core
        self.across = self.shard + 1 - 2 * self.x
        first = lax.max(self.z - 1, 1 - self.z)
        third = 3 * (1 - lax.div(self.z, 2))
        self.levels = [self.z, first, 6 - self.z - first - third, third]
        self.up = lax.min(self.shard + 2, 6 + self.x)
        self.down = lax.max(self.shard - 2, self.x)
        self.cousins = [self.rep] + [sibling(self.rep, o) for o in (1, 2, 3)]
        self.send, self.recv = send, recv
        self.count, self.open = 0, {}

    def event(self):
        self.count += 1
        return self.count - 1

    def place(self, n, side):
        return self.levels[n] * 2 + (self.x if side == 0 else 1 - self.x)

    def cycle(self, d):
        return lax.rem(self.z + d, 4) * 2 + self.x

    def copy(self, event, source, target, rep, shard):
        return pltpu.make_async_remote_copy(
            src_ref=source,
            dst_ref=target,
            send_sem=self.send.at[event],
            recv_sem=self.recv.at[event],
            device_id=(rep, shard),
            device_id_type=pl.DeviceIdType.MESH,
        )

    def put(self, event, source, target, rep, shard, cond=True):
        when(cond, self.copy(event, source, target, rep, shard).start)
        self.open[event] = (cond, source)

    def got(self, event, like, cond=True):
        when(cond, self.copy(event, like, like, self.mate, self.shard).wait_recv)

    def settle(self, event):
        cond, source = self.open.pop(event)
        when(cond, self.copy(event, source, source, self.mate, self.shard).wait_send)

    def close(self):
        for event, (cond, source) in self.open.items():
            when(cond, self.copy(event, source, source, self.mate, self.shard).wait_send)

    def meet(self, z_ways, others):
        barrier = pltpu.get_barrier_semaphore()

        def greet(rep, shard):
            pl.semaphore_signal(
                barrier, inc=1, device_id=(rep, shard), device_id_type=pl.DeviceIdType.MESH
            )

        count = len(others)
        for rep, shard in others:
            greet(rep, shard)
        if z_ways == "line":
            when(self.z < 3, lambda: greet(self.rep, self.up))
            when(self.z > 0, lambda: greet(self.rep, self.down))
            count = count + lax.min(self.z, 1) + lax.min(3 - self.z, 1)
        if z_ways == "all":
            for d in (1, 2, 3):
                greet(self.rep, self.cycle(d))
            count = count + 3
        pl.semaphore_wait(barrier, count)


class Line:
    def __init__(self, net, bank, ways=4):
        self.net, self.bank = net, bank
        self.events = {(way, k): net.event() for way in range(ways) for k in range(-3, 4)}
        self.spots = {0: (net.shard, True)}
        for k in (1, 2, 3):
            self.spots[k] = (lax.min(net.shard + 2 * k, 6 + net.x), net.z < 4 - k)
            self.spots[-k] = (lax.max(net.shard - 2 * k, net.x), net.z >= k)
        self.flips = {k: spot + 1 - 2 * net.x for k, (spot, _) in self.spots.items()}
        self.onward = {k: both(self.spots[k][1], net.z < 3) for k in self.spots}
        self.back = {k: both(self.spots[k][1], net.z > 0) for k in self.spots}

    def spread(self, k, source):
        net, (spot, here) = self.net, self.spots[k]
        target = self.bank.at[net.core, spot]
        if -3 < k <= 0:
            event = self.events[0, k - 1]
            net.put(event, source, target, net.rep, net.up, self.onward[k])
        if 0 <= k < 3:
            event = self.events[0, k + 1]
            net.put(event, source, target, net.rep, net.down, self.back[k])
        net.put(self.events[1, k], source, target, net.rep, net.across, here)
        net.put(self.events[2, k], source, target, net.mate, net.shard, here)

    def along(self, k):
        spot, here = self.spots[k]
        piece = self.bank.at[self.net.core, spot]
        self.net.got(self.events[0, k], piece, here)
        self.spread(k, piece)

    def over(self, k):
        net, here = self.net, self.spots[k][1]
        piece = self.bank.at[net.core, self.flips[k]]
        net.got(self.events[1, k], piece, here)
        net.put(self.events[3, k], piece, piece, net.mate, net.shard, here)

    def finish(self):
        other = 1 - self.net.core
        for k in (0, 1, -1, 2, -2, 3, -3):
            spot, here = self.spots[k]
            self.net.got(self.events[2, k], self.bank.at[other, spot], here)
            self.net.got(self.events[3, k], self.bank.at[other, self.flips[k]], here)


class Spread:
    def __init__(self, net, piece, bank):
        self.net, self.piece, self.bank = net, piece, bank
        self.line = Line(net, bank, 8)
        self.events, self.spots, self.flips = self.line.events, self.line.spots, self.line.flips
        self.half = piece.shape[1] // 2
        y = lax.div(net.rep, 2)
        self.rows = [pl.ds(pl.multiple_of(n * self.half, 128), self.half) for n in (y, 1 - y)]
        self.far = net.cousins[2]

    def view(self, core, spot, rows):
        return self.bank.at[core, spot, :, self.rows[rows], :]

    def begin(self):
        net = self.net
        source = self.piece.at[:, self.rows[0], :]
        target = self.view(net.core, net.shard, 0)
        net.put(self.events[0, -1], source, target, net.rep, net.up, self.line.onward[0])
        net.put(self.events[0, 1], source, target, net.rep, net.down, self.line.back[0])
        net.put(self.events[1, 0], source, target, net.rep, net.across)
        whole = self.bank.at[net.core, net.shard]
        net.put(self.events[2, 0], self.piece, whole, net.mate, net.shard)

    def hand(self, way, k, here, piece):
        net = self.net
        net.put(self.events[way + 4, k], piece, piece, self.far, net.shard, here)
        net.put(self.events[way + 2, k], piece, piece, net.mate, net.shard, here)

    def along(self, k):
        net, (spot, here) = self.net, self.spots[k]
        piece = self.view(net.core, spot, 0)
        net.got(self.events[0, k], piece, here)
        if -3 < k < 0:
            net.put(self.events[0, k - 1], piece, piece, net.rep, net.up, self.line.onward[k])
        if 0 < k < 3:
            net.put(self.events[0, k + 1], piece, piece, net.rep, net.down, self.line.back[k])
        net.put(self.events[1, k], piece, piece, net.rep, net.across, here)
        self.hand(0, k, here, piece)

    def over(self, k):
        net, here = self.net, self.spots[k][1]
        piece = self.view(net.core, self.flips[k], 0)
        net.got(self.events[1, k], piece, here)
        self.hand(1, k, here, piece)

    def relay(self, way, k):
        net, here = self.net, self.spots[k][1]
        spot = self.spots[k][0] if way == 0 else self.flips[k]
        piece = self.view(net.core, spot, 1)
        net.got(self.events[way + 4, k], piece, here)
        net.put(self.events[way + 6, k], piece, piece, net.mate, net.shard, here)

    def finish(self):
        net, other = self.net, 1 - self.net.core
        net.got(self.events[2, 0], self.bank.at[other, net.shard])
        for k in (0, 1, -1, 2, -2, 3, -3):
            spot, here = self.spots[k]
            if k:
                net.got(self.events[2, k], self.view(other, spot, 0), here)
                net.got(self.events[6, k], self.view(other, spot, 1), here)
            net.got(self.events[3, k], self.view(other, self.flips[k], 0), here)
            net.got(self.events[7, k], self.view(other, self.flips[k], 1), here)


def exchange(net, sources, targets):
    events = [net.event() for _ in range(3)]
    for o in (2, 3, 1):
        net.put(events[o - 1], sources[o - 1], targets[o - 1], net.cousins[o], net.shard)
    return [(events[o], targets[o]) for o in range(3)]


def head_kernel(
    routes, routes_t, cot, x, wq_in, wk_in, wv_in, wo_in, small, cosine, sine,
    e_gate, e_up, e_down, s_gate, s_up, s_down,
    *refs,
):
    width = x.shape[1]
    half = width // SLOTS
    outs, (c1, c2, c3, experts) = refs[:13], refs[13:17]
    bank, packed, piece, e_raw, s_raw, pack_sems, out_sems, send, recv, own_sem = refs[17:27]
    rank, slot, q, k, v, wq, wk, wv, wo, ext, c0, expert_piece, shared_piece = refs[27:]
    stores = copies_of(zip(refs[27:], outs), out_sems)
    net = Net(send, recv)
    units = s_raw.shape[0]
    cut = pl.ds(pl.multiple_of(net.core * units, 128), units)
    packs = copies_of(
        (
            (e_gate.at[net.rep], expert_piece.at[0]),
            (e_up.at[net.rep], expert_piece.at[1]),
            (e_down.at[net.rep], e_raw),
            (s_gate.at[:, cut], shared_piece.at[0]),
            (s_up.at[:, cut], shared_piece.at[1]),
            (s_down.at[cut, :], s_raw),
        ),
        pack_sems,
    )
    for copy in packs:
        copy.start()
    for core, (low, high) in enumerate(((wq_in, wk_in), (wv_in, wo_in))):

        @pl.when(net.core == core)
        def _():
            piece[0:half, :] = low[...]
            piece[half : 2 * half, :] = high[...]

    piece[2 * half : 2 * half + 16, :] = small[...]
    line = Line(net, bank)
    e_events = [net.event() for _ in range(3)]
    mine, most = experts.at[net.shard], experts.at[net.shard, pl.ds(0, 2)]
    peers = [(net.cousins[o], net.shard) for o in (1, 2, 3)]
    net.meet("line", peers + [(net.rep, net.across)])
    line.spread(0, piece)
    own = pltpu.make_async_copy(piece, bank.at[net.core, net.shard], own_sem)
    own.start()
    route_slots(net.rep, routes, routes_t, rank, slot)
    events = [net.event() for _ in range(3)]
    for o, far in ((2, c2), (3, c3), (1, c1)):
        pack_row(net.rep, rank, cot, o, packed.at[o - 1])
        net.put(events[o - 1], packed.at[o - 1], far, net.cousins[o], net.shard)
    arrivals = [(events[0], c1), (events[1], c2), (events[2], c3)]
    pack_row(net.rep, rank, cot, 0, c0)
    for copy in packs:
        copy.wait()
    expert_piece[2] = e_raw[...].astype(F32).T.astype(BF)
    shared_piece[2] = s_raw[...].astype(F32).T.astype(BF)
    line.along(1)
    line.along(-1)
    line.over(0)
    line.along(2)
    line.along(-2)
    net.put(e_events[0], expert_piece, mine, net.rep, net.up, net.z < 3)
    net.put(e_events[1], expert_piece, mine, net.rep, net.down, net.z > 0)
    line.over(1)
    line.over(-1)
    line.along(3)
    line.along(-3)
    net.put(e_events[2], expert_piece.at[pl.ds(0, 2)], most, net.rep, net.across)
    for step in (2, -2, 3, -3):
        line.over(step)
    own.wait()
    line.finish()
    gathered = bank[0, 0, 2 * half : 2 * half + 16, :].astype(F32)
    for j in range(1, SLOTS):
        gathered = gathered + bank[0, j, 2 * half : 2 * half + 16, :].astype(F32)
    ext[...] = gathered
    for j in range(SLOTS):
        at = slice(j * half, (j + 1) * half)
        wq[at, :] = bank[0, j, 0:half, :]
        wk[at, :] = bank[0, j, half : 2 * half, :]
        wv[at, :] = bank[1, j, 0:half, :]
        wo[at, :] = bank[1, j, half : 2 * half, :]
    qkv_rows(x, ext, cosine, sine, wq, wk, wv, q, k, v)
    for copy in stores:
        copy.start()
    for event, like in arrivals:
        net.got(event, like)
    net.got(e_events[0], mine, net.z > 0)
    net.got(e_events[1], mine, net.z < 3)
    net.got(e_events[2], most)
    for copy in stores:
        copy.wait()
    net.close()


def plain_head_kernel(
    routes, routes_t, cot, x, cosine, sine, wq, wk, wv, ext,
    rank, slot, q, k, v, c0, c1, c2, c3,
):
    rep = lax.axis_index("rep")
    route_slots(rep, routes, routes_t, rank, slot)
    pack_rows(rep, rank, cot, (c0, c1, c2, c3))
    qkv_rows(x, ext, cosine, sine, wq, wk, wv, q, k, v)


def fill_bias(starts, bias):
    tokens = bias.shape[0]

    def tile(t, carry):
        at = pl.ds(pl.multiple_of(t * TILE, TILE), TILE)
        query = iota((TILE, tokens), 0) + t * TILE
        key = iota((TILE, tokens), 1)
        allowed = key <= query
        for n in range(2):
            begin = starts[0, n]
            inside = (query >= begin) & (query < begin + PIECE)
            allowed = allowed | (inside & (key >= begin) & (key < begin + PIECE))
        bias[at, :] = jnp.where(allowed, 0.0, MASKED)
        return carry

    lax.fori_loop(0, tokens // TILE, tile, 0)


def keep_half(block, h):
    low = iota(block.shape, 1) < 64
    return jnp.where(low if h == 0 else ~low, block.astype(F32), 0.0).astype(BF)


def biased(scores, bias, begin, free, end):
    tail = scores[:, free:] + bias[begin : begin + TILE, free:end]
    return tail if free == 0 else jnp.concatenate([scores[:, :free], tail], axis=1)


def attend_pairs(q, k, v, out, lse, bias, step):
    tokens, width = q.shape

    def pair(i, carry):
        step(i)
        cols = pl.ds(pl.multiple_of(i * 128, 128), 128)
        keys = k[:, cols]
        low = iota((tokens, 128), 1) < 64
        values = v[:, cols].astype(F32)
        value_one = [
            jnp.where(low, values, 1.0).astype(BF),
            jnp.where(low, 1.0, values).astype(BF),
        ]
        low = iota((TILE, 128), 1) < 64
        for t in range(tokens // TILE):
            begin = t * TILE
            end = min(tokens, begin + TILE + PIECE)
            block = q[begin : begin + TILE, cols]
            results, totals = [], []
            for h in range(2):
                scores = nt(keep_half(block, h), keys[:end])
                scores = biased(scores, bias, begin, begin, end)
                row_max = jnp.max(scores, axis=1, keepdims=True)
                probs = jnp.exp(scores - row_max).astype(BF)
                mixed = nn(probs, value_one[h][:end])
                total = pltpu.roll(mixed, 64, 1)
                results.append(mixed / total)
                totals.append(row_max + jnp.log(total))
            out[begin : begin + TILE, cols] = jnp.where(low, results[0], results[1]).astype(BF)
            lse[begin : begin + TILE, cols] = jnp.where(low, totals[0], totals[1])
        return carry

    lax.fori_loop(0, width // 128, pair, 0)


def router_rows(ext):
    rows = jnp.where(iota(ext.shape, 0) < 4, ext[...], 0.0)
    return jnp.concatenate([rows, jnp.zeros((112, ext.shape[1]), F32)], axis=0).astype(BF)


def route_probs(normed, router):
    logits = nt(normed, router)
    logits = jnp.where(iota(logits.shape, 1) < 4, logits, MASKED)
    raised = jnp.exp(logits - jnp.max(logits, axis=1, keepdims=True))
    return raised / jnp.sum(raised, axis=1, keepdims=True)


def middle_rows(rep, x, attended, wo, ext, rank, middle, normed, probs, packed):
    tokens = x.shape[0]
    gain = ext[5:6, :]
    router = router_rows(ext)

    def tile(t, carry):
        at = pl.ds(pl.multiple_of(t * TILE, TILE), TILE)
        rows = x[at, :].astype(F32) + nn(attended[at, :], wo[...])
        scale = lax.rsqrt(jnp.mean(rows * rows, axis=1, keepdims=True) + EPSILON)
        middle[at, :] = rows
        unit = (rows * scale * gain).astype(BF)
        normed[at, :] = unit
        probs[at, :] = route_probs(unit, router)
        return carry

    lax.fori_loop(0, tokens // TILE, tile, 0)
    pack_rows(rep, rank, normed, packed)


def forward_kernel(
    starts, q, k, v, x, wo, ext, rank, shared_piece, expert_piece, expert_in,
    *refs,
):
    outs, shared_bank, experts = refs[:9], refs[9], refs[10]
    bias, out_sems, send, recv = refs[11:15]
    attended, lse, middle, normed, probs, x0, x1, x2, x3 = refs[15:]
    stores = copies_of(zip(refs[15:], outs), out_sems)
    net = Net(send, recv)
    spread = Spread(net, shared_piece, shared_bank)
    events = [net.event() for _ in range(4)]
    inner = (net.z > 0) & (net.z < 3)
    low, high = experts.at[net.down], experts.at[net.up]
    rest, last = experts.at[net.shard, pl.ds(2, 1)], expert_piece.at[pl.ds(2, 1)]
    near = experts.at[net.place(1, 0), pl.ds(0, 2)]
    net.meet("line", [(net.mate, net.shard), (net.rep, net.across), (spread.far, net.shard)])
    spread.begin()
    fill_bias(starts, bias)

    def step(i):
        @pl.when(i == 1)
        def _():
            spread.along(1)
            spread.along(-1)
            spread.over(0)

        @pl.when(i == 3)
        def _():
            spread.along(2)
            spread.along(-2)
            spread.over(1)
            spread.over(-1)

        @pl.when(i == 5)
        def _():
            spread.along(3)
            spread.along(-3)
            net.put(events[0], low, low, net.rep, net.up, inner)
            net.put(events[1], high, high, net.rep, net.down, inner)
            net.put(events[2], last, rest, net.rep, net.across)
            net.put(events[3], near, near, net.rep, net.across)
            spread.over(2)
            spread.over(-2)

    attend_pairs(q, k, v, attended, lse, bias, step)
    for copy in stores[:2]:
        copy.start()
    spread.over(3)
    spread.over(-3)
    for way, k_step in ((1, 0), (0, 1), (0, -1)):
        spread.relay(way, k_step)
    middle_rows(net.rep, x, attended, wo, ext, rank, middle, normed, probs, (x0, x1, x2, x3))
    for copy in stores[2:]:
        copy.start()
    for way, k_step in ((1, 1), (1, -1), (0, 2), (0, -2), (1, 2), (1, -2)):
        spread.relay(way, k_step)
    for way, k_step in ((0, 3), (0, -3), (1, 3), (1, -3)):
        spread.relay(way, k_step)
    spread.finish()
    net.got(events[0], low, net.z > 1)
    net.got(events[1], low, net.z < 2)
    net.got(events[2], rest)
    net.got(events[3], near)
    for copy in stores:
        copy.wait()
    net.close()


def plain_forward_kernel(
    starts, q, k, v, x, wo, ext, rank,
    attended, lse, middle, normed, probs, x0, x1, x2, x3, bias,
):
    fill_bias(starts, bias)
    attend_pairs(q, k, v, attended, lse, bias, lambda i: None)
    rep = lax.axis_index("rep")
    middle_rows(rep, x, attended, wo, ext, rank, middle, normed, probs, (x0, x1, x2, x3))


CHUNK, CHUNKS = 512, 4


def unit_bank(
    expert, ext, xs, cs, source, target, before, unit, outs, dxs, scratch, ready=None,
    emit=None,
):
    out_acc, dx_acc, gate, wbuf, stage, dw_out, in_sems, out_sems, xc = scratch[:9]
    routed = expert is not None
    blocks, rows = len(xs), xs[0].shape[0]
    per = CHUNK // unit

    def loads(of, buffer, sems, k, b):
        return [
            pltpu.make_async_copy(
                of(k * per + i), buffer.at[b, :, :, pl.ds(i * unit, unit)], sems.at[b, i]
            )
            for i in range(per)
        ]

    def stores(k, b):
        return [
            pltpu.make_async_copy(
                dw_out.at[b, :, :, pl.ds(i * unit, unit)],
                target(k * per + i),
                out_sems.at[b, i],
            )
            for i in range(per)
        ]

    def start_loads(k, b):
        if ready is not None:
            ready(k)
        for copy in loads(source, wbuf, in_sems, k, b):
            copy.start()
        if before is not None:
            for copy in loads(before, scratch[9], scratch[10], k, b):
                copy.start()

    start_loads(0, 0)
    out_acc[...] = jnp.zeros_like(out_acc)
    dx_acc[...] = jnp.zeros_like(dx_acc)
    for n in range(blocks):
        xc[0, n * rows : (n + 1) * rows, :] = xs[n][...]
        xc[1, n * rows : (n + 1) * rows, :] = cs[n][...]
    if routed:
        router = router_rows(ext)
        for n in range(blocks):
            probs = route_probs(xs[n][...], router)
            lane = iota(probs.shape, 1)
            gate[n] = jnp.sum(jnp.where(lane == expert, probs, 0.0), axis=1, keepdims=True)

    def chunk(k, carry):
        b = lax.rem(k, 2)
        for copy in loads(source, wbuf, in_sems, 0, b):
            copy.wait()
        for n in range(blocks):
            x, c = xs[n][...], cs[n][...]
            wg, wu, wd = wbuf[b, 0], wbuf[b, 1], wbuf[b, 2]
            gate_h, up_h, back_h = nn(x, wg), nn(x, wu), nn(c, wd)
            sigma = 0.5 * jnp.tanh(0.5 * gate_h) + 0.5
            silu = gate_h * sigma
            hidden = silu * up_h
            if routed:
                share = gate[n]
                scaled = back_h * share
                weighted = (hidden * share).astype(BF)
            else:
                scaled, weighted = back_h, hidden.astype(BF)
            d_up = (scaled * silu).astype(BF)
            d_gate = (scaled * up_h * (sigma + silu * (1.0 - sigma))).astype(BF)
            product = nt(hidden.astype(BF), wd)
            d_rows = nt(d_gate, wg) + nt(d_up, wu)
            at = slice(n * rows, (n + 1) * rows)
            stage[0, at, :] = d_gate
            stage[1, at, :] = d_up
            stage[2, at, :] = weighted
            if routed:
                pairs = (hidden * back_h).astype(BF)
                d_share = nt(jnp.ones((16, CHUNK), BF), pairs)

            out_acc[n] += product
            dx_acc[n, 0:rows, :] += d_rows
            if routed:
                dx_acc[n, rows : rows + 16, 0:rows] += d_share

        for nxt in range(1, CHUNKS):

            @pl.when(k + 1 == nxt)
            def _():
                start_loads(nxt, nxt % 2)

        @pl.when(k >= 2)
        def _():
            for copy in stores(0, b):
                copy.wait()

        if before is not None:
            for copy in loads(before, scratch[9], scratch[10], 0, b):
                copy.wait()
        for i in range(3):
            part = tn(xc[i // 2], stage[i])
            if before is not None:
                part = part + scratch[9][b, i].astype(F32)
            dw_out[b, i] = part.astype(BF)
        for now in range(CHUNKS):

            @pl.when(k == now)
            def _():
                for copy in stores(now, now % 2):
                    copy.start()
                if emit is not None:
                    emit(now)

        return carry

    lax.fori_loop(0, CHUNKS, chunk, 0)
    for n in range(blocks):
        outs[n][...] = out_acc[n].astype(BF)
        dxs[n][...] = dx_acc[n].astype(BF)
    for b in range(2):
        for copy in stores(0, b):
            copy.wait()


def unit_scratch(blocks, rows, extra, width, per, chained):
    scratch = [
        pltpu.VMEM((blocks, rows, width), F32),
        pltpu.VMEM((blocks, rows + extra, width), F32),
        pltpu.VMEM((blocks, rows, 1), F32),
        pltpu.VMEM((2, 3, width, CHUNK), BF),
        pltpu.VMEM((3, blocks * rows, CHUNK), BF),
        pltpu.VMEM((2, 3, width, CHUNK), BF),
        pltpu.SemaphoreType.DMA((2, per)),
        pltpu.SemaphoreType.DMA((2, per)),
        pltpu.VMEM((2, blocks * rows, width), BF),
    ]
    if chained:
        scratch += [
            pltpu.VMEM((2, 3, width, CHUNK), BF),
            pltpu.SemaphoreType.DMA((2, per)),
        ]
    return scratch


def shared_kernel(
    x, c, piece, bank, x1, x2, x3, expert_in,
    out, dx, grads_own, grads_other, shared_mate, y1, y2, y3, experts,
    send, recv, *scratch,
):
    net = Net(send, recv)
    events = [net.event() for _ in range(4)]
    core_events = [net.event() for _ in range(8)]
    peers = [(net.cousins[o], net.shard) for o in (1, 2, 3)]
    net.meet("line", peers + [(net.rep, net.across)])
    arrivals = exchange(net, (x1, x2, x3), (y1, y2, y3))
    near, second = experts.at[net.place(1, 0), pl.ds(2, 1)], experts.at[net.place(2, 0)]
    net.put(events[0], near, near, net.rep, net.across)
    net.put(events[1], second, second, net.rep, net.across)
    below = experts.at[lax.max(net.shard - 4, net.x)]
    above = experts.at[lax.min(net.shard + 4, 6 + net.x)]
    net.put(events[2], below, below, net.rep, net.up, net.z == 2)
    net.put(events[3], above, above, net.rep, net.down, net.z == 1)
    spots = [net.place(n % 4, n // 4 % 2) for n in range(8)]
    halves = [net.core, 1 - net.core]
    done = scratch[5]
    slices = [done.at[n // 4, :, :, pl.ds(n % 4 * 128, 128)] for n in range(8)]
    places = [shared_mate.at[spot] for spot in spots]

    def source(n):
        return piece if n == 0 else bank.at[halves[n // 8], spots[n % 8]]

    def target(n):
        return (grads_own, grads_other)[n // 8].at[spots[n % 8]]

    def emit(now):
        if now >= 2:
            for n in range(4 * now - 8, 4 * now - 4):
                net.put(core_events[n], slices[n], places[n], net.mate, net.shard)

    unit_bank(
        None, None, [x], [c], source, target, None, 128, [out], [dx], scratch, None, emit
    )
    for event, like in arrivals:
        net.got(event, like)
    net.got(events[0], near)
    net.got(events[1], second)
    net.got(events[2], second, net.z == 3)
    net.got(events[3], second, net.z == 0)
    for n in range(8):
        net.got(core_events[n], places[n])
    net.close()


def far_kernel(
    ext, xa, xb, ca, cb, expert_piece, shared_own, shared_mate, expert_in,
    oa, ob, da, db, grads, shared_keep, shared_y, experts,
    part_a, part_b, part_sems, send, recv, *scratch,
):
    net = Net(send, recv)
    events = [net.event() for _ in range(9)]
    far = net.cousins[2]
    parts = copies_of(((shared_own, part_a), (shared_mate, part_b)), part_sems)
    for copy in parts:
        copy.start()
    net.meet("none", [(net.rep, net.across), (far, net.shard)])
    last = experts.at[net.place(3, 0)]
    net.put(events[0], last, last, net.rep, net.across)
    spots = [net.place(n // 2, n % 2) for n in range(8)]
    y, quarter = lax.div(net.rep, 2), part_a.shape[2] // 2
    rows = [pl.ds(pl.multiple_of(n * quarter, 128), quarter) for n in (y, 1 - y)]
    keep = pltpu.make_async_copy(part_a.at[:, :, rows[0], :], shared_keep, part_sems.at[2])
    away = [part_a.at[j, :, rows[1], :] for j in range(SLOTS)]

    def source(n):
        return expert_piece if n == 0 else experts.at[spots[n]]

    def target(n):
        return grads.at[spots[n]]

    def ready(k):
        if k == 3:
            net.got(events[0], last)

    for copy in parts:
        copy.wait()

    def add(j, carry):
        part_a[j] = part_a[j] + part_b[j]
        return carry

    lax.fori_loop(0, SLOTS, add, 0)
    for j in range(SLOTS):
        net.put(events[1 + j], away[j], shared_y.at[j], far, net.shard)
    keep.start()
    unit_bank(
        net.rep, ext, [xa, xb], [ca, cb], source, target, None, 256, [oa, ob], [da, db],
        scratch, ready,
    )
    keep.wait()
    for j in range(SLOTS):
        net.got(events[1 + j], shared_y.at[j])
    net.close()


def near_kernel(
    ext, xa, xb, ca, cb, expert_piece, experts, before, far_a, far_b,
    shared_keep, shared_y,
    oa, ob, da, shared_total, grads, back_a, back_b, back_c, expert_x,
    db, part_a, part_b, from_x, from_z, third, sems, send, recv, *scratch,
):
    net = Net(send, recv)
    events = [net.event() for _ in range(4)]
    x_events = [net.event() for _ in range(4)]
    z_events = [net.event() for _ in range(3)]
    peers = [(net.cousins[o], net.shard) for o in (1, 2, 3)]
    one = pltpu.make_async_copy(shared_keep, part_a, sems.at[0])
    two = pltpu.make_async_copy(shared_y, part_b, sems.at[1])
    one.start()
    two.start()
    net.meet("all", peers + [(net.rep, net.across)])
    net.put(events[0], far_a, back_a, net.cousins[2], net.shard)
    net.put(events[1], far_b, back_b, net.cousins[3], net.shard)
    one.wait()
    two.wait()

    def add(j, carry):
        part_a[j] = part_a[j] + part_b[j]
        return carry

    lax.fori_loop(0, SLOTS, add, 0)
    mine = [net.cycle(d) for d in range(4)]
    theirs = [spot + 1 - 2 * net.x for spot in mine]
    for d in (2, 1, 3, 0):
        net.put(x_events[d], part_a.at[theirs[d]], from_x.at[d], net.rep, net.across)
    pieces, lands = [part_a.at[spot] for spot in mine], [from_x.at[d] for d in range(4)]
    ends = [from_z.at[d] for d in range(3)]
    spots = [net.place(3 - n // 2, n % 2) for n in range(8)]
    own_slot = 6
    done, target = scratch[5], expert_x.at[net.levels[3]]

    def source(n):
        return expert_piece if n == own_slot else experts.at[spots[n]]

    def ready(k):
        if k == 2:
            for d in (2, 1, 3, 0):
                net.got(x_events[d], lands[d])
                part_a[mine[d]] = part_a[mine[d]] + from_x[d]
                if d:
                    net.put(z_events[d - 1], pieces[d], ends[d - 1], net.rep, mine[d])

    def emit(now):
        if now == 0:
            third[...] = done[0, :, :, 256:512]
            net.put(events[3], third, target, net.rep, net.across)

    unit_bank(
        net.rep, ext, [xa, xb], [ca, cb], source,
        lambda n: grads.at[spots[n]], lambda n: before.at[spots[n]],
        256, [oa, ob], [da, db], scratch, ready, emit,
    )
    net.put(events[2], db, back_c, net.mate, net.shard)
    total = part_a[mine[0]].astype(F32)
    for d in (1, 2, 3):
        net.got(z_events[d - 1], ends[d - 1])
        total = total + from_z[d - 1].astype(F32)
    shared_total[...] = total.astype(BF)
    net.got(events[0], back_a)
    net.got(events[1], back_b)
    net.got(events[2], back_c)
    net.got(events[3], target)
    net.close()


def plain_bank_kernel(blocks, unit, routed, chained, ext, *refs):
    refs = list(refs)

    def take(n):
        taken = refs[:n]
        del refs[:n]
        return taken

    xs, cs = take(blocks), take(blocks)
    bank = take(1)[0]
    before = take(1)[0] if chained else None
    outs, dxs = take(blocks), take(blocks)
    grads = take(1)[0]
    unit_bank(
        lax.axis_index("rep") if routed else None,
        ext, xs, cs,
        lambda n: bank.at[n],
        lambda n: grads.at[n],
        (lambda n: before.at[n]) if chained else None,
        unit, outs, dxs, refs,
    )


def plain_bank(ext, xs, cs, bank, before, routed):
    blocks, (rows, width) = len(xs), xs[0].shape
    chained = before is not None
    extra, unit = (16 if routed else 0), bank.shape[3]
    operands = [ext, *xs, *cs, bank] + ([before] if chained else [])
    outs = [shape((rows, width))] * blocks + [shape((rows + extra, width))] * blocks
    results = call(
        functools.partial(plain_bank_kernel, blocks, unit, routed, chained),
        outs + [shape(bank.shape)],
        [VMEM] * (1 + 2 * blocks) + [ANY] * (2 if chained else 1),
        [VMEM] * (2 * blocks) + [ANY],
        unit_scratch(blocks, rows, extra, width, CHUNK // unit, chained),
        flops=18 * blocks * rows * width * 4 * CHUNK,
        moved=30 * 2**20,
    )(*operands)
    return results[:blocks], results[blocks : 2 * blocks], results[2 * blocks]


def combine_rows(
    slot, d0, d1, d2, d3, d_shared, probs, middle, normed, cot, ext, attended, wo,
    d_middle, d_attended, grad_ext, branch, router_acc, gain_acc,
):
    tokens, width = middle.shape
    rep = lax.axis_index("rep")
    gain = ext[5:6, :]
    router = router_rows(ext)
    router_acc[...] = jnp.zeros_like(router_acc)
    gain_acc[...] = jnp.zeros_like(gain_acc)

    def tile(t, carry):
        at = pl.ds(pl.multiple_of(t * TILE, TILE), TILE)
        slot_one, slot_two = slot[at, 0:1], slot[at, 64:65]
        d_normed = d_shared[at, :].astype(F32)
        lane = iota((TILE, 128), 1)
        d_gates = jnp.zeros((TILE, 128), F32)
        for o, d in enumerate((d0, d1, d2, d3)):
            place = (iota((TILE, CAP), 1) + o * CAP).astype(F32)
            hit = (place == slot_one) | (place == slot_two)
            d_normed = d_normed + nn(ones_where(hit), d[0:CAP, :])
            share = d[CAP : CAP + 16, 0:CAP].astype(F32)[0:1, :]
            d_share = jnp.sum(jnp.where(hit, share, 0.0), axis=1, keepdims=True)
            d_gates = d_gates + jnp.where(lane == sibling(rep, o), d_share, 0.0)
        p = probs[at, :]
        inner = jnp.sum(d_gates * p, axis=1, keepdims=True)
        d_logits = (p * (d_gates - inner)).astype(BF)
        d_normed = d_normed + nn(d_logits, router)
        router_acc[...] += tn(d_logits, normed[at, :])
        rows = middle[at, :]
        scale = lax.rsqrt(jnp.mean(rows * rows, axis=1, keepdims=True) + EPSILON)
        unit = rows * scale
        gain_acc[...] += jnp.sum((d_normed * unit).reshape(TILE // 8, 8, width), axis=0)
        w = d_normed * gain
        inner = jnp.mean(w * unit, axis=1, keepdims=True)
        total = cot[at, :].astype(F32) + scale * (w - unit * inner)
        d_middle[at, :] = total
        rounded = total.astype(BF)
        branch[at, :] = rounded
        d_attended[at, :] = nt(rounded, wo[...]).astype(BF)
        return carry

    lax.fori_loop(0, tokens // TILE, tile, 0)
    row = iota((16, width), 0)
    total = jnp.sum(gain_acc[...], axis=0, keepdims=True)
    grad_ext[...] = jnp.where(row < 4, router_acc[0:16, :], jnp.where(row == 5, total, 0.0))


def output_rows(slot, o0, o1, o2, o3, shared, probs, middle, out, first, last):
    rep = lax.axis_index("rep")

    def tile(t, carry):
        at = pl.ds(pl.multiple_of(t * TILE, TILE), TILE)
        slot_one, slot_two = slot[at, 0:1], slot[at, 64:65]
        total = middle[at, :] + shared[at, :].astype(F32)
        p = probs[at, :]
        lane = iota((TILE, 128), 1)
        for o, rows in enumerate((o0, o1, o2, o3)):
            place = (iota((TILE, CAP), 1) + o * CAP).astype(F32)
            hit = (place == slot_one) | (place == slot_two)
            share = jnp.sum(jnp.where(lane == sibling(rep, o), p, 0.0), axis=1, keepdims=True)
            total = total + nn(jnp.where(hit, share, 0.0).astype(BF), rows[...])
        out[at, :] = total.astype(BF)
        return carry

    lax.fori_loop(first, last, tile, 0)


def back_pairs(
    q, k, v, d_out, out, lse, cosine, sine, dq, dk, dv, bias, dk_acc, dv_acc, step
):
    tokens, width = q.shape

    def pair(i, carry):
        step(i)
        cols = pl.ds(pl.multiple_of(i * 128, 128), 128)
        keys, values = k[:, cols], v[:, cols]
        half_keys = [keep_half(keys, 0), keep_half(keys, 1)]
        dk_acc[...] = jnp.zeros_like(dk_acc)
        dv_acc[...] = jnp.zeros_like(dv_acc)
        low = iota((TILE, 128), 1) < 64
        for t in range(tokens // TILE):
            begin = t * TILE
            end = min(tokens, begin + TILE + PIECE)
            at = slice(begin, begin + TILE)
            block, grad = q[at, cols], d_out[at, cols]
            product = grad.astype(F32) * out[at, cols].astype(F32)
            block_lse = lse[at, cols]
            d_block = None
            for h in range(2):
                block_h, grad_h = keep_half(block, h), keep_half(grad, h)
                scores = nt(block_h, keys[:end])
                scores = biased(scores, bias, begin, begin, end)
                probs = jnp.exp(scores - block_lse[:, 64 * h : 64 * h + 1])
                d_probs = nt(grad_h, values[:end])
                inner = jnp.sum(
                    jnp.where(low if h == 0 else ~low, product, 0.0), axis=1, keepdims=True
                )
                d_scores = (probs * (d_probs - inner)).astype(BF)
                part = nn(d_scores, half_keys[h][:end])
                d_block = part if d_block is None else d_block + part
                dk_acc[0:end, :] += tn(d_scores, block_h)
                dv_acc[0:end, :] += tn(probs.astype(BF), grad_h)
            dq[at, cols] = spin(d_block * 0.125, cosine[at, :], -sine[at, :]).astype(BF)
        dk[:, cols] = spin(dk_acc[...], cosine[...], -sine[...]).astype(BF)
        dv[:, cols] = dv_acc[...].astype(BF)
        return carry

    lax.fori_loop(0, width // 128, pair, 0)


def copies_of(pairs, sems):
    return [pltpu.make_async_copy(a, b, sems.at[i]) for i, (a, b) in enumerate(pairs)]


def fetch(sources, targets, sems):
    copies = copies_of(zip(sources, targets), sems)
    for copy in copies:
        copy.start()
    for copy in copies:
        copy.wait()


class Chain:
    def __init__(self, net, own, from_x, up_in, down_in, held, spare, sems):
        self.net, self.own, self.from_x = net, own, from_x
        self.into, self.held, self.spare, self.sems = (up_in, down_in), held, spare, sems
        keys = [(way, d, m) for way in range(2) for d in (1, 2, 3) for m in range(3)]
        self.events = {key: net.event() for key in keys}
        self.spots = [net.place(n, 0) for n in range(4)]
        self.sends, self.gets = {}, {}
        z = net.z
        for d in (1, 2, 3):
            up, down = lax.min(z + d, 3), lax.max(z - d, 0)
            for m in range(3):
                self.sends[0, d, m] = (held.at[up, m], z < 4 - d)
                self.sends[1, d, m] = (held.at[down, m], z > d - 1)
            self.gets[0, d] = (lax.min(z + d - 1, 3), (z > 0) & (z < 5 - d))
            self.gets[1, d] = (lax.max(z - d + 1, 0), (z < 3) & (z > d - 2))

    def level(self, n):
        to = self.net.levels[n]
        far = self.from_x.at[to]
        fetch([self.own.at[self.spots[n]], far], [self.held.at[to], self.spare.at[0]], self.sems)
        self.held[to] = self.held[to] + self.spare[0]

    def send(self, d, m):
        net = self.net
        for way, to in ((0, net.up), (1, net.down)):
            source, here = self.sends[way, d, m]
            target = self.into[way].at[d - 1, m]
            net.put(self.events[way, d, m], source, target, net.rep, to, here)

    def take(self, d, m):
        net = self.net
        for way in range(2):
            to, here = self.gets[way, d]

            def add():
                source = self.into[way].at[d - 1, m]
                event = self.events[way, d, m]
                net.copy(event, source, source, net.mate, net.shard).wait_recv()
                fetch([source], [self.spare.at[0, m]], self.sems)
                self.held[to, m] = self.held[to, m] + self.spare[0, m]

            when(here, add)


BACK_ROWS = 19


def back_kernel(starts, *refs):
    raw, refs = refs[:BACK_ROWS], refs[BACK_ROWS:]
    o1, o2, o3, grads, expert_x_in = refs[:5]
    outs, expert_total = refs[5:11], refs[11]
    r1, r2, r3, up_in, down_in, expert_x = refs[12:18]
    d_attended, branch, router_acc, gain_acc, bias, dk_acc, dv_acc = refs[18:25]
    local = refs[25 : 25 + BACK_ROWS]
    held, spare, sems, load_sems, out_sems, send, recv = refs[25 + BACK_ROWS : 32 + BACK_ROWS]
    d_middle, grad_wo, grad_ext, dq, dk, dv = refs[32 + BACK_ROWS :]
    stores = copies_of(zip((d_middle, grad_wo, grad_ext, dq, dk, dv), outs), out_sems)
    slot, d0, d1, d2, d3, d_shared, probs, middle, normed, cot, ext, attended, wo = local[:13]
    cosine, sine, q, k, v, lse = local[13:]
    loads = copies_of(zip(raw, local), load_sems)
    for copy in loads:
        copy.start()
    net = Net(send, recv)
    x_events = [net.event() for _ in range(3)]
    chain = Chain(net, grads, expert_x, up_in, down_in, held, spare, sems)
    peers = [(net.cousins[o], net.shard) for o in (1, 2, 3)]
    net.meet("line", peers + [(net.rep, net.across)])
    targets = [expert_x.at[net.levels[n]] for n in range(3)]
    for n in (2, 1, 0):
        source = grads.at[net.place(n, 1)]
        net.put(x_events[n], source, targets[n], net.rep, net.across)
    arrivals = exchange(net, (o1, o2, o3), (r1, r2, r3))
    chain.level(3)
    for m in range(3):
        chain.send(3, m)
    fill_bias(starts, bias)
    for copy in loads:
        copy.wait()
    combine_rows(
        slot, d0, d1, d2, d3, d_shared, probs, middle, normed, cot, ext, attended, wo,
        d_middle, d_attended, grad_ext, branch, router_acc, gain_acc,
    )
    stores[0].start()
    stores[2].start()
    net.got(x_events[2], targets[2])
    chain.level(2)
    for m in range(3):
        chain.take(3, m)
        chain.send(2, m)
    grad_wo[...] = tn(attended[...], branch[...]).astype(BF)
    stores[1].start()

    def step(i):
        @pl.when(i == 3)
        def _():
            net.got(x_events[1], targets[1])
            chain.level(1)

        @pl.when(i == 4)
        def _():
            for m in range(3):
                chain.take(2, m)
                chain.send(1, m)

    back_pairs(
        q, k, v, d_attended, attended, lse, cosine, sine, dq, dk, dv, bias, dk_acc, dv_acc, step
    )
    for copy in stores[3:]:
        copy.start()
    net.got(x_events[0], targets[0])
    chain.level(0)
    for event, like in arrivals:
        net.got(event, like)
    for m in range(3):
        chain.take(1, m)
    expert_total[...] = held[net.z]
    for copy in stores:
        copy.wait()
    net.close()


def plain_back_kernel(
    starts, slot, d0, d1, d2, d3, d_shared, probs, middle, normed, cot, ext, attended, wo,
    q, k, v, lse, cosine, sine,
    d_middle, grad_wo, grad_ext, dq, dk, dv,
    d_attended, branch, router_acc, gain_acc, bias, dk_acc, dv_acc,
):
    combine_rows(
        slot, d0, d1, d2, d3, d_shared, probs, middle, normed, cot, ext, attended, wo,
        d_middle, d_attended, grad_ext, branch, router_acc, gain_acc,
    )
    grad_wo[...] = tn(attended[...], branch[...]).astype(BF)
    fill_bias(starts, bias)
    back_pairs(
        q, k, v, d_attended, attended, lse, cosine, sine, dq, dk, dv, bias, dk_acc, dv_acc,
        lambda i: None,
    )


def norm_rows(x, ext, normed_all):
    gain = ext[4:5, :]

    def tile(t, carry):
        at = pl.ds(pl.multiple_of(t * TILE, TILE), TILE)
        rows = x[at, :].astype(F32)
        scale = lax.rsqrt(jnp.mean(rows * rows, axis=1, keepdims=True) + EPSILON)
        normed_all[at, :] = (rows * scale * gain).astype(BF)
        return carry

    lax.fori_loop(0, x.shape[0] // TILE, tile, 0)


def input_grad(x, ext, dq, dk, dv, wq, wk, wv, d_middle, grad_in, gain_acc, first, last):
    width = x.shape[1]
    gain = ext[4:5, :]

    def tile(t, carry):
        at = pl.ds(pl.multiple_of(t * TILE, TILE), TILE)
        rows = x[at, :].astype(F32)
        scale = lax.rsqrt(jnp.mean(rows * rows, axis=1, keepdims=True) + EPSILON)
        unit = rows * scale
        d_normed = nt(dq[at, :], wq[...]) + nt(dk[at, :], wk[...]) + nt(dv[at, :], wv[...])
        gain_acc[...] += jnp.sum((d_normed * unit).reshape(TILE // 8, 8, width), axis=0)
        w = d_normed * gain
        inner = jnp.mean(w * unit, axis=1, keepdims=True)
        grad_in[at, :] = d_middle[at, :] + scale * (w - unit * inner)
        return carry

    lax.fori_loop(first, last, tile, 0)


def tail_kernel(
    x, ext, dq, dk_in, dv, wq_in, wk_in, wv_in, grad_wo_in, grad_ext,
    d_middle_in, slot_in, o0_in, o1_in, o2_in, o3_in, shared_in, probs_in, middle_in,
    expert_total, shared_total,
    grad_in, outputs, weights, small, shared_far, shared_mate, shared_cross, e1, e2, e3,
    normed_all, gain_acc, gw, from_mate, from_x, from_z, from_y, result, from_core,
    tiny, tiny_in, dk, grad_wo, wq, wk, wv,
    d_middle, slot, o0, o1, o2, o3, shared_out, probs, middle, load_sems,
    send, recv,
):
    width = x.shape[1]
    half = width // SLOTS
    net = Net(send, recv)
    e_events = [net.event() for _ in range(3)]
    s_events = [net.event() for _ in range(3)]
    m_events = [net.event() for _ in range(2)]
    x_events = [[net.event() for _ in range(2)] for _ in range(4)]
    z_events = [[net.event() for _ in range(2)] for _ in range(3)]
    y_events = [net.event() for _ in range(2)]
    c_events = [net.event() for _ in range(2)]
    t_events = [net.event() for _ in range(6)]
    net.meet(
        "all", [(net.mate, net.shard), (net.cousins[2], net.shard), (net.rep, net.across)]
    )
    far = net.cousins[2]
    net.put(s_events[0], shared_total, shared_far, far, net.shard)
    net.put(s_events[1], shared_total, shared_mate, net.mate, net.shard)
    net.put(e_events[1], expert_total, e2, far, net.shard)
    net.put(e_events[0], expert_total, e1, net.mate, net.shard)
    pairs = (
        (dk_in, dk), (grad_wo_in, grad_wo), (wq_in, wq), (wk_in, wk), (wv_in, wv),
        (d_middle_in, d_middle), (slot_in, slot), (o0_in, o0), (o1_in, o1), (o2_in, o2),
        (o3_in, o3), (shared_in, shared_out), (probs_in, probs), (middle_in, middle),
    )
    loads = [pltpu.make_async_copy(a, b, load_sems.at[i]) for i, (a, b) in enumerate(pairs)]
    for copy in loads:
        copy.start()
    norm_rows(x, ext, normed_all)
    spots = [lax.rem(i + 2 * net.core, 4) for i in range(4)]

    def rows_of(spot):
        return pl.ds(pl.multiple_of(spot * half, 32), half)

    mine = [rows_of(net.cycle(d)) for d in range(4)]
    theirs = [rows_of(net.cycle(d) + 1 - 2 * net.x) for d in range(4)]

    def hand(i):
        net.put(m_events[i], gw.at[2 + i], from_mate.at[i], net.mate, net.shard)

    def cross(i):
        net.got(m_events[i], from_mate.at[i])
        gw[i] = gw[i] + from_mate[i]
        for d in (2, 1, 3, 0):
            source = gw.at[i, theirs[d]]
            net.put(x_events[d][i], source, from_x.at[d, i], net.rep, net.across)

    gw[spots[0]] = tn(normed_all[...], dq[...]).astype(BF)
    gw[spots[2]] = tn(normed_all[...], dv[...]).astype(BF)
    hand(0)
    loads[0].wait()
    loads[1].wait()
    gw[spots[1]] = tn(normed_all[...], dk[...]).astype(BF)
    gw[spots[3]] = grad_wo[...]
    hand(1)
    cross(0)
    cross(1)
    gain_acc[...] = jnp.zeros_like(gain_acc)
    for copy in loads[2:]:
        copy.wait()
    count = x.shape[0] // TILE

    def inputs(first, last):
        input_grad(x, ext, dq, dk, dv, wq, wk, wv, d_middle, grad_in, gain_acc, first, last)

    def results(first, last):
        output_rows(
            slot, o0, o1, o2, o3, shared_out, probs, middle, outputs, first, last
        )

    def add_across(d, i):
        net.got(x_events[d][i], from_x.at[d, i])
        gw[i, mine[d], :] = gw[i, mine[d], :] + from_x[d, i]
        if d:
            net.put(
                z_events[d - 1][i], gw.at[i, mine[d]], from_z.at[d - 1, i],
                net.rep, net.cycle(d),
            )

    def add_along(i):
        total = gw[i, mine[0], :].astype(F32)
        for d in (1, 2, 3):
            net.got(z_events[d - 1][i], from_z.at[d - 1, i])
            total = total + from_z[d - 1, i].astype(F32)
        result[0, i] = total.astype(BF)
        net.put(y_events[i], result.at[0, i], from_y.at[i], far, net.shard)

    def tiny_add(n, target_rep, target_shard):
        net.got(t_events[n], tiny_in.at[n])
        tiny[n + 1] = (tiny[n].astype(F32) + tiny_in[n].astype(F32)).astype(BF)
        if target_rep is not None:
            source, target = tiny.at[n + 1], tiny_in.at[n + 1]
            net.put(t_events[n + 1], source, target, target_rep, target_shard)

    inputs(0, 2)
    add_across(2, 0)
    add_across(1, 0)
    inputs(2, 3)
    add_across(3, 0)
    inputs(3, count)
    add_across(0, 0)
    row = iota((16, width), 0)
    total = jnp.sum(gain_acc[...], axis=0, keepdims=True)
    tiny[0] = (grad_ext[...] + jnp.where(row == 4, total, 0.0)).astype(BF)
    net.put(t_events[0], tiny.at[0], tiny_in.at[0], net.mate, net.shard)
    results(0, 1)
    add_across(2, 1)
    tiny_add(0, net.rep, net.across)
    results(1, 2)
    add_across(1, 1)
    tiny_add(1, far, net.shard)
    add_along(0)
    results(2, 3)
    add_across(3, 1)
    tiny_add(2, None, None)
    for d in (1, 2, 3):
        net.put(t_events[2 + d], tiny.at[3], tiny_in.at[2 + d], net.rep, net.cycle(d))
    net.got(s_events[0], shared_far)
    net.put(s_events[2], shared_far, shared_cross, net.mate, net.shard)
    results(3, count)
    add_across(0, 1)
    net.got(e_events[1], e2)
    net.put(e_events[2], e2, e3, net.mate, net.shard)
    total = tiny[3].astype(F32)
    for d in (1, 2, 3):
        net.got(t_events[2 + d], tiny_in.at[2 + d])
        total = total + tiny_in[2 + d].astype(F32)
    small[...] = total.astype(BF).astype(F32)
    add_along(1)
    for i in range(2):
        net.got(y_events[i], from_y.at[i])
        result[1, i] = (result[0, i].astype(F32) + from_y[i].astype(F32)).astype(BF)
        net.put(c_events[i], result.at[1, i], from_core.at[i], net.mate, net.shard)
        weights[spots[i]] = result[1, i].astype(F32)
    for i in range(2):
        net.got(c_events[i], from_core.at[i])
        weights[spots[2 + i]] = from_core[i].astype(F32)
    net.got(e_events[0], e1)
    net.got(s_events[1], shared_mate)
    net.got(s_events[2], shared_cross)
    net.got(e_events[2], e3)
    net.close()


def plain_tail_kernel(
    x, ext, dq, dk, dv, wq, wk, wv, d_middle,
    slot, o0, o1, o2, o3, shared_out, probs, middle,
    grad_in, outputs, gw, gain, normed_all, gain_acc,
):
    norm_rows(x, ext, normed_all)
    for i, d in enumerate((dq, dk, dv)):
        gw[i] = tn(normed_all[...], d[...]).astype(BF)
    gain_acc[...] = jnp.zeros_like(gain_acc)
    count = x.shape[0] // TILE
    input_grad(x, ext, dq, dk, dv, wq, wk, wv, d_middle, grad_in, gain_acc, 0, count)
    gain[...] = gain_acc[...]
    output_rows(
        slot, o0, o1, o2, o3, shared_out, probs, middle, outputs, 0, x.shape[0] // TILE
    )


def finish_kernel(
    e0, e1, e2, e3, wide, plain, q0, q1, q2, q3, weights, small,
    gate, up, down, wide_out, plain_out, s_gate, s_up, s_down,
    grad_q, grad_k, grad_v, grad_o, gain_one, gain_two, grad_router,
    part, wide_in, plain_in, ready_gate, ready_up, ready_down, in_sems, out_sems,
):
    rep, shard = lax.axis_index("rep"), lax.axis_index("shard")
    pairs = [(e, part.at[o]) for o, e in enumerate((e0, e1, e2, e3))]
    loads = copies_of(pairs + [(wide, wide_in), (plain, plain_in)], in_sems)
    for copy in loads:
        copy.start()
    stores = []
    for o in range(4):
        at = sibling(rep, o)
        pairs = [(ready_gate.at[o], gate.at[at]), (ready_up.at[o], up.at[at])]
        pairs.append((ready_down.at[o], down.at[at]))
        loads[o].wait()
        ready_gate[o] = part[o, 0].astype(F32)
        ready_up[o] = part[o, 1].astype(F32)
        ready_down[o] = part[o, 2].astype(F32).T
        made = [pltpu.make_async_copy(a, b, out_sems.at[3 * o + i]) for i, (a, b) in enumerate(pairs)]
        for copy in made:
            copy.start()
        stores += made
    passed = ((wide_in, wide_out), (plain_in, plain_out))
    for i, (a, b) in enumerate(passed):
        loads[4 + i].wait()
        copy = pltpu.make_async_copy(a, b, out_sems.at[12 + i])
        copy.start()
        stores.append(copy)
    quarter, span = q0.shape[1:]
    for o, piece in enumerate((q0, q1, q2, q3)):
        owner = sibling(rep, o)
        rows = pl.ds(pl.multiple_of(lax.div(owner, 2) * quarter, 128), quarter)
        cols = pl.ds(pl.multiple_of(lax.rem(owner, 2) * span, 128), span)
        s_gate[rows, cols] = piece[0].astype(F32)
        s_up[rows, cols] = piece[1].astype(F32)
        s_down[cols, rows] = piece[2].astype(F32).T
    for i, out in enumerate((grad_q, grad_k, grad_v, grad_o)):
        out[...] = weights[i]
    rows, width = weights.shape[1:]
    tiny = small[...].astype(BF)
    pick = ones_where(iota((width, rows), 0) == iota((width, rows), 1) + shard * rows)
    gains = nn(tiny, pick)
    gain_one[...] = gains[4:5, :]
    gain_two[...] = gains[5:6, :]
    grad_router[...] = dot(pick, tiny, 0, 1)[:, 0:4]
    for copy in stores:
        copy.wait()


def rope_tables(length, head_dim):
    positions = np.arange(length, dtype=np.float32)
    inverse_freq = np.float32(10000.0) ** (
        np.float32(-2.0) * np.arange(head_dim // 2, dtype=np.float32) / np.float32(head_dim)
    )
    angle = positions[:, None] * inverse_freq[None, :]
    cosine, sine = np.cos(angle), np.sin(angle)
    return (
        jnp.asarray(np.concatenate([cosine] * 4, axis=1)),
        jnp.asarray(np.concatenate([-sine, sine, -sine, sine], axis=1)),
    )


def body(
    inputs,
    piece_starts,
    routes,
    attn_gain,
    query_weight,
    key_weight,
    value_weight,
    out_weight,
    ffn_gain,
    router_weight,
    expert_gate,
    expert_up,
    expert_down,
    shared_gate,
    shared_up,
    shared_down,
    cotangent,
):
    _, tokens, width = inputs.shape
    shards = lax.axis_size("shard")
    rep, shard = lax.axis_index("rep"), lax.axis_index("shard")
    core = rep % 2
    ringed = shards == SLOTS
    rows = width // shards
    units = shared_gate.shape[1]
    x, cot, chosen = inputs[0], cotangent[0], routes[0]
    small = jnp.concatenate([router_weight.T, attn_gain[None], ffn_gain[None]], axis=0)
    small = jnp.pad(small, ((0, 10), (0, 0)))
    small = lax.dynamic_update_slice(jnp.zeros((16, width), BF), small, (0, shard * rows))
    if not ringed:
        wq, wk, wv, wo = [
            lax.all_gather(w, "shard", axis=0, tiled=True)
            for w in (query_weight, key_weight, value_weight, out_weight)
        ]
        ext = lax.psum(small.astype(F32), "shard")
        shared_pack = jnp.stack([shared_gate, shared_up, shared_down.T])
        my_half = lax.dynamic_slice_in_dim(shared_pack, core * (units // 2), units // 2, 2)
        expert_pack = jnp.stack([expert_gate[rep], expert_up[rep], expert_down[rep].T])

    cosine, sine = rope_tables(tokens, width // HEADS)
    token_f = shape((tokens, width))
    square = shape((width, width))
    packed = [shape((CAP, width))] * 4
    outs = [shape((8, tokens), F32), shape((tokens, 128), F32)] + [token_f] * 3
    work = 2 * tokens * width * (CAP * 4 + 3 * width)
    if ringed:
        expert_shape, half_shape = shape((3, width, units)), shape((3, width, units // 2))
        firsts = outs + [square] * 4 + [shape((16, width), F32), packed[0]]
        firsts += [expert_shape, half_shape]
        rank, slot, q, k, v, wq, wk, wv, wo, ext, cot_own, expert_pack, my_half, *heads = call(
            head_kernel,
            firsts + packed[1:] + [shape((SLOTS,) + expert_shape.shape)],
            [VMEM] * 11 + [ANY] * 6,
            [ANY] * 17,
            [
                pltpu.VMEM((2, SLOTS, 2 * rows + 16, width), BF),
                pltpu.VMEM((3, CAP, width), BF),
                pltpu.VMEM((2 * rows + 16, width), BF),
                pltpu.VMEM((units, width), BF),
                pltpu.VMEM((units // 2, width), BF),
                pltpu.SemaphoreType.DMA((6,)),
                pltpu.SemaphoreType.DMA((13,)),
                pltpu.SemaphoreType.DMA((34,)),
                pltpu.SemaphoreType.DMA((34,)),
                pltpu.SemaphoreType.DMA,
            ]
            + [pltpu.VMEM(a.shape, a.dtype) for a in firsts],
            flops=work,
            moved=24 * 2**20,
            group=0,
        )(
            chosen, chosen.T, cot, x, query_weight, key_weight, value_weight, out_weight, small,
            cosine, sine, expert_gate, expert_up, expert_down, shared_gate, shared_up, shared_down,
        )
        *cot_in, expert_bank = heads
        cot_in = [cot_own, *cot_in]
    else:
        rank, slot, q, k, v, *cot_out = call(
            plain_head_kernel, outs + packed, [VMEM] * 10, [VMEM] * 9, flops=work,
            moved=24 * 2**20,
        )(chosen, chosen.T, cot, x, cosine, sine, wq, wk, wv, ext)
        cot_in = [cot_out[0]] + [to_rep(cot_out[o], o) for o in (1, 2, 3)]

    outs = [token_f, shape((tokens, width), F32), shape((tokens, width), F32), token_f]
    outs += [shape((tokens, 128), F32)] + packed
    work = 2 * tokens * width * (8 * tokens + width + 4 * CAP)
    bias = pltpu.VMEM((tokens, tokens), F32)
    if ringed:
        attended, lse, middle, normed, probs, *x_out, shared_bank, expert_bank = call(
            forward_kernel,
            outs + [shape((2, SLOTS) + my_half.shape), shape((SLOTS,) + expert_pack.shape)],
            [SMEM] + [VMEM] * 7 + [ANY] * 3,
            [ANY] * 11,
            [
                bias,
                pltpu.SemaphoreType.DMA((9,)),
                pltpu.SemaphoreType.DMA((60,)),
                pltpu.SemaphoreType.DMA((60,)),
            ]
            + [pltpu.VMEM(a.shape, a.dtype) for a in outs],
            flops=work,
            moved=30 * 2**20,
            group=1,
            alias={10: 10},
        )(piece_starts, q, k, v, x, wo, ext, rank, my_half, expert_pack, expert_bank)
    else:
        attended, lse, middle, normed, probs, *x_out = call(
            plain_forward_kernel, outs, [SMEM] + [VMEM] * 7, [VMEM] * 9, [bias], flops=work,
            moved=30 * 2**20,
        )(piece_starts, q, k, v, x, wo, ext, rank)

    rows_out = shape((CAP, width))
    rows_back = shape((CAP + 16, width))
    if ringed:
        half_grads = shape((SLOTS,) + my_half.shape)
        shared_out, shared_dx, grads_own, _, shared_mate, y1, y2, y3, expert_bank = call(
            shared_kernel,
            [token_f] * 2 + [half_grads] * 3 + packed[:3] + [shape(expert_bank.shape)],
            [VMEM] * 2 + [ANY] * 6,
            [VMEM] * 2 + [ANY] * 7,
            [pltpu.SemaphoreType.DMA((15,)), pltpu.SemaphoreType.DMA((15,))]
            + unit_scratch(1, tokens, 0, width, 4, False),
            flops=18 * tokens * width * CHUNK * CHUNKS,
            moved=30 * 2**20,
            group=2,
            alias={7: 8},
        )(normed, cot, my_half, shared_bank, *x_out[1:], expert_bank)
        x_in = [x_out[0], y1, y2, y3]
        bank = shape(expert_bank.shape)
        quarter = (3, width // 2, units // 2)
        quarters = (SLOTS,) + quarter
        far_a, far_b, da, db, before, shared_keep, shared_y, expert_bank = call(
            far_kernel,
            [rows_out] * 2 + [rows_back] * 2 + [bank, shape(quarters), shape(quarters), bank],
            [VMEM] * 5 + [ANY] * 4,
            [VMEM] * 4 + [ANY] * 4,
            [
                pltpu.VMEM(half_grads.shape, BF),
                pltpu.VMEM(half_grads.shape, BF),
                pltpu.SemaphoreType.DMA((3,)),
                pltpu.SemaphoreType.DMA((9,)),
                pltpu.SemaphoreType.DMA((9,)),
            ]
            + unit_scratch(2, CAP, 16, width, 2, False),
            flops=36 * CAP * width * CHUNK * CHUNKS,
            moved=30 * 2**20,
            group=3,
            alias={8: 7},
        )(ext, *x_in[2:], *cot_in[2:], expert_pack, grads_own, shared_mate, expert_bank)
        bank_x, bank_z = (4,) + expert_pack.shape, (3,) + expert_pack.shape
        near_a, near_b, d0, shared_total, grads, d2, d3, d1, expert_x = call(
            near_kernel,
            [rows_out] * 2 + [rows_back, shape(quarter), bank] + [rows_back] * 3 + [shape(bank_x)],
            [VMEM] * 5 + [ANY] * 7,
            [VMEM] * 4 + [ANY] * 5,
            [
                pltpu.VMEM((CAP + 16, width), BF),
                pltpu.VMEM(quarters, BF),
                pltpu.VMEM(quarters, BF),
                pltpu.VMEM((4,) + quarter, BF),
                pltpu.VMEM((3,) + quarter, BF),
                pltpu.VMEM(expert_pack.shape, BF),
                pltpu.SemaphoreType.DMA((2,)),
                pltpu.SemaphoreType.DMA((11,)),
                pltpu.SemaphoreType.DMA((11,)),
            ]
            + unit_scratch(2, CAP, 16, width, 2, True),
            flops=36 * CAP * width * CHUNK * CHUNKS,
            moved=30 * 2**20,
            group=4,
        )(
            ext, *x_in[:2], *cot_in[:2], expert_pack, expert_bank, before, da, db,
            shared_keep, shared_y,
        )
        d_rows = [d0, d1, d2, d3]
    else:

        def slotted(part):
            every = lax.all_gather(part, "shard")
            every = every.reshape(SLOTS, shards // SLOTS, 3, width, part.shape[2])
            return every.transpose(0, 2, 3, 1, 4).reshape(SLOTS, 3, width, -1)

        shared_bank = slotted(my_half)
        shared_bank = jnp.concatenate([shared_bank, to_rep(shared_bank, 1)], axis=0)
        expert_bank = slotted(expert_pack)
        x_in = [x_out[0]] + [to_rep(x_out[o], o) for o in (1, 2, 3)]
        (shared_out,), (shared_dx,), shared_grads = plain_bank(
            ext, [normed], [cot], shared_bank, None, False
        )
        grads_own, grads_other = shared_grads[:SLOTS], shared_grads[SLOTS:]
        (far_a, far_b), (da, db), before = plain_bank(
            ext, x_in[2:], cot_in[2:], expert_bank, None, True
        )
        (near_a, near_b), (d0, d1), grads = plain_bank(
            ext, x_in[:2], cot_in[:2], expert_bank, before, True
        )
        d_rows = [d0, to_rep(d1, 1), to_rep(da, 2), to_rep(db, 3)]
    wide = shape((tokens, width), F32)
    outs = [wide, square, shape((16, width), F32)] + [token_f] * 3
    operands = (piece_starts, slot, *d_rows, shared_dx, probs, middle, normed, cot, ext, attended)
    operands += (wo,)
    specs = [SMEM] + [VMEM] * 15
    scratch = [
        pltpu.VMEM((tokens, width), BF),
        pltpu.VMEM((tokens, width), BF),
        pltpu.VMEM((128, width), F32),
        pltpu.VMEM((8, width), F32),
        bias,
        pltpu.VMEM((tokens, 128), F32),
        pltpu.VMEM((tokens, 128), F32),
    ]
    work = 2 * tokens * width * (2 * width + 4 * CAP) + 40 * tokens * tokens * width
    if ringed:
        late = (*operands[1:], cosine, sine, q, k, v, lse)
        d_middle, grad_wo, grad_ext, dq, dk, dv, expert_total, *back = call(
            back_kernel,
            outs
            + [shape(expert_pack.shape)]
            + [rows_out] * 3
            + [shape(bank_z), shape(bank_z), shape(bank_x)],
            [SMEM] + [ANY] * (len(late) + 5),
            [ANY] * 6 + [VMEM] + [ANY] * 6,
            scratch
            + [pltpu.VMEM(a.shape, a.dtype) for a in late]
            + [
                pltpu.VMEM(bank_x, BF),
                pltpu.VMEM((1,) + expert_pack.shape, BF),
                pltpu.SemaphoreType.DMA((2,)),
                pltpu.SemaphoreType.DMA((len(late),)),
                pltpu.SemaphoreType.DMA((6,)),
                pltpu.SemaphoreType.DMA((24,)),
                pltpu.SemaphoreType.DMA((24,)),
            ]
            + [pltpu.VMEM(a.shape, a.dtype) for a in outs],
            flops=work,
            moved=40 * 2**20,
            group=5,
            alias={24: 12},
        )(piece_starts, *late, near_b, far_a, far_b, grads, expert_x)
        operands = (x, ext, dq, dk, dv, wq, wk, wv, grad_wo, grad_ext)
        operands += (d_middle, slot, near_a, *back[:3], shared_out, probs, middle)
        strip = (2, width // SLOTS, width)
        grad_in, outputs, weights, small, *rest = call(
            tail_kernel,
            [wide, token_f, shape((4, rows, width), F32), shape((16, width), F32)]
            + [shape(quarter)] * 3
            + [shape(expert_pack.shape)] * 3,
            [VMEM] * 3 + [ANY, VMEM] + [ANY] * 4 + [VMEM] + [ANY] * 11,
            [VMEM] * 4 + [ANY] * 6,
            [
                pltpu.VMEM((tokens, width), BF),
                pltpu.VMEM((8, width), F32),
                pltpu.VMEM((4, width, width), BF),
                pltpu.VMEM((2, width, width), BF),
                pltpu.VMEM((4,) + strip, BF),
                pltpu.VMEM((3,) + strip, BF),
                pltpu.VMEM(strip, BF),
                pltpu.VMEM((2,) + strip, BF),
                pltpu.VMEM(strip, BF),
                pltpu.VMEM((4, 16, width), BF),
                pltpu.VMEM((6, 16, width), BF),
                pltpu.VMEM((tokens, width), BF),
                pltpu.VMEM((width, width), BF),
                pltpu.VMEM((width, width), BF),
                pltpu.VMEM((width, width), BF),
                pltpu.VMEM((width, width), BF),
                pltpu.VMEM((tokens, width), F32),
                pltpu.VMEM((tokens, 128), F32),
                pltpu.VMEM((CAP, width), BF),
                pltpu.VMEM((CAP, width), BF),
                pltpu.VMEM((CAP, width), BF),
                pltpu.VMEM((CAP, width), BF),
                pltpu.VMEM((tokens, width), BF),
                pltpu.VMEM((tokens, 128), F32),
                pltpu.VMEM((tokens, width), F32),
                pltpu.SemaphoreType.DMA((14,)),
                pltpu.SemaphoreType.DMA((32,)),
                pltpu.SemaphoreType.DMA((32,)),
            ],
            flops=2 * tokens * width * (6 * width + 4 * CAP),
            moved=40 * 2**20,
            group=6,
        )(*operands, expert_total, shared_total)
        banks = [shape((4, width, units), F32)] * 2 + [shape((4, units, width), F32)]
        banks += [shape((width, units), F32)] * 2 + [shape((units, width), F32)]
        shared_far, shared_mate, shared_cross, *experts = rest
        *finals, grad_q, grad_k, grad_v, grad_o, gain_one, gain_two, grad_router = call(
            finish_kernel,
            banks[:3] + [wide, token_f] + banks[3:] + [shape((rows, width), F32)] * 4
            + [shape((1, rows), F32)] * 2 + [shape((rows, 4), F32)],
            [ANY] * 6 + [VMEM] * 6,
            [ANY] * 5 + [VMEM] * 10,
            [
                pltpu.VMEM((4,) + expert_pack.shape, BF),
                pltpu.VMEM((tokens, width), F32),
                pltpu.VMEM((tokens, width), BF),
            ]
            + [pltpu.VMEM(b.shape, F32) for b in banks[:3]]
            + [pltpu.SemaphoreType.DMA((6,)), pltpu.SemaphoreType.DMA((14,))],
            moved=26 * 2**20,
        )(
            expert_total, *experts, grad_in, outputs,
            shared_total, shared_mate, shared_far, shared_cross, weights, small,
        )
        grad_in, outputs = finals.pop(3), finals.pop(3)
        gain_one, gain_two = gain_one[0], gain_two[0]
    else:
        d_middle, grad_wo, grad_ext, dq, dk, dv = call(
            plain_back_kernel, outs, specs + [VMEM] * 4, [VMEM] * 6, scratch, flops=work,
            moved=40 * 2**20,
        )(*operands, q, k, v, lse, cosine, sine)
        out_rows = [near_a, to_rep(near_b, 1), to_rep(far_a, 2), to_rep(far_b, 3)]
        grad_in, outputs, gw, gain = call(
            plain_tail_kernel,
            [wide, token_f, shape((3, width, width)), shape((8, width), F32)],
            [VMEM] * 17,
            [VMEM] * 4,
            [pltpu.VMEM((tokens, width), BF), pltpu.VMEM((8, width), F32)],
            flops=2 * tokens * width * (6 * width + 4 * CAP),
            moved=40 * 2**20,
        )(
            x, ext, dq, dk, dv, wq, wk, wv, d_middle, slot, *out_rows, shared_out, probs, middle
        )

        def over_rep(total):
            return lax.psum(total.astype(BF), "rep").astype(F32)

        def unslot(every, part_units):
            every = every.reshape(SLOTS, 3, width, shards // SLOTS, part_units)
            every = every.transpose(0, 3, 1, 2, 4).reshape(shards, 3, width, part_units)
            return lax.psum_scatter(every, "shard", scatter_dimension=0)

        grad_q, grad_k, grad_v, grad_o = (
            over_rep(lax.psum_scatter(w, "shard", tiled=True))
            for w in (gw[0], gw[1], gw[2], grad_wo)
        )
        small = grad_ext.at[4].add(jnp.sum(gain, axis=0))
        small = lax.psum(small, ("rep", "shard"))
        shared_sum = grads_own.astype(F32) + to_rep(grads_other, 1).astype(F32)
        total = unslot(shared_sum.astype(BF), units // 2).astype(F32)
        total = (total + to_rep(total.astype(BF), 2).astype(F32)).astype(BF)
        mate = to_rep(total, 1)
        shared_full = jnp.concatenate(
            [jnp.where(core == 0, total, mate), jnp.where(core == 0, mate, total)], axis=2
        ).astype(F32)
        expert_total = unslot(grads, units).astype(BF)
        parts = jnp.stack([expert_total] + [to_rep(expert_total, o) for o in (1, 2, 3)])
        full = jnp.take(parts, jnp.arange(4) ^ rep, axis=0).astype(F32)
        finals = (full[:, 0], full[:, 1], full[:, 2].transpose(0, 2, 1))
        finals += (shared_full[0], shared_full[1], shared_full[2].T)
        tiny = lax.dynamic_slice(small, (0, shard * rows), (16, rows))
        gain_one, gain_two, grad_router = tiny[4], tiny[5], tiny[:4].T
    return (
        outputs[None],
        grad_in[None],
        gain_one,
        grad_q,
        grad_k,
        grad_v,
        grad_o,
        gain_two,
        grad_router,
        *finals,
    )


def solution(mesh):
    in_specs = (
        P(("rep", "shard"), None, None),
        P(("rep", "shard"), None),
        P(("rep", "shard"), None, None),
        P("shard"),
        P("shard", None),
        P("shard", None),
        P("shard", None),
        P("shard", None),
        P("shard"),
        P("shard", None),
        P(None, None, "shard"),
        P(None, None, "shard"),
        P(None, "shard", None),
        P(None, "shard"),
        P(None, "shard"),
        P("shard", None),
        P(("rep", "shard"), None, None),
    )
    out_specs = (
        P(("rep", "shard"), None, None),
        P(("rep", "shard"), None, None),
        P("shard"),
        P("shard", None),
        P("shard", None),
        P("shard", None),
        P("shard", None),
        P("shard"),
        P("shard", None),
        P(None, None, "shard"),
        P(None, None, "shard"),
        P(None, "shard", None),
        P(None, "shard"),
        P(None, "shard"),
        P("shard", None),
    )
    return jax.shard_map(body, mesh=mesh, in_specs=in_specs, out_specs=out_specs, check_vma=False)
```

```python
import functools

import jax
import jax.numpy as jnp
import numpy as np
from jax import lax
from jax.experimental import pallas as pl
from jax.experimental.pallas import tpu as pltpu
from jax.sharding import PartitionSpec as P

HEADS = 12
PIECE = 256
CAP = 576
EPSILON = 1e-06
MASKED = -1e30
F32, BF = jnp.float32, jnp.bfloat16
AXES = ("rep", "shard")
TILE = 256
SLOTS = 8
VMEM_LIMIT = 62 * 2**20
ANY = pl.BlockSpec(memory_space=pl.ANY)
SMEM = pl.BlockSpec(memory_space=pltpu.SMEM)
VMEM = pl.BlockSpec(memory_space=pltpu.VMEM)


def dot(a, b, i, j):
    return lax.dot_general(a, b, (((i,), (j,)), ((), ())), preferred_element_type=F32)


def nn(a, b):
    return dot(a, b, 1, 0)


def nt(a, b):
    return dot(a, b, 1, 1)


def tn(a, b):
    return dot(a, b, 0, 0)


def iota(shape, dim):
    return lax.broadcasted_iota(jnp.int32, shape, dim)


def ones_where(cond):
    return jnp.where(cond, 1.0, 0.0).astype(BF)


def call(
    kernel, out_shape, in_specs, out_specs, scratch=(), flops=0, moved=0, grid=None, group=None,
    alias=None,
):
    extra = {} if grid is None else {"grid": grid}
    params = {} if group is None else {"collective_id": group, "has_side_effects": True}
    return pl.pallas_call(
        kernel,
        out_shape=out_shape,
        in_specs=in_specs,
        out_specs=out_specs,
        scratch_shapes=list(scratch),
        input_output_aliases=alias or {},
        compiler_params=pltpu.CompilerParams(vmem_limit_bytes=VMEM_LIMIT, **params),
        cost_estimate=pl.CostEstimate(flops=flops, bytes_accessed=moved, transcendentals=0),
        **extra,
    )


def shape(dims, dtype=BF):
    return jax.ShapeDtypeStruct(dims, dtype)


def permute(x, move):
    reps, shards = lax.axis_size("rep"), lax.axis_size("shard")
    pairs = []
    for r in range(reps):
        for s in range(shards):
            to_r, to_s = move(r, s)
            pairs.append((r * shards + s, to_r * shards + to_s))
    return lax.ppermute(x, AXES, pairs)


def to_rep(x, offset):
    return permute(x, lambda r, s: (r ^ offset, s))


def spin(block, cosine, sine):
    lane = iota(block.shape, 1)
    partner = jnp.where(lane % 64 < 32, pltpu.roll(block, 96, 1), pltpu.roll(block, 32, 1))
    return block * cosine + partner * sine


def sibling(rep, o):
    return 2 * lax.rem(lax.div(rep, 2) + o // 2, 2) + lax.rem(lax.rem(rep, 2) + o % 2, 2)


def route_slots(rep, routes, routes_t, rank_out, slot_out):
    tokens = routes.shape[0]
    first, second = routes_t[0:1, :], routes_t[1:2, :]
    expert = iota((8, tokens), 0)
    chosen = (expert == first) | (expert == second)
    upper = ones_where(iota((tokens, tokens), 0) <= iota((tokens, tokens), 1))
    rank = nn(ones_where(chosen), upper) - 1.0
    rank_out[...] = jnp.where(chosen, rank, -1.0)
    lane = iota((tokens, 128), 1)
    one, two = routes[:, 0:1], routes[:, 1:2]
    lower = ones_where(iota((tokens, tokens), 0) >= iota((tokens, tokens), 1))
    place = nn(lower, ones_where((lane == one) | (lane == two))) - 1.0
    for o in range(1, 4):
        place = place + jnp.where(lane == sibling(rep, o), float(o * CAP), 0.0)
    slot_one = jnp.sum(jnp.where(lane == one, place, 0.0), axis=1, keepdims=True)
    slot_two = jnp.sum(jnp.where(lane == two, place, 0.0), axis=1, keepdims=True)
    slot_out[...] = jnp.where(lane < 64, slot_one, slot_two)


def pack_row(rep, rank, source, o, out):
    row = rank[pl.ds(sibling(rep, o), 1), :]
    pick = ones_where(iota((CAP, source.shape[0]), 0).astype(F32) == row)
    out[...] = nn(pick, source[...]).astype(BF)


def pack_rows(rep, rank, source, packed):
    for o, out in enumerate(packed):
        pack_row(rep, rank, source, o, out)


def qkv_rows(x, ext, cosine, sine, wq, wk, wv, q, k, v):
    tokens, width = x.shape
    gain = ext[4:5, :]

    def tile(t, carry):
        at = pl.ds(pl.multiple_of(t * TILE, TILE), TILE)
        rows_in = x[at, :].astype(F32)
        scale = lax.rsqrt(jnp.mean(rows_in * rows_in, axis=1, keepdims=True) + EPSILON)
        normed = (rows_in * scale * gain).astype(BF)
        cos_t, sin_t = cosine[at, :], sine[at, :]
        for weight, out, factor in ((wq, q, 0.125), (wk, k, 1.0)):
            full = nn(normed, weight[...])
            for b in range(width // 128):
                turned = spin(full[:, b * 128 : (b + 1) * 128], cos_t, sin_t)
                out[at, b * 128 : (b + 1) * 128] = turned.astype(BF) * jnp.asarray(factor, BF)
        v[at, :] = nn(normed, wv[...]).astype(BF)
        return carry

    lax.fori_loop(0, tokens // TILE, tile, 0)


def when(cond, body):
    if cond is True:
        body()
    elif cond is not False:
        pl.when(cond)(body)


def both(one, two):
    if one is True or two is False:
        return two
    if two is True or one is False:
        return one
    return one & two


class Net:
    def __init__(self, send, recv):
        self.rep, self.shard = lax.axis_index("rep"), lax.axis_index("shard")
        self.core, self.z = lax.rem(self.rep, 2), lax.div(self.shard, 2)
        self.x = lax.rem(self.shard, 2)
        self.mate = self.rep + 1 - 2 * self.core
        self.across = self.shard + 1 - 2 * self.x
        first = lax.max(self.z - 1, 1 - self.z)
        third = 3 * (1 - lax.div(self.z, 2))
        self.levels = [self.z, first, 6 - self.z - first - third, third]
        self.up = lax.min(self.shard + 2, 6 + self.x)
        self.down = lax.max(self.shard - 2, self.x)
        self.cousins = [self.rep] + [sibling(self.rep, o) for o in (1, 2, 3)]
        self.send, self.recv = send, recv
        self.count, self.open = 0, {}

    def event(self):
        self.count += 1
        return self.count - 1

    def place(self, n, side):
        return self.levels[n] * 2 + (self.x if side == 0 else 1 - self.x)

    def cycle(self, d):
        return lax.rem(self.z + d, 4) * 2 + self.x

    def copy(self, event, source, target, rep, shard):
        return pltpu.make_async_remote_copy(
            src_ref=source,
            dst_ref=target,
            send_sem=self.send.at[event],
            recv_sem=self.recv.at[event],
            device_id=(rep, shard),
            device_id_type=pl.DeviceIdType.MESH,
        )

    def put(self, event, source, target, rep, shard, cond=True):
        when(cond, self.copy(event, source, target, rep, shard).start)
        self.open[event] = (cond, source)

    def got(self, event, like, cond=True):
        when(cond, self.copy(event, like, like, self.mate, self.shard).wait_recv)

    def settle(self, event):
        cond, source = self.open.pop(event)
        when(cond, self.copy(event, source, source, self.mate, self.shard).wait_send)

    def close(self):
        for event, (cond, source) in self.open.items():
            when(cond, self.copy(event, source, source, self.mate, self.shard).wait_send)

    def meet(self, z_ways, others):
        barrier = pltpu.get_barrier_semaphore()

        def greet(rep, shard):
            pl.semaphore_signal(
                barrier, inc=1, device_id=(rep, shard), device_id_type=pl.DeviceIdType.MESH
            )

        count = len(others)
        for rep, shard in others:
            greet(rep, shard)
        if z_ways == "line":
            when(self.z < 3, lambda: greet(self.rep, self.up))
            when(self.z > 0, lambda: greet(self.rep, self.down))
            count = count + lax.min(self.z, 1) + lax.min(3 - self.z, 1)
        if z_ways == "all":
            for d in (1, 2, 3):
                greet(self.rep, self.cycle(d))
            count = count + 3
        pl.semaphore_wait(barrier, count)


class Line:
    def __init__(self, net, bank, ways=4):
        self.net, self.bank = net, bank
        self.events = {(way, k): net.event() for way in range(ways) for k in range(-3, 4)}
        self.spots = {0: (net.shard, True)}
        for k in (1, 2, 3):
            self.spots[k] = (lax.min(net.shard + 2 * k, 6 + net.x), net.z < 4 - k)
            self.spots[-k] = (lax.max(net.shard - 2 * k, net.x), net.z >= k)
        self.flips = {k: spot + 1 - 2 * net.x for k, (spot, _) in self.spots.items()}
        self.onward = {k: both(self.spots[k][1], net.z < 3) for k in self.spots}
        self.back = {k: both(self.spots[k][1], net.z > 0) for k in self.spots}

    def spread(self, k, source):
        net, (spot, here) = self.net, self.spots[k]
        target = self.bank.at[net.core, spot]
        if -3 < k <= 0:
            event = self.events[0, k - 1]
            net.put(event, source, target, net.rep, net.up, self.onward[k])
        if 0 <= k < 3:
            event = self.events[0, k + 1]
            net.put(event, source, target, net.rep, net.down, self.back[k])
        net.put(self.events[1, k], source, target, net.rep, net.across, here)
        net.put(self.events[2, k], source, target, net.mate, net.shard, here)

    def along(self, k):
        spot, here = self.spots[k]
        piece = self.bank.at[self.net.core, spot]
        self.net.got(self.events[0, k], piece, here)
        self.spread(k, piece)

    def over(self, k):
        net, here = self.net, self.spots[k][1]
        piece = self.bank.at[net.core, self.flips[k]]
        net.got(self.events[1, k], piece, here)
        net.put(self.events[3, k], piece, piece, net.mate, net.shard, here)

    def finish(self):
        other = 1 - self.net.core
        for k in (0, 1, -1, 2, -2, 3, -3):
            spot, here = self.spots[k]
            self.net.got(self.events[2, k], self.bank.at[other, spot], here)
            self.net.got(self.events[3, k], self.bank.at[other, self.flips[k]], here)


class Spread:
    def __init__(self, net, piece, bank):
        self.net, self.piece, self.bank = net, piece, bank
        self.line = Line(net, bank, 8)
        self.events, self.spots, self.flips = self.line.events, self.line.spots, self.line.flips
        self.half = piece.shape[1] // 2
        y = lax.div(net.rep, 2)
        self.rows = [pl.ds(pl.multiple_of(n * self.half, 128), self.half) for n in (y, 1 - y)]
        self.far = net.cousins[2]

    def view(self, core, spot, rows):
        return self.bank.at[core, spot, :, self.rows[rows], :]

    def begin(self):
        net = self.net
        source = self.piece.at[:, self.rows[0], :]
        target = self.view(net.core, net.shard, 0)
        net.put(self.events[0, -1], source, target, net.rep, net.up, self.line.onward[0])
        net.put(self.events[0, 1], source, target, net.rep, net.down, self.line.back[0])
        net.put(self.events[1, 0], source, target, net.rep, net.across)
        whole = self.bank.at[net.core, net.shard]
        net.put(self.events[2, 0], self.piece, whole, net.mate, net.shard)

    def hand(self, way, k, here, piece):
        net = self.net
        net.put(self.events[way + 4, k], piece, piece, self.far, net.shard, here)
        net.put(self.events[way + 2, k], piece, piece, net.mate, net.shard, here)

    def along(self, k):
        net, (spot, here) = self.net, self.spots[k]
        piece = self.view(net.core, spot, 0)
        net.got(self.events[0, k], piece, here)
        if -3 < k < 0:
            net.put(self.events[0, k - 1], piece, piece, net.rep, net.up, self.line.onward[k])
        if 0 < k < 3:
            net.put(self.events[0, k + 1], piece, piece, net.rep, net.down, self.line.back[k])
        net.put(self.events[1, k], piece, piece, net.rep, net.across, here)
        self.hand(0, k, here, piece)

    def over(self, k):
        net, here = self.net, self.spots[k][1]
        piece = self.view(net.core, self.flips[k], 0)
        net.got(self.events[1, k], piece, here)
        self.hand(1, k, here, piece)

    def relay(self, way, k):
        net, here = self.net, self.spots[k][1]
        spot = self.spots[k][0] if way == 0 else self.flips[k]
        piece = self.view(net.core, spot, 1)
        net.got(self.events[way + 4, k], piece, here)
        net.put(self.events[way + 6, k], piece, piece, net.mate, net.shard, here)

    def finish(self):
        net, other = self.net, 1 - self.net.core
        net.got(self.events[2, 0], self.bank.at[other, net.shard])
        for k in (0, 1, -1, 2, -2, 3, -3):
            spot, here = self.spots[k]
            if k:
                net.got(self.events[2, k], self.view(other, spot, 0), here)
                net.got(self.events[6, k], self.view(other, spot, 1), here)
            net.got(self.events[3, k], self.view(other, self.flips[k], 0), here)
            net.got(self.events[7, k], self.view(other, self.flips[k], 1), here)


def exchange(net, sources, targets):
    events = [net.event() for _ in range(3)]
    for o in (2, 3, 1):
        net.put(events[o - 1], sources[o - 1], targets[o - 1], net.cousins[o], net.shard)
    return [(events[o], targets[o]) for o in range(3)]


def head_kernel(
    routes, routes_t, cot, x, wq_in, wk_in, wv_in, wo_in, small, cosine, sine,
    e_gate, e_up, e_down, s_gate, s_up, s_down,
    *refs,
):
    width = x.shape[1]
    half = width // SLOTS
    outs, (c1, c2, c3, experts) = refs[:13], refs[13:17]
    bank, packed, piece, e_raw, s_raw, pack_sems, out_sems, send, recv, own_sem = refs[17:27]
    rank, slot, q, k, v, wq, wk, wv, wo, ext, c0, expert_piece, shared_piece = refs[27:]
    stores = copies_of(zip(refs[27:], outs), out_sems)
    net = Net(send, recv)
    units = s_raw.shape[0]
    cut = pl.ds(pl.multiple_of(net.core * units, 128), units)
    packs = copies_of(
        (
            (e_gate.at[net.rep], expert_piece.at[0]),
            (e_up.at[net.rep], expert_piece.at[1]),
            (e_down.at[net.rep], e_raw),
            (s_gate.at[:, cut], shared_piece.at[0]),
            (s_up.at[:, cut], shared_piece.at[1]),
            (s_down.at[cut, :], s_raw),
        ),
        pack_sems,
    )
    for copy in packs:
        copy.start()
    for core, (low, high) in enumerate(((wq_in, wk_in), (wv_in, wo_in))):

        @pl.when(net.core == core)
        def _():
            piece[0:half, :] = low[...]
            piece[half : 2 * half, :] = high[...]

    piece[2 * half : 2 * half + 16, :] = small[...]
    line = Line(net, bank)
    e_events = [net.event() for _ in range(3)]
    mine, most = experts.at[net.shard], experts.at[net.shard, pl.ds(0, 2)]
    peers = [(net.cousins[o], net.shard) for o in (1, 2, 3)]
    net.meet("line", peers + [(net.rep, net.across)])
    line.spread(0, piece)
    own = pltpu.make_async_copy(piece, bank.at[net.core, net.shard], own_sem)
    own.start()
    route_slots(net.rep, routes, routes_t, rank, slot)
    events = [net.event() for _ in range(3)]
    for o, far in ((2, c2), (3, c3), (1, c1)):
        pack_row(net.rep, rank, cot, o, packed.at[o - 1])
        net.put(events[o - 1], packed.at[o - 1], far, net.cousins[o], net.shard)
    arrivals = [(events[0], c1), (events[1], c2), (events[2], c3)]
    pack_row(net.rep, rank, cot, 0, c0)
    for copy in packs:
        copy.wait()
    expert_piece[2] = e_raw[...].astype(F32).T.astype(BF)
    shared_piece[2] = s_raw[...].astype(F32).T.astype(BF)
    line.along(1)
    line.along(-1)
    line.over(0)
    line.along(2)
    line.along(-2)
    net.put(e_events[0], expert_piece, mine, net.rep, net.up, net.z < 3)
    net.put(e_events[1], expert_piece, mine, net.rep, net.down, net.z > 0)
    line.over(1)
    line.over(-1)
    line.along(3)
    line.along(-3)
    net.put(e_events[2], expert_piece.at[pl.ds(0, 2)], most, net.rep, net.across)
    for step in (2, -2, 3, -3):
        line.over(step)
    own.wait()
    line.finish()
    gathered = bank[0, 0, 2 * half : 2 * half + 16, :].astype(F32)
    for j in range(1, SLOTS):
        gathered = gathered + bank[0, j, 2 * half : 2 * half + 16, :].astype(F32)
    ext[...] = gathered
    for j in range(SLOTS):
        at = slice(j * half, (j + 1) * half)
        wq[at, :] = bank[0, j, 0:half, :]
        wk[at, :] = bank[0, j, half : 2 * half, :]
        wv[at, :] = bank[1, j, 0:half, :]
        wo[at, :] = bank[1, j, half : 2 * half, :]
    qkv_rows(x, ext, cosine, sine, wq, wk, wv, q, k, v)
    for copy in stores:
        copy.start()
    for event, like in arrivals:
        net.got(event, like)
    net.got(e_events[0], mine, net.z > 0)
    net.got(e_events[1], mine, net.z < 3)
    net.got(e_events[2], most)
    for copy in stores:
        copy.wait()
    net.close()


def plain_head_kernel(
    routes, routes_t, cot, x, cosine, sine, wq, wk, wv, ext,
    rank, slot, q, k, v, c0, c1, c2, c3,
):
    rep = lax.axis_index("rep")
    route_slots(rep, routes, routes_t, rank, slot)
    pack_rows(rep, rank, cot, (c0, c1, c2, c3))
    qkv_rows(x, ext, cosine, sine, wq, wk, wv, q, k, v)


def fill_bias(starts, bias):
    tokens = bias.shape[0]

    def tile(t, carry):
        at = pl.ds(pl.multiple_of(t * TILE, TILE), TILE)
        query = iota((TILE, tokens), 0) + t * TILE
        key = iota((TILE, tokens), 1)
        allowed = key <= query
        for n in range(2):
            begin = starts[0, n]
            inside = (query >= begin) & (query < begin + PIECE)
            allowed = allowed | (inside & (key >= begin) & (key < begin + PIECE))
        bias[at, :] = jnp.where(allowed, 0.0, MASKED)
        return carry

    lax.fori_loop(0, tokens // TILE, tile, 0)


def keep_half(block, h):
    low = iota(block.shape, 1) < 64
    return jnp.where(low if h == 0 else ~low, block.astype(F32), 0.0).astype(BF)


def biased(scores, bias, begin, free, end):
    tail = scores[:, free:] + bias[begin : begin + TILE, free:end]
    return tail if free == 0 else jnp.concatenate([scores[:, :free], tail], axis=1)


def attend_pairs(q, k, v, out, lse, bias, step):
    tokens, width = q.shape

    def pair(i, carry):
        step(i)
        cols = pl.ds(pl.multiple_of(i * 128, 128), 128)
        keys = k[:, cols]
        low = iota((tokens, 128), 1) < 64
        values = v[:, cols].astype(F32)
        value_one = [
            jnp.where(low, values, 1.0).astype(BF),
            jnp.where(low, 1.0, values).astype(BF),
        ]
        low = iota((TILE, 128), 1) < 64
        for t in range(tokens // TILE):
            begin = t * TILE
            end = min(tokens, begin + TILE + PIECE)
            block = q[begin : begin + TILE, cols]
            results, totals = [], []
            for h in range(2):
                scores = nt(keep_half(block, h), keys[:end])
                scores = biased(scores, bias, begin, begin, end)
                row_max = jnp.max(scores, axis=1, keepdims=True)
                probs = jnp.exp(scores - row_max).astype(BF)
                mixed = nn(probs, value_one[h][:end])
                total = pltpu.roll(mixed, 64, 1)
                results.append(mixed / total)
                totals.append(row_max + jnp.log(total))
            out[begin : begin + TILE, cols] = jnp.where(low, results[0], results[1]).astype(BF)
            lse[begin : begin + TILE, cols] = jnp.where(low, totals[0], totals[1])
        return carry

    lax.fori_loop(0, width // 128, pair, 0)


def router_rows(ext):
    rows = jnp.where(iota(ext.shape, 0) < 4, ext[...], 0.0)
    return jnp.concatenate([rows, jnp.zeros((112, ext.shape[1]), F32)], axis=0).astype(BF)


def route_probs(normed, router):
    logits = nt(normed, router)
    logits = jnp.where(iota(logits.shape, 1) < 4, logits, MASKED)
    raised = jnp.exp(logits - jnp.max(logits, axis=1, keepdims=True))
    return raised / jnp.sum(raised, axis=1, keepdims=True)


def middle_rows(rep, x, attended, wo, ext, rank, middle, normed, probs, packed):
    tokens = x.shape[0]
    gain = ext[5:6, :]
    router = router_rows(ext)

    def tile(t, carry):
        at = pl.ds(pl.multiple_of(t * TILE, TILE), TILE)
        rows = x[at, :].astype(F32) + nn(attended[at, :], wo[...])
        scale = lax.rsqrt(jnp.mean(rows * rows, axis=1, keepdims=True) + EPSILON)
        middle[at, :] = rows
        unit = (rows * scale * gain).astype(BF)
        normed[at, :] = unit
        probs[at, :] = route_probs(unit, router)
        return carry

    lax.fori_loop(0, tokens // TILE, tile, 0)
    pack_rows(rep, rank, normed, packed)


def forward_kernel(
    starts, q, k, v, x, wo, ext, rank, shared_piece, expert_piece, expert_in,
    *refs,
):
    outs, shared_bank, experts = refs[:9], refs[9], refs[10]
    bias, out_sems, send, recv = refs[11:15]
    attended, lse, middle, normed, probs, x0, x1, x2, x3 = refs[15:]
    stores = copies_of(zip(refs[15:], outs), out_sems)
    net = Net(send, recv)
    spread = Spread(net, shared_piece, shared_bank)
    events = [net.event() for _ in range(4)]
    inner = (net.z > 0) & (net.z < 3)
    low, high = experts.at[net.down], experts.at[net.up]
    rest, last = experts.at[net.shard, pl.ds(2, 1)], expert_piece.at[pl.ds(2, 1)]
    near = experts.at[net.place(1, 0), pl.ds(0, 2)]
    net.meet("line", [(net.mate, net.shard), (net.rep, net.across), (spread.far, net.shard)])
    spread.begin()
    fill_bias(starts, bias)

    def step(i):
        @pl.when(i == 1)
        def _():
            spread.along(1)
            spread.along(-1)
            spread.over(0)

        @pl.when(i == 3)
        def _():
            spread.along(2)
            spread.along(-2)
            spread.over(1)
            spread.over(-1)
            net.put(events[2], last, rest, net.rep, net.across)

        @pl.when(i == 5)
        def _():
            spread.along(3)
            spread.along(-3)
            net.put(events[0], low, low, net.rep, net.up, inner)
            net.put(events[1], high, high, net.rep, net.down, inner)
            net.put(events[3], near, near, net.rep, net.across)
            spread.over(2)
            spread.over(-2)

    attend_pairs(q, k, v, attended, lse, bias, step)
    for copy in stores[:2]:
        copy.start()
    spread.over(3)
    spread.over(-3)
    for way, k_step in ((1, 0), (0, 1), (0, -1)):
        spread.relay(way, k_step)
    middle_rows(net.rep, x, attended, wo, ext, rank, middle, normed, probs, (x0, x1, x2, x3))
    for copy in stores[2:]:
        copy.start()
    for way, k_step in ((1, 1), (1, -1), (0, 2), (0, -2), (1, 2), (1, -2)):
        spread.relay(way, k_step)
    for way, k_step in ((0, 3), (0, -3), (1, 3), (1, -3)):
        spread.relay(way, k_step)
    spread.finish()
    net.got(events[0], low, net.z > 1)
    net.got(events[1], low, net.z < 2)
    net.got(events[2], rest)
    net.got(events[3], near)
    for copy in stores:
        copy.wait()
    net.close()


def plain_forward_kernel(
    starts, q, k, v, x, wo, ext, rank,
    attended, lse, middle, normed, probs, x0, x1, x2, x3, bias,
):
    fill_bias(starts, bias)
    attend_pairs(q, k, v, attended, lse, bias, lambda i: None)
    rep = lax.axis_index("rep")
    middle_rows(rep, x, attended, wo, ext, rank, middle, normed, probs, (x0, x1, x2, x3))


CHUNK, CHUNKS = 512, 4


def unit_bank(
    expert, ext, xs, cs, source, target, before, unit, outs, dxs, scratch, ready=None,
    emit=None,
):
    out_acc, dx_acc, gate, wbuf, stage, dw_out, in_sems, out_sems, xc = scratch[:9]
    routed = expert is not None
    blocks, rows = len(xs), xs[0].shape[0]
    per = CHUNK // unit

    def loads(of, buffer, sems, k, b):
        return [
            pltpu.make_async_copy(
                of(k * per + i), buffer.at[b, :, :, pl.ds(i * unit, unit)], sems.at[b, i]
            )
            for i in range(per)
        ]

    def stores(k, b):
        return [
            pltpu.make_async_copy(
                dw_out.at[b, :, :, pl.ds(i * unit, unit)],
                target(k * per + i),
                out_sems.at[b, i],
            )
            for i in range(per)
        ]

    def start_loads(k, b):
        if ready is not None:
            ready(k)
        for copy in loads(source, wbuf, in_sems, k, b):
            copy.start()
        if before is not None:
            for copy in loads(before, scratch[9], scratch[10], k, b):
                copy.start()

    start_loads(0, 0)
    out_acc[...] = jnp.zeros_like(out_acc)
    dx_acc[...] = jnp.zeros_like(dx_acc)
    for n in range(blocks):
        xc[0, n * rows : (n + 1) * rows, :] = xs[n][...]
        xc[1, n * rows : (n + 1) * rows, :] = cs[n][...]
    if routed:
        router = router_rows(ext)
        for n in range(blocks):
            probs = route_probs(xs[n][...], router)
            lane = iota(probs.shape, 1)
            gate[n] = jnp.sum(jnp.where(lane == expert, probs, 0.0), axis=1, keepdims=True)

    def chunk(k, carry):
        b = lax.rem(k, 2)
        for copy in loads(source, wbuf, in_sems, 0, b):
            copy.wait()
        for n in range(blocks):
            x, c = xs[n][...], cs[n][...]
            wg, wu, wd = wbuf[b, 0], wbuf[b, 1], wbuf[b, 2]
            gate_h, up_h, back_h = nn(x, wg), nn(x, wu), nn(c, wd)
            sigma = 0.5 * jnp.tanh(0.5 * gate_h) + 0.5
            silu = gate_h * sigma
            hidden = silu * up_h
            if routed:
                share = gate[n]
                scaled = back_h * share
                weighted = (hidden * share).astype(BF)
            else:
                scaled, weighted = back_h, hidden.astype(BF)
            d_up = (scaled * silu).astype(BF)
            d_gate = (scaled * up_h * (sigma + silu * (1.0 - sigma))).astype(BF)
            product = nt(hidden.astype(BF), wd)
            d_rows = nt(d_gate, wg) + nt(d_up, wu)
            at = slice(n * rows, (n + 1) * rows)
            stage[0, at, :] = d_gate
            stage[1, at, :] = d_up
            stage[2, at, :] = weighted
            if routed:
                pairs = (hidden * back_h).astype(BF)
                d_share = nt(jnp.ones((16, CHUNK), BF), pairs)

            out_acc[n] += product
            dx_acc[n, 0:rows, :] += d_rows
            if routed:
                dx_acc[n, rows : rows + 16, 0:rows] += d_share

        for nxt in range(1, CHUNKS):

            @pl.when(k + 1 == nxt)
            def _():
                start_loads(nxt, nxt % 2)

        @pl.when(k >= 2)
        def _():
            for copy in stores(0, b):
                copy.wait()

        if before is not None:
            for copy in loads(before, scratch[9], scratch[10], 0, b):
                copy.wait()
        for i in range(3):
            part = tn(xc[i // 2], stage[i])
            if before is not None:
                part = part + scratch[9][b, i].astype(F32)
            dw_out[b, i] = part.astype(BF)
        for now in range(CHUNKS):

            @pl.when(k == now)
            def _():
                for copy in stores(now, now % 2):
                    copy.start()
                if emit is not None:
                    emit(now)

        return carry

    lax.fori_loop(0, CHUNKS, chunk, 0)
    for n in range(blocks):
        outs[n][...] = out_acc[n].astype(BF)
        dxs[n][...] = dx_acc[n].astype(BF)
    for b in range(2):
        for copy in stores(0, b):
            copy.wait()


def unit_scratch(blocks, rows, extra, width, per, chained):
    scratch = [
        pltpu.VMEM((blocks, rows, width), F32),
        pltpu.VMEM((blocks, rows + extra, width), F32),
        pltpu.VMEM((blocks, rows, 1), F32),
        pltpu.VMEM((2, 3, width, CHUNK), BF),
        pltpu.VMEM((3, blocks * rows, CHUNK), BF),
        pltpu.VMEM((2, 3, width, CHUNK), BF),
        pltpu.SemaphoreType.DMA((2, per)),
        pltpu.SemaphoreType.DMA((2, per)),
        pltpu.VMEM((2, blocks * rows, width), BF),
    ]
    if chained:
        scratch += [
            pltpu.VMEM((2, 3, width, CHUNK), BF),
            pltpu.SemaphoreType.DMA((2, per)),
        ]
    return scratch


def shared_kernel(
    x, c, piece, bank, x1, x2, x3, expert_in,
    out, dx, grads_own, grads_other, shared_mate, y1, y2, y3, experts,
    send, recv, *scratch,
):
    net = Net(send, recv)
    events = [net.event() for _ in range(4)]
    core_events = [net.event() for _ in range(8)]
    peers = [(net.cousins[o], net.shard) for o in (1, 2, 3)]
    net.meet("line", peers + [(net.rep, net.across)])
    arrivals = exchange(net, (x1, x2, x3), (y1, y2, y3))
    near, second = experts.at[net.place(1, 0), pl.ds(2, 1)], experts.at[net.place(2, 0)]
    net.put(events[0], near, near, net.rep, net.across)
    net.put(events[1], second, second, net.rep, net.across)
    below = experts.at[lax.max(net.shard - 4, net.x)]
    above = experts.at[lax.min(net.shard + 4, 6 + net.x)]
    net.put(events[2], below, below, net.rep, net.up, net.z == 2)
    net.put(events[3], above, above, net.rep, net.down, net.z == 1)
    spots = [net.place(n % 4, n // 4 % 2) for n in range(8)]
    halves = [net.core, 1 - net.core]
    done = scratch[5]
    slices = [done.at[n // 4, :, :, pl.ds(n % 4 * 128, 128)] for n in range(8)]
    places = [shared_mate.at[spot] for spot in spots]

    def source(n):
        return piece if n == 0 else bank.at[halves[n // 8], spots[n % 8]]

    def target(n):
        return (grads_own, grads_other)[n // 8].at[spots[n % 8]]

    def emit(now):
        if now >= 2:
            for n in range(4 * now - 8, 4 * now - 4):
                net.put(core_events[n], slices[n], places[n], net.mate, net.shard)

    unit_bank(
        None, None, [x], [c], source, target, None, 128, [out], [dx], scratch, None, emit
    )
    for event, like in arrivals:
        net.got(event, like)
    net.got(events[0], near)
    net.got(events[1], second)
    net.got(events[2], second, net.z == 3)
    net.got(events[3], second, net.z == 0)
    for n in range(8):
        net.got(core_events[n], places[n])
    net.close()


def far_kernel(
    ext, xa, xb, ca, cb, expert_piece, shared_own, shared_mate, expert_in,
    oa, ob, da, db, grads, shared_keep, shared_y, experts,
    part_a, part_b, part_sems, send, recv, *scratch,
):
    net = Net(send, recv)
    events = [net.event() for _ in range(9)]
    far = net.cousins[2]
    parts = copies_of(((shared_own, part_a), (shared_mate, part_b)), part_sems)
    for copy in parts:
        copy.start()
    net.meet("none", [(net.rep, net.across), (far, net.shard)])
    last = experts.at[net.place(3, 0)]
    net.put(events[0], last, last, net.rep, net.across)
    spots = [net.place(n // 2, n % 2) for n in range(8)]
    y, quarter = lax.div(net.rep, 2), part_a.shape[2] // 2
    rows = [pl.ds(pl.multiple_of(n * quarter, 128), quarter) for n in (y, 1 - y)]
    keep = pltpu.make_async_copy(part_a.at[:, :, rows[0], :], shared_keep, part_sems.at[2])
    away = [part_a.at[j, :, rows[1], :] for j in range(SLOTS)]

    def source(n):
        return expert_piece if n == 0 else experts.at[spots[n]]

    def target(n):
        return grads.at[spots[n]]

    def ready(k):
        if k == 3:
            net.got(events[0], last)

    for copy in parts:
        copy.wait()

    def add(j, carry):
        part_a[j] = part_a[j] + part_b[j]
        return carry

    lax.fori_loop(0, SLOTS, add, 0)
    for j in range(SLOTS):
        net.put(events[1 + j], away[j], shared_y.at[j], far, net.shard)
    keep.start()
    unit_bank(
        net.rep, ext, [xa, xb], [ca, cb], source, target, None, 256, [oa, ob], [da, db],
        scratch, ready,
    )
    keep.wait()
    for j in range(SLOTS):
        net.got(events[1 + j], shared_y.at[j])
    net.close()


def near_kernel(
    ext, xa, xb, ca, cb, expert_piece, experts, before, far_a, far_b,
    shared_keep, shared_y,
    oa, ob, da, shared_total, grads, back_a, back_b, back_c, expert_x,
    db, part_a, part_b, from_x, from_z, third, sems, send, recv, *scratch,
):
    net = Net(send, recv)
    events = [net.event() for _ in range(4)]
    x_events = [net.event() for _ in range(4)]
    z_events = [net.event() for _ in range(3)]
    peers = [(net.cousins[o], net.shard) for o in (1, 2, 3)]
    one = pltpu.make_async_copy(shared_keep, part_a, sems.at[0])
    two = pltpu.make_async_copy(shared_y, part_b, sems.at[1])
    one.start()
    two.start()
    net.meet("all", peers + [(net.rep, net.across)])
    net.put(events[0], far_a, back_a, net.cousins[2], net.shard)
    net.put(events[1], far_b, back_b, net.cousins[3], net.shard)
    one.wait()
    two.wait()

    def add(j, carry):
        part_a[j] = part_a[j] + part_b[j]
        return carry

    lax.fori_loop(0, SLOTS, add, 0)
    mine = [net.cycle(d) for d in range(4)]
    theirs = [spot + 1 - 2 * net.x for spot in mine]
    for d in (2, 1, 3, 0):
        net.put(x_events[d], part_a.at[theirs[d]], from_x.at[d], net.rep, net.across)
    pieces, lands = [part_a.at[spot] for spot in mine], [from_x.at[d] for d in range(4)]
    ends = [from_z.at[d] for d in range(3)]
    spots = [net.place(3 - n // 2, n % 2) for n in range(8)]
    own_slot = 6
    done, target = scratch[5], expert_x.at[net.levels[3]]

    def source(n):
        return expert_piece if n == own_slot else experts.at[spots[n]]

    def ready(k):
        if k == 2:
            for d in (2, 1, 3, 0):
                net.got(x_events[d], lands[d])
                part_a[mine[d]] = part_a[mine[d]] + from_x[d]
                if d:
                    net.put(z_events[d - 1], pieces[d], ends[d - 1], net.rep, mine[d])

    def emit(now):
        if now == 0:
            third[...] = done[0, :, :, 256:512]
            net.put(events[3], third, target, net.rep, net.across)

    unit_bank(
        net.rep, ext, [xa, xb], [ca, cb], source,
        lambda n: grads.at[spots[n]], lambda n: before.at[spots[n]],
        256, [oa, ob], [da, db], scratch, ready, emit,
    )
    net.put(events[2], db, back_c, net.mate, net.shard)
    total = part_a[mine[0]].astype(F32)
    for d in (1, 2, 3):
        net.got(z_events[d - 1], ends[d - 1])
        total = total + from_z[d - 1].astype(F32)
    shared_total[...] = total.astype(BF)
    net.got(events[0], back_a)
    net.got(events[1], back_b)
    net.got(events[2], back_c)
    net.got(events[3], target)
    net.close()


def plain_bank_kernel(blocks, unit, routed, chained, ext, *refs):
    refs = list(refs)

    def take(n):
        taken = refs[:n]
        del refs[:n]
        return taken

    xs, cs = take(blocks), take(blocks)
    bank = take(1)[0]
    before = take(1)[0] if chained else None
    outs, dxs = take(blocks), take(blocks)
    grads = take(1)[0]
    unit_bank(
        lax.axis_index("rep") if routed else None,
        ext, xs, cs,
        lambda n: bank.at[n],
        lambda n: grads.at[n],
        (lambda n: before.at[n]) if chained else None,
        unit, outs, dxs, refs,
    )


def plain_bank(ext, xs, cs, bank, before, routed):
    blocks, (rows, width) = len(xs), xs[0].shape
    chained = before is not None
    extra, unit = (16 if routed else 0), bank.shape[3]
    operands = [ext, *xs, *cs, bank] + ([before] if chained else [])
    outs = [shape((rows, width))] * blocks + [shape((rows + extra, width))] * blocks
    results = call(
        functools.partial(plain_bank_kernel, blocks, unit, routed, chained),
        outs + [shape(bank.shape)],
        [VMEM] * (1 + 2 * blocks) + [ANY] * (2 if chained else 1),
        [VMEM] * (2 * blocks) + [ANY],
        unit_scratch(blocks, rows, extra, width, CHUNK // unit, chained),
        flops=18 * blocks * rows * width * 4 * CHUNK,
        moved=30 * 2**20,
    )(*operands)
    return results[:blocks], results[blocks : 2 * blocks], results[2 * blocks]


def combine_rows(
    slot, d0, d1, d2, d3, d_shared, probs, middle, normed, cot, ext, attended, wo,
    d_middle, d_attended, grad_ext, branch, router_acc, gain_acc,
):
    tokens, width = middle.shape
    rep = lax.axis_index("rep")
    gain = ext[5:6, :]
    router = router_rows(ext)
    router_acc[...] = jnp.zeros_like(router_acc)
    gain_acc[...] = jnp.zeros_like(gain_acc)

    def tile(t, carry):
        at = pl.ds(pl.multiple_of(t * TILE, TILE), TILE)
        slot_one, slot_two = slot[at, 0:1], slot[at, 64:65]
        d_normed = d_shared[at, :].astype(F32)
        lane = iota((TILE, 128), 1)
        d_gates = jnp.zeros((TILE, 128), F32)
        for o, d in enumerate((d0, d1, d2, d3)):
            place = (iota((TILE, CAP), 1) + o * CAP).astype(F32)
            hit = (place == slot_one) | (place == slot_two)
            d_normed = d_normed + nn(ones_where(hit), d[0:CAP, :])
            share = d[CAP : CAP + 16, 0:CAP].astype(F32)[0:1, :]
            d_share = jnp.sum(jnp.where(hit, share, 0.0), axis=1, keepdims=True)
            d_gates = d_gates + jnp.where(lane == sibling(rep, o), d_share, 0.0)
        p = probs[at, :]
        inner = jnp.sum(d_gates * p, axis=1, keepdims=True)
        d_logits = (p * (d_gates - inner)).astype(BF)
        d_normed = d_normed + nn(d_logits, router)
        router_acc[...] += tn(d_logits, normed[at, :])
        rows = middle[at, :]
        scale = lax.rsqrt(jnp.mean(rows * rows, axis=1, keepdims=True) + EPSILON)
        unit = rows * scale
        gain_acc[...] += jnp.sum((d_normed * unit).reshape(TILE // 8, 8, width), axis=0)
        w = d_normed * gain
        inner = jnp.mean(w * unit, axis=1, keepdims=True)
        total = cot[at, :].astype(F32) + scale * (w - unit * inner)
        d_middle[at, :] = total
        rounded = total.astype(BF)
        branch[at, :] = rounded
        d_attended[at, :] = nt(rounded, wo[...]).astype(BF)
        return carry

    lax.fori_loop(0, tokens // TILE, tile, 0)
    row = iota((16, width), 0)
    total = jnp.sum(gain_acc[...], axis=0, keepdims=True)
    grad_ext[...] = jnp.where(row < 4, router_acc[0:16, :], jnp.where(row == 5, total, 0.0))


def output_rows(slot, o0, o1, o2, o3, shared, probs, middle, out, first, last):
    rep = lax.axis_index("rep")

    def tile(t, carry):
        at = pl.ds(pl.multiple_of(t * TILE, TILE), TILE)
        slot_one, slot_two = slot[at, 0:1], slot[at, 64:65]
        total = middle[at, :] + shared[at, :].astype(F32)
        p = probs[at, :]
        lane = iota((TILE, 128), 1)
        for o, rows in enumerate((o0, o1, o2, o3)):
            place = (iota((TILE, CAP), 1) + o * CAP).astype(F32)
            hit = (place == slot_one) | (place == slot_two)
            share = jnp.sum(jnp.where(lane == sibling(rep, o), p, 0.0), axis=1, keepdims=True)
            total = total + nn(jnp.where(hit, share, 0.0).astype(BF), rows[...])
        out[at, :] = total.astype(BF)
        return carry

    lax.fori_loop(first, last, tile, 0)


def back_pairs(
    q, k, v, d_out, out, lse, cosine, sine, dq, dk, dv, bias, dk_acc, dv_acc, step
):
    tokens, width = q.shape

    def pair(i, carry):
        step(i)
        cols = pl.ds(pl.multiple_of(i * 128, 128), 128)
        keys, values = k[:, cols], v[:, cols]
        half_keys = [keep_half(keys, 0), keep_half(keys, 1)]
        dk_acc[...] = jnp.zeros_like(dk_acc)
        dv_acc[...] = jnp.zeros_like(dv_acc)
        low = iota((TILE, 128), 1) < 64
        for t in range(tokens // TILE):
            begin = t * TILE
            end = min(tokens, begin + TILE + PIECE)
            at = slice(begin, begin + TILE)
            block, grad = q[at, cols], d_out[at, cols]
            product = grad.astype(F32) * out[at, cols].astype(F32)
            block_lse = lse[at, cols]
            d_block = None
            for h in range(2):
                block_h, grad_h = keep_half(block, h), keep_half(grad, h)
                scores = nt(block_h, keys[:end])
                scores = biased(scores, bias, begin, begin, end)
                probs = jnp.exp(scores - block_lse[:, 64 * h : 64 * h + 1])
                d_probs = nt(grad_h, values[:end])
                inner = jnp.sum(
                    jnp.where(low if h == 0 else ~low, product, 0.0), axis=1, keepdims=True
                )
                d_scores = (probs * (d_probs - inner)).astype(BF)
                part = nn(d_scores, half_keys[h][:end])
                d_block = part if d_block is None else d_block + part
                dk_acc[0:end, :] += tn(d_scores, block_h)
                dv_acc[0:end, :] += tn(probs.astype(BF), grad_h)
            dq[at, cols] = spin(d_block * 0.125, cosine[at, :], -sine[at, :]).astype(BF)
        dk[:, cols] = spin(dk_acc[...], cosine[...], -sine[...]).astype(BF)
        dv[:, cols] = dv_acc[...].astype(BF)
        return carry

    lax.fori_loop(0, width // 128, pair, 0)


def copies_of(pairs, sems):
    return [pltpu.make_async_copy(a, b, sems.at[i]) for i, (a, b) in enumerate(pairs)]


def fetch(sources, targets, sems):
    copies = copies_of(zip(sources, targets), sems)
    for copy in copies:
        copy.start()
    for copy in copies:
        copy.wait()


class Chain:
    def __init__(self, net, own, from_x, up_in, down_in, held, spare, sems):
        self.net, self.own, self.from_x = net, own, from_x
        self.into, self.held, self.spare, self.sems = (up_in, down_in), held, spare, sems
        keys = [(way, d, m) for way in range(2) for d in (1, 2, 3) for m in range(3)]
        self.events = {key: net.event() for key in keys}
        self.spots = [net.place(n, 0) for n in range(4)]
        self.sends, self.gets = {}, {}
        z = net.z
        for d in (1, 2, 3):
            up, down = lax.min(z + d, 3), lax.max(z - d, 0)
            for m in range(3):
                self.sends[0, d, m] = (held.at[up, m], z < 4 - d)
                self.sends[1, d, m] = (held.at[down, m], z > d - 1)
            self.gets[0, d] = (lax.min(z + d - 1, 3), (z > 0) & (z < 5 - d))
            self.gets[1, d] = (lax.max(z - d + 1, 0), (z < 3) & (z > d - 2))

    def level(self, n):
        to = self.net.levels[n]
        far = self.from_x.at[to]
        fetch([self.own.at[self.spots[n]], far], [self.held.at[to], self.spare.at[0]], self.sems)
        self.held[to] = self.held[to] + self.spare[0]

    def send(self, d, m):
        net = self.net
        for way, to in ((0, net.up), (1, net.down)):
            source, here = self.sends[way, d, m]
            target = self.into[way].at[d - 1, m]
            net.put(self.events[way, d, m], source, target, net.rep, to, here)

    def take(self, d, m):
        net = self.net
        for way in range(2):
            to, here = self.gets[way, d]

            def add():
                source = self.into[way].at[d - 1, m]
                event = self.events[way, d, m]
                net.copy(event, source, source, net.mate, net.shard).wait_recv()
                fetch([source], [self.spare.at[0, m]], self.sems)
                self.held[to, m] = self.held[to, m] + self.spare[0, m]

            when(here, add)


BACK_ROWS = 19


def back_kernel(starts, *refs):
    raw, refs = refs[:BACK_ROWS], refs[BACK_ROWS:]
    o1, o2, o3, grads, expert_x_in = refs[:5]
    outs, expert_total = refs[5:11], refs[11]
    r1, r2, r3, up_in, down_in, expert_x = refs[12:18]
    d_attended, branch, router_acc, gain_acc, bias, dk_acc, dv_acc = refs[18:25]
    local = refs[25 : 25 + BACK_ROWS]
    held, spare, sems, load_sems, out_sems, send, recv = refs[25 + BACK_ROWS : 32 + BACK_ROWS]
    d_middle, grad_wo, grad_ext, dq, dk, dv = refs[32 + BACK_ROWS :]
    stores = copies_of(zip((d_middle, grad_wo, grad_ext, dq, dk, dv), outs), out_sems)
    slot, d0, d1, d2, d3, d_shared, probs, middle, normed, cot, ext, attended, wo = local[:13]
    cosine, sine, q, k, v, lse = local[13:]
    loads = copies_of(zip(raw, local), load_sems)
    for copy in loads:
        copy.start()
    net = Net(send, recv)
    x_events = [net.event() for _ in range(3)]
    chain = Chain(net, grads, expert_x, up_in, down_in, held, spare, sems)
    peers = [(net.cousins[o], net.shard) for o in (1, 2, 3)]
    net.meet("line", peers + [(net.rep, net.across)])
    targets = [expert_x.at[net.levels[n]] for n in range(3)]
    for n in (2, 1, 0):
        source = grads.at[net.place(n, 1)]
        net.put(x_events[n], source, targets[n], net.rep, net.across)
    arrivals = exchange(net, (o1, o2, o3), (r1, r2, r3))
    chain.level(3)
    for m in range(3):
        chain.send(3, m)
    fill_bias(starts, bias)
    for copy in loads:
        copy.wait()
    combine_rows(
        slot, d0, d1, d2, d3, d_shared, probs, middle, normed, cot, ext, attended, wo,
        d_middle, d_attended, grad_ext, branch, router_acc, gain_acc,
    )
    stores[0].start()
    stores[2].start()
    net.got(x_events[2], targets[2])
    chain.level(2)
    for m in range(3):
        chain.take(3, m)
        chain.send(2, m)
    grad_wo[...] = tn(attended[...], branch[...]).astype(BF)
    stores[1].start()

    def step(i):
        @pl.when(i == 3)
        def _():
            net.got(x_events[1], targets[1])
            chain.level(1)
            for m in range(3):
                chain.take(2, m)
                chain.send(1, m)

    back_pairs(
        q, k, v, d_attended, attended, lse, cosine, sine, dq, dk, dv, bias, dk_acc, dv_acc, step
    )
    for copy in stores[3:]:
        copy.start()
    net.got(x_events[0], targets[0])
    chain.level(0)
    for event, like in arrivals:
        net.got(event, like)
    for m in range(3):
        chain.take(1, m)
    expert_total[...] = held[net.z]
    for copy in stores:
        copy.wait()
    net.close()


def plain_back_kernel(
    starts, slot, d0, d1, d2, d3, d_shared, probs, middle, normed, cot, ext, attended, wo,
    q, k, v, lse, cosine, sine,
    d_middle, grad_wo, grad_ext, dq, dk, dv,
    d_attended, branch, router_acc, gain_acc, bias, dk_acc, dv_acc,
):
    combine_rows(
        slot, d0, d1, d2, d3, d_shared, probs, middle, normed, cot, ext, attended, wo,
        d_middle, d_attended, grad_ext, branch, router_acc, gain_acc,
    )
    grad_wo[...] = tn(attended[...], branch[...]).astype(BF)
    fill_bias(starts, bias)
    back_pairs(
        q, k, v, d_attended, attended, lse, cosine, sine, dq, dk, dv, bias, dk_acc, dv_acc,
        lambda i: None,
    )


def norm_rows(x, ext, normed_all):
    gain = ext[4:5, :]

    def tile(t, carry):
        at = pl.ds(pl.multiple_of(t * TILE, TILE), TILE)
        rows = x[at, :].astype(F32)
        scale = lax.rsqrt(jnp.mean(rows * rows, axis=1, keepdims=True) + EPSILON)
        normed_all[at, :] = (rows * scale * gain).astype(BF)
        return carry

    lax.fori_loop(0, x.shape[0] // TILE, tile, 0)


def input_grad(x, ext, dq, dk, dv, wq, wk, wv, d_middle, grad_in, gain_acc, first, last):
    width = x.shape[1]
    gain = ext[4:5, :]

    def tile(t, carry):
        at = pl.ds(pl.multiple_of(t * TILE, TILE), TILE)
        rows = x[at, :].astype(F32)
        scale = lax.rsqrt(jnp.mean(rows * rows, axis=1, keepdims=True) + EPSILON)
        unit = rows * scale
        d_normed = nt(dq[at, :], wq[...]) + nt(dk[at, :], wk[...]) + nt(dv[at, :], wv[...])
        gain_acc[...] += jnp.sum((d_normed * unit).reshape(TILE // 8, 8, width), axis=0)
        w = d_normed * gain
        inner = jnp.mean(w * unit, axis=1, keepdims=True)
        grad_in[at, :] = d_middle[at, :] + scale * (w - unit * inner)
        return carry

    lax.fori_loop(first, last, tile, 0)


def tail_kernel(
    x, ext, dq, dk_in, dv, wq_in, wk_in, wv_in, grad_wo_in, grad_ext,
    d_middle_in, slot_in, o0_in, o1_in, o2_in, o3_in, shared_in, probs_in, middle_in,
    expert_total, shared_total,
    grad_in, outputs, weights, small, shared_far, shared_mate, shared_cross, e1, e2, e3,
    normed_all, gain_acc, gw, from_mate, from_x, from_z, from_y, result, from_core,
    tiny, tiny_in, dk, grad_wo, wq, wk, wv,
    d_middle, slot, o0, o1, o2, o3, shared_out, probs, middle, load_sems,
    send, recv,
):
    width = x.shape[1]
    half = width // SLOTS
    net = Net(send, recv)
    e_events = [net.event() for _ in range(3)]
    s_events = [net.event() for _ in range(3)]
    m_events = [net.event() for _ in range(2)]
    x_events = [[net.event() for _ in range(2)] for _ in range(4)]
    z_events = [[net.event() for _ in range(2)] for _ in range(3)]
    y_events = [net.event() for _ in range(2)]
    c_events = [net.event() for _ in range(2)]
    t_events = [net.event() for _ in range(6)]
    net.meet(
        "all", [(net.mate, net.shard), (net.cousins[2], net.shard), (net.rep, net.across)]
    )
    far = net.cousins[2]
    net.put(s_events[0], shared_total, shared_far, far, net.shard)
    net.put(s_events[1], shared_total, shared_mate, net.mate, net.shard)
    net.put(e_events[1], expert_total, e2, far, net.shard)
    net.put(e_events[0], expert_total, e1, net.mate, net.shard)
    pairs = (
        (dk_in, dk), (grad_wo_in, grad_wo), (wq_in, wq), (wk_in, wk), (wv_in, wv),
        (d_middle_in, d_middle), (slot_in, slot), (o0_in, o0), (o1_in, o1), (o2_in, o2),
        (o3_in, o3), (shared_in, shared_out), (probs_in, probs), (middle_in, middle),
    )
    loads = [pltpu.make_async_copy(a, b, load_sems.at[i]) for i, (a, b) in enumerate(pairs)]
    for copy in loads:
        copy.start()
    norm_rows(x, ext, normed_all)
    spots = [lax.rem(i + 2 * net.core, 4) for i in range(4)]

    def rows_of(spot):
        return pl.ds(pl.multiple_of(spot * half, 32), half)

    mine = [rows_of(net.cycle(d)) for d in range(4)]
    theirs = [rows_of(net.cycle(d) + 1 - 2 * net.x) for d in range(4)]

    def hand(i):
        net.put(m_events[i], gw.at[2 + i], from_mate.at[i], net.mate, net.shard)

    def cross(i):
        net.got(m_events[i], from_mate.at[i])
        gw[i] = gw[i] + from_mate[i]
        for d in (2, 1, 3, 0):
            source = gw.at[i, theirs[d]]
            net.put(x_events[d][i], source, from_x.at[d, i], net.rep, net.across)

    gw[spots[0]] = tn(normed_all[...], dq[...]).astype(BF)
    gw[spots[2]] = tn(normed_all[...], dv[...]).astype(BF)
    hand(0)
    loads[0].wait()
    loads[1].wait()
    gw[spots[1]] = tn(normed_all[...], dk[...]).astype(BF)
    gw[spots[3]] = grad_wo[...]
    hand(1)
    cross(0)
    cross(1)
    gain_acc[...] = jnp.zeros_like(gain_acc)
    for copy in loads[2:]:
        copy.wait()
    count = x.shape[0] // TILE

    def inputs(first, last):
        input_grad(x, ext, dq, dk, dv, wq, wk, wv, d_middle, grad_in, gain_acc, first, last)

    def results(first, last):
        output_rows(
            slot, o0, o1, o2, o3, shared_out, probs, middle, outputs, first, last
        )

    def add_across(d, i):
        net.got(x_events[d][i], from_x.at[d, i])
        gw[i, mine[d], :] = gw[i, mine[d], :] + from_x[d, i]
        if d:
            net.put(
                z_events[d - 1][i], gw.at[i, mine[d]], from_z.at[d - 1, i],
                net.rep, net.cycle(d),
            )

    def add_along(i):
        total = gw[i, mine[0], :].astype(F32)
        for d in (1, 2, 3):
            net.got(z_events[d - 1][i], from_z.at[d - 1, i])
            total = total + from_z[d - 1, i].astype(F32)
        result[0, i] = total.astype(BF)
        net.put(y_events[i], result.at[0, i], from_y.at[i], far, net.shard)

    def tiny_add(n, target_rep, target_shard):
        net.got(t_events[n], tiny_in.at[n])
        tiny[n + 1] = (tiny[n].astype(F32) + tiny_in[n].astype(F32)).astype(BF)
        if target_rep is not None:
            source, target = tiny.at[n + 1], tiny_in.at[n + 1]
            net.put(t_events[n + 1], source, target, target_rep, target_shard)

    inputs(0, 2)
    add_across(2, 0)
    add_across(1, 0)
    inputs(2, 3)
    add_across(3, 0)
    inputs(3, count)
    add_across(0, 0)
    row = iota((16, width), 0)
    total = jnp.sum(gain_acc[...], axis=0, keepdims=True)
    tiny[0] = (grad_ext[...] + jnp.where(row == 4, total, 0.0)).astype(BF)
    net.put(t_events[0], tiny.at[0], tiny_in.at[0], net.mate, net.shard)
    results(0, 1)
    add_across(2, 1)
    tiny_add(0, net.rep, net.across)
    results(1, 2)
    add_across(1, 1)
    tiny_add(1, far, net.shard)
    add_along(0)
    results(2, 3)
    add_across(3, 1)
    tiny_add(2, None, None)
    for d in (1, 2, 3):
        net.put(t_events[2 + d], tiny.at[3], tiny_in.at[2 + d], net.rep, net.cycle(d))
    net.got(s_events[0], shared_far)
    net.put(s_events[2], shared_far, shared_cross, net.mate, net.shard)
    results(3, count)
    add_across(0, 1)
    net.got(e_events[1], e2)
    net.put(e_events[2], e2, e3, net.mate, net.shard)
    total = tiny[3].astype(F32)
    for d in (1, 2, 3):
        net.got(t_events[2 + d], tiny_in.at[2 + d])
        total = total + tiny_in[2 + d].astype(F32)
    small[...] = total.astype(BF).astype(F32)
    add_along(1)
    for i in range(2):
        net.got(y_events[i], from_y.at[i])
        result[1, i] = (result[0, i].astype(F32) + from_y[i].astype(F32)).astype(BF)
        net.put(c_events[i], result.at[1, i], from_core.at[i], net.mate, net.shard)
        weights[spots[i]] = result[1, i].astype(F32)
    for i in range(2):
        net.got(c_events[i], from_core.at[i])
        weights[spots[2 + i]] = from_core[i].astype(F32)
    net.got(e_events[0], e1)
    net.got(s_events[1], shared_mate)
    net.got(s_events[2], shared_cross)
    net.got(e_events[2], e3)
    net.close()


def plain_tail_kernel(
    x, ext, dq, dk, dv, wq, wk, wv, d_middle,
    slot, o0, o1, o2, o3, shared_out, probs, middle,
    grad_in, outputs, gw, gain, normed_all, gain_acc,
):
    norm_rows(x, ext, normed_all)
    for i, d in enumerate((dq, dk, dv)):
        gw[i] = tn(normed_all[...], d[...]).astype(BF)
    gain_acc[...] = jnp.zeros_like(gain_acc)
    count = x.shape[0] // TILE
    input_grad(x, ext, dq, dk, dv, wq, wk, wv, d_middle, grad_in, gain_acc, 0, count)
    gain[...] = gain_acc[...]
    output_rows(
        slot, o0, o1, o2, o3, shared_out, probs, middle, outputs, 0, x.shape[0] // TILE
    )


def finish_kernel(
    e0, e1, e2, e3, wide, plain, q0, q1, q2, q3, weights, small,
    gate, up, down, wide_out, plain_out, s_gate_out, s_up_out, s_down_out,
    grad_q, grad_k, grad_v, grad_o, gain_one, gain_two, grad_router,
    part, wide_in, plain_in, quarters, weights_in, s_gate, s_up, s_down,
    ready_gate, ready_up, ready_down, in_sems, out_sems,
):
    rep, shard = lax.axis_index("rep"), lax.axis_index("shard")
    pairs = [(e, part.at[o]) for o, e in enumerate((e0, e1, e2, e3))]
    pairs += [(wide, wide_in), (plain, plain_in), (weights, weights_in)]
    pairs += [(q, quarters.at[o]) for o, q in enumerate((q0, q1, q2, q3))]
    loads = copies_of(pairs, in_sems)
    for copy in loads:
        copy.start()
    stores = []
    for o in range(4):
        at = sibling(rep, o)
        pairs = [(ready_gate.at[o], gate.at[at]), (ready_up.at[o], up.at[at])]
        pairs.append((ready_down.at[o], down.at[at]))
        loads[o].wait()
        ready_gate[o] = part[o, 0].astype(F32)
        ready_up[o] = part[o, 1].astype(F32)
        ready_down[o] = part[o, 2].astype(F32).T
        made = [pltpu.make_async_copy(a, b, out_sems.at[3 * o + i]) for i, (a, b) in enumerate(pairs)]
        for copy in made:
            copy.start()
        stores += made
    passed = [(wide_in, wide_out), (plain_in, plain_out)]
    grads = (grad_q, grad_k, grad_v, grad_o)
    passed += [(weights_in.at[i], out) for i, out in enumerate(grads)]
    for copy in loads[4:7]:
        copy.wait()
    made = [pltpu.make_async_copy(a, b, out_sems.at[12 + i]) for i, (a, b) in enumerate(passed)]
    quarter, span = q0.shape[1:]
    for copy in loads[7:]:
        copy.wait()
    for copy in made:
        copy.start()
    stores += made
    for o in range(4):
        piece, owner = quarters.at[o], sibling(rep, o)
        rows = pl.ds(pl.multiple_of(lax.div(owner, 2) * quarter, 128), quarter)
        cols = pl.ds(pl.multiple_of(lax.rem(owner, 2) * span, 128), span)
        s_gate[rows, cols] = piece[0].astype(F32)
        s_up[rows, cols] = piece[1].astype(F32)
        s_down[cols, rows] = piece[2].astype(F32).T
    pairs = ((s_gate, s_gate_out), (s_up, s_up_out), (s_down, s_down_out))
    made = [pltpu.make_async_copy(a, b, out_sems.at[18 + i]) for i, (a, b) in enumerate(pairs)]
    for copy in made:
        copy.start()
    stores += made
    rows, width = weights_in.shape[1:]
    tiny = small[...].astype(BF)
    pick = ones_where(iota((width, rows), 0) == iota((width, rows), 1) + shard * rows)
    gains = nn(tiny, pick)
    gain_one[...] = gains[4:5, :]
    gain_two[...] = gains[5:6, :]
    grad_router[...] = dot(pick, tiny, 0, 1)[:, 0:4]
    for copy in stores:
        copy.wait()


def rope_tables(length, head_dim):
    positions = np.arange(length, dtype=np.float32)
    inverse_freq = np.float32(10000.0) ** (
        np.float32(-2.0) * np.arange(head_dim // 2, dtype=np.float32) / np.float32(head_dim)
    )
    angle = positions[:, None] * inverse_freq[None, :]
    cosine, sine = np.cos(angle), np.sin(angle)
    return (
        jnp.asarray(np.concatenate([cosine] * 4, axis=1)),
        jnp.asarray(np.concatenate([-sine, sine, -sine, sine], axis=1)),
    )


def body(
    inputs,
    piece_starts,
    routes,
    attn_gain,
    query_weight,
    key_weight,
    value_weight,
    out_weight,
    ffn_gain,
    router_weight,
    expert_gate,
    expert_up,
    expert_down,
    shared_gate,
    shared_up,
    shared_down,
    cotangent,
):
    _, tokens, width = inputs.shape
    shards = lax.axis_size("shard")
    rep, shard = lax.axis_index("rep"), lax.axis_index("shard")
    core = rep % 2
    ringed = shards == SLOTS
    rows = width // shards
    units = shared_gate.shape[1]
    x, cot, chosen = inputs[0], cotangent[0], routes[0]
    small = jnp.concatenate([router_weight.T, attn_gain[None], ffn_gain[None]], axis=0)
    small = jnp.pad(small, ((0, 10), (0, 0)))
    small = lax.dynamic_update_slice(jnp.zeros((16, width), BF), small, (0, shard * rows))
    if not ringed:
        wq, wk, wv, wo = [
            lax.all_gather(w, "shard", axis=0, tiled=True)
            for w in (query_weight, key_weight, value_weight, out_weight)
        ]
        ext = lax.psum(small.astype(F32), "shard")
        shared_pack = jnp.stack([shared_gate, shared_up, shared_down.T])
        my_half = lax.dynamic_slice_in_dim(shared_pack, core * (units // 2), units // 2, 2)
        expert_pack = jnp.stack([expert_gate[rep], expert_up[rep], expert_down[rep].T])

    cosine, sine = rope_tables(tokens, width // HEADS)
    token_f = shape((tokens, width))
    square = shape((width, width))
    packed = [shape((CAP, width))] * 4
    outs = [shape((8, tokens), F32), shape((tokens, 128), F32)] + [token_f] * 3
    work = 2 * tokens * width * (CAP * 4 + 3 * width)
    if ringed:
        expert_shape, half_shape = shape((3, width, units)), shape((3, width, units // 2))
        firsts = outs + [square] * 4 + [shape((16, width), F32), packed[0]]
        firsts += [expert_shape, half_shape]
        rank, slot, q, k, v, wq, wk, wv, wo, ext, cot_own, expert_pack, my_half, *heads = call(
            head_kernel,
            firsts + packed[1:] + [shape((SLOTS,) + expert_shape.shape)],
            [VMEM] * 11 + [ANY] * 6,
            [ANY] * 17,
            [
                pltpu.VMEM((2, SLOTS, 2 * rows + 16, width), BF),
                pltpu.VMEM((3, CAP, width), BF),
                pltpu.VMEM((2 * rows + 16, width), BF),
                pltpu.VMEM((units, width), BF),
                pltpu.VMEM((units // 2, width), BF),
                pltpu.SemaphoreType.DMA((6,)),
                pltpu.SemaphoreType.DMA((13,)),
                pltpu.SemaphoreType.DMA((34,)),
                pltpu.SemaphoreType.DMA((34,)),
                pltpu.SemaphoreType.DMA,
            ]
            + [pltpu.VMEM(a.shape, a.dtype) for a in firsts],
            flops=work,
            moved=24 * 2**20,
            group=0,
        )(
            chosen, chosen.T, cot, x, query_weight, key_weight, value_weight, out_weight, small,
            cosine, sine, expert_gate, expert_up, expert_down, shared_gate, shared_up, shared_down,
        )
        *cot_in, expert_bank = heads
        cot_in = [cot_own, *cot_in]
    else:
        rank, slot, q, k, v, *cot_out = call(
            plain_head_kernel, outs + packed, [VMEM] * 10, [VMEM] * 9, flops=work,
            moved=24 * 2**20,
        )(chosen, chosen.T, cot, x, cosine, sine, wq, wk, wv, ext)
        cot_in = [cot_out[0]] + [to_rep(cot_out[o], o) for o in (1, 2, 3)]

    outs = [token_f, shape((tokens, width), F32), shape((tokens, width), F32), token_f]
    outs += [shape((tokens, 128), F32)] + packed
    work = 2 * tokens * width * (8 * tokens + width + 4 * CAP)
    bias = pltpu.VMEM((tokens, tokens), F32)
    if ringed:
        attended, lse, middle, normed, probs, *x_out, shared_bank, expert_bank = call(
            forward_kernel,
            outs + [shape((2, SLOTS) + my_half.shape), shape((SLOTS,) + expert_pack.shape)],
            [SMEM] + [VMEM] * 7 + [ANY] * 3,
            [ANY] * 11,
            [
                bias,
                pltpu.SemaphoreType.DMA((9,)),
                pltpu.SemaphoreType.DMA((60,)),
                pltpu.SemaphoreType.DMA((60,)),
            ]
            + [pltpu.VMEM(a.shape, a.dtype) for a in outs],
            flops=work,
            moved=30 * 2**20,
            group=1,
            alias={10: 10},
        )(piece_starts, q, k, v, x, wo, ext, rank, my_half, expert_pack, expert_bank)
    else:
        attended, lse, middle, normed, probs, *x_out = call(
            plain_forward_kernel, outs, [SMEM] + [VMEM] * 7, [VMEM] * 9, [bias], flops=work,
            moved=30 * 2**20,
        )(piece_starts, q, k, v, x, wo, ext, rank)

    rows_out = shape((CAP, width))
    rows_back = shape((CAP + 16, width))
    if ringed:
        half_grads = shape((SLOTS,) + my_half.shape)
        shared_out, shared_dx, grads_own, _, shared_mate, y1, y2, y3, expert_bank = call(
            shared_kernel,
            [token_f] * 2 + [half_grads] * 3 + packed[:3] + [shape(expert_bank.shape)],
            [VMEM] * 2 + [ANY] * 6,
            [VMEM] * 2 + [ANY] * 7,
            [pltpu.SemaphoreType.DMA((15,)), pltpu.SemaphoreType.DMA((15,))]
            + unit_scratch(1, tokens, 0, width, 4, False),
            flops=18 * tokens * width * CHUNK * CHUNKS,
            moved=30 * 2**20,
            group=2,
            alias={7: 8},
        )(normed, cot, my_half, shared_bank, *x_out[1:], expert_bank)
        x_in = [x_out[0], y1, y2, y3]
        bank = shape(expert_bank.shape)
        quarter = (3, width // 2, units // 2)
        quarters = (SLOTS,) + quarter
        far_a, far_b, da, db, before, shared_keep, shared_y, expert_bank = call(
            far_kernel,
            [rows_out] * 2 + [rows_back] * 2 + [bank, shape(quarters), shape(quarters), bank],
            [VMEM] * 5 + [ANY] * 4,
            [VMEM] * 4 + [ANY] * 4,
            [
                pltpu.VMEM(half_grads.shape, BF),
                pltpu.VMEM(half_grads.shape, BF),
                pltpu.SemaphoreType.DMA((3,)),
                pltpu.SemaphoreType.DMA((9,)),
                pltpu.SemaphoreType.DMA((9,)),
            ]
            + unit_scratch(2, CAP, 16, width, 2, False),
            flops=36 * CAP * width * CHUNK * CHUNKS,
            moved=30 * 2**20,
            group=3,
            alias={8: 7},
        )(ext, *x_in[2:], *cot_in[2:], expert_pack, grads_own, shared_mate, expert_bank)
        bank_x, bank_z = (4,) + expert_pack.shape, (3,) + expert_pack.shape
        near_a, near_b, d0, shared_total, grads, d2, d3, d1, expert_x = call(
            near_kernel,
            [rows_out] * 2 + [rows_back, shape(quarter), bank] + [rows_back] * 3 + [shape(bank_x)],
            [VMEM] * 5 + [ANY] * 7,
            [VMEM] * 4 + [ANY] * 5,
            [
                pltpu.VMEM((CAP + 16, width), BF),
                pltpu.VMEM(quarters, BF),
                pltpu.VMEM(quarters, BF),
                pltpu.VMEM((4,) + quarter, BF),
                pltpu.VMEM((3,) + quarter, BF),
                pltpu.VMEM(expert_pack.shape, BF),
                pltpu.SemaphoreType.DMA((2,)),
                pltpu.SemaphoreType.DMA((11,)),
                pltpu.SemaphoreType.DMA((11,)),
            ]
            + unit_scratch(2, CAP, 16, width, 2, True),
            flops=36 * CAP * width * CHUNK * CHUNKS,
            moved=30 * 2**20,
            group=4,
        )(
            ext, *x_in[:2], *cot_in[:2], expert_pack, expert_bank, before, da, db,
            shared_keep, shared_y,
        )
        d_rows = [d0, d1, d2, d3]
    else:

        def slotted(part):
            every = lax.all_gather(part, "shard")
            every = every.reshape(SLOTS, shards // SLOTS, 3, width, part.shape[2])
            return every.transpose(0, 2, 3, 1, 4).reshape(SLOTS, 3, width, -1)

        shared_bank = slotted(my_half)
        shared_bank = jnp.concatenate([shared_bank, to_rep(shared_bank, 1)], axis=0)
        expert_bank = slotted(expert_pack)
        x_in = [x_out[0]] + [to_rep(x_out[o], o) for o in (1, 2, 3)]
        (shared_out,), (shared_dx,), shared_grads = plain_bank(
            ext, [normed], [cot], shared_bank, None, False
        )
        grads_own, grads_other = shared_grads[:SLOTS], shared_grads[SLOTS:]
        (far_a, far_b), (da, db), before = plain_bank(
            ext, x_in[2:], cot_in[2:], expert_bank, None, True
        )
        (near_a, near_b), (d0, d1), grads = plain_bank(
            ext, x_in[:2], cot_in[:2], expert_bank, before, True
        )
        d_rows = [d0, to_rep(d1, 1), to_rep(da, 2), to_rep(db, 3)]
    wide = shape((tokens, width), F32)
    outs = [wide, square, shape((16, width), F32)] + [token_f] * 3
    operands = (piece_starts, slot, *d_rows, shared_dx, probs, middle, normed, cot, ext, attended)
    operands += (wo,)
    specs = [SMEM] + [VMEM] * 15
    scratch = [
        pltpu.VMEM((tokens, width), BF),
        pltpu.VMEM((tokens, width), BF),
        pltpu.VMEM((128, width), F32),
        pltpu.VMEM((8, width), F32),
        bias,
        pltpu.VMEM((tokens, 128), F32),
        pltpu.VMEM((tokens, 128), F32),
    ]
    work = 2 * tokens * width * (2 * width + 4 * CAP) + 40 * tokens * tokens * width
    if ringed:
        late = (*operands[1:], cosine, sine, q, k, v, lse)
        d_middle, grad_wo, grad_ext, dq, dk, dv, expert_total, *back = call(
            back_kernel,
            outs
            + [shape(expert_pack.shape)]
            + [rows_out] * 3
            + [shape(bank_z), shape(bank_z), shape(bank_x)],
            [SMEM] + [ANY] * (len(late) + 5),
            [ANY] * 6 + [VMEM] + [ANY] * 6,
            scratch
            + [pltpu.VMEM(a.shape, a.dtype) for a in late]
            + [
                pltpu.VMEM(bank_x, BF),
                pltpu.VMEM((1,) + expert_pack.shape, BF),
                pltpu.SemaphoreType.DMA((2,)),
                pltpu.SemaphoreType.DMA((len(late),)),
                pltpu.SemaphoreType.DMA((6,)),
                pltpu.SemaphoreType.DMA((24,)),
                pltpu.SemaphoreType.DMA((24,)),
            ]
            + [pltpu.VMEM(a.shape, a.dtype) for a in outs],
            flops=work,
            moved=40 * 2**20,
            group=5,
            alias={24: 12},
        )(piece_starts, *late, near_b, far_a, far_b, grads, expert_x)
        operands = (x, ext, dq, dk, dv, wq, wk, wv, grad_wo, grad_ext)
        operands += (d_middle, slot, near_a, *back[:3], shared_out, probs, middle)
        strip = (2, width // SLOTS, width)
        grad_in, outputs, weights, small, *rest = call(
            tail_kernel,
            [wide, token_f, shape((4, rows, width), F32), shape((16, width), F32)]
            + [shape(quarter)] * 3
            + [shape(expert_pack.shape)] * 3,
            [VMEM] * 3 + [ANY, VMEM] + [ANY] * 4 + [VMEM] + [ANY] * 11,
            [VMEM] * 4 + [ANY] * 6,
            [
                pltpu.VMEM((tokens, width), BF),
                pltpu.VMEM((8, width), F32),
                pltpu.VMEM((4, width, width), BF),
                pltpu.VMEM((2, width, width), BF),
                pltpu.VMEM((4,) + strip, BF),
                pltpu.VMEM((3,) + strip, BF),
                pltpu.VMEM(strip, BF),
                pltpu.VMEM((2,) + strip, BF),
                pltpu.VMEM(strip, BF),
                pltpu.VMEM((4, 16, width), BF),
                pltpu.VMEM((6, 16, width), BF),
                pltpu.VMEM((tokens, width), BF),
                pltpu.VMEM((width, width), BF),
                pltpu.VMEM((width, width), BF),
                pltpu.VMEM((width, width), BF),
                pltpu.VMEM((width, width), BF),
                pltpu.VMEM((tokens, width), F32),
                pltpu.VMEM((tokens, 128), F32),
                pltpu.VMEM((CAP, width), BF),
                pltpu.VMEM((CAP, width), BF),
                pltpu.VMEM((CAP, width), BF),
                pltpu.VMEM((CAP, width), BF),
                pltpu.VMEM((tokens, width), BF),
                pltpu.VMEM((tokens, 128), F32),
                pltpu.VMEM((tokens, width), F32),
                pltpu.SemaphoreType.DMA((14,)),
                pltpu.SemaphoreType.DMA((32,)),
                pltpu.SemaphoreType.DMA((32,)),
            ],
            flops=2 * tokens * width * (6 * width + 4 * CAP),
            moved=40 * 2**20,
            group=6,
        )(*operands, expert_total, shared_total)
        banks = [shape((4, width, units), F32)] * 2 + [shape((4, units, width), F32)]
        banks += [shape((width, units), F32)] * 2 + [shape((units, width), F32)]
        shared_far, shared_mate, shared_cross, *experts = rest
        *finals, grad_q, grad_k, grad_v, grad_o, gain_one, gain_two, grad_router = call(
            finish_kernel,
            banks[:3] + [wide, token_f] + banks[3:] + [shape((rows, width), F32)] * 4
            + [shape((1, rows), F32)] * 2 + [shape((rows, 4), F32)],
            [ANY] * 11 + [VMEM],
            [ANY] * 12 + [VMEM] * 3,
            [
                pltpu.VMEM((4,) + expert_pack.shape, BF),
                pltpu.VMEM((tokens, width), F32),
                pltpu.VMEM((tokens, width), BF),
                pltpu.VMEM((4,) + quarter, BF),
                pltpu.VMEM((4, rows, width), F32),
            ]
            + [pltpu.VMEM(b.shape, F32) for b in banks[3:] + banks[:3]]
            + [pltpu.SemaphoreType.DMA((11,)), pltpu.SemaphoreType.DMA((21,))],
            moved=26 * 2**20,
        )(
            expert_total, *experts, grad_in, outputs,
            shared_total, shared_mate, shared_far, shared_cross, weights, small,
        )
        grad_in, outputs = finals.pop(3), finals.pop(3)
        gain_one, gain_two = gain_one[0], gain_two[0]
    else:
        d_middle, grad_wo, grad_ext, dq, dk, dv = call(
            plain_back_kernel, outs, specs + [VMEM] * 4, [VMEM] * 6, scratch, flops=work,
            moved=40 * 2**20,
        )(*operands, q, k, v, lse, cosine, sine)
        out_rows = [near_a, to_rep(near_b, 1), to_rep(far_a, 2), to_rep(far_b, 3)]
        grad_in, outputs, gw, gain = call(
            plain_tail_kernel,
            [wide, token_f, shape((3, width, width)), shape((8, width), F32)],
            [VMEM] * 17,
            [VMEM] * 4,
            [pltpu.VMEM((tokens, width), BF), pltpu.VMEM((8, width), F32)],
            flops=2 * tokens * width * (6 * width + 4 * CAP),
            moved=40 * 2**20,
        )(
            x, ext, dq, dk, dv, wq, wk, wv, d_middle, slot, *out_rows, shared_out, probs, middle
        )

        def over_rep(total):
            return lax.psum(total.astype(BF), "rep").astype(F32)

        def unslot(every, part_units):
            every = every.reshape(SLOTS, 3, width, shards // SLOTS, part_units)
            every = every.transpose(0, 3, 1, 2, 4).reshape(shards, 3, width, part_units)
            return lax.psum_scatter(every, "shard", scatter_dimension=0)

        grad_q, grad_k, grad_v, grad_o = (
            over_rep(lax.psum_scatter(w, "shard", tiled=True))
            for w in (gw[0], gw[1], gw[2], grad_wo)
        )
        small = grad_ext.at[4].add(jnp.sum(gain, axis=0))
        small = lax.psum(small, ("rep", "shard"))
        shared_sum = grads_own.astype(F32) + to_rep(grads_other, 1).astype(F32)
        total = unslot(shared_sum.astype(BF), units // 2).astype(F32)
        total = (total + to_rep(total.astype(BF), 2).astype(F32)).astype(BF)
        mate = to_rep(total, 1)
        shared_full = jnp.concatenate(
            [jnp.where(core == 0, total, mate), jnp.where(core == 0, mate, total)], axis=2
        ).astype(F32)
        expert_total = unslot(grads, units).astype(BF)
        parts = jnp.stack([expert_total] + [to_rep(expert_total, o) for o in (1, 2, 3)])
        full = jnp.take(parts, jnp.arange(4) ^ rep, axis=0).astype(F32)
        finals = (full[:, 0], full[:, 1], full[:, 2].transpose(0, 2, 1))
        finals += (shared_full[0], shared_full[1], shared_full[2].T)
        tiny = lax.dynamic_slice(small, (0, shard * rows), (16, rows))
        gain_one, gain_two, grad_router = tiny[4], tiny[5], tiny[:4].T
    return (
        outputs[None],
        grad_in[None],
        gain_one,
        grad_q,
        grad_k,
        grad_v,
        grad_o,
        gain_two,
        grad_router,
        *finals,
    )


def solution(mesh):
    in_specs = (
        P(("rep", "shard"), None, None),
        P(("rep", "shard"), None),
        P(("rep", "shard"), None, None),
        P("shard"),
        P("shard", None),
        P("shard", None),
        P("shard", None),
        P("shard", None),
        P("shard"),
        P("shard", None),
        P(None, None, "shard"),
        P(None, None, "shard"),
        P(None, "shard", None),
        P(None, "shard"),
        P(None, "shard"),
        P("shard", None),
        P(("rep", "shard"), None, None),
    )
    out_specs = (
        P(("rep", "shard"), None, None),
        P(("rep", "shard"), None, None),
        P("shard"),
        P("shard", None),
        P("shard", None),
        P("shard", None),
        P("shard", None),
        P("shard"),
        P("shard", None),
        P(None, None, "shard"),
        P(None, None, "shard"),
        P(None, "shard", None),
        P(None, "shard"),
        P(None, "shard"),
        P("shard", None),
    )
    return jax.shard_map(body, mesh=mesh, in_specs=in_specs, out_specs=out_specs, check_vma=False)
```

```python
import functools

import jax
import jax.numpy as jnp
import numpy as np
from jax import lax
from jax.experimental import pallas as pl
from jax.experimental.pallas import tpu as pltpu
from jax.sharding import PartitionSpec as P

HEADS = 12
PIECE = 256
CAP = 576
EPSILON = 1e-06
MASKED = -1e30
F32, BF = jnp.float32, jnp.bfloat16
AXES = ("rep", "shard")
TILE = 256
SLOTS = 8
VMEM_LIMIT = 62 * 2**20
ANY = pl.BlockSpec(memory_space=pl.ANY)
SMEM = pl.BlockSpec(memory_space=pltpu.SMEM)
VMEM = pl.BlockSpec(memory_space=pltpu.VMEM)


def dot(a, b, i, j):
    return lax.dot_general(a, b, (((i,), (j,)), ((), ())), preferred_element_type=F32)


def nn(a, b):
    return dot(a, b, 1, 0)


def nt(a, b):
    return dot(a, b, 1, 1)


def tn(a, b):
    return dot(a, b, 0, 0)


def iota(shape, dim):
    return lax.broadcasted_iota(jnp.int32, shape, dim)


def ones_where(cond):
    return jnp.where(cond, 1.0, 0.0).astype(BF)


def call(
    kernel, out_shape, in_specs, out_specs, scratch=(), flops=0, moved=0, grid=None, group=None,
    alias=None,
):
    extra = {} if grid is None else {"grid": grid}
    params = {} if group is None else {"collective_id": group, "has_side_effects": True}
    return pl.pallas_call(
        kernel,
        out_shape=out_shape,
        in_specs=in_specs,
        out_specs=out_specs,
        scratch_shapes=list(scratch),
        input_output_aliases=alias or {},
        compiler_params=pltpu.CompilerParams(vmem_limit_bytes=VMEM_LIMIT, **params),
        cost_estimate=pl.CostEstimate(flops=flops, bytes_accessed=moved, transcendentals=0),
        **extra,
    )


def shape(dims, dtype=BF):
    return jax.ShapeDtypeStruct(dims, dtype)


def permute(x, move):
    reps, shards = lax.axis_size("rep"), lax.axis_size("shard")
    pairs = []
    for r in range(reps):
        for s in range(shards):
            to_r, to_s = move(r, s)
            pairs.append((r * shards + s, to_r * shards + to_s))
    return lax.ppermute(x, AXES, pairs)


def to_rep(x, offset):
    return permute(x, lambda r, s: (r ^ offset, s))


def spin(block, cosine, sine):
    lane = iota(block.shape, 1)
    partner = jnp.where(lane % 64 < 32, pltpu.roll(block, 96, 1), pltpu.roll(block, 32, 1))
    return block * cosine + partner * sine


def sibling(rep, o):
    return 2 * lax.rem(lax.div(rep, 2) + o // 2, 2) + lax.rem(lax.rem(rep, 2) + o % 2, 2)


def route_slots(rep, routes_t, rank_out, slot_out):
    tokens = routes_t.shape[1]
    first, second = routes_t[0:1, :], routes_t[1:2, :]
    expert = iota((8, tokens), 0)
    chosen = (expert == first) | (expert == second)
    upper = ones_where(iota((tokens, tokens), 0) <= iota((tokens, tokens), 1))
    rank = nn(ones_where(chosen), upper) - 1.0
    rank_out[...] = jnp.where(chosen, rank, -1.0)
    filler = jnp.zeros((6, tokens), F32)
    named = jnp.concatenate([routes_t[...].astype(F32), filler], axis=0).T
    lane = iota((tokens, 128), 1)
    one, two = named[:, 0:1], named[:, 1:2]
    lane_f = lane.astype(F32)
    lower = ones_where(iota((tokens, tokens), 0) >= iota((tokens, tokens), 1))
    place = nn(lower, ones_where((lane_f == one) | (lane_f == two))) - 1.0
    for o in range(1, 4):
        place = place + jnp.where(lane == sibling(rep, o), float(o * CAP), 0.0)
    slot_one = jnp.sum(jnp.where(lane_f == one, place, 0.0), axis=1, keepdims=True)
    slot_two = jnp.sum(jnp.where(lane_f == two, place, 0.0), axis=1, keepdims=True)
    slot_out[...] = jnp.where(lane < 64, slot_one, slot_two)


def pack_row(rep, rank, source, o, out):
    row = rank[pl.ds(sibling(rep, o), 1), :]
    pick = ones_where(iota((CAP, source.shape[0]), 0).astype(F32) == row)
    out[...] = nn(pick, source[...]).astype(BF)


def pack_rows(rep, rank, source, packed):
    for o, out in enumerate(packed):
        pack_row(rep, rank, source, o, out)


def qkv_rows(x, ext, cosine, sine, wq, wk, wv, q, k, v):
    tokens, width = x.shape
    gain = ext[4:5, :]

    def tile(t, carry):
        at = pl.ds(pl.multiple_of(t * TILE, TILE), TILE)
        rows_in = x[at, :].astype(F32)
        scale = lax.rsqrt(jnp.mean(rows_in * rows_in, axis=1, keepdims=True) + EPSILON)
        normed = (rows_in * scale * gain).astype(BF)
        cos_t, sin_t = cosine[at, :], sine[at, :]
        for weight, out, factor in ((wq, q, 0.125), (wk, k, 1.0)):
            full = nn(normed, weight[...])
            for b in range(width // 128):
                turned = spin(full[:, b * 128 : (b + 1) * 128], cos_t, sin_t)
                out[at, b * 128 : (b + 1) * 128] = turned.astype(BF) * jnp.asarray(factor, BF)
        v[at, :] = nn(normed, wv[...]).astype(BF)
        return carry

    lax.fori_loop(0, tokens // TILE, tile, 0)


def when(cond, body):
    if cond is True:
        body()
    elif cond is not False:
        pl.when(cond)(body)


def both(one, two):
    if one is True or two is False:
        return two
    if two is True or one is False:
        return one
    return one & two


class Net:
    def __init__(self, send, recv):
        self.rep, self.shard = lax.axis_index("rep"), lax.axis_index("shard")
        self.core, self.z = lax.rem(self.rep, 2), lax.div(self.shard, 2)
        self.x = lax.rem(self.shard, 2)
        self.mate = self.rep + 1 - 2 * self.core
        self.across = self.shard + 1 - 2 * self.x
        first = lax.max(self.z - 1, 1 - self.z)
        third = 3 * (1 - lax.div(self.z, 2))
        self.levels = [self.z, first, 6 - self.z - first - third, third]
        self.up = lax.min(self.shard + 2, 6 + self.x)
        self.down = lax.max(self.shard - 2, self.x)
        self.cousins = [self.rep] + [sibling(self.rep, o) for o in (1, 2, 3)]
        self.send, self.recv = send, recv
        self.count, self.open = 0, {}

    def event(self):
        self.count += 1
        return self.count - 1

    def place(self, n, side):
        return self.levels[n] * 2 + (self.x if side == 0 else 1 - self.x)

    def cycle(self, d):
        return lax.rem(self.z + d, 4) * 2 + self.x

    def copy(self, event, source, target, rep, shard):
        return pltpu.make_async_remote_copy(
            src_ref=source,
            dst_ref=target,
            send_sem=self.send.at[event],
            recv_sem=self.recv.at[event],
            device_id=(rep, shard),
            device_id_type=pl.DeviceIdType.MESH,
        )

    def put(self, event, source, target, rep, shard, cond=True):
        when(cond, self.copy(event, source, target, rep, shard).start)
        self.open[event] = (cond, source)

    def got(self, event, like, cond=True):
        when(cond, self.copy(event, like, like, self.mate, self.shard).wait_recv)

    def settle(self, event):
        cond, source = self.open.pop(event)
        when(cond, self.copy(event, source, source, self.mate, self.shard).wait_send)

    def close(self):
        for event, (cond, source) in self.open.items():
            when(cond, self.copy(event, source, source, self.mate, self.shard).wait_send)

    def meet(self, z_ways, others):
        barrier = pltpu.get_barrier_semaphore()

        def greet(rep, shard):
            pl.semaphore_signal(
                barrier, inc=1, device_id=(rep, shard), device_id_type=pl.DeviceIdType.MESH
            )

        count = len(others)
        for rep, shard in others:
            greet(rep, shard)
        if z_ways == "line":
            when(self.z < 3, lambda: greet(self.rep, self.up))
            when(self.z > 0, lambda: greet(self.rep, self.down))
            count = count + lax.min(self.z, 1) + lax.min(3 - self.z, 1)
        if z_ways == "all":
            for d in (1, 2, 3):
                greet(self.rep, self.cycle(d))
            count = count + 3
        pl.semaphore_wait(barrier, count)


class Line:
    def __init__(self, net, bank, ways=4):
        self.net, self.bank = net, bank
        self.events = {(way, k): net.event() for way in range(ways) for k in range(-3, 4)}
        self.spots = {0: (net.shard, True)}
        for k in (1, 2, 3):
            self.spots[k] = (lax.min(net.shard + 2 * k, 6 + net.x), net.z < 4 - k)
            self.spots[-k] = (lax.max(net.shard - 2 * k, net.x), net.z >= k)
        self.flips = {k: spot + 1 - 2 * net.x for k, (spot, _) in self.spots.items()}
        self.onward = {k: both(self.spots[k][1], net.z < 3) for k in self.spots}
        self.back = {k: both(self.spots[k][1], net.z > 0) for k in self.spots}

    def spread(self, k, source):
        net, (spot, here) = self.net, self.spots[k]
        target = self.bank.at[net.core, spot]
        if -3 < k <= 0:
            event = self.events[0, k - 1]
            net.put(event, source, target, net.rep, net.up, self.onward[k])
        if 0 <= k < 3:
            event = self.events[0, k + 1]
            net.put(event, source, target, net.rep, net.down, self.back[k])
        net.put(self.events[1, k], source, target, net.rep, net.across, here)
        net.put(self.events[2, k], source, target, net.mate, net.shard, here)

    def along(self, k):
        spot, here = self.spots[k]
        piece = self.bank.at[self.net.core, spot]
        self.net.got(self.events[0, k], piece, here)
        self.spread(k, piece)

    def over(self, k):
        net, here = self.net, self.spots[k][1]
        piece = self.bank.at[net.core, self.flips[k]]
        net.got(self.events[1, k], piece, here)
        net.put(self.events[3, k], piece, piece, net.mate, net.shard, here)

    def finish(self):
        other = 1 - self.net.core
        for k in (0, 1, -1, 2, -2, 3, -3):
            spot, here = self.spots[k]
            self.net.got(self.events[2, k], self.bank.at[other, spot], here)
            self.net.got(self.events[3, k], self.bank.at[other, self.flips[k]], here)


class Spread:
    def __init__(self, net, piece, bank):
        self.net, self.piece, self.bank = net, piece, bank
        self.line = Line(net, bank, 8)
        self.events, self.spots, self.flips = self.line.events, self.line.spots, self.line.flips
        self.half = piece.shape[1] // 2
        y = lax.div(net.rep, 2)
        self.rows = [pl.ds(pl.multiple_of(n * self.half, 128), self.half) for n in (y, 1 - y)]
        self.far = net.cousins[2]

    def view(self, core, spot, rows):
        return self.bank.at[core, spot, :, self.rows[rows], :]

    def begin(self):
        net = self.net
        source = self.piece.at[:, self.rows[0], :]
        target = self.view(net.core, net.shard, 0)
        net.put(self.events[0, -1], source, target, net.rep, net.up, self.line.onward[0])
        net.put(self.events[0, 1], source, target, net.rep, net.down, self.line.back[0])
        net.put(self.events[1, 0], source, target, net.rep, net.across)
        whole = self.bank.at[net.core, net.shard]
        net.put(self.events[2, 0], self.piece, whole, net.mate, net.shard)

    def hand(self, way, k, here, piece):
        net = self.net
        net.put(self.events[way + 4, k], piece, piece, self.far, net.shard, here)
        net.put(self.events[way + 2, k], piece, piece, net.mate, net.shard, here)

    def along(self, k):
        net, (spot, here) = self.net, self.spots[k]
        piece = self.view(net.core, spot, 0)
        net.got(self.events[0, k], piece, here)
        if -3 < k < 0:
            net.put(self.events[0, k - 1], piece, piece, net.rep, net.up, self.line.onward[k])
        if 0 < k < 3:
            net.put(self.events[0, k + 1], piece, piece, net.rep, net.down, self.line.back[k])
        net.put(self.events[1, k], piece, piece, net.rep, net.across, here)
        self.hand(0, k, here, piece)

    def over(self, k):
        net, here = self.net, self.spots[k][1]
        piece = self.view(net.core, self.flips[k], 0)
        net.got(self.events[1, k], piece, here)
        self.hand(1, k, here, piece)

    def relay(self, way, k):
        net, here = self.net, self.spots[k][1]
        spot = self.spots[k][0] if way == 0 else self.flips[k]
        piece = self.view(net.core, spot, 1)
        net.got(self.events[way + 4, k], piece, here)
        net.put(self.events[way + 6, k], piece, piece, net.mate, net.shard, here)

    def finish(self):
        net, other = self.net, 1 - self.net.core
        net.got(self.events[2, 0], self.bank.at[other, net.shard])
        for k in (0, 1, -1, 2, -2, 3, -3):
            spot, here = self.spots[k]
            if k:
                net.got(self.events[2, k], self.view(other, spot, 0), here)
                net.got(self.events[6, k], self.view(other, spot, 1), here)
            net.got(self.events[3, k], self.view(other, self.flips[k], 0), here)
            net.got(self.events[7, k], self.view(other, self.flips[k], 1), here)


def exchange(net, sources, targets):
    events = [net.event() for _ in range(3)]
    for o in (2, 3, 1):
        net.put(events[o - 1], sources[o - 1], targets[o - 1], net.cousins[o], net.shard)
    return [(events[o], targets[o]) for o in range(3)]


def head_kernel(
    routes_t, cot, x, wq_in, wk_in, wv_in, wo_in, small, cosine, sine,
    e_gate, e_up, e_down, s_gate, s_up, s_down,
    *refs,
):
    width = x.shape[1]
    half = width // SLOTS
    outs, (c1, c2, c3, experts) = refs[:13], refs[13:17]
    bank, packed, piece, e_raw, s_raw, pack_sems, out_sems, send, recv, own_sem = refs[17:27]
    rank, slot, q, k, v, wq, wk, wv, wo, ext, c0, expert_piece, shared_piece = refs[27:]
    stores = copies_of(zip(refs[27:], outs), out_sems)
    net = Net(send, recv)
    units = s_raw.shape[0]
    cut = pl.ds(pl.multiple_of(net.core * units, 128), units)
    packs = copies_of(
        (
            (e_gate.at[net.rep], expert_piece.at[0]),
            (e_up.at[net.rep], expert_piece.at[1]),
            (e_down.at[net.rep], e_raw),
            (s_gate.at[:, cut], shared_piece.at[0]),
            (s_up.at[:, cut], shared_piece.at[1]),
            (s_down.at[cut, :], s_raw),
        ),
        pack_sems,
    )
    for copy in packs:
        copy.start()
    for core, (low, high) in enumerate(((wq_in, wk_in), (wv_in, wo_in))):

        @pl.when(net.core == core)
        def _():
            piece[0:half, :] = low[...]
            piece[half : 2 * half, :] = high[...]

    piece[2 * half : 2 * half + 16, :] = small[...]
    line = Line(net, bank)
    e_events = [net.event() for _ in range(3)]
    mine, most = experts.at[net.shard], experts.at[net.shard, pl.ds(0, 2)]
    peers = [(net.cousins[o], net.shard) for o in (1, 2, 3)]
    net.meet("line", peers + [(net.rep, net.across)])
    line.spread(0, piece)
    own = pltpu.make_async_copy(piece, bank.at[net.core, net.shard], own_sem)
    own.start()
    route_slots(net.rep, routes_t, rank, slot)
    events = [net.event() for _ in range(3)]
    for o, far in ((2, c2), (3, c3), (1, c1)):
        pack_row(net.rep, rank, cot, o, packed.at[o - 1])
        net.put(events[o - 1], packed.at[o - 1], far, net.cousins[o], net.shard)
    arrivals = [(events[0], c1), (events[1], c2), (events[2], c3)]
    pack_row(net.rep, rank, cot, 0, c0)
    for copy in packs:
        copy.wait()
    expert_piece[2] = e_raw[...].astype(F32).T.astype(BF)
    shared_piece[2] = s_raw[...].astype(F32).T.astype(BF)
    line.along(1)
    line.along(-1)
    line.over(0)
    line.along(2)
    line.along(-2)
    net.put(e_events[0], expert_piece, mine, net.rep, net.up, net.z < 3)
    net.put(e_events[1], expert_piece, mine, net.rep, net.down, net.z > 0)
    line.over(1)
    line.over(-1)
    line.along(3)
    line.along(-3)
    net.put(e_events[2], expert_piece.at[pl.ds(0, 2)], most, net.rep, net.across)
    for step in (2, -2, 3, -3):
        line.over(step)
    own.wait()
    line.finish()
    gathered = bank[0, 0, 2 * half : 2 * half + 16, :].astype(F32)
    for j in range(1, SLOTS):
        gathered = gathered + bank[0, j, 2 * half : 2 * half + 16, :].astype(F32)
    ext[...] = gathered
    for j in range(SLOTS):
        at = slice(j * half, (j + 1) * half)
        wq[at, :] = bank[0, j, 0:half, :]
        wk[at, :] = bank[0, j, half : 2 * half, :]
        wv[at, :] = bank[1, j, 0:half, :]
        wo[at, :] = bank[1, j, half : 2 * half, :]
    qkv_rows(x, ext, cosine, sine, wq, wk, wv, q, k, v)
    for copy in stores:
        copy.start()
    for event, like in arrivals:
        net.got(event, like)
    net.got(e_events[0], mine, net.z > 0)
    net.got(e_events[1], mine, net.z < 3)
    net.got(e_events[2], most)
    for copy in stores:
        copy.wait()
    net.close()


def plain_head_kernel(
    routes_t, cot, x, cosine, sine, wq, wk, wv, ext,
    rank, slot, q, k, v, c0, c1, c2, c3,
):
    rep = lax.axis_index("rep")
    route_slots(rep, routes_t, rank, slot)
    pack_rows(rep, rank, cot, (c0, c1, c2, c3))
    qkv_rows(x, ext, cosine, sine, wq, wk, wv, q, k, v)


def fill_bias(starts, bias):
    tokens = bias.shape[0]

    def tile(t, carry):
        at = pl.ds(pl.multiple_of(t * TILE, TILE), TILE)
        query = iota((TILE, tokens), 0) + t * TILE
        key = iota((TILE, tokens), 1)
        allowed = key <= query
        for n in range(2):
            begin = starts[0, n]
            inside = (query >= begin) & (query < begin + PIECE)
            allowed = allowed | (inside & (key >= begin) & (key < begin + PIECE))
        bias[at, :] = jnp.where(allowed, 0.0, MASKED)
        return carry

    lax.fori_loop(0, tokens // TILE, tile, 0)


def keep_half(block, h):
    low = iota(block.shape, 1) < 64
    return jnp.where(low if h == 0 else ~low, block.astype(F32), 0.0).astype(BF)


def biased(scores, bias, begin, free, end):
    tail = scores[:, free:] + bias[begin : begin + TILE, free:end]
    return tail if free == 0 else jnp.concatenate([scores[:, :free], tail], axis=1)


def attend_pairs(q, k, v, out, lse, bias, step):
    tokens, width = q.shape

    def pair(i, carry):
        step(i)
        cols = pl.ds(pl.multiple_of(i * 128, 128), 128)
        keys = k[:, cols]
        low = iota((tokens, 128), 1) < 64
        values = v[:, cols].astype(F32)
        value_one = [
            jnp.where(low, values, 1.0).astype(BF),
            jnp.where(low, 1.0, values).astype(BF),
        ]
        low = iota((TILE, 128), 1) < 64
        for t in range(tokens // TILE):
            begin = t * TILE
            end = min(tokens, begin + TILE + PIECE)
            block = q[begin : begin + TILE, cols]
            results, totals = [], []
            for h in range(2):
                scores = nt(keep_half(block, h), keys[:end])
                scores = biased(scores, bias, begin, begin, end)
                row_max = jnp.max(scores, axis=1, keepdims=True)
                probs = jnp.exp(scores - row_max).astype(BF)
                mixed = nn(probs, value_one[h][:end])
                total = pltpu.roll(mixed, 64, 1)
                results.append(mixed / total)
                totals.append(row_max + jnp.log(total))
            out[begin : begin + TILE, cols] = jnp.where(low, results[0], results[1]).astype(BF)
            lse[begin : begin + TILE, cols] = jnp.where(low, totals[0], totals[1])
        return carry

    lax.fori_loop(0, width // 128, pair, 0)


def router_rows(ext):
    rows = jnp.where(iota(ext.shape, 0) < 4, ext[...], 0.0)
    return jnp.concatenate([rows, jnp.zeros((112, ext.shape[1]), F32)], axis=0).astype(BF)


def route_probs(normed, router):
    logits = nt(normed, router)
    logits = jnp.where(iota(logits.shape, 1) < 4, logits, MASKED)
    raised = jnp.exp(logits - jnp.max(logits, axis=1, keepdims=True))
    return raised / jnp.sum(raised, axis=1, keepdims=True)


def middle_rows(rep, x, attended, wo, ext, rank, middle, normed, probs, packed):
    tokens = x.shape[0]
    gain = ext[5:6, :]
    router = router_rows(ext)

    def tile(t, carry):
        at = pl.ds(pl.multiple_of(t * TILE, TILE), TILE)
        rows = x[at, :].astype(F32) + nn(attended[at, :], wo[...])
        scale = lax.rsqrt(jnp.mean(rows * rows, axis=1, keepdims=True) + EPSILON)
        middle[at, :] = rows
        unit = (rows * scale * gain).astype(BF)
        normed[at, :] = unit
        probs[at, :] = route_probs(unit, router)
        return carry

    lax.fori_loop(0, tokens // TILE, tile, 0)
    pack_rows(rep, rank, normed, packed)


def forward_kernel(
    starts, q, k, v, x, wo, ext, rank, shared_piece, expert_piece, expert_in,
    *refs,
):
    outs, shared_bank, experts = refs[:9], refs[9], refs[10]
    bias, out_sems, send, recv = refs[11:15]
    attended, lse, middle, normed, probs, x0, x1, x2, x3 = refs[15:]
    stores = copies_of(zip(refs[15:], outs), out_sems)
    net = Net(send, recv)
    spread = Spread(net, shared_piece, shared_bank)
    events = [net.event() for _ in range(4)]
    inner = (net.z > 0) & (net.z < 3)
    low, high = experts.at[net.down], experts.at[net.up]
    rest, last = experts.at[net.shard, pl.ds(2, 1)], expert_piece.at[pl.ds(2, 1)]
    near = experts.at[net.place(1, 0), pl.ds(0, 2)]
    net.meet("line", [(net.mate, net.shard), (net.rep, net.across), (spread.far, net.shard)])
    spread.begin()
    fill_bias(starts, bias)

    def step(i):
        @pl.when(i == 1)
        def _():
            spread.along(1)
            spread.along(-1)
            spread.over(0)

        @pl.when(i == 3)
        def _():
            spread.along(2)
            spread.along(-2)
            spread.over(1)
            spread.over(-1)
            net.put(events[2], last, rest, net.rep, net.across)

        @pl.when(i == 5)
        def _():
            spread.along(3)
            spread.along(-3)
            net.put(events[0], low, low, net.rep, net.up, inner)
            net.put(events[1], high, high, net.rep, net.down, inner)
            net.put(events[3], near, near, net.rep, net.across)
            spread.over(2)
            spread.over(-2)

    attend_pairs(q, k, v, attended, lse, bias, step)
    for copy in stores[:2]:
        copy.start()
    spread.over(3)
    spread.over(-3)
    for way, k_step in ((1, 0), (0, 1), (0, -1)):
        spread.relay(way, k_step)
    middle_rows(net.rep, x, attended, wo, ext, rank, middle, normed, probs, (x0, x1, x2, x3))
    for copy in stores[2:]:
        copy.start()
    for way, k_step in ((1, 1), (1, -1), (0, 2), (0, -2), (1, 2), (1, -2)):
        spread.relay(way, k_step)
    for way, k_step in ((0, 3), (0, -3), (1, 3), (1, -3)):
        spread.relay(way, k_step)
    spread.finish()
    net.got(events[0], low, net.z > 1)
    net.got(events[1], low, net.z < 2)
    net.got(events[2], rest)
    net.got(events[3], near)
    for copy in stores:
        copy.wait()
    net.close()


def plain_forward_kernel(
    starts, q, k, v, x, wo, ext, rank,
    attended, lse, middle, normed, probs, x0, x1, x2, x3, bias,
):
    fill_bias(starts, bias)
    attend_pairs(q, k, v, attended, lse, bias, lambda i: None)
    rep = lax.axis_index("rep")
    middle_rows(rep, x, attended, wo, ext, rank, middle, normed, probs, (x0, x1, x2, x3))


CHUNK, CHUNKS = 512, 4


def unit_bank(
    expert, ext, xs, cs, source, target, before, unit, outs, dxs, scratch, ready=None,
    emit=None,
):
    out_acc, dx_acc, gate, wbuf, stage, dw_out, in_sems, out_sems, xc = scratch[:9]
    routed = expert is not None
    blocks, rows = len(xs), xs[0].shape[0]
    per = CHUNK // unit

    def loads(of, buffer, sems, k, b):
        return [
            pltpu.make_async_copy(
                of(k * per + i), buffer.at[b, :, :, pl.ds(i * unit, unit)], sems.at[b, i]
            )
            for i in range(per)
        ]

    def stores(k, b):
        return [
            pltpu.make_async_copy(
                dw_out.at[b, :, :, pl.ds(i * unit, unit)],
                target(k * per + i),
                out_sems.at[b, i],
            )
            for i in range(per)
        ]

    def start_loads(k, b):
        if ready is not None:
            ready(k)
        for copy in loads(source, wbuf, in_sems, k, b):
            copy.start()
        if before is not None:
            for copy in loads(before, scratch[9], scratch[10], k, b):
                copy.start()

    start_loads(0, 0)
    out_acc[...] = jnp.zeros_like(out_acc)
    dx_acc[...] = jnp.zeros_like(dx_acc)
    for n in range(blocks):
        xc[0, n * rows : (n + 1) * rows, :] = xs[n][...]
        xc[1, n * rows : (n + 1) * rows, :] = cs[n][...]
    if routed:
        router = router_rows(ext)
        for n in range(blocks):
            probs = route_probs(xs[n][...], router)
            lane = iota(probs.shape, 1)
            gate[n] = jnp.sum(jnp.where(lane == expert, probs, 0.0), axis=1, keepdims=True)

    def chunk(k, carry):
        b = lax.rem(k, 2)
        for copy in loads(source, wbuf, in_sems, 0, b):
            copy.wait()
        for n in range(blocks):
            x, c = xs[n][...], cs[n][...]
            wg, wu, wd = wbuf[b, 0], wbuf[b, 1], wbuf[b, 2]
            gate_h, up_h, back_h = nn(x, wg), nn(x, wu), nn(c, wd)
            sigma = 0.5 * jnp.tanh(0.5 * gate_h) + 0.5
            silu = gate_h * sigma
            hidden = silu * up_h
            if routed:
                share = gate[n]
                scaled = back_h * share
                weighted = (hidden * share).astype(BF)
            else:
                scaled, weighted = back_h, hidden.astype(BF)
            d_up = (scaled * silu).astype(BF)
            d_gate = (scaled * up_h * (sigma + silu * (1.0 - sigma))).astype(BF)
            product = nt(hidden.astype(BF), wd)
            d_rows = nt(d_gate, wg) + nt(d_up, wu)
            at = slice(n * rows, (n + 1) * rows)
            stage[0, at, :] = d_gate
            stage[1, at, :] = d_up
            stage[2, at, :] = weighted
            if routed:
                pairs = (hidden * back_h).astype(BF)
                d_share = nt(jnp.ones((16, CHUNK), BF), pairs)

            out_acc[n] += product
            dx_acc[n, 0:rows, :] += d_rows
            if routed:
                dx_acc[n, rows : rows + 16, 0:rows] += d_share

        for nxt in range(1, CHUNKS):

            @pl.when(k + 1 == nxt)
            def _():
                start_loads(nxt, nxt % 2)

        @pl.when(k >= 2)
        def _():
            for copy in stores(0, b):
                copy.wait()

        if before is not None:
            for copy in loads(before, scratch[9], scratch[10], 0, b):
                copy.wait()
        for i in range(3):
            part = tn(xc[i // 2], stage[i])
            if before is not None:
                part = part + scratch[9][b, i].astype(F32)
            dw_out[b, i] = part.astype(BF)
        for now in range(CHUNKS):

            @pl.when(k == now)
            def _():
                for copy in stores(now, now % 2):
                    copy.start()
                if emit is not None:
                    emit(now)

        return carry

    lax.fori_loop(0, CHUNKS, chunk, 0)
    for n in range(blocks):
        outs[n][...] = out_acc[n].astype(BF)
        dxs[n][...] = dx_acc[n].astype(BF)
    for b in range(2):
        for copy in stores(0, b):
            copy.wait()


def unit_scratch(blocks, rows, extra, width, per, chained):
    scratch = [
        pltpu.VMEM((blocks, rows, width), F32),
        pltpu.VMEM((blocks, rows + extra, width), F32),
        pltpu.VMEM((blocks, rows, 1), F32),
        pltpu.VMEM((2, 3, width, CHUNK), BF),
        pltpu.VMEM((3, blocks * rows, CHUNK), BF),
        pltpu.VMEM((2, 3, width, CHUNK), BF),
        pltpu.SemaphoreType.DMA((2, per)),
        pltpu.SemaphoreType.DMA((2, per)),
        pltpu.VMEM((2, blocks * rows, width), BF),
    ]
    if chained:
        scratch += [
            pltpu.VMEM((2, 3, width, CHUNK), BF),
            pltpu.SemaphoreType.DMA((2, per)),
        ]
    return scratch


def shared_kernel(
    x, c, piece, bank, x1, x2, x3, expert_in,
    out, dx, grads_own, grads_other, shared_mate, y1, y2, y3, experts,
    send, recv, *scratch,
):
    net = Net(send, recv)
    events = [net.event() for _ in range(4)]
    core_events = [net.event() for _ in range(8)]
    peers = [(net.cousins[o], net.shard) for o in (1, 2, 3)]
    net.meet("line", peers + [(net.rep, net.across)])
    arrivals = exchange(net, (x1, x2, x3), (y1, y2, y3))
    near, second = experts.at[net.place(1, 0), pl.ds(2, 1)], experts.at[net.place(2, 0)]
    net.put(events[0], near, near, net.rep, net.across)
    net.put(events[1], second, second, net.rep, net.across)
    below = experts.at[lax.max(net.shard - 4, net.x)]
    above = experts.at[lax.min(net.shard + 4, 6 + net.x)]
    net.put(events[2], below, below, net.rep, net.up, net.z == 2)
    net.put(events[3], above, above, net.rep, net.down, net.z == 1)
    spots = [net.place(n % 4, n // 4 % 2) for n in range(8)]
    halves = [net.core, 1 - net.core]
    done = scratch[5]
    slices = [done.at[n // 4, :, :, pl.ds(n % 4 * 128, 128)] for n in range(8)]
    places = [shared_mate.at[spot] for spot in spots]

    def source(n):
        return piece if n == 0 else bank.at[halves[n // 8], spots[n % 8]]

    def target(n):
        return (grads_own, grads_other)[n // 8].at[spots[n % 8]]

    def emit(now):
        if now >= 2:
            for n in range(4 * now - 8, 4 * now - 4):
                net.put(core_events[n], slices[n], places[n], net.mate, net.shard)

    unit_bank(
        None, None, [x], [c], source, target, None, 128, [out], [dx], scratch, None, emit
    )
    for event, like in arrivals:
        net.got(event, like)
    net.got(events[0], near)
    net.got(events[1], second)
    net.got(events[2], second, net.z == 3)
    net.got(events[3], second, net.z == 0)
    for n in range(8):
        net.got(core_events[n], places[n])
    net.close()


def far_kernel(
    ext, xa, xb, ca, cb, expert_piece, shared_own, shared_mate, expert_in,
    oa, ob, da, db, grads, shared_keep, shared_y, experts,
    part_a, part_b, part_sems, send, recv, *scratch,
):
    net = Net(send, recv)
    events = [net.event() for _ in range(9)]
    far = net.cousins[2]
    parts = copies_of(((shared_own, part_a), (shared_mate, part_b)), part_sems)
    for copy in parts:
        copy.start()
    net.meet("none", [(net.rep, net.across), (far, net.shard)])
    last = experts.at[net.place(3, 0)]
    net.put(events[0], last, last, net.rep, net.across)
    spots = [net.place(n // 2, n % 2) for n in range(8)]
    y, quarter = lax.div(net.rep, 2), part_a.shape[2] // 2
    rows = [pl.ds(pl.multiple_of(n * quarter, 128), quarter) for n in (y, 1 - y)]
    keep = pltpu.make_async_copy(part_a.at[:, :, rows[0], :], shared_keep, part_sems.at[2])
    away = [part_a.at[j, :, rows[1], :] for j in range(SLOTS)]

    def source(n):
        return expert_piece if n == 0 else experts.at[spots[n]]

    def target(n):
        return grads.at[spots[n]]

    def ready(k):
        if k == 3:
            net.got(events[0], last)

    for copy in parts:
        copy.wait()

    def add(j, carry):
        part_a[j] = part_a[j] + part_b[j]
        return carry

    lax.fori_loop(0, SLOTS, add, 0)
    for j in range(SLOTS):
        net.put(events[1 + j], away[j], shared_y.at[j], far, net.shard)
    keep.start()
    unit_bank(
        net.rep, ext, [xa, xb], [ca, cb], source, target, None, 256, [oa, ob], [da, db],
        scratch, ready,
    )
    keep.wait()
    for j in range(SLOTS):
        net.got(events[1 + j], shared_y.at[j])
    net.close()


def near_kernel(
    ext, xa, xb, ca, cb, expert_piece, experts, before, far_a, far_b,
    shared_keep, shared_y,
    oa, ob, da, shared_total, grads, back_a, back_b, back_c, expert_x,
    db, part_a, part_b, from_x, from_z, third, sems, send, recv, *scratch,
):
    net = Net(send, recv)
    events = [net.event() for _ in range(4)]
    x_events = [net.event() for _ in range(4)]
    z_events = [net.event() for _ in range(3)]
    peers = [(net.cousins[o], net.shard) for o in (1, 2, 3)]
    one = pltpu.make_async_copy(shared_keep, part_a, sems.at[0])
    two = pltpu.make_async_copy(shared_y, part_b, sems.at[1])
    one.start()
    two.start()
    net.meet("all", peers + [(net.rep, net.across)])
    net.put(events[0], far_a, back_a, net.cousins[2], net.shard)
    net.put(events[1], far_b, back_b, net.cousins[3], net.shard)
    one.wait()
    two.wait()

    def add(j, carry):
        part_a[j] = part_a[j] + part_b[j]
        return carry

    lax.fori_loop(0, SLOTS, add, 0)
    mine = [net.cycle(d) for d in range(4)]
    theirs = [spot + 1 - 2 * net.x for spot in mine]
    for d in (2, 1, 3, 0):
        net.put(x_events[d], part_a.at[theirs[d]], from_x.at[d], net.rep, net.across)
    pieces, lands = [part_a.at[spot] for spot in mine], [from_x.at[d] for d in range(4)]
    ends = [from_z.at[d] for d in range(3)]
    spots = [net.place(3 - n // 2, n % 2) for n in range(8)]
    own_slot = 6
    done, target = scratch[5], expert_x.at[net.levels[3]]

    def source(n):
        return expert_piece if n == own_slot else experts.at[spots[n]]

    def ready(k):
        if k == 2:
            for d in (2, 1, 3, 0):
                net.got(x_events[d], lands[d])
                part_a[mine[d]] = part_a[mine[d]] + from_x[d]
                if d:
                    net.put(z_events[d - 1], pieces[d], ends[d - 1], net.rep, mine[d])

    def emit(now):
        if now == 0:
            third[...] = done[0, :, :, 256:512]
            net.put(events[3], third, target, net.rep, net.across)

    unit_bank(
        net.rep, ext, [xa, xb], [ca, cb], source,
        lambda n: grads.at[spots[n]], lambda n: before.at[spots[n]],
        256, [oa, ob], [da, db], scratch, ready, emit,
    )
    net.put(events[2], db, back_c, net.mate, net.shard)
    total = part_a[mine[0]].astype(F32)
    for d in (1, 2, 3):
        net.got(z_events[d - 1], ends[d - 1])
        total = total + from_z[d - 1].astype(F32)
    shared_total[...] = total.astype(BF)
    net.got(events[0], back_a)
    net.got(events[1], back_b)
    net.got(events[2], back_c)
    net.got(events[3], target)
    net.close()


def plain_bank_kernel(blocks, unit, routed, chained, ext, *refs):
    refs = list(refs)

    def take(n):
        taken = refs[:n]
        del refs[:n]
        return taken

    xs, cs = take(blocks), take(blocks)
    bank = take(1)[0]
    before = take(1)[0] if chained else None
    outs, dxs = take(blocks), take(blocks)
    grads = take(1)[0]
    unit_bank(
        lax.axis_index("rep") if routed else None,
        ext, xs, cs,
        lambda n: bank.at[n],
        lambda n: grads.at[n],
        (lambda n: before.at[n]) if chained else None,
        unit, outs, dxs, refs,
    )


def plain_bank(ext, xs, cs, bank, before, routed):
    blocks, (rows, width) = len(xs), xs[0].shape
    chained = before is not None
    extra, unit = (16 if routed else 0), bank.shape[3]
    operands = [ext, *xs, *cs, bank] + ([before] if chained else [])
    outs = [shape((rows, width))] * blocks + [shape((rows + extra, width))] * blocks
    results = call(
        functools.partial(plain_bank_kernel, blocks, unit, routed, chained),
        outs + [shape(bank.shape)],
        [VMEM] * (1 + 2 * blocks) + [ANY] * (2 if chained else 1),
        [VMEM] * (2 * blocks) + [ANY],
        unit_scratch(blocks, rows, extra, width, CHUNK // unit, chained),
        flops=18 * blocks * rows * width * 4 * CHUNK,
        moved=30 * 2**20,
    )(*operands)
    return results[:blocks], results[blocks : 2 * blocks], results[2 * blocks]


def combine_rows(
    slot, d0, d1, d2, d3, d_shared, probs, middle, normed, cot, ext, attended, wo,
    d_middle, d_attended, grad_ext, branch, router_acc, gain_acc,
):
    tokens, width = middle.shape
    rep = lax.axis_index("rep")
    gain = ext[5:6, :]
    router = router_rows(ext)
    router_acc[...] = jnp.zeros_like(router_acc)
    gain_acc[...] = jnp.zeros_like(gain_acc)

    def tile(t, carry):
        at = pl.ds(pl.multiple_of(t * TILE, TILE), TILE)
        slot_one, slot_two = slot[at, 0:1], slot[at, 64:65]
        d_normed = d_shared[at, :].astype(F32)
        lane = iota((TILE, 128), 1)
        d_gates = jnp.zeros((TILE, 128), F32)
        for o, d in enumerate((d0, d1, d2, d3)):
            place = (iota((TILE, CAP), 1) + o * CAP).astype(F32)
            hit = (place == slot_one) | (place == slot_two)
            d_normed = d_normed + nn(ones_where(hit), d[0:CAP, :])
            share = d[CAP : CAP + 16, 0:CAP].astype(F32)[0:1, :]
            d_share = jnp.sum(jnp.where(hit, share, 0.0), axis=1, keepdims=True)
            d_gates = d_gates + jnp.where(lane == sibling(rep, o), d_share, 0.0)
        p = probs[at, :]
        inner = jnp.sum(d_gates * p, axis=1, keepdims=True)
        d_logits = (p * (d_gates - inner)).astype(BF)
        d_normed = d_normed + nn(d_logits, router)
        router_acc[...] += tn(d_logits, normed[at, :])
        rows = middle[at, :]
        scale = lax.rsqrt(jnp.mean(rows * rows, axis=1, keepdims=True) + EPSILON)
        unit = rows * scale
        gain_acc[...] += jnp.sum((d_normed * unit).reshape(TILE // 8, 8, width), axis=0)
        w = d_normed * gain
        inner = jnp.mean(w * unit, axis=1, keepdims=True)
        total = cot[at, :].astype(F32) + scale * (w - unit * inner)
        d_middle[at, :] = total
        rounded = total.astype(BF)
        branch[at, :] = rounded
        d_attended[at, :] = nt(rounded, wo[...]).astype(BF)
        return carry

    lax.fori_loop(0, tokens // TILE, tile, 0)
    row = iota((16, width), 0)
    total = jnp.sum(gain_acc[...], axis=0, keepdims=True)
    grad_ext[...] = jnp.where(row < 4, router_acc[0:16, :], jnp.where(row == 5, total, 0.0))


def output_rows(slot, o0, o1, o2, o3, shared, probs, middle, out, first, last):
    rep = lax.axis_index("rep")

    def tile(t, carry):
        at = pl.ds(pl.multiple_of(t * TILE, TILE), TILE)
        slot_one, slot_two = slot[at, 0:1], slot[at, 64:65]
        total = middle[at, :] + shared[at, :].astype(F32)
        p = probs[at, :]
        lane = iota((TILE, 128), 1)
        for o, rows in enumerate((o0, o1, o2, o3)):
            place = (iota((TILE, CAP), 1) + o * CAP).astype(F32)
            hit = (place == slot_one) | (place == slot_two)
            share = jnp.sum(jnp.where(lane == sibling(rep, o), p, 0.0), axis=1, keepdims=True)
            total = total + nn(jnp.where(hit, share, 0.0).astype(BF), rows[...])
        out[at, :] = total.astype(BF)
        return carry

    lax.fori_loop(first, last, tile, 0)


def back_pairs(
    q, k, v, d_out, out, lse, cosine, sine, dq, dk, dv, bias, dk_acc, dv_acc, step
):
    tokens, width = q.shape

    def pair(i, carry):
        step(i)
        cols = pl.ds(pl.multiple_of(i * 128, 128), 128)
        keys, values = k[:, cols], v[:, cols]
        half_keys = [keep_half(keys, 0), keep_half(keys, 1)]
        dk_acc[...] = jnp.zeros_like(dk_acc)
        dv_acc[...] = jnp.zeros_like(dv_acc)
        low = iota((TILE, 128), 1) < 64
        for t in range(tokens // TILE):
            begin = t * TILE
            end = min(tokens, begin + TILE + PIECE)
            at = slice(begin, begin + TILE)
            block, grad = q[at, cols], d_out[at, cols]
            product = grad.astype(F32) * out[at, cols].astype(F32)
            block_lse = lse[at, cols]
            d_block = None
            for h in range(2):
                block_h, grad_h = keep_half(block, h), keep_half(grad, h)
                scores = nt(block_h, keys[:end])
                scores = biased(scores, bias, begin, begin, end)
                probs = jnp.exp(scores - block_lse[:, 64 * h : 64 * h + 1])
                d_probs = nt(grad_h, values[:end])
                inner = jnp.sum(
                    jnp.where(low if h == 0 else ~low, product, 0.0), axis=1, keepdims=True
                )
                d_scores = (probs * (d_probs - inner)).astype(BF)
                part = nn(d_scores, half_keys[h][:end])
                d_block = part if d_block is None else d_block + part
                dk_acc[0:end, :] += tn(d_scores, block_h)
                dv_acc[0:end, :] += tn(probs.astype(BF), grad_h)
            dq[at, cols] = spin(d_block * 0.125, cosine[at, :], -sine[at, :]).astype(BF)
        dk[:, cols] = spin(dk_acc[...], cosine[...], -sine[...]).astype(BF)
        dv[:, cols] = dv_acc[...].astype(BF)
        return carry

    lax.fori_loop(0, width // 128, pair, 0)


def copies_of(pairs, sems):
    return [pltpu.make_async_copy(a, b, sems.at[i]) for i, (a, b) in enumerate(pairs)]


def fetch(sources, targets, sems):
    copies = copies_of(zip(sources, targets), sems)
    for copy in copies:
        copy.start()
    for copy in copies:
        copy.wait()


class Chain:
    def __init__(self, net, own, from_x, up_in, down_in, held, spare, sems):
        self.net, self.own, self.from_x = net, own, from_x
        self.into, self.held, self.spare, self.sems = (up_in, down_in), held, spare, sems
        keys = [(way, d, m) for way in range(2) for d in (1, 2, 3) for m in range(3)]
        self.events = {key: net.event() for key in keys}
        self.spots = [net.place(n, 0) for n in range(4)]
        self.sends, self.gets = {}, {}
        z = net.z
        for d in (1, 2, 3):
            up, down = lax.min(z + d, 3), lax.max(z - d, 0)
            for m in range(3):
                self.sends[0, d, m] = (held.at[up, m], z < 4 - d)
                self.sends[1, d, m] = (held.at[down, m], z > d - 1)
            self.gets[0, d] = (lax.min(z + d - 1, 3), (z > 0) & (z < 5 - d))
            self.gets[1, d] = (lax.max(z - d + 1, 0), (z < 3) & (z > d - 2))

    def level(self, n):
        to = self.net.levels[n]
        far = self.from_x.at[to]
        fetch([self.own.at[self.spots[n]], far], [self.held.at[to], self.spare.at[0]], self.sems)
        self.held[to] = self.held[to] + self.spare[0]

    def send(self, d, m):
        net = self.net
        for way, to in ((0, net.up), (1, net.down)):
            source, here = self.sends[way, d, m]
            target = self.into[way].at[d - 1, m]
            net.put(self.events[way, d, m], source, target, net.rep, to, here)

    def take(self, d, m):
        net = self.net
        for way in range(2):
            to, here = self.gets[way, d]

            def add():
                source = self.into[way].at[d - 1, m]
                event = self.events[way, d, m]
                net.copy(event, source, source, net.mate, net.shard).wait_recv()
                fetch([source], [self.spare.at[0, m]], self.sems)
                self.held[to, m] = self.held[to, m] + self.spare[0, m]

            when(here, add)


BACK_ROWS = 19


def back_kernel(starts, *refs):
    raw, refs = refs[:BACK_ROWS], refs[BACK_ROWS:]
    o1, o2, o3, grads, expert_x_in = refs[:5]
    outs, expert_total = refs[5:11], refs[11]
    r1, r2, r3, up_in, down_in, expert_x = refs[12:18]
    d_attended, branch, router_acc, gain_acc, bias, dk_acc, dv_acc = refs[18:25]
    local = refs[25 : 25 + BACK_ROWS]
    held, spare, sems, load_sems, out_sems, send, recv = refs[25 + BACK_ROWS : 32 + BACK_ROWS]
    d_middle, grad_wo, grad_ext, dq, dk, dv = refs[32 + BACK_ROWS :]
    stores = copies_of(zip((d_middle, grad_wo, grad_ext, dq, dk, dv), outs), out_sems)
    slot, d0, d1, d2, d3, d_shared, probs, middle, normed, cot, ext, attended, wo = local[:13]
    cosine, sine, q, k, v, lse = local[13:]
    loads = copies_of(zip(raw, local), load_sems)
    for copy in loads:
        copy.start()
    net = Net(send, recv)
    x_events = [net.event() for _ in range(3)]
    chain = Chain(net, grads, expert_x, up_in, down_in, held, spare, sems)
    peers = [(net.cousins[o], net.shard) for o in (1, 2, 3)]
    net.meet("line", peers + [(net.rep, net.across)])
    targets = [expert_x.at[net.levels[n]] for n in range(3)]
    for n in (2, 1, 0):
        source = grads.at[net.place(n, 1)]
        net.put(x_events[n], source, targets[n], net.rep, net.across)
    arrivals = exchange(net, (o1, o2, o3), (r1, r2, r3))
    chain.level(3)
    for m in range(3):
        chain.send(3, m)
    fill_bias(starts, bias)
    for copy in loads:
        copy.wait()
    combine_rows(
        slot, d0, d1, d2, d3, d_shared, probs, middle, normed, cot, ext, attended, wo,
        d_middle, d_attended, grad_ext, branch, router_acc, gain_acc,
    )
    stores[0].start()
    stores[2].start()
    net.got(x_events[2], targets[2])
    chain.level(2)
    for m in range(3):
        chain.take(3, m)
        chain.send(2, m)
    grad_wo[...] = tn(attended[...], branch[...]).astype(BF)
    stores[1].start()

    def step(i):
        @pl.when(i == 3)
        def _():
            net.got(x_events[1], targets[1])
            chain.level(1)
            for m in range(3):
                chain.take(2, m)
                chain.send(1, m)

    back_pairs(
        q, k, v, d_attended, attended, lse, cosine, sine, dq, dk, dv, bias, dk_acc, dv_acc, step
    )
    for copy in stores[3:]:
        copy.start()
    net.got(x_events[0], targets[0])
    chain.level(0)
    for event, like in arrivals:
        net.got(event, like)
    for m in range(3):
        chain.take(1, m)
    expert_total[...] = held[net.z]
    for copy in stores:
        copy.wait()
    net.close()


def plain_back_kernel(
    starts, slot, d0, d1, d2, d3, d_shared, probs, middle, normed, cot, ext, attended, wo,
    q, k, v, lse, cosine, sine,
    d_middle, grad_wo, grad_ext, dq, dk, dv,
    d_attended, branch, router_acc, gain_acc, bias, dk_acc, dv_acc,
):
    combine_rows(
        slot, d0, d1, d2, d3, d_shared, probs, middle, normed, cot, ext, attended, wo,
        d_middle, d_attended, grad_ext, branch, router_acc, gain_acc,
    )
    grad_wo[...] = tn(attended[...], branch[...]).astype(BF)
    fill_bias(starts, bias)
    back_pairs(
        q, k, v, d_attended, attended, lse, cosine, sine, dq, dk, dv, bias, dk_acc, dv_acc,
        lambda i: None,
    )


def norm_rows(x, ext, normed_all):
    gain = ext[4:5, :]

    def tile(t, carry):
        at = pl.ds(pl.multiple_of(t * TILE, TILE), TILE)
        rows = x[at, :].astype(F32)
        scale = lax.rsqrt(jnp.mean(rows * rows, axis=1, keepdims=True) + EPSILON)
        normed_all[at, :] = (rows * scale * gain).astype(BF)
        return carry

    lax.fori_loop(0, x.shape[0] // TILE, tile, 0)


def input_grad(x, ext, dq, dk, dv, wq, wk, wv, d_middle, grad_in, gain_acc, first, last):
    width = x.shape[1]
    gain = ext[4:5, :]

    def tile(t, carry):
        at = pl.ds(pl.multiple_of(t * TILE, TILE), TILE)
        rows = x[at, :].astype(F32)
        scale = lax.rsqrt(jnp.mean(rows * rows, axis=1, keepdims=True) + EPSILON)
        unit = rows * scale
        d_normed = nt(dq[at, :], wq[...]) + nt(dk[at, :], wk[...]) + nt(dv[at, :], wv[...])
        gain_acc[...] += jnp.sum((d_normed * unit).reshape(TILE // 8, 8, width), axis=0)
        w = d_normed * gain
        inner = jnp.mean(w * unit, axis=1, keepdims=True)
        grad_in[at, :] = d_middle[at, :] + scale * (w - unit * inner)
        return carry

    lax.fori_loop(first, last, tile, 0)


def tail_kernel(
    x, ext, dq, dk_in, dv, wq_in, wk_in, wv_in, grad_wo_in, grad_ext,
    d_middle_in, slot_in, o0_in, o1_in, o2_in, o3_in, shared_in, probs_in, middle_in,
    expert_total, shared_total,
    grad_in, outputs, weights, small, shared_far, shared_mate, shared_cross, e1, e2, e3,
    normed_all, gain_acc, gw, from_mate, from_x, from_z, from_y, result, from_core,
    tiny, tiny_in, dk, grad_wo, wq, wk, wv,
    d_middle, slot, o0, o1, o2, o3, shared_out, probs, middle, load_sems,
    send, recv,
):
    width = x.shape[1]
    half = width // SLOTS
    net = Net(send, recv)
    e_events = [net.event() for _ in range(3)]
    s_events = [net.event() for _ in range(3)]
    m_events = [net.event() for _ in range(2)]
    x_events = [[net.event() for _ in range(2)] for _ in range(4)]
    z_events = [[net.event() for _ in range(2)] for _ in range(3)]
    y_events = [net.event() for _ in range(2)]
    c_events = [net.event() for _ in range(2)]
    t_events = [net.event() for _ in range(6)]
    net.meet(
        "all", [(net.mate, net.shard), (net.cousins[2], net.shard), (net.rep, net.across)]
    )
    far = net.cousins[2]
    net.put(s_events[0], shared_total, shared_far, far, net.shard)
    net.put(s_events[1], shared_total, shared_mate, net.mate, net.shard)
    net.put(e_events[1], expert_total, e2, far, net.shard)
    net.put(e_events[0], expert_total, e1, net.mate, net.shard)
    pairs = (
        (dk_in, dk), (grad_wo_in, grad_wo), (wq_in, wq), (wk_in, wk), (wv_in, wv),
        (d_middle_in, d_middle), (slot_in, slot), (o0_in, o0), (o1_in, o1), (o2_in, o2),
        (o3_in, o3), (shared_in, shared_out), (probs_in, probs), (middle_in, middle),
    )
    loads = [pltpu.make_async_copy(a, b, load_sems.at[i]) for i, (a, b) in enumerate(pairs)]
    for copy in loads:
        copy.start()
    norm_rows(x, ext, normed_all)
    spots = [lax.rem(i + 2 * net.core, 4) for i in range(4)]

    def rows_of(spot):
        return pl.ds(pl.multiple_of(spot * half, 32), half)

    mine = [rows_of(net.cycle(d)) for d in range(4)]
    theirs = [rows_of(net.cycle(d) + 1 - 2 * net.x) for d in range(4)]

    def hand(i):
        net.put(m_events[i], gw.at[2 + i], from_mate.at[i], net.mate, net.shard)

    def cross(i):
        net.got(m_events[i], from_mate.at[i])
        gw[i] = gw[i] + from_mate[i]
        for d in (2, 1, 3, 0):
            source = gw.at[i, theirs[d]]
            net.put(x_events[d][i], source, from_x.at[d, i], net.rep, net.across)

    gw[spots[0]] = tn(normed_all[...], dq[...]).astype(BF)
    gw[spots[2]] = tn(normed_all[...], dv[...]).astype(BF)
    hand(0)
    loads[0].wait()
    loads[1].wait()
    gw[spots[1]] = tn(normed_all[...], dk[...]).astype(BF)
    gw[spots[3]] = grad_wo[...]
    hand(1)
    cross(0)
    cross(1)
    gain_acc[...] = jnp.zeros_like(gain_acc)
    for copy in loads[2:]:
        copy.wait()
    count = x.shape[0] // TILE

    def inputs(first, last):
        input_grad(x, ext, dq, dk, dv, wq, wk, wv, d_middle, grad_in, gain_acc, first, last)

    def results(first, last):
        output_rows(
            slot, o0, o1, o2, o3, shared_out, probs, middle, outputs, first, last
        )

    def add_across(d, i):
        net.got(x_events[d][i], from_x.at[d, i])
        gw[i, mine[d], :] = gw[i, mine[d], :] + from_x[d, i]
        if d:
            net.put(
                z_events[d - 1][i], gw.at[i, mine[d]], from_z.at[d - 1, i],
                net.rep, net.cycle(d),
            )

    def add_along(i):
        total = gw[i, mine[0], :].astype(F32)
        for d in (1, 2, 3):
            net.got(z_events[d - 1][i], from_z.at[d - 1, i])
            total = total + from_z[d - 1, i].astype(F32)
        result[0, i] = total.astype(BF)
        net.put(y_events[i], result.at[0, i], from_y.at[i], far, net.shard)

    def tiny_add(n, target_rep, target_shard):
        net.got(t_events[n], tiny_in.at[n])
        tiny[n + 1] = (tiny[n].astype(F32) + tiny_in[n].astype(F32)).astype(BF)
        if target_rep is not None:
            source, target = tiny.at[n + 1], tiny_in.at[n + 1]
            net.put(t_events[n + 1], source, target, target_rep, target_shard)

    inputs(0, 2)
    add_across(2, 0)
    add_across(1, 0)
    inputs(2, 3)
    add_across(3, 0)
    inputs(3, count)
    add_across(0, 0)
    row = iota((16, width), 0)
    total = jnp.sum(gain_acc[...], axis=0, keepdims=True)
    tiny[0] = (grad_ext[...] + jnp.where(row == 4, total, 0.0)).astype(BF)
    net.put(t_events[0], tiny.at[0], tiny_in.at[0], net.mate, net.shard)
    results(0, 1)
    add_across(2, 1)
    tiny_add(0, net.rep, net.across)
    results(1, 2)
    add_across(1, 1)
    tiny_add(1, far, net.shard)
    add_along(0)
    results(2, 3)
    add_across(3, 1)
    tiny_add(2, None, None)
    for d in (1, 2, 3):
        net.put(t_events[2 + d], tiny.at[3], tiny_in.at[2 + d], net.rep, net.cycle(d))
    net.got(s_events[0], shared_far)
    net.put(s_events[2], shared_far, shared_cross, net.mate, net.shard)
    results(3, count)
    add_across(0, 1)
    net.got(e_events[1], e2)
    net.put(e_events[2], e2, e3, net.mate, net.shard)
    total = tiny[3].astype(F32)
    for d in (1, 2, 3):
        net.got(t_events[2 + d], tiny_in.at[2 + d])
        total = total + tiny_in[2 + d].astype(F32)
    small[...] = total.astype(BF).astype(F32)
    add_along(1)
    for i in range(2):
        net.got(y_events[i], from_y.at[i])
        result[1, i] = (result[0, i].astype(F32) + from_y[i].astype(F32)).astype(BF)
        net.put(c_events[i], result.at[1, i], from_core.at[i], net.mate, net.shard)
        weights[spots[i]] = result[1, i].astype(F32)
    for i in range(2):
        net.got(c_events[i], from_core.at[i])
        weights[spots[2 + i]] = from_core[i].astype(F32)
    net.got(e_events[0], e1)
    net.got(s_events[1], shared_mate)
    net.got(s_events[2], shared_cross)
    net.got(e_events[2], e3)
    net.close()


def plain_tail_kernel(
    x, ext, dq, dk, dv, wq, wk, wv, d_middle,
    slot, o0, o1, o2, o3, shared_out, probs, middle,
    grad_in, outputs, gw, gain, normed_all, gain_acc,
):
    norm_rows(x, ext, normed_all)
    for i, d in enumerate((dq, dk, dv)):
        gw[i] = tn(normed_all[...], d[...]).astype(BF)
    gain_acc[...] = jnp.zeros_like(gain_acc)
    count = x.shape[0] // TILE
    input_grad(x, ext, dq, dk, dv, wq, wk, wv, d_middle, grad_in, gain_acc, 0, count)
    gain[...] = gain_acc[...]
    output_rows(
        slot, o0, o1, o2, o3, shared_out, probs, middle, outputs, 0, x.shape[0] // TILE
    )


def finish_kernel(
    e0, e1, e2, e3, wide, plain, q0, q1, q2, q3, weights, small,
    gate, up, down, wide_out, plain_out, s_gate, s_up, s_down,
    grad_q, grad_k, grad_v, grad_o, gain_one, gain_two, grad_router,
    part, wide_in, plain_in, ready_gate, ready_up, ready_down, in_sems, out_sems,
):
    rep, shard = lax.axis_index("rep"), lax.axis_index("shard")
    pairs = [(e, part.at[o]) for o, e in enumerate((e0, e1, e2, e3))]
    loads = copies_of(pairs + [(wide, wide_in), (plain, plain_in)], in_sems)
    for copy in loads:
        copy.start()
    stores = []
    for o in range(4):
        at = sibling(rep, o)
        pairs = [(ready_gate.at[o], gate.at[at]), (ready_up.at[o], up.at[at])]
        pairs.append((ready_down.at[o], down.at[at]))
        loads[o].wait()
        ready_gate[o] = part[o, 0].astype(F32)
        ready_up[o] = part[o, 1].astype(F32)
        ready_down[o] = part[o, 2].astype(F32).T
        made = [pltpu.make_async_copy(a, b, out_sems.at[3 * o + i]) for i, (a, b) in enumerate(pairs)]
        for copy in made:
            copy.start()
        stores += made
    passed = ((wide_in, wide_out), (plain_in, plain_out))
    for i, (a, b) in enumerate(passed):
        loads[4 + i].wait()
        copy = pltpu.make_async_copy(a, b, out_sems.at[12 + i])
        copy.start()
        stores.append(copy)
    quarter, span = q0.shape[1:]
    for o, piece in enumerate((q0, q1, q2, q3)):
        owner = sibling(rep, o)
        rows = pl.ds(pl.multiple_of(lax.div(owner, 2) * quarter, 128), quarter)
        cols = pl.ds(pl.multiple_of(lax.rem(owner, 2) * span, 128), span)
        s_gate[rows, cols] = piece[0].astype(F32)
        s_up[rows, cols] = piece[1].astype(F32)
        s_down[cols, rows] = piece[2].astype(F32).T
    for i, out in enumerate((grad_q, grad_k, grad_v, grad_o)):
        out[...] = weights[i]
    rows, width = weights.shape[1:]
    tiny = small[...].astype(BF)
    pick = ones_where(iota((width, rows), 0) == iota((width, rows), 1) + shard * rows)
    gains = nn(tiny, pick)
    gain_one[...] = gains[4:5, :]
    gain_two[...] = gains[5:6, :]
    grad_router[...] = dot(pick, tiny, 0, 1)[:, 0:4]
    for copy in stores:
        copy.wait()


def rope_tables(length, head_dim):
    positions = np.arange(length, dtype=np.float32)
    inverse_freq = np.float32(10000.0) ** (
        np.float32(-2.0) * np.arange(head_dim // 2, dtype=np.float32) / np.float32(head_dim)
    )
    angle = positions[:, None] * inverse_freq[None, :]
    cosine, sine = np.cos(angle), np.sin(angle)
    return (
        jnp.asarray(np.concatenate([cosine] * 4, axis=1)),
        jnp.asarray(np.concatenate([-sine, sine, -sine, sine], axis=1)),
    )


def body(
    inputs,
    piece_starts,
    routes,
    attn_gain,
    query_weight,
    key_weight,
    value_weight,
    out_weight,
    ffn_gain,
    router_weight,
    expert_gate,
    expert_up,
    expert_down,
    shared_gate,
    shared_up,
    shared_down,
    cotangent,
):
    _, tokens, width = inputs.shape
    shards = lax.axis_size("shard")
    rep, shard = lax.axis_index("rep"), lax.axis_index("shard")
    core = rep % 2
    ringed = shards == SLOTS
    rows = width // shards
    units = shared_gate.shape[1]
    x, cot, chosen = inputs[0], cotangent[0], routes[0]
    small = jnp.concatenate([router_weight.T, attn_gain[None], ffn_gain[None]], axis=0)
    small = jnp.pad(small, ((0, 10), (0, 0)))
    small = lax.dynamic_update_slice(jnp.zeros((16, width), BF), small, (0, shard * rows))
    if not ringed:
        wq, wk, wv, wo = [
            lax.all_gather(w, "shard", axis=0, tiled=True)
            for w in (query_weight, key_weight, value_weight, out_weight)
        ]
        ext = lax.psum(small.astype(F32), "shard")
        shared_pack = jnp.stack([shared_gate, shared_up, shared_down.T])
        my_half = lax.dynamic_slice_in_dim(shared_pack, core * (units // 2), units // 2, 2)
        expert_pack = jnp.stack([expert_gate[rep], expert_up[rep], expert_down[rep].T])

    cosine, sine = rope_tables(tokens, width // HEADS)
    token_f = shape((tokens, width))
    square = shape((width, width))
    packed = [shape((CAP, width))] * 4
    outs = [shape((8, tokens), F32), shape((tokens, 128), F32)] + [token_f] * 3
    work = 2 * tokens * width * (CAP * 4 + 3 * width)
    if ringed:
        expert_shape, half_shape = shape((3, width, units)), shape((3, width, units // 2))
        firsts = outs + [square] * 4 + [shape((16, width), F32), packed[0]]
        firsts += [expert_shape, half_shape]
        rank, slot, q, k, v, wq, wk, wv, wo, ext, cot_own, expert_pack, my_half, *heads = call(
            head_kernel,
            firsts + packed[1:] + [shape((SLOTS,) + expert_shape.shape)],
            [VMEM] * 10 + [ANY] * 6,
            [ANY] * 17,
            [
                pltpu.VMEM((2, SLOTS, 2 * rows + 16, width), BF),
                pltpu.VMEM((3, CAP, width), BF),
                pltpu.VMEM((2 * rows + 16, width), BF),
                pltpu.VMEM((units, width), BF),
                pltpu.VMEM((units // 2, width), BF),
                pltpu.SemaphoreType.DMA((6,)),
                pltpu.SemaphoreType.DMA((13,)),
                pltpu.SemaphoreType.DMA((34,)),
                pltpu.SemaphoreType.DMA((34,)),
                pltpu.SemaphoreType.DMA,
            ]
            + [pltpu.VMEM(a.shape, a.dtype) for a in firsts],
            flops=work,
            moved=24 * 2**20,
            group=0,
        )(
            chosen.T, cot, x, query_weight, key_weight, value_weight, out_weight, small,
            cosine, sine, expert_gate, expert_up, expert_down, shared_gate, shared_up, shared_down,
        )
        *cot_in, expert_bank = heads
        cot_in = [cot_own, *cot_in]
    else:
        rank, slot, q, k, v, *cot_out = call(
            plain_head_kernel, outs + packed, [VMEM] * 9, [VMEM] * 9, flops=work,
            moved=24 * 2**20,
        )(chosen.T, cot, x, cosine, sine, wq, wk, wv, ext)
        cot_in = [cot_out[0]] + [to_rep(cot_out[o], o) for o in (1, 2, 3)]

    outs = [token_f, shape((tokens, width), F32), shape((tokens, width), F32), token_f]
    outs += [shape((tokens, 128), F32)] + packed
    work = 2 * tokens * width * (8 * tokens + width + 4 * CAP)
    bias = pltpu.VMEM((tokens, tokens), F32)
    if ringed:
        attended, lse, middle, normed, probs, *x_out, shared_bank, expert_bank = call(
            forward_kernel,
            outs + [shape((2, SLOTS) + my_half.shape), shape((SLOTS,) + expert_pack.shape)],
            [SMEM] + [VMEM] * 7 + [ANY] * 3,
            [ANY] * 11,
            [
                bias,
                pltpu.SemaphoreType.DMA((9,)),
                pltpu.SemaphoreType.DMA((60,)),
                pltpu.SemaphoreType.DMA((60,)),
            ]
            + [pltpu.VMEM(a.shape, a.dtype) for a in outs],
            flops=work,
            moved=30 * 2**20,
            group=1,
            alias={10: 10},
        )(piece_starts, q, k, v, x, wo, ext, rank, my_half, expert_pack, expert_bank)
    else:
        attended, lse, middle, normed, probs, *x_out = call(
            plain_forward_kernel, outs, [SMEM] + [VMEM] * 7, [VMEM] * 9, [bias], flops=work,
            moved=30 * 2**20,
        )(piece_starts, q, k, v, x, wo, ext, rank)

    rows_out = shape((CAP, width))
    rows_back = shape((CAP + 16, width))
    if ringed:
        half_grads = shape((SLOTS,) + my_half.shape)
        shared_out, shared_dx, grads_own, _, shared_mate, y1, y2, y3, expert_bank = call(
            shared_kernel,
            [token_f] * 2 + [half_grads] * 3 + packed[:3] + [shape(expert_bank.shape)],
            [VMEM] * 2 + [ANY] * 6,
            [VMEM] * 2 + [ANY] * 7,
            [pltpu.SemaphoreType.DMA((15,)), pltpu.SemaphoreType.DMA((15,))]
            + unit_scratch(1, tokens, 0, width, 4, False),
            flops=18 * tokens * width * CHUNK * CHUNKS,
            moved=30 * 2**20,
            group=2,
            alias={7: 8},
        )(normed, cot, my_half, shared_bank, *x_out[1:], expert_bank)
        x_in = [x_out[0], y1, y2, y3]
        bank = shape(expert_bank.shape)
        quarter = (3, width // 2, units // 2)
        quarters = (SLOTS,) + quarter
        far_a, far_b, da, db, before, shared_keep, shared_y, expert_bank = call(
            far_kernel,
            [rows_out] * 2 + [rows_back] * 2 + [bank, shape(quarters), shape(quarters), bank],
            [VMEM] * 5 + [ANY] * 4,
            [VMEM] * 4 + [ANY] * 4,
            [
                pltpu.VMEM(half_grads.shape, BF),
                pltpu.VMEM(half_grads.shape, BF),
                pltpu.SemaphoreType.DMA((3,)),
                pltpu.SemaphoreType.DMA((9,)),
                pltpu.SemaphoreType.DMA((9,)),
            ]
            + unit_scratch(2, CAP, 16, width, 2, False),
            flops=36 * CAP * width * CHUNK * CHUNKS,
            moved=30 * 2**20,
            group=3,
            alias={8: 7},
        )(ext, *x_in[2:], *cot_in[2:], expert_pack, grads_own, shared_mate, expert_bank)
        bank_x, bank_z = (4,) + expert_pack.shape, (3,) + expert_pack.shape
        near_a, near_b, d0, shared_total, grads, d2, d3, d1, expert_x = call(
            near_kernel,
            [rows_out] * 2 + [rows_back, shape(quarter), bank] + [rows_back] * 3 + [shape(bank_x)],
            [VMEM] * 5 + [ANY] * 7,
            [VMEM] * 4 + [ANY] * 5,
            [
                pltpu.VMEM((CAP + 16, width), BF),
                pltpu.VMEM(quarters, BF),
                pltpu.VMEM(quarters, BF),
                pltpu.VMEM((4,) + quarter, BF),
                pltpu.VMEM((3,) + quarter, BF),
                pltpu.VMEM(expert_pack.shape, BF),
                pltpu.SemaphoreType.DMA((2,)),
                pltpu.SemaphoreType.DMA((11,)),
                pltpu.SemaphoreType.DMA((11,)),
            ]
            + unit_scratch(2, CAP, 16, width, 2, True),
            flops=36 * CAP * width * CHUNK * CHUNKS,
            moved=30 * 2**20,
            group=4,
        )(
            ext, *x_in[:2], *cot_in[:2], expert_pack, expert_bank, before, da, db,
            shared_keep, shared_y,
        )
        d_rows = [d0, d1, d2, d3]
    else:

        def slotted(part):
            every = lax.all_gather(part, "shard")
            every = every.reshape(SLOTS, shards // SLOTS, 3, width, part.shape[2])
            return every.transpose(0, 2, 3, 1, 4).reshape(SLOTS, 3, width, -1)

        shared_bank = slotted(my_half)
        shared_bank = jnp.concatenate([shared_bank, to_rep(shared_bank, 1)], axis=0)
        expert_bank = slotted(expert_pack)
        x_in = [x_out[0]] + [to_rep(x_out[o], o) for o in (1, 2, 3)]
        (shared_out,), (shared_dx,), shared_grads = plain_bank(
            ext, [normed], [cot], shared_bank, None, False
        )
        grads_own, grads_other = shared_grads[:SLOTS], shared_grads[SLOTS:]
        (far_a, far_b), (da, db), before = plain_bank(
            ext, x_in[2:], cot_in[2:], expert_bank, None, True
        )
        (near_a, near_b), (d0, d1), grads = plain_bank(
            ext, x_in[:2], cot_in[:2], expert_bank, before, True
        )
        d_rows = [d0, to_rep(d1, 1), to_rep(da, 2), to_rep(db, 3)]
    wide = shape((tokens, width), F32)
    outs = [wide, square, shape((16, width), F32)] + [token_f] * 3
    operands = (piece_starts, slot, *d_rows, shared_dx, probs, middle, normed, cot, ext, attended)
    operands += (wo,)
    specs = [SMEM] + [VMEM] * 15
    scratch = [
        pltpu.VMEM((tokens, width), BF),
        pltpu.VMEM((tokens, width), BF),
        pltpu.VMEM((128, width), F32),
        pltpu.VMEM((8, width), F32),
        bias,
        pltpu.VMEM((tokens, 128), F32),
        pltpu.VMEM((tokens, 128), F32),
    ]
    work = 2 * tokens * width * (2 * width + 4 * CAP) + 40 * tokens * tokens * width
    if ringed:
        late = (*operands[1:], cosine, sine, q, k, v, lse)
        d_middle, grad_wo, grad_ext, dq, dk, dv, expert_total, *back = call(
            back_kernel,
            outs
            + [shape(expert_pack.shape)]
            + [rows_out] * 3
            + [shape(bank_z), shape(bank_z), shape(bank_x)],
            [SMEM] + [ANY] * (len(late) + 5),
            [ANY] * 6 + [VMEM] + [ANY] * 6,
            scratch
            + [pltpu.VMEM(a.shape, a.dtype) for a in late]
            + [
                pltpu.VMEM(bank_x, BF),
                pltpu.VMEM((1,) + expert_pack.shape, BF),
                pltpu.SemaphoreType.DMA((2,)),
                pltpu.SemaphoreType.DMA((len(late),)),
                pltpu.SemaphoreType.DMA((6,)),
                pltpu.SemaphoreType.DMA((24,)),
                pltpu.SemaphoreType.DMA((24,)),
            ]
            + [pltpu.VMEM(a.shape, a.dtype) for a in outs],
            flops=work,
            moved=40 * 2**20,
            group=5,
            alias={24: 12},
        )(piece_starts, *late, near_b, far_a, far_b, grads, expert_x)
        operands = (x, ext, dq, dk, dv, wq, wk, wv, grad_wo, grad_ext)
        operands += (d_middle, slot, near_a, *back[:3], shared_out, probs, middle)
        strip = (2, width // SLOTS, width)
        grad_in, outputs, weights, small, *rest = call(
            tail_kernel,
            [wide, token_f, shape((4, rows, width), F32), shape((16, width), F32)]
            + [shape(quarter)] * 3
            + [shape(expert_pack.shape)] * 3,
            [VMEM] * 3 + [ANY, VMEM] + [ANY] * 4 + [VMEM] + [ANY] * 11,
            [VMEM] * 4 + [ANY] * 6,
            [
                pltpu.VMEM((tokens, width), BF),
                pltpu.VMEM((8, width), F32),
                pltpu.VMEM((4, width, width), BF),
                pltpu.VMEM((2, width, width), BF),
                pltpu.VMEM((4,) + strip, BF),
                pltpu.VMEM((3,) + strip, BF),
                pltpu.VMEM(strip, BF),
                pltpu.VMEM((2,) + strip, BF),
                pltpu.VMEM(strip, BF),
                pltpu.VMEM((4, 16, width), BF),
                pltpu.VMEM((6, 16, width), BF),
                pltpu.VMEM((tokens, width), BF),
                pltpu.VMEM((width, width), BF),
                pltpu.VMEM((width, width), BF),
                pltpu.VMEM((width, width), BF),
                pltpu.VMEM((width, width), BF),
                pltpu.VMEM((tokens, width), F32),
                pltpu.VMEM((tokens, 128), F32),
                pltpu.VMEM((CAP, width), BF),
                pltpu.VMEM((CAP, width), BF),
                pltpu.VMEM((CAP, width), BF),
                pltpu.VMEM((CAP, width), BF),
                pltpu.VMEM((tokens, width), BF),
                pltpu.VMEM((tokens, 128), F32),
                pltpu.VMEM((tokens, width), F32),
                pltpu.SemaphoreType.DMA((14,)),
                pltpu.SemaphoreType.DMA((32,)),
                pltpu.SemaphoreType.DMA((32,)),
            ],
            flops=2 * tokens * width * (6 * width + 4 * CAP),
            moved=40 * 2**20,
            group=6,
        )(*operands, expert_total, shared_total)
        banks = [shape((4, width, units), F32)] * 2 + [shape((4, units, width), F32)]
        banks += [shape((width, units), F32)] * 2 + [shape((units, width), F32)]
        shared_far, shared_mate, shared_cross, *experts = rest
        *finals, grad_q, grad_k, grad_v, grad_o, gain_one, gain_two, grad_router = call(
            finish_kernel,
            banks[:3] + [wide, token_f] + banks[3:] + [shape((rows, width), F32)] * 4
            + [shape((1, rows), F32)] * 2 + [shape((rows, 4), F32)],
            [ANY] * 6 + [VMEM] * 6,
            [ANY] * 5 + [VMEM] * 10,
            [
                pltpu.VMEM((4,) + expert_pack.shape, BF),
                pltpu.VMEM((tokens, width), F32),
                pltpu.VMEM((tokens, width), BF),
            ]
            + [pltpu.VMEM(b.shape, F32) for b in banks[:3]]
            + [pltpu.SemaphoreType.DMA((6,)), pltpu.SemaphoreType.DMA((14,))],
            moved=26 * 2**20,
        )(
            expert_total, *experts, grad_in, outputs,
            shared_total, shared_mate, shared_far, shared_cross, weights, small,
        )
        grad_in, outputs = finals.pop(3), finals.pop(3)
        gain_one, gain_two = gain_one[0], gain_two[0]
    else:
        d_middle, grad_wo, grad_ext, dq, dk, dv = call(
            plain_back_kernel, outs, specs + [VMEM] * 4, [VMEM] * 6, scratch, flops=work,
            moved=40 * 2**20,
        )(*operands, q, k, v, lse, cosine, sine)
        out_rows = [near_a, to_rep(near_b, 1), to_rep(far_a, 2), to_rep(far_b, 3)]
        grad_in, outputs, gw, gain = call(
            plain_tail_kernel,
            [wide, token_f, shape((3, width, width)), shape((8, width), F32)],
            [VMEM] * 17,
            [VMEM] * 4,
            [pltpu.VMEM((tokens, width), BF), pltpu.VMEM((8, width), F32)],
            flops=2 * tokens * width * (6 * width + 4 * CAP),
            moved=40 * 2**20,
        )(
            x, ext, dq, dk, dv, wq, wk, wv, d_middle, slot, *out_rows, shared_out, probs, middle
        )

        def over_rep(total):
            return lax.psum(total.astype(BF), "rep").astype(F32)

        def unslot(every, part_units):
            every = every.reshape(SLOTS, 3, width, shards // SLOTS, part_units)
            every = every.transpose(0, 3, 1, 2, 4).reshape(shards, 3, width, part_units)
            return lax.psum_scatter(every, "shard", scatter_dimension=0)

        grad_q, grad_k, grad_v, grad_o = (
            over_rep(lax.psum_scatter(w, "shard", tiled=True))
            for w in (gw[0], gw[1], gw[2], grad_wo)
        )
        small = grad_ext.at[4].add(jnp.sum(gain, axis=0))
        small = lax.psum(small, ("rep", "shard"))
        shared_sum = grads_own.astype(F32) + to_rep(grads_other, 1).astype(F32)
        total = unslot(shared_sum.astype(BF), units // 2).astype(F32)
        total = (total + to_rep(total.astype(BF), 2).astype(F32)).astype(BF)
        mate = to_rep(total, 1)
        shared_full = jnp.concatenate(
            [jnp.where(core == 0, total, mate), jnp.where(core == 0, mate, total)], axis=2
        ).astype(F32)
        expert_total = unslot(grads, units).astype(BF)
        parts = jnp.stack([expert_total] + [to_rep(expert_total, o) for o in (1, 2, 3)])
        full = jnp.take(parts, jnp.arange(4) ^ rep, axis=0).astype(F32)
        finals = (full[:, 0], full[:, 1], full[:, 2].transpose(0, 2, 1))
        finals += (shared_full[0], shared_full[1], shared_full[2].T)
        tiny = lax.dynamic_slice(small, (0, shard * rows), (16, rows))
        gain_one, gain_two, grad_router = tiny[4], tiny[5], tiny[:4].T
    return (
        outputs[None],
        grad_in[None],
        gain_one,
        grad_q,
        grad_k,
        grad_v,
        grad_o,
        gain_two,
        grad_router,
        *finals,
    )


def solution(mesh):
    in_specs = (
        P(("rep", "shard"), None, None),
        P(("rep", "shard"), None),
        P(("rep", "shard"), None, None),
        P("shard"),
        P("shard", None),
        P("shard", None),
        P("shard", None),
        P("shard", None),
        P("shard"),
        P("shard", None),
        P(None, None, "shard"),
        P(None, None, "shard"),
        P(None, "shard", None),
        P(None, "shard"),
        P(None, "shard"),
        P("shard", None),
        P(("rep", "shard"), None, None),
    )
    out_specs = (
        P(("rep", "shard"), None, None),
        P(("rep", "shard"), None, None),
        P("shard"),
        P("shard", None),
        P("shard", None),
        P("shard", None),
        P("shard", None),
        P("shard"),
        P("shard", None),
        P(None, None, "shard"),
        P(None, None, "shard"),
        P(None, "shard", None),
        P(None, "shard"),
        P(None, "shard"),
        P("shard", None),
    )
    return jax.shard_map(body, mesh=mesh, in_specs=in_specs, out_specs=out_specs, check_vma=False)
```
